32 devices in a mesh: dp: 8 (over z, y), rep: 4 (over x, core).
Axes of the slice: x: 2, y: 2, z: 4, core: 2. Of those that a mesh axis runs over, the one named last changes fastest.
Arguments:
- hidden_in: bfloat16 [32768, 768], P(('dp', 'rep')), may hold values from -6 to 6
- segments: int32 [64, 512], P(('dp', 'rep')), may hold values from 0 to 15, never falling along the last dimension, each value on 1 to 64 neighbouring positions
- partner: int32 [1024], P(('dp', 'rep')), may hold values from 0 to 1023, as said below
- attn_weights: float32 [768, 3072], P(None, ('dp', 'rep'))
- ffn_weights: float32 [768, 6144], P(None, ('dp', 'rep'))
- vectors: float32 [9216], P(('dp', 'rep'))
- attn_momentum: float32 [768, 3072], P(None, ('dp', 'rep')), may hold values from -6 to 6
- ffn_momentum: float32 [768, 6144], P(None, ('dp', 'rep')), may hold values from -6 to 6
- vector_momentum: float32 [9216], P(('dp', 'rep')), may hold values from -6 to 6
- attn_averaged: float32 [768, 3072], P(None, ('dp', 'rep')), may hold values from -0.21875 to 0.21875
- ffn_averaged: float32 [768, 6144], P(None, ('dp', 'rep')), may hold values from -0.21875 to 0.21875
- vector_averaged: float32 [9216], P(('dp', 'rep')), may hold values from -4 to 4
Outputs:
- mean_loss: float32 [], replicated
- input_grad: float32 [32768, 768], P(('dp', 'rep'))
- attn_grad: float32 [768, 3072], P(None, ('dp', 'rep'))
- ffn_grad: float32 [768, 6144], P(None, ('dp', 'rep'))
- vector_grad: float32 [9216], P(('dp', 'rep'))
- attn_new: float32 [768, 3072], P(None, ('dp', 'rep'))
- ffn_new: float32 [768, 6144], P(None, ('dp', 'rep'))
- vector_new: float32 [9216], P(('dp', 'rep'))
- attn_moment: float32 [768, 3072], P(None, ('dp', 'rep'))
- ffn_moment: float32 [768, 6144], P(None, ('dp', 'rep'))
- vector_moment: float32 [9216], P(('dp', 'rep'))
- attn_average: float32 [768, 3072], P(None, ('dp', 'rep'))
- ffn_average: float32 [768, 6144], P(None, ('dp', 'rep'))
- vector_average: float32 [9216], P(('dp', 'rep'))
The draws below stay inside these ranges and needn't reach their ends.
Inputs may be any that keep to these rules, and one draw needn't show every extreme that they name: `segments`: in each row the segment numbers never fall; every number of 0 to 15 covers 1 to 64 positions, and some number covers exactly 64. partner pairs the texts: partner[partner[t]] = t and partner[t] != t for every text t.
All inputs are finite; a program needn't handle non-finite values.
Results may differ from the reference program's by a relative error of at most 0.01.
The reference program's roundings to bfloat16 on the way count: a program that leaves them out, or rounds other values in their place, can miss the bound.
Values may be sent and summed in bfloat16 or wider, within the bound.
A program may use at most 192 MiB of HBM per device.

```python
import math
import jax
import jax.numpy as jnp
import numpy as np
from jax import lax

D = 768
HEADS = 12
HD = 64
FF = 3072
SEQ = 512
SEGS = 16
SEG_MOST = 64
ROWS = 64
TOKENS = 32768
TEXTS = 1024
VECS = 9216


def base_draw(key, shape):
    return jax.random.normal(key, shape, jnp.float32)


def draw_attn_weights(key, part):
    values = base_draw(key, (D, 4 * D))
    column = jnp.arange(4 * D)
    factor = jnp.where(column < 3 * D, 1.0, 4.0) / math.sqrt(D)
    return values * factor[None, :]


def draw_ffn_weights(key, part):
    values = base_draw(key, (D, 2 * FF))
    column = jnp.arange(2 * FF)
    factor = jnp.where(column < FF, 1.0 / math.sqrt(D), 1.0 / math.sqrt(FF))
    return values * factor[None, :]


def draw_vectors(key, part):
    total_len = 8 * D + FF
    position = jnp.arange(total_len)
    is_gain = (position >= 3 * D) & (position < 4 * D) | (position >= 6 * D + FF) & (position < 7 * D + FF)
    gain_part = 1.0 + 0.3 * jax.random.uniform(jax.random.fold_in(key, 1), (total_len,), jnp.float32, -1.0, 1.0)
    bias_part = 0.1 * base_draw(jax.random.fold_in(key, 2), (total_len,))
    return jnp.where(is_gain, gain_part, bias_part)


def draw_partner(key, part):
    order = jax.random.permutation(key, TEXTS).astype(jnp.int32)
    firsts = order[0::2]
    seconds = order[1::2]
    paired = jnp.zeros((TEXTS,), jnp.int32)
    paired = paired.at[firsts].set(seconds)
    return paired.at[seconds].set(firsts)


def shard_levels(key, shape, shards, low, largest):
    level = 1.0
    for dim, parts in shards:
        steps = jax.random.uniform(jax.random.fold_in(jax.random.fold_in(key, 6), dim), (parts,), jnp.float32, low / len(shards), largest / len(shards))
        level = level * jnp.repeat(jnp.exp(steps), shape[dim] // parts).reshape((-1,) + (1,) * (len(shape) - 1 - dim))
    return level


def length_profile(number_of, total, bound, slope):
    portions = [(1 << 20) // math.isqrt(standing ** slope) + 1 for standing in range(2, number_of + 1)]
    rest, given = total - bound - (number_of - 1), [1] * (number_of - 1)
    while rest > 0:
        free = [i for i in range(number_of - 1) if given[i] < bound]
        pool, budget = sum([portions[i] for i in free]), rest
        for i in free:
            addition = min(bound - given[i], max(1, budget * portions[i] // pool), rest)
            given[i] = given[i] + addition
            rest = rest - addition
    return np.array([bound] + given)


def uneven(stream_key, count, total, reach, slope):
    if count == 2:
        one = jax.random.randint(stream_key, (), max(1, total - reach), min(reach, total - 1) + 1)
        return jnp.stack([one, total - one])
    sizes = jnp.asarray(length_profile(count, total, reach, slope), jnp.int32)
    couples = (count - 1) // 2
    giver, sink = sizes[1:1 + 2 * couples:2], sizes[2:2 + 2 * couples:2]
    room = jnp.minimum(giver - 1, reach - sink)
    passed = jax.random.randint(jax.random.fold_in(stream_key, 1), (couples,), 0, 1 << 20) % (room + 1)
    sizes = sizes.at[1:1 + 2 * couples:2].set(giver - passed).at[2:2 + 2 * couples:2].set(sink + passed)
    return sizes[jax.random.permutation(jax.random.fold_in(stream_key, 2), count)]


def gaussian(stream_key, dims, width, bound, pieces=(), dtype=jnp.bfloat16):
    level = shard_levels(stream_key, dims, pieces, -0.22, 0.18) if pieces else 1.0
    entries = jax.random.normal(stream_key, dims, jnp.float32) * width * level
    return jnp.minimum(jnp.maximum(entries, -bound), bound).astype(dtype)


def setup_inputs(seed: int = 0) -> dict:
    arg_keys = jax.random.split(jax.random.key(seed), 13)
    hidden_in = gaussian(arg_keys[0], (TOKENS, D), 1.0, 6.0, ((0, 32),))
    segments = jax.vmap(lambda own: jnp.searchsorted(jnp.cumsum(uneven(own, SEGS, SEQ, SEG_MOST, 2)), jnp.arange(SEQ), side="right"))(jax.random.split(arg_keys[1], ROWS)).reshape((ROWS, SEQ)).astype(jnp.int32)
    partner = draw_partner(jax.random.fold_in(arg_keys[12], 71), 0)
    attn_weights = draw_attn_weights(jax.random.fold_in(arg_keys[12], 71), 0)
    ffn_weights = draw_ffn_weights(jax.random.fold_in(arg_keys[12], 71), 0)
    vectors = draw_vectors(jax.random.fold_in(arg_keys[12], 71), 0)
    attn_momentum = gaussian(arg_keys[6], (D, 4 * D), (0.004 * TOKENS ** 0.5), 6.0, ((1, 32),), jnp.float32)
    ffn_momentum = gaussian(arg_keys[7], (D, 2 * FF), (0.004 * TOKENS ** 0.5), 6.0, ((1, 32),), jnp.float32)
    vector_momentum = gaussian(arg_keys[8], (VECS,), (0.004 * TOKENS ** 0.5), 6.0, ((0, 32),), jnp.float32)
    attn_averaged = gaussian(arg_keys[9], (D, 4 * D), D ** -0.5, 0.21875, ((1, 32),), jnp.float32)
    ffn_averaged = gaussian(arg_keys[10], (D, 2 * FF), D ** -0.5, 0.21875, ((1, 32),), jnp.float32)
    vector_averaged = gaussian(arg_keys[11], (VECS,), 0.5, 4.0, ((0, 32),), jnp.float32)
    return dict(hidden_in=hidden_in, segments=segments, partner=partner, attn_weights=attn_weights, ffn_weights=ffn_weights, vectors=vectors, attn_momentum=attn_momentum, ffn_momentum=ffn_momentum, vector_momentum=vector_momentum, attn_averaged=attn_averaged, ffn_averaged=ffn_averaged, vector_averaged=vector_averaged)


@jax.custom_vjp
def low(v):
    return lax.optimization_barrier(v.astype(jnp.bfloat16)).astype(jnp.float32)

@jax.custom_vjp
def lowbit_pullback_pass(v):
    return v

def low_keep(v):
    return (low(v), None)

def low_pass(kept, grad):
    return (grad,)

def back_keep(v):
    return (v, None)

def back_low(kept, grad):
    return (low(grad),)
low.defvjp(low_keep, low_pass)
lowbit_pullback_pass.defvjp(back_keep, back_low)
ln_epsilon = 1e-12
pool_epsilon = 1e-06
logit_divisor = 0.025
learn_rate = 0.01
momentum_rate = 0.9
decay_rate = 0.01
average_rate = 0.75
masked_value = -1e+30
finest_arithmetic = lax.Precision.HIGHEST

def layer_norm(values, gain, shift):
    per_line_average = lax.optimization_barrier(jnp.mean(values, -1, keepdims=True))
    centred = values - per_line_average
    variance = lax.optimization_barrier(jnp.mean(centred * centred, -1, keepdims=True))
    return centred * lax.rsqrt(variance + ln_epsilon) * gain + shift

def block_rows(attn_w, ffn_w, vector_all, rows_in, row_segments):
    group_size = rows_in.shape[0]
    tokens_in = rows_in.reshape(group_size * SEQ, D)
    query_bias = vector_all[0:D]
    value_bias = vector_all[D:2 * D]
    output_bias = vector_all[2 * D:3 * D]
    gain_first = vector_all[3 * D:4 * D]
    shift_first = vector_all[4 * D:5 * D]
    upper_bias = vector_all[5 * D:5 * D + FF]
    lower_bias = vector_all[5 * D + FF:6 * D + FF]
    gain_second = vector_all[6 * D + FF:7 * D + FF]
    shift_second = vector_all[7 * D + FF:8 * D + FF]
    w_qkv = attn_w[:, :3 * D]
    w_output = attn_w[:, 3 * D:]
    w_upper = ffn_w[:, :FF]
    w_lower = ffn_w[:, FF:]
    qkv_bias = jnp.concatenate([query_bias, jnp.zeros((D,), jnp.float32), value_bias])
    qkv_rows = lowbit_pullback_pass(low(jnp.dot(tokens_in, w_qkv, precision=finest_arithmetic) + qkv_bias))
    heads = qkv_rows.reshape(group_size, SEQ, 3, HEADS, HD)
    query_rows = heads[:, :, 0]
    key_rows = heads[:, :, 1]
    value_rows = heads[:, :, 2]
    scores = lowbit_pullback_pass(jnp.einsum('gqhd,gkhd->ghqk', query_rows, key_rows, precision=finest_arithmetic) * (1.0 / math.sqrt(HD)))
    same_text = row_segments[:, None, :, None] == row_segments[:, None, None, :]
    scores = jnp.where(same_text, scores, masked_value)
    shifted = scores - lax.optimization_barrier(jnp.max(scores, -1, keepdims=True))
    exp_scores = jnp.exp(shifted)
    attn_probs = exp_scores / lax.optimization_barrier(jnp.sum(exp_scores, -1, keepdims=True))
    mixed = jnp.einsum('ghqk,gkhd->gqhd', low(attn_probs), value_rows, precision=finest_arithmetic)
    mixed = lowbit_pullback_pass(low(mixed.reshape(group_size * SEQ, D)))
    branch = lowbit_pullback_pass(jnp.dot(mixed, w_output, precision=finest_arithmetic)) + output_bias
    normed = low(layer_norm(tokens_in + branch, gain_first, shift_first))
    upper = lowbit_pullback_pass(jnp.dot(normed, w_upper, precision=finest_arithmetic)) + upper_bias
    active = low(jax.nn.gelu(upper, approximate=False))
    lowered = lowbit_pullback_pass(lax.dot_general(active, w_lower, (((1,), (1,)), ((), ())), precision=finest_arithmetic)) + lower_bias
    result = layer_norm(normed + lowered, gain_second, shift_second)
    text_ids = jnp.arange(SEGS)
    one_hot = (row_segments[:, None, :] == text_ids[None, :, None]).astype(jnp.float32)
    counts = lax.optimization_barrier(jnp.sum(one_hot, -1, keepdims=True))
    pooled = jnp.einsum('gts,gsd->gtd', one_hot, result.reshape(group_size, SEQ, D), precision=finest_arithmetic) / counts
    return pooled.reshape(group_size * SEGS, D)

def apply_update(weight, grad, moment, average, decay):
    step_grad = grad + decay * weight
    new_moment = momentum_rate * moment + step_grad
    new_weight = weight - learn_rate * (step_grad + momentum_rate * new_moment)
    fresh_running_mean = average_rate * average + (1.0 - average_rate) * new_weight
    return (new_weight, new_moment, fresh_running_mean)

def reference(hidden_in, segments, partner, attn_weights, ffn_weights, vectors, attn_momentum, ffn_momentum, vector_momentum, attn_averaged, ffn_averaged, vector_averaged):
    inputs = hidden_in.astype(jnp.float32)
    rows_total = inputs.shape[0] // SEQ
    group_size = math.gcd(rows_total, 8)
    checked = jax.checkpoint(block_rows)

    def objective(attn_w, ffn_w, vector_all, tokens_all):
        attn_low = low(attn_w)
        ffn_low = low(ffn_w)
        vector_low = low(vector_all)
        grouped = tokens_all.reshape(rows_total // group_size, group_size, SEQ, D)
        grouped_segments = segments.reshape(rows_total // group_size, group_size, SEQ)
        pooled = lax.map(lambda group_args: checked(attn_low, ffn_low, vector_low, group_args[0], group_args[1]), (grouped, grouped_segments))
        pooled = pooled.reshape(-1, D)
        inv_norm = lax.rsqrt(lax.optimization_barrier(jnp.sum(pooled * pooled, -1, keepdims=True)) + pool_epsilon)
        passage_vectors = low(pooled * inv_norm)
        cosine_logits = lowbit_pullback_pass(jnp.dot(passage_vectors, passage_vectors.T, precision=finest_arithmetic) / logit_divisor)
        index_cols = jnp.arange(cosine_logits.shape[0])
        self_pair = index_cols[:, None] == index_cols[None, :]
        masked = jnp.where(self_pair, masked_value, cosine_logits)
        row_max = lax.optimization_barrier(jnp.max(masked, -1))
        log_norm = row_max + jnp.log(lax.optimization_barrier(jnp.sum(jnp.exp(masked - row_max[:, None]), -1)))
        positive = lax.optimization_barrier(jnp.sum(jnp.where(index_cols[None, :] == partner[:, None], cosine_logits, 0.0), -1))
        return jnp.sum(log_norm - positive)
    total, pullback = jax.vjp(objective, attn_weights, ffn_weights, vectors, inputs)
    attn_grad, ffn_grad, vector_grad, input_grad = pullback(jnp.ones((), jnp.float32))
    mean_loss = total / partner.shape[0]
    attn_new, attn_moment, attn_average = apply_update(attn_weights, attn_grad, attn_momentum, attn_averaged, decay_rate)
    ffn_new, ffn_moment, ffn_average = apply_update(ffn_weights, ffn_grad, ffn_momentum, ffn_averaged, decay_rate)
    vector_new, vector_moment, vector_average = apply_update(vectors, vector_grad, vector_momentum, vector_averaged, 0.0)
    return (mean_loss, input_grad, attn_grad, ffn_grad, vector_grad, attn_new, ffn_new, vector_new, attn_moment, ffn_moment, vector_moment, attn_average, ffn_average, vector_average)
```

```python
import functools
import math

import jax
import jax.numpy as jnp
from jax import lax
from jax.experimental import pallas as pl
from jax.experimental.pallas import tpu as pltpu
from jax.sharding import PartitionSpec as P

MESH = pl.DeviceIdType.MESH
AXES = ("dp", "rep")

HEADS = 12
HD = 64
SEGS = 16


ln_epsilon = 1e-12
pool_epsilon = 1e-06
logit_divisor = 0.025
learn_rate = 0.01
momentum_rate = 0.9
decay_rate = 0.01
average_rate = 0.75
masked_value = -1e30


def layer_norm_parts(values, gain, shift):
    per_line_average = jnp.mean(values, -1, keepdims=True)
    centred = values - per_line_average
    inverse = lax.rsqrt(jnp.mean(centred * centred, -1, keepdims=True) + ln_epsilon)
    normal_part = centred * inverse
    return (normal_part * gain + shift, normal_part, inverse)


def layer_norm_back(grad_out, normal_part, inverse, gain):
    scaled = grad_out * gain
    grad_in = inverse * (
        scaled
        - jnp.mean(scaled, -1, keepdims=True)
        - normal_part * jnp.mean(scaled * normal_part, -1, keepdims=True)
    )
    return (grad_in, jnp.sum(grad_out * normal_part, 0), jnp.sum(grad_out, 0))


def row_scores(query_one, key_one, segment_one, scale):
    scores = (
        jnp.einsum("qhd,khd->hqk", query_one, key_one, preferred_element_type=jnp.float32) * scale
    )
    same_text = segment_one[:, None] == segment_one[None, :]
    return jnp.where(same_text[None], scores, masked_value)


def attend_rows(query_rows, key_rows, value_rows, row_segments):
    scale = 1.0 / math.sqrt(query_rows.shape[-1])

    def one_row(row_args):
        query_one, key_one, value_one, segment_one = row_args
        scores = row_scores(query_one, key_one, segment_one, scale)
        row_max = jnp.max(scores, -1, keepdims=True)
        exp_scores = jnp.exp(scores - row_max)
        sums = jnp.sum(exp_scores, -1, keepdims=True)
        attn_probs = exp_scores / sums
        mixed = jnp.einsum(
            "hqk,khd->qhd",
            attn_probs.astype(jnp.bfloat16),
            value_one,
            preferred_element_type=jnp.float32,
        )
        return (mixed.astype(jnp.bfloat16), (row_max + jnp.log(sums))[..., 0])

    return lax.map(one_row, (query_rows, key_rows, value_rows, row_segments))


def attend_back(query_rows, key_rows, value_rows, row_segments, log_norm, grad_mixed):
    scale = 1.0 / math.sqrt(query_rows.shape[-1])

    def one_row(row_args):
        query_one, key_one, value_one, segment_one, norm_one, grad_one = row_args
        scores = row_scores(query_one, key_one, segment_one, scale)
        attn_probs = jnp.exp(scores - norm_one[..., None])
        grad_value = jnp.einsum(
            "hqk,qhd->khd",
            attn_probs.astype(jnp.bfloat16),
            grad_one,
            preferred_element_type=jnp.float32,
        )
        grad_probs = jnp.einsum(
            "qhd,khd->hqk", grad_one, value_one, preferred_element_type=jnp.float32
        )
        inner = jnp.sum(attn_probs * grad_probs, -1, keepdims=True)
        grad_scores = (attn_probs * (grad_probs - inner)).astype(jnp.bfloat16)
        grad_query = (
            jnp.einsum("hqk,khd->qhd", grad_scores, key_one, preferred_element_type=jnp.float32)
            * scale
        )
        grad_key = (
            jnp.einsum("hqk,qhd->khd", grad_scores, query_one, preferred_element_type=jnp.float32)
            * scale
        )
        return jnp.concatenate([grad_query, grad_key, grad_value], axis=1)

    return lax.map(one_row, (query_rows, key_rows, value_rows, row_segments, log_norm, grad_mixed))


def apply_update(weight, grad, moment, average, decay):
    step_grad = grad + decay * weight
    new_moment = momentum_rate * moment + step_grad
    new_weight = weight - learn_rate * (step_grad + momentum_rate * new_moment)
    fresh_running_mean = average_rate * average + (1.0 - average_rate) * new_weight
    return (new_weight, new_moment, fresh_running_mean)


def flat_index(sizes):
    idx = 0
    for name, size in zip(AXES, sizes):
        idx = idx * size + lax.axis_index(name)
    return idx


def device_of(flat, sizes):
    coords = []
    for size in reversed(sizes):
        coords.append(lax.rem(flat, size))
        flat = flat // size
    return tuple(reversed(coords))


def enter_all(n, sizes, me):
    barrier = pltpu.get_barrier_semaphore()

    def greet(k, carry):
        peer = lax.rem(me + k, n)
        pl.semaphore_signal(barrier, inc=1, device_id=device_of(peer, sizes), device_id_type=MESH)
        return carry

    lax.fori_loop(1, n, greet, 0)
    pl.semaphore_wait(barrier, n - 1)


def gather_kernel(n, sizes, x_ref, out_ref, send_sem, recv_sem):
    me = flat_index(sizes)
    enter_all(n, sizes, me)

    def send(k, carry):
        peer = lax.rem(me + k, n)
        pltpu.make_async_remote_copy(
            src_ref=x_ref, dst_ref=out_ref.at[me], send_sem=send_sem.at[k], recv_sem=recv_sem.at[me],
            device_id=device_of(peer, sizes), device_id_type=MESH,
        ).start()
        return carry

    lax.fori_loop(1, n, send, 0)
    out_ref[me] = x_ref[...]

    def finish(k, carry):
        peer = lax.rem(me + k, n)
        src = lax.rem(me + n - k, n)
        pltpu.make_async_remote_copy(
            src_ref=x_ref, dst_ref=out_ref.at[me], send_sem=send_sem.at[k], recv_sem=recv_sem.at[me],
            device_id=device_of(peer, sizes), device_id_type=MESH,
        ).wait_send()
        pltpu.make_async_remote_copy(
            src_ref=x_ref, dst_ref=out_ref.at[src], send_sem=send_sem.at[k], recv_sem=recv_sem.at[src],
            device_id=device_of(src, sizes), device_id_type=MESH,
        ).wait_recv()
        return carry

    lax.fori_loop(1, n, finish, 0)


def small_gather(x, sizes, cid):
    n = math.prod(sizes)
    return pl.pallas_call(
        functools.partial(gather_kernel, n, sizes),
        out_shape=jax.ShapeDtypeStruct((n,) + x.shape, x.dtype),
        in_specs=[pl.BlockSpec(memory_space=pltpu.VMEM)],
        out_specs=pl.BlockSpec(memory_space=pltpu.VMEM),
        scratch_shapes=[pltpu.SemaphoreType.DMA((n,)), pltpu.SemaphoreType.DMA((n,))],
        compiler_params=pltpu.CompilerParams(collective_id=cid, has_side_effects=True),
    )(x)


def scatter_kernel(n, sizes, x_ref, out_ref, send_sem, recv_sem):
    me = flat_index(sizes)
    enter_all(n, sizes, me)

    def send(k, carry):
        peer = lax.rem(me + k, n)
        pltpu.make_async_remote_copy(
            src_ref=x_ref.at[peer], dst_ref=out_ref.at[me], send_sem=send_sem.at[k], recv_sem=recv_sem.at[me],
            device_id=device_of(peer, sizes), device_id_type=MESH,
        ).start()
        return carry

    lax.fori_loop(1, n, send, 0)
    out_ref[me] = x_ref[me]

    def finish(k, carry):
        peer = lax.rem(me + k, n)
        src = lax.rem(me + n - k, n)
        pltpu.make_async_remote_copy(
            src_ref=x_ref.at[peer], dst_ref=out_ref.at[me], send_sem=send_sem.at[k], recv_sem=recv_sem.at[me],
            device_id=device_of(peer, sizes), device_id_type=MESH,
        ).wait_send()
        pltpu.make_async_remote_copy(
            src_ref=x_ref.at[src], dst_ref=out_ref.at[src], send_sem=send_sem.at[k], recv_sem=recv_sem.at[src],
            device_id=device_of(src, sizes), device_id_type=MESH,
        ).wait_recv()
        return carry

    lax.fori_loop(1, n, finish, 0)


def small_scatter(x, sizes, cid):
    n = math.prod(sizes)
    return pl.pallas_call(
        functools.partial(scatter_kernel, n, sizes),
        out_shape=jax.ShapeDtypeStruct(x.shape, x.dtype),
        in_specs=[pl.BlockSpec(memory_space=pltpu.VMEM)],
        out_specs=pl.BlockSpec(memory_space=pltpu.VMEM),
        scratch_shapes=[pltpu.SemaphoreType.DMA((n,)), pltpu.SemaphoreType.DMA((n,))],
        compiler_params=pltpu.CompilerParams(collective_id=cid, has_side_effects=True),
    )(x)


def contrastive(embed_b, gathered, partner_all, me):
    own_texts = embed_b.shape[0]
    all_texts = gathered.shape[0]
    chunk = min(all_texts, 1024)
    on_rows = (((1,), (1,)), ((), ()))

    def chunk_stats(c):
        rows_b = lax.dynamic_slice_in_dim(gathered, c * chunk, chunk)
        sim = lax.dot_general(rows_b, gathered, on_rows, preferred_element_type=jnp.float32) / logit_divisor
        column_ids = lax.broadcasted_iota(jnp.int32, sim.shape, 1)
        row_ids = lax.broadcasted_iota(jnp.int32, sim.shape, 0) + c * chunk
        masked = jnp.where(column_ids == row_ids, masked_value, sim)
        row_max = jnp.max(masked, -1, keepdims=True)
        log_sum = row_max + jnp.log(jnp.sum(jnp.exp(masked - row_max), -1, keepdims=True))
        wanted = lax.dynamic_slice_in_dim(partner_all, c * chunk, chunk)
        positive = jnp.sum(jnp.where(column_ids == wanted[:, None], sim, 0.0), -1)
        return log_sum[:, 0], positive

    if all_texts == chunk:
        log_sum_all, positive_all = chunk_stats(0)
    else:
        log_sum_all, positive_all = lax.map(chunk_stats, jnp.arange(all_texts // chunk))
        log_sum_all = log_sum_all.reshape(-1)
        positive_all = positive_all.reshape(-1)
    mean_loss = jnp.sum(log_sum_all - positive_all) / all_texts

    own_start = me * own_texts
    own_ids = lax.broadcasted_iota(jnp.int32, (own_texts,), 0) + own_start
    own_partner = lax.dynamic_slice_in_dim(partner_all, own_start, own_texts)
    own_log_sum = lax.dynamic_slice_in_dim(log_sum_all, own_start, own_texts)

    sim_rows = lax.dot_general(embed_b, gathered, on_rows, preferred_element_type=jnp.float32) / logit_divisor
    column_ids = lax.broadcasted_iota(jnp.int32, sim_rows.shape, 1)
    masked_rows = jnp.where(column_ids == own_ids[:, None], masked_value, sim_rows)
    grad_rows = (
        jnp.exp(masked_rows - own_log_sum[:, None]) - (column_ids == own_partner[:, None]).astype(jnp.float32)
    ).astype(jnp.bfloat16)

    sim_cols = lax.dot_general(gathered, embed_b, on_rows, preferred_element_type=jnp.float32) / logit_divisor
    row_ids = lax.broadcasted_iota(jnp.int32, sim_cols.shape, 0)
    masked_cols = jnp.where(row_ids == own_ids[None, :], masked_value, sim_cols)
    grad_cols = (
        jnp.exp(masked_cols - log_sum_all[:, None]) - (partner_all[:, None] == own_ids[None, :]).astype(jnp.float32)
    ).astype(jnp.bfloat16)

    on_tokens = (((0,), (0,)), ((), ()))
    embedding_gradient = (
        jnp.dot(grad_rows, gathered, preferred_element_type=jnp.float32)
        + lax.dot_general(grad_cols, gathered, on_tokens, preferred_element_type=jnp.float32)
    ) / logit_divisor
    return mean_loss, embedding_gradient


def shards(
    hidden_in,
    segments,
    partner,
    attn_weights,
    ffn_weights,
    vectors,
    attn_momentum,
    ffn_momentum,
    vector_momentum,
    attn_averaged,
    ffn_averaged,
    vector_averaged,
):
    sizes = tuple(lax.axis_size(name) for name in AXES)
    n_dev = math.prod(sizes)
    me = flat_index(sizes)
    vec_len = vectors.shape[0]
    small = jnp.concatenate([vectors, partner.astype(jnp.float32)])[None, :]
    small_all = small_gather(small, sizes, 0)[:, 0, :]
    vector_full = small_all[:, :vec_len].reshape(-1).astype(jnp.bfloat16)
    partner_all = small_all[:, vec_len:].reshape(-1).astype(jnp.int32)
    attn_full, ffn_full = (
        lax.all_gather(attn_weights.astype(jnp.bfloat16), AXES, axis=1, tiled=True),
        lax.all_gather(ffn_weights.astype(jnp.bfloat16), AXES, axis=1, tiled=True),
    )
    width = attn_full.shape[0]
    hidden = ffn_full.shape[1] // 2
    vector_f = vector_full.astype(jnp.float32)
    query_bias = vector_f[0:width]
    value_bias = vector_f[width : 2 * width]
    output_bias = vector_f[2 * width : 3 * width]
    gain_first = vector_f[3 * width : 4 * width]
    shift_first = vector_f[4 * width : 5 * width]
    upper_bias = vector_f[5 * width : 5 * width + hidden]
    lower_bias = vector_f[5 * width + hidden : 6 * width + hidden]
    gain_second = vector_f[6 * width + hidden : 7 * width + hidden]
    shift_second = vector_f[7 * width + hidden : 8 * width + hidden]
    w_qkv = attn_full[:, : 3 * width]
    w_output = attn_full[:, 3 * width :]
    w_upper = ffn_full[:, :hidden]
    w_lower = ffn_full[:, hidden:]
    rows_dev, seq_len = segments.shape
    tokens_n = rows_dev * seq_len
    on_rows = (((1,), (1,)), ((), ()))
    on_tokens = (((0,), (0,)), ((), ()))
    qkv_bias = jnp.concatenate([query_bias, jnp.zeros_like(query_bias), value_bias])
    qkv_rows = (jnp.dot(hidden_in, w_qkv, preferred_element_type=jnp.float32) + qkv_bias).astype(
        jnp.bfloat16
    )
    heads = qkv_rows.reshape(rows_dev, seq_len, 3, HEADS, HD)
    query_rows = heads[:, :, 0]
    key_rows = heads[:, :, 1]
    value_rows = heads[:, :, 2]
    mixed, log_norm = attend_rows(query_rows, key_rows, value_rows, segments)
    mixed_flat = mixed.reshape(tokens_n, width)
    first_sum = (
        hidden_in.astype(jnp.float32)
        + jnp.dot(mixed_flat, w_output, preferred_element_type=jnp.float32)
        + output_bias
    )
    normed, normal_one, inverse_one = layer_norm_parts(first_sum, gain_first, shift_first)
    normed_b = normed.astype(jnp.bfloat16)
    upper = jnp.dot(normed_b, w_upper, preferred_element_type=jnp.float32) + upper_bias
    active_b = jax.nn.gelu(upper, approximate=False).astype(jnp.bfloat16)
    second_sum = (
        normed_b.astype(jnp.float32)
        + lax.dot_general(active_b, w_lower, on_rows, preferred_element_type=jnp.float32)
        + lower_bias
    )
    result, normal_two, inverse_two = layer_norm_parts(second_sum, gain_second, shift_second)
    text_ids = jnp.arange(SEGS, dtype=jnp.int32)
    one_hot = (segments[:, None, :] == text_ids[None, :, None]).astype(jnp.float32)
    counts = jnp.sum(one_hot, -1, keepdims=True)
    pooled = (
        jnp.einsum(
            "rts,rsd->rtd",
            one_hot,
            result.reshape(rows_dev, seq_len, width),
            precision=lax.Precision.HIGHEST,
        )
        / counts
    ).reshape(-1, width)
    inv_norm = lax.rsqrt(jnp.sum(pooled * pooled, -1, keepdims=True) + pool_epsilon)
    embed_b = (pooled * inv_norm).astype(jnp.bfloat16)
    gathered_embeddings = lax.all_gather(embed_b, AXES, axis=0, tiled=True)
    mean_loss, embedding_gradient = contrastive(embed_b, gathered_embeddings, partner_all, me)
    grad_pooled = inv_norm * embedding_gradient - pooled * (
        inv_norm * inv_norm * inv_norm
    ) * jnp.sum(embedding_gradient * pooled, -1, keepdims=True)
    derivative_output = jnp.einsum(
        "rts,rtd->rsd",
        one_hot,
        grad_pooled.reshape(rows_dev, SEGS, width) / counts,
        precision=lax.Precision.HIGHEST,
    ).reshape(tokens_n, width)
    grad_second, gain_two_grad, shift_two_grad = layer_norm_back(
        derivative_output, normal_two, inverse_two, gain_second
    )
    lower_bias_grad = jnp.sum(grad_second, 0)
    lower_grad_b = grad_second.astype(jnp.bfloat16)
    lower_w_grad = lax.dot_general(
        lower_grad_b, active_b, on_tokens, preferred_element_type=jnp.float32
    )
    grad_active = jnp.dot(lower_grad_b, w_lower, preferred_element_type=jnp.float32)
    cumulative = 0.5 * (1.0 + lax.erf(upper / math.sqrt(2.0)))
    density = jnp.exp(-0.5 * upper * upper) / math.sqrt(2.0 * math.pi)
    grad_upper = grad_active * (cumulative + upper * density)
    upper_bias_grad = jnp.sum(grad_upper, 0)
    upper_grad_b = grad_upper.astype(jnp.bfloat16)
    upper_w_grad = lax.dot_general(
        normed_b, upper_grad_b, on_tokens, preferred_element_type=jnp.float32
    )
    ffn_grad = jnp.concatenate([upper_w_grad, lower_w_grad], 1)
    grad_normed = (
        lax.dot_general(upper_grad_b, w_upper, on_rows, preferred_element_type=jnp.float32)
        + grad_second
    )
    grad_first, gain_one_grad, shift_one_grad = layer_norm_back(
        grad_normed, normal_one, inverse_one, gain_first
    )
    output_bias_grad = jnp.sum(grad_first, 0)
    first_grad_b = grad_first.astype(jnp.bfloat16)
    output_w_grad = lax.dot_general(
        mixed_flat, first_grad_b, on_tokens, preferred_element_type=jnp.float32
    )
    grad_mixed = lax.dot_general(
        first_grad_b, w_output, on_rows, preferred_element_type=jnp.float32
    ).astype(jnp.bfloat16)
    grad_mixed = grad_mixed.reshape(rows_dev, seq_len, HEADS, HD)
    qkv_grad = attend_back(
        query_rows, key_rows, value_rows, segments, log_norm, grad_mixed
    ).reshape(tokens_n, 3 * width)
    qkv_grad_b = qkv_grad.astype(jnp.bfloat16)
    qkv_grad_f = qkv_grad_b.astype(jnp.float32)
    query_bias_grad = jnp.sum(qkv_grad_f[:, :width], 0)
    value_bias_grad = jnp.sum(qkv_grad_f[:, 2 * width :], 0)
    qkv_w_grad = lax.dot_general(
        hidden_in, qkv_grad_b, on_tokens, preferred_element_type=jnp.float32
    )
    input_grad = (
        lax.dot_general(qkv_grad_b, w_qkv, on_rows, preferred_element_type=jnp.float32) + grad_first
    )
    attn_grad = jnp.concatenate([qkv_w_grad, output_w_grad], 1)
    vector_grad = jnp.concatenate(
        [
            query_bias_grad,
            value_bias_grad,
            output_bias_grad,
            gain_one_grad,
            shift_one_grad,
            upper_bias_grad,
            lower_bias_grad,
            gain_two_grad,
            shift_two_grad,
        ]
    )
    vector_slots = small_scatter(vector_grad.reshape(n_dev, 1, -1), sizes, 1)
    vector_reduced = jnp.sum(vector_slots[:, 0, :], 0)
    attn_reduced, ffn_reduced = (
        lax.psum_scatter(attn_grad, AXES, scatter_dimension=1, tiled=True),
        lax.psum_scatter(ffn_grad, AXES, scatter_dimension=1, tiled=True),
    )
    attn_new, attn_moment, attn_average = apply_update(
        attn_weights, attn_reduced, attn_momentum, attn_averaged, decay_rate
    )
    ffn_new, ffn_moment, ffn_average = apply_update(
        ffn_weights, ffn_reduced, ffn_momentum, ffn_averaged, decay_rate
    )
    vector_new, vector_moment, vector_average = apply_update(
        vectors, vector_reduced, vector_momentum, vector_averaged, 0.0
    )
    return (
        mean_loss,
        input_grad,
        attn_reduced,
        ffn_reduced,
        vector_reduced,
        attn_new,
        ffn_new,
        vector_new,
        attn_moment,
        ffn_moment,
        vector_moment,
        attn_average,
        ffn_average,
        vector_average,
    )


def solution(mesh):
    in_specs = (
        P(("dp", "rep"), None),
        P(("dp", "rep"), None),
        P(("dp", "rep")),
        P(None, ("dp", "rep")),
        P(None, ("dp", "rep")),
        P(("dp", "rep")),
        P(None, ("dp", "rep")),
        P(None, ("dp", "rep")),
        P(("dp", "rep")),
        P(None, ("dp", "rep")),
        P(None, ("dp", "rep")),
        P(("dp", "rep")),
    )
    out_specs = (
        P(),
        P(("dp", "rep"), None),
        P(None, ("dp", "rep")),
        P(None, ("dp", "rep")),
        P(("dp", "rep")),
        P(None, ("dp", "rep")),
        P(None, ("dp", "rep")),
        P(("dp", "rep")),
        P(None, ("dp", "rep")),
        P(None, ("dp", "rep")),
        P(("dp", "rep")),
        P(None, ("dp", "rep")),
        P(None, ("dp", "rep")),
        P(("dp", "rep")),
    )
    return jax.shard_map(shards, mesh=mesh, in_specs=in_specs, out_specs=out_specs, check_vma=False)
```

```python
import functools
import math

import jax
import jax.numpy as jnp
from jax import lax
from jax.experimental import pallas as pl
from jax.experimental.pallas import tpu as pltpu
from jax.sharding import PartitionSpec as P

MESH = pl.DeviceIdType.MESH
GRAD_SEND = jnp.float32
AXES = ("dp", "rep")

HEADS = 12
HD = 64
SEGS = 16


ln_epsilon = 1e-12
pool_epsilon = 1e-06
logit_divisor = 0.025
learn_rate = 0.01
momentum_rate = 0.9
decay_rate = 0.01
average_rate = 0.75
masked_value = -1e30


def layer_norm_parts(values, gain, shift):
    per_line_average = jnp.mean(values, -1, keepdims=True)
    centred = values - per_line_average
    inverse = lax.rsqrt(jnp.mean(centred * centred, -1, keepdims=True) + ln_epsilon)
    normal_part = centred * inverse
    return (normal_part * gain + shift, normal_part, inverse)


def layer_norm_back(grad_out, normal_part, inverse, gain):
    scaled = grad_out * gain
    grad_in = inverse * (
        scaled
        - jnp.mean(scaled, -1, keepdims=True)
        - normal_part * jnp.mean(scaled * normal_part, -1, keepdims=True)
    )
    return (grad_in, jnp.sum(grad_out * normal_part, 0), jnp.sum(grad_out, 0))


def row_scores(query_one, key_one, segment_one, scale):
    scores = (
        jnp.einsum("qhd,khd->hqk", query_one, key_one, preferred_element_type=jnp.float32) * scale
    )
    same_text = segment_one[:, None] == segment_one[None, :]
    return jnp.where(same_text[None], scores, masked_value)


def attend_rows(query_rows, key_rows, value_rows, row_segments):
    scale = 1.0 / math.sqrt(query_rows.shape[-1])

    def one_row(row_args):
        query_one, key_one, value_one, segment_one = row_args
        scores = row_scores(query_one, key_one, segment_one, scale)
        row_max = jnp.max(scores, -1, keepdims=True)
        exp_scores = jnp.exp(scores - row_max)
        sums = jnp.sum(exp_scores, -1, keepdims=True)
        attn_probs = exp_scores / sums
        mixed = jnp.einsum(
            "hqk,khd->qhd",
            attn_probs.astype(jnp.bfloat16),
            value_one,
            preferred_element_type=jnp.float32,
        )
        return (mixed.astype(jnp.bfloat16), (row_max + jnp.log(sums))[..., 0])

    return lax.map(one_row, (query_rows, key_rows, value_rows, row_segments))


def attend_back(query_rows, key_rows, value_rows, row_segments, log_norm, grad_mixed):
    scale = 1.0 / math.sqrt(query_rows.shape[-1])

    def one_row(row_args):
        query_one, key_one, value_one, segment_one, norm_one, grad_one = row_args
        scores = row_scores(query_one, key_one, segment_one, scale)
        attn_probs = jnp.exp(scores - norm_one[..., None])
        grad_value = jnp.einsum(
            "hqk,qhd->khd",
            attn_probs.astype(jnp.bfloat16),
            grad_one,
            preferred_element_type=jnp.float32,
        )
        grad_probs = jnp.einsum(
            "qhd,khd->hqk", grad_one, value_one, preferred_element_type=jnp.float32
        )
        inner = jnp.sum(attn_probs * grad_probs, -1, keepdims=True)
        grad_scores = (attn_probs * (grad_probs - inner)).astype(jnp.bfloat16)
        grad_query = (
            jnp.einsum("hqk,khd->qhd", grad_scores, key_one, preferred_element_type=jnp.float32)
            * scale
        )
        grad_key = (
            jnp.einsum("hqk,qhd->khd", grad_scores, query_one, preferred_element_type=jnp.float32)
            * scale
        )
        return jnp.concatenate([grad_query, grad_key, grad_value], axis=1)

    return lax.map(one_row, (query_rows, key_rows, value_rows, row_segments, log_norm, grad_mixed))


def apply_update(weight, grad, moment, average, decay):
    step_grad = grad + decay * weight
    new_moment = momentum_rate * moment + step_grad
    new_weight = weight - learn_rate * (step_grad + momentum_rate * new_moment)
    fresh_running_mean = average_rate * average + (1.0 - average_rate) * new_weight
    return (new_weight, new_moment, fresh_running_mean)


def bf16_round(values):
    return lax.reduce_precision(values, exponent_bits=8, mantissa_bits=7)


def flat_index(sizes):
    idx = 0
    for name, size in zip(AXES, sizes):
        idx = idx * size + lax.axis_index(name)
    return idx


def device_of(flat, sizes):
    coords = []
    for size in reversed(sizes):
        coords.append(lax.rem(flat, size))
        flat = flat // size
    return tuple(reversed(coords))


def enter_all(n, sizes, me):
    barrier = pltpu.get_barrier_semaphore()

    def greet(k, carry):
        peer = lax.rem(me + k, n)
        pl.semaphore_signal(barrier, inc=1, device_id=device_of(peer, sizes), device_id_type=MESH)
        return carry

    lax.fori_loop(1, n, greet, 0)
    pl.semaphore_wait(barrier, n - 1)


def gather_kernel(n, sizes, x_ref, out_ref, send_sem, recv_sem):
    me = flat_index(sizes)
    enter_all(n, sizes, me)

    def send(k, carry):
        peer = lax.rem(me + k, n)
        pltpu.make_async_remote_copy(
            src_ref=x_ref, dst_ref=out_ref.at[me], send_sem=send_sem.at[k], recv_sem=recv_sem.at[me],
            device_id=device_of(peer, sizes), device_id_type=MESH,
        ).start()
        return carry

    lax.fori_loop(1, n, send, 0)
    out_ref[me] = x_ref[...]

    def finish(k, carry):
        peer = lax.rem(me + k, n)
        src = lax.rem(me + n - k, n)
        pltpu.make_async_remote_copy(
            src_ref=x_ref, dst_ref=out_ref.at[me], send_sem=send_sem.at[k], recv_sem=recv_sem.at[me],
            device_id=device_of(peer, sizes), device_id_type=MESH,
        ).wait_send()
        pltpu.make_async_remote_copy(
            src_ref=x_ref, dst_ref=out_ref.at[src], send_sem=send_sem.at[k], recv_sem=recv_sem.at[src],
            device_id=device_of(src, sizes), device_id_type=MESH,
        ).wait_recv()
        return carry

    lax.fori_loop(1, n, finish, 0)


def small_gather(x, sizes, cid):
    n = math.prod(sizes)
    return pl.pallas_call(
        functools.partial(gather_kernel, n, sizes),
        out_shape=jax.ShapeDtypeStruct((n,) + x.shape, x.dtype),
        in_specs=[pl.BlockSpec(memory_space=pltpu.VMEM)],
        out_specs=pl.BlockSpec(memory_space=pltpu.VMEM),
        scratch_shapes=[pltpu.SemaphoreType.DMA((n,)), pltpu.SemaphoreType.DMA((n,))],
        compiler_params=pltpu.CompilerParams(collective_id=cid, has_side_effects=True),
    )(x)


def scatter_kernel(n, sizes, x_ref, out_ref, send_sem, recv_sem):
    me = flat_index(sizes)
    enter_all(n, sizes, me)

    def send(k, carry):
        peer = lax.rem(me + k, n)
        pltpu.make_async_remote_copy(
            src_ref=x_ref.at[peer], dst_ref=out_ref.at[me], send_sem=send_sem.at[k], recv_sem=recv_sem.at[me],
            device_id=device_of(peer, sizes), device_id_type=MESH,
        ).start()
        return carry

    lax.fori_loop(1, n, send, 0)
    out_ref[me] = x_ref[me]

    def finish(k, carry):
        peer = lax.rem(me + k, n)
        src = lax.rem(me + n - k, n)
        pltpu.make_async_remote_copy(
            src_ref=x_ref.at[peer], dst_ref=out_ref.at[me], send_sem=send_sem.at[k], recv_sem=recv_sem.at[me],
            device_id=device_of(peer, sizes), device_id_type=MESH,
        ).wait_send()
        pltpu.make_async_remote_copy(
            src_ref=x_ref.at[src], dst_ref=out_ref.at[src], send_sem=send_sem.at[k], recv_sem=recv_sem.at[src],
            device_id=device_of(src, sizes), device_id_type=MESH,
        ).wait_recv()
        return carry

    lax.fori_loop(1, n, finish, 0)


def small_scatter(x, sizes, cid):
    n = math.prod(sizes)
    return pl.pallas_call(
        functools.partial(scatter_kernel, n, sizes),
        out_shape=jax.ShapeDtypeStruct(x.shape, x.dtype),
        in_specs=[pl.BlockSpec(memory_space=pltpu.VMEM)],
        out_specs=pl.BlockSpec(memory_space=pltpu.VMEM),
        scratch_shapes=[pltpu.SemaphoreType.DMA((n,)), pltpu.SemaphoreType.DMA((n,))],
        compiler_params=pltpu.CompilerParams(collective_id=cid, has_side_effects=True),
    )(x)


def contrastive(embed_b, gathered, partner_all, me):
    own_texts = embed_b.shape[0]
    all_texts = gathered.shape[0]
    chunk = min(all_texts, 1024)
    on_rows = (((1,), (1,)), ((), ()))

    def chunk_stats(c):
        rows_b = lax.dynamic_slice_in_dim(gathered, c * chunk, chunk)
        sim = lax.dot_general(rows_b, gathered, on_rows, preferred_element_type=jnp.float32) / logit_divisor
        column_ids = lax.broadcasted_iota(jnp.int32, sim.shape, 1)
        row_ids = lax.broadcasted_iota(jnp.int32, sim.shape, 0) + c * chunk
        masked = jnp.where(column_ids == row_ids, masked_value, sim)
        row_max = jnp.max(masked, -1, keepdims=True)
        log_sum = row_max + jnp.log(jnp.sum(jnp.exp(masked - row_max), -1, keepdims=True))
        wanted = lax.dynamic_slice_in_dim(partner_all, c * chunk, chunk)
        positive = jnp.sum(jnp.where(column_ids == wanted[:, None], sim, 0.0), -1)
        return log_sum[:, 0], positive

    if all_texts == chunk:
        log_sum_all, positive_all = chunk_stats(0)
    else:
        log_sum_all, positive_all = lax.map(chunk_stats, jnp.arange(all_texts // chunk))
        log_sum_all = log_sum_all.reshape(-1)
        positive_all = positive_all.reshape(-1)
    mean_loss = jnp.sum(log_sum_all - positive_all) / all_texts

    own_start = me * own_texts
    own_ids = lax.broadcasted_iota(jnp.int32, (own_texts,), 0) + own_start
    own_partner = lax.dynamic_slice_in_dim(partner_all, own_start, own_texts)
    own_log_sum = lax.dynamic_slice_in_dim(log_sum_all, own_start, own_texts)

    sim_rows = lax.dot_general(embed_b, gathered, on_rows, preferred_element_type=jnp.float32) / logit_divisor
    column_ids = lax.broadcasted_iota(jnp.int32, sim_rows.shape, 1)
    masked_rows = jnp.where(column_ids == own_ids[:, None], masked_value, sim_rows)
    grad_rows = (
        jnp.exp(masked_rows - own_log_sum[:, None]) - (column_ids == own_partner[:, None]).astype(jnp.float32)
    ).astype(jnp.bfloat16)

    sim_cols = lax.dot_general(gathered, embed_b, on_rows, preferred_element_type=jnp.float32) / logit_divisor
    row_ids = lax.broadcasted_iota(jnp.int32, sim_cols.shape, 0)
    masked_cols = jnp.where(row_ids == own_ids[None, :], masked_value, sim_cols)
    grad_cols = (
        jnp.exp(masked_cols - log_sum_all[:, None]) - (partner_all[:, None] == own_ids[None, :]).astype(jnp.float32)
    ).astype(jnp.bfloat16)

    on_tokens = (((0,), (0,)), ((), ()))
    embedding_gradient = (
        jnp.dot(grad_rows, gathered, preferred_element_type=jnp.float32)
        + lax.dot_general(grad_cols, gathered, on_tokens, preferred_element_type=jnp.float32)
    ) / logit_divisor
    return mean_loss, embedding_gradient


def shards(
    hidden_in,
    segments,
    partner,
    attn_weights,
    ffn_weights,
    vectors,
    attn_momentum,
    ffn_momentum,
    vector_momentum,
    attn_averaged,
    ffn_averaged,
    vector_averaged,
):
    sizes = tuple(lax.axis_size(name) for name in AXES)
    n_dev = math.prod(sizes)
    me = flat_index(sizes)
    vec_len = vectors.shape[0]
    small = jnp.concatenate([vectors, partner.astype(jnp.float32)])[None, :]
    small_all = small_gather(small, sizes, 0)[:, 0, :]
    vector_f = bf16_round(small_all[:, :vec_len].reshape(-1))
    partner_all = small_all[:, vec_len:].reshape(-1).astype(jnp.int32)
    attn_full, ffn_full = (
        lax.all_gather(attn_weights.astype(jnp.bfloat16), AXES, axis=1, tiled=True),
        lax.all_gather(ffn_weights.astype(jnp.bfloat16), AXES, axis=1, tiled=True),
    )
    width = attn_full.shape[0]
    hidden = ffn_full.shape[1] // 2
    query_bias = vector_f[0:width]
    value_bias = vector_f[width : 2 * width]
    output_bias = vector_f[2 * width : 3 * width]
    gain_first = vector_f[3 * width : 4 * width]
    shift_first = vector_f[4 * width : 5 * width]
    upper_bias = vector_f[5 * width : 5 * width + hidden]
    lower_bias = vector_f[5 * width + hidden : 6 * width + hidden]
    gain_second = vector_f[6 * width + hidden : 7 * width + hidden]
    shift_second = vector_f[7 * width + hidden : 8 * width + hidden]
    w_qkv = attn_full[:, : 3 * width]
    w_output = attn_full[:, 3 * width :]
    w_upper = ffn_full[:, :hidden]
    w_lower = ffn_full[:, hidden:]
    rows_dev, seq_len = segments.shape
    tokens_n = rows_dev * seq_len
    on_rows = (((1,), (1,)), ((), ()))
    on_tokens = (((0,), (0,)), ((), ()))
    qkv_bias = jnp.concatenate([query_bias, jnp.zeros_like(query_bias), value_bias])
    qkv_rows = (jnp.dot(hidden_in, w_qkv, preferred_element_type=jnp.float32) + qkv_bias).astype(
        jnp.bfloat16
    )
    heads = qkv_rows.reshape(rows_dev, seq_len, 3, HEADS, HD)
    query_rows = heads[:, :, 0]
    key_rows = heads[:, :, 1]
    value_rows = heads[:, :, 2]
    mixed, log_norm = attend_rows(query_rows, key_rows, value_rows, segments)
    mixed_flat = mixed.reshape(tokens_n, width)
    first_sum = (
        hidden_in.astype(jnp.float32)
        + jnp.dot(mixed_flat, w_output, preferred_element_type=jnp.float32)
        + output_bias
    )
    normed, normal_one, inverse_one = layer_norm_parts(first_sum, gain_first, shift_first)
    normed_r = bf16_round(normed)
    normed_b = normed_r.astype(jnp.bfloat16)
    upper = jnp.dot(normed_b, w_upper, preferred_element_type=jnp.float32) + upper_bias
    active_b = jax.nn.gelu(upper, approximate=False).astype(jnp.bfloat16)
    second_sum = (
        normed_r
        + lax.dot_general(active_b, w_lower, on_rows, preferred_element_type=jnp.float32)
        + lower_bias
    )
    result, normal_two, inverse_two = layer_norm_parts(second_sum, gain_second, shift_second)
    text_ids = jnp.arange(SEGS, dtype=jnp.int32)
    one_hot = (segments[:, None, :] == text_ids[None, :, None]).astype(jnp.float32)
    counts = jnp.sum(one_hot, -1, keepdims=True)
    pooled = (
        jnp.einsum(
            "rts,rsd->rtd",
            one_hot,
            result.reshape(rows_dev, seq_len, width),
            precision=lax.Precision.HIGHEST,
        )
        / counts
    ).reshape(-1, width)
    inv_norm = lax.rsqrt(jnp.sum(pooled * pooled, -1, keepdims=True) + pool_epsilon)
    embed_b = (pooled * inv_norm).astype(jnp.bfloat16)
    gathered_embeddings = lax.all_gather(embed_b, AXES, axis=0, tiled=True)
    mean_loss, embedding_gradient = contrastive(embed_b, gathered_embeddings, partner_all, me)
    grad_pooled = inv_norm * embedding_gradient - pooled * (
        inv_norm * inv_norm * inv_norm
    ) * jnp.sum(embedding_gradient * pooled, -1, keepdims=True)
    derivative_output = jnp.einsum(
        "rts,rtd->rsd",
        one_hot,
        grad_pooled.reshape(rows_dev, SEGS, width) / counts,
        precision=lax.Precision.HIGHEST,
    ).reshape(tokens_n, width)
    grad_second, gain_two_grad, shift_two_grad = layer_norm_back(
        derivative_output, normal_two, inverse_two, gain_second
    )
    lower_bias_grad = jnp.sum(grad_second, 0)
    lower_grad_b = grad_second.astype(jnp.bfloat16)
    lower_w_grad_t = lax.dot_general(
        active_b, lower_grad_b, on_tokens, preferred_element_type=jnp.float32
    )
    grad_active = jnp.dot(lower_grad_b, w_lower, preferred_element_type=jnp.float32)
    cumulative = 0.5 * (1.0 + lax.erf(upper / math.sqrt(2.0)))
    density = jnp.exp(-0.5 * upper * upper) / math.sqrt(2.0 * math.pi)
    grad_upper = grad_active * (cumulative + upper * density)
    upper_bias_grad = jnp.sum(grad_upper, 0)
    upper_grad_b = grad_upper.astype(jnp.bfloat16)
    upper_w_grad_t = lax.dot_general(
        upper_grad_b, normed_b, on_tokens, preferred_element_type=jnp.float32
    )
    ffn_grad_t = jnp.concatenate([upper_w_grad_t, lower_w_grad_t], 0)
    grad_normed = (
        lax.dot_general(upper_grad_b, w_upper, on_rows, preferred_element_type=jnp.float32)
        + grad_second
    )
    grad_first, gain_one_grad, shift_one_grad = layer_norm_back(
        grad_normed, normal_one, inverse_one, gain_first
    )
    output_bias_grad = jnp.sum(grad_first, 0)
    first_grad_b = grad_first.astype(jnp.bfloat16)
    output_w_grad_t = lax.dot_general(
        first_grad_b, mixed_flat, on_tokens, preferred_element_type=jnp.float32
    )
    grad_mixed = lax.dot_general(
        first_grad_b, w_output, on_rows, preferred_element_type=jnp.float32
    ).astype(jnp.bfloat16)
    grad_mixed = grad_mixed.reshape(rows_dev, seq_len, HEADS, HD)
    qkv_grad = attend_back(
        query_rows, key_rows, value_rows, segments, log_norm, grad_mixed
    ).reshape(tokens_n, 3 * width)
    qkv_grad_f = bf16_round(qkv_grad)
    qkv_grad_b = qkv_grad_f.astype(jnp.bfloat16)
    query_bias_grad = jnp.sum(qkv_grad_f[:, :width], 0)
    value_bias_grad = jnp.sum(qkv_grad_f[:, 2 * width :], 0)
    qkv_w_grad_t = lax.dot_general(
        qkv_grad_b, hidden_in, on_tokens, preferred_element_type=jnp.float32
    )
    input_grad = (
        lax.dot_general(qkv_grad_b, w_qkv, on_rows, preferred_element_type=jnp.float32) + grad_first
    )
    attn_grad_t = jnp.concatenate([qkv_w_grad_t, output_w_grad_t], 0)
    vector_grad = jnp.concatenate(
        [
            query_bias_grad,
            value_bias_grad,
            output_bias_grad,
            gain_one_grad,
            shift_one_grad,
            upper_bias_grad,
            lower_bias_grad,
            gain_two_grad,
            shift_two_grad,
        ]
    )
    vector_slots = small_scatter(vector_grad.reshape(n_dev, 1, -1), sizes, 1)
    vector_reduced = jnp.sum(vector_slots[:, 0, :], 0)
    attn_cols = attn_grad_t.shape[0] // n_dev
    joined = jnp.concatenate(
        [attn_grad_t.reshape(n_dev, attn_cols, width), ffn_grad_t.reshape(n_dev, -1, width)], 1
    ).reshape(-1, width)
    joined_reduced = lax.psum_scatter(joined.astype(GRAD_SEND), AXES, scatter_dimension=0, tiled=True)
    joined_reduced = joined_reduced.astype(jnp.float32)
    attn_reduced = joined_reduced[:attn_cols].T
    ffn_reduced = joined_reduced[attn_cols:].T
    attn_new, attn_moment, attn_average = apply_update(
        attn_weights, attn_reduced, attn_momentum, attn_averaged, decay_rate
    )
    ffn_new, ffn_moment, ffn_average = apply_update(
        ffn_weights, ffn_reduced, ffn_momentum, ffn_averaged, decay_rate
    )
    vector_new, vector_moment, vector_average = apply_update(
        vectors, vector_reduced, vector_momentum, vector_averaged, 0.0
    )
    return (
        mean_loss,
        input_grad,
        attn_reduced,
        ffn_reduced,
        vector_reduced,
        attn_new,
        ffn_new,
        vector_new,
        attn_moment,
        ffn_moment,
        vector_moment,
        attn_average,
        ffn_average,
        vector_average,
    )


def solution(mesh):
    in_specs = (
        P(("dp", "rep"), None),
        P(("dp", "rep"), None),
        P(("dp", "rep")),
        P(None, ("dp", "rep")),
        P(None, ("dp", "rep")),
        P(("dp", "rep")),
        P(None, ("dp", "rep")),
        P(None, ("dp", "rep")),
        P(("dp", "rep")),
        P(None, ("dp", "rep")),
        P(None, ("dp", "rep")),
        P(("dp", "rep")),
    )
    out_specs = (
        P(),
        P(("dp", "rep"), None),
        P(None, ("dp", "rep")),
        P(None, ("dp", "rep")),
        P(("dp", "rep")),
        P(None, ("dp", "rep")),
        P(None, ("dp", "rep")),
        P(("dp", "rep")),
        P(None, ("dp", "rep")),
        P(None, ("dp", "rep")),
        P(("dp", "rep")),
        P(None, ("dp", "rep")),
        P(None, ("dp", "rep")),
        P(("dp", "rep")),
    )
    return jax.shard_map(shards, mesh=mesh, in_specs=in_specs, out_specs=out_specs, check_vma=False)
```

```python
import functools
import math

import jax
import jax.numpy as jnp
from jax import lax
from jax.experimental import pallas as pl
from jax.experimental.pallas import tpu as pltpu
from jax.sharding import PartitionSpec as P

MESH = pl.DeviceIdType.MESH
GRAD_SEND = jnp.bfloat16
AXES = ("dp", "rep")

HEADS = 12
HD = 64
SEGS = 16


ln_epsilon = 1e-12
pool_epsilon = 1e-06
logit_divisor = 0.025
learn_rate = 0.01
momentum_rate = 0.9
decay_rate = 0.01
average_rate = 0.75
masked_value = -1e30


def layer_norm_parts(values, gain, shift):
    per_line_average = jnp.mean(values, -1, keepdims=True)
    centred = values - per_line_average
    inverse = lax.rsqrt(jnp.mean(centred * centred, -1, keepdims=True) + ln_epsilon)
    normal_part = centred * inverse
    return (normal_part * gain + shift, normal_part, inverse)


def layer_norm_back(grad_out, normal_part, inverse, gain):
    scaled = grad_out * gain
    grad_in = inverse * (
        scaled
        - jnp.mean(scaled, -1, keepdims=True)
        - normal_part * jnp.mean(scaled * normal_part, -1, keepdims=True)
    )
    return (grad_in, jnp.sum(grad_out * normal_part, 0), jnp.sum(grad_out, 0))


def row_scores(query_one, key_one, segment_one, scale):
    scores = (
        jnp.einsum("qhd,khd->hqk", query_one, key_one, preferred_element_type=jnp.float32) * scale
    )
    same_text = segment_one[:, None] == segment_one[None, :]
    return jnp.where(same_text[None], scores, masked_value)


def attend_rows(query_rows, key_rows, value_rows, row_segments):
    scale = 1.0 / math.sqrt(query_rows.shape[-1])

    def one_row(row_args):
        query_one, key_one, value_one, segment_one = row_args
        scores = row_scores(query_one, key_one, segment_one, scale)
        row_max = jnp.max(scores, -1, keepdims=True)
        exp_scores = jnp.exp(scores - row_max)
        sums = jnp.sum(exp_scores, -1, keepdims=True)
        attn_probs = exp_scores / sums
        mixed = jnp.einsum(
            "hqk,khd->qhd",
            attn_probs.astype(jnp.bfloat16),
            value_one,
            preferred_element_type=jnp.float32,
        )
        return (mixed.astype(jnp.bfloat16), (row_max + jnp.log(sums))[..., 0])

    return lax.map(one_row, (query_rows, key_rows, value_rows, row_segments))


def attend_back(query_rows, key_rows, value_rows, row_segments, log_norm, grad_mixed):
    scale = 1.0 / math.sqrt(query_rows.shape[-1])

    def one_row(row_args):
        query_one, key_one, value_one, segment_one, norm_one, grad_one = row_args
        scores = row_scores(query_one, key_one, segment_one, scale)
        attn_probs = jnp.exp(scores - norm_one[..., None])
        grad_value = jnp.einsum(
            "hqk,qhd->khd",
            attn_probs.astype(jnp.bfloat16),
            grad_one,
            preferred_element_type=jnp.float32,
        )
        grad_probs = jnp.einsum(
            "qhd,khd->hqk", grad_one, value_one, preferred_element_type=jnp.float32
        )
        inner = jnp.sum(attn_probs * grad_probs, -1, keepdims=True)
        grad_scores = (attn_probs * (grad_probs - inner)).astype(jnp.bfloat16)
        grad_query = (
            jnp.einsum("hqk,khd->qhd", grad_scores, key_one, preferred_element_type=jnp.float32)
            * scale
        )
        grad_key = (
            jnp.einsum("hqk,qhd->khd", grad_scores, query_one, preferred_element_type=jnp.float32)
            * scale
        )
        return jnp.concatenate([grad_query, grad_key, grad_value], axis=1)

    return lax.map(one_row, (query_rows, key_rows, value_rows, row_segments, log_norm, grad_mixed))


def apply_update(weight, grad, moment, average, decay):
    step_grad = grad + decay * weight
    new_moment = momentum_rate * moment + step_grad
    new_weight = weight - learn_rate * (step_grad + momentum_rate * new_moment)
    fresh_running_mean = average_rate * average + (1.0 - average_rate) * new_weight
    return (new_weight, new_moment, fresh_running_mean)


def bf16_round(values):
    return lax.reduce_precision(values, exponent_bits=8, mantissa_bits=7)


def flat_index(sizes):
    idx = 0
    for name, size in zip(AXES, sizes):
        idx = idx * size + lax.axis_index(name)
    return idx


def device_of(flat, sizes):
    coords = []
    for size in reversed(sizes):
        coords.append(lax.rem(flat, size))
        flat = flat // size
    return tuple(reversed(coords))


def enter_all(n, sizes, me):
    barrier = pltpu.get_barrier_semaphore()

    def greet(k, carry):
        peer = lax.rem(me + k, n)
        pl.semaphore_signal(barrier, inc=1, device_id=device_of(peer, sizes), device_id_type=MESH)
        return carry

    lax.fori_loop(1, n, greet, 0)
    pl.semaphore_wait(barrier, n - 1)


def gather_kernel(n, sizes, x_ref, out_ref, send_sem, recv_sem):
    me = flat_index(sizes)
    enter_all(n, sizes, me)

    def send(k, carry):
        peer = lax.rem(me + k, n)
        pltpu.make_async_remote_copy(
            src_ref=x_ref, dst_ref=out_ref.at[me], send_sem=send_sem.at[k], recv_sem=recv_sem.at[me],
            device_id=device_of(peer, sizes), device_id_type=MESH,
        ).start()
        return carry

    lax.fori_loop(1, n, send, 0)
    out_ref[me] = x_ref[...]

    def finish(k, carry):
        peer = lax.rem(me + k, n)
        src = lax.rem(me + n - k, n)
        pltpu.make_async_remote_copy(
            src_ref=x_ref, dst_ref=out_ref.at[me], send_sem=send_sem.at[k], recv_sem=recv_sem.at[me],
            device_id=device_of(peer, sizes), device_id_type=MESH,
        ).wait_send()
        pltpu.make_async_remote_copy(
            src_ref=x_ref, dst_ref=out_ref.at[src], send_sem=send_sem.at[k], recv_sem=recv_sem.at[src],
            device_id=device_of(src, sizes), device_id_type=MESH,
        ).wait_recv()
        return carry

    lax.fori_loop(1, n, finish, 0)


def small_gather(x, sizes, cid):
    n = math.prod(sizes)
    return pl.pallas_call(
        functools.partial(gather_kernel, n, sizes),
        out_shape=jax.ShapeDtypeStruct((n,) + x.shape, x.dtype),
        in_specs=[pl.BlockSpec(memory_space=pltpu.VMEM)],
        out_specs=pl.BlockSpec(memory_space=pltpu.VMEM),
        scratch_shapes=[pltpu.SemaphoreType.DMA((n,)), pltpu.SemaphoreType.DMA((n,))],
        compiler_params=pltpu.CompilerParams(collective_id=cid, has_side_effects=True),
    )(x)


def scatter_kernel(n, sizes, x_ref, out_ref, send_sem, recv_sem):
    me = flat_index(sizes)
    enter_all(n, sizes, me)

    def send(k, carry):
        peer = lax.rem(me + k, n)
        pltpu.make_async_remote_copy(
            src_ref=x_ref.at[peer], dst_ref=out_ref.at[me], send_sem=send_sem.at[k], recv_sem=recv_sem.at[me],
            device_id=device_of(peer, sizes), device_id_type=MESH,
        ).start()
        return carry

    lax.fori_loop(1, n, send, 0)
    out_ref[me] = x_ref[me]

    def finish(k, carry):
        peer = lax.rem(me + k, n)
        src = lax.rem(me + n - k, n)
        pltpu.make_async_remote_copy(
            src_ref=x_ref.at[peer], dst_ref=out_ref.at[me], send_sem=send_sem.at[k], recv_sem=recv_sem.at[me],
            device_id=device_of(peer, sizes), device_id_type=MESH,
        ).wait_send()
        pltpu.make_async_remote_copy(
            src_ref=x_ref.at[src], dst_ref=out_ref.at[src], send_sem=send_sem.at[k], recv_sem=recv_sem.at[src],
            device_id=device_of(src, sizes), device_id_type=MESH,
        ).wait_recv()
        return carry

    lax.fori_loop(1, n, finish, 0)


def small_scatter(x, sizes, cid):
    n = math.prod(sizes)
    return pl.pallas_call(
        functools.partial(scatter_kernel, n, sizes),
        out_shape=jax.ShapeDtypeStruct(x.shape, x.dtype),
        in_specs=[pl.BlockSpec(memory_space=pltpu.VMEM)],
        out_specs=pl.BlockSpec(memory_space=pltpu.VMEM),
        scratch_shapes=[pltpu.SemaphoreType.DMA((n,)), pltpu.SemaphoreType.DMA((n,))],
        compiler_params=pltpu.CompilerParams(collective_id=cid, has_side_effects=True),
    )(x)


def contrastive(embed_b, gathered, partner_all, me):
    own_texts = embed_b.shape[0]
    all_texts = gathered.shape[0]
    chunk = min(all_texts, 1024)
    on_rows = (((1,), (1,)), ((), ()))

    def chunk_stats(c):
        rows_b = lax.dynamic_slice_in_dim(gathered, c * chunk, chunk)
        sim = lax.dot_general(rows_b, gathered, on_rows, preferred_element_type=jnp.float32) / logit_divisor
        column_ids = lax.broadcasted_iota(jnp.int32, sim.shape, 1)
        row_ids = lax.broadcasted_iota(jnp.int32, sim.shape, 0) + c * chunk
        masked = jnp.where(column_ids == row_ids, masked_value, sim)
        row_max = jnp.max(masked, -1, keepdims=True)
        log_sum = row_max + jnp.log(jnp.sum(jnp.exp(masked - row_max), -1, keepdims=True))
        wanted = lax.dynamic_slice_in_dim(partner_all, c * chunk, chunk)
        positive = jnp.sum(jnp.where(column_ids == wanted[:, None], sim, 0.0), -1)
        return log_sum[:, 0], positive

    if all_texts == chunk:
        log_sum_all, positive_all = chunk_stats(0)
    else:
        log_sum_all, positive_all = lax.map(chunk_stats, jnp.arange(all_texts // chunk))
        log_sum_all = log_sum_all.reshape(-1)
        positive_all = positive_all.reshape(-1)
    mean_loss = jnp.sum(log_sum_all - positive_all) / all_texts

    own_start = me * own_texts
    own_ids = lax.broadcasted_iota(jnp.int32, (own_texts,), 0) + own_start
    own_partner = lax.dynamic_slice_in_dim(partner_all, own_start, own_texts)
    own_log_sum = lax.dynamic_slice_in_dim(log_sum_all, own_start, own_texts)

    sim_rows = lax.dot_general(embed_b, gathered, on_rows, preferred_element_type=jnp.float32) / logit_divisor
    column_ids = lax.broadcasted_iota(jnp.int32, sim_rows.shape, 1)
    masked_rows = jnp.where(column_ids == own_ids[:, None], masked_value, sim_rows)
    grad_rows = (
        jnp.exp(masked_rows - own_log_sum[:, None]) - (column_ids == own_partner[:, None]).astype(jnp.float32)
    ).astype(jnp.bfloat16)

    sim_cols = lax.dot_general(gathered, embed_b, on_rows, preferred_element_type=jnp.float32) / logit_divisor
    row_ids = lax.broadcasted_iota(jnp.int32, sim_cols.shape, 0)
    masked_cols = jnp.where(row_ids == own_ids[None, :], masked_value, sim_cols)
    grad_cols = (
        jnp.exp(masked_cols - log_sum_all[:, None]) - (partner_all[:, None] == own_ids[None, :]).astype(jnp.float32)
    ).astype(jnp.bfloat16)

    on_tokens = (((0,), (0,)), ((), ()))
    embedding_gradient = (
        jnp.dot(grad_rows, gathered, preferred_element_type=jnp.float32)
        + lax.dot_general(grad_cols, gathered, on_tokens, preferred_element_type=jnp.float32)
    ) / logit_divisor
    return mean_loss, embedding_gradient


def shards(
    hidden_in,
    segments,
    partner,
    attn_weights,
    ffn_weights,
    vectors,
    attn_momentum,
    ffn_momentum,
    vector_momentum,
    attn_averaged,
    ffn_averaged,
    vector_averaged,
):
    sizes = tuple(lax.axis_size(name) for name in AXES)
    n_dev = math.prod(sizes)
    me = flat_index(sizes)
    vec_len = vectors.shape[0]
    small = jnp.concatenate([vectors, partner.astype(jnp.float32)])[None, :]
    small_all = small_gather(small, sizes, 0)[:, 0, :]
    vector_f = bf16_round(small_all[:, :vec_len].reshape(-1))
    partner_all = small_all[:, vec_len:].reshape(-1).astype(jnp.int32)
    attn_full, ffn_full = (
        lax.all_gather(attn_weights.astype(jnp.bfloat16), AXES, axis=1, tiled=True),
        lax.all_gather(ffn_weights.astype(jnp.bfloat16), AXES, axis=1, tiled=True),
    )
    width = attn_full.shape[0]
    hidden = ffn_full.shape[1] // 2
    query_bias = vector_f[0:width]
    value_bias = vector_f[width : 2 * width]
    output_bias = vector_f[2 * width : 3 * width]
    gain_first = vector_f[3 * width : 4 * width]
    shift_first = vector_f[4 * width : 5 * width]
    upper_bias = vector_f[5 * width : 5 * width + hidden]
    lower_bias = vector_f[5 * width + hidden : 6 * width + hidden]
    gain_second = vector_f[6 * width + hidden : 7 * width + hidden]
    shift_second = vector_f[7 * width + hidden : 8 * width + hidden]
    w_qkv = attn_full[:, : 3 * width]
    w_output = attn_full[:, 3 * width :]
    w_upper = ffn_full[:, :hidden]
    w_lower = ffn_full[:, hidden:]
    rows_dev, seq_len = segments.shape
    tokens_n = rows_dev * seq_len
    on_rows = (((1,), (1,)), ((), ()))
    on_tokens = (((0,), (0,)), ((), ()))
    qkv_bias = jnp.concatenate([query_bias, jnp.zeros_like(query_bias), value_bias])
    qkv_rows = (jnp.dot(hidden_in, w_qkv, preferred_element_type=jnp.float32) + qkv_bias).astype(
        jnp.bfloat16
    )
    heads = qkv_rows.reshape(rows_dev, seq_len, 3, HEADS, HD)
    query_rows = heads[:, :, 0]
    key_rows = heads[:, :, 1]
    value_rows = heads[:, :, 2]
    mixed, log_norm = attend_rows(query_rows, key_rows, value_rows, segments)
    mixed_flat = mixed.reshape(tokens_n, width)
    first_sum = (
        hidden_in.astype(jnp.float32)
        + jnp.dot(mixed_flat, w_output, preferred_element_type=jnp.float32)
        + output_bias
    )
    normed, normal_one, inverse_one = layer_norm_parts(first_sum, gain_first, shift_first)
    normed_r = bf16_round(normed)
    normed_b = normed_r.astype(jnp.bfloat16)
    upper = jnp.dot(normed_b, w_upper, preferred_element_type=jnp.float32) + upper_bias
    active_b = jax.nn.gelu(upper, approximate=False).astype(jnp.bfloat16)
    second_sum = (
        normed_r
        + lax.dot_general(active_b, w_lower, on_rows, preferred_element_type=jnp.float32)
        + lower_bias
    )
    result, normal_two, inverse_two = layer_norm_parts(second_sum, gain_second, shift_second)
    text_ids = jnp.arange(SEGS, dtype=jnp.int32)
    one_hot = (segments[:, None, :] == text_ids[None, :, None]).astype(jnp.float32)
    counts = jnp.sum(one_hot, -1, keepdims=True)
    pooled = (
        jnp.einsum(
            "rts,rsd->rtd",
            one_hot,
            result.reshape(rows_dev, seq_len, width),
            precision=lax.Precision.HIGHEST,
        )
        / counts
    ).reshape(-1, width)
    inv_norm = lax.rsqrt(jnp.sum(pooled * pooled, -1, keepdims=True) + pool_epsilon)
    embed_b = (pooled * inv_norm).astype(jnp.bfloat16)
    gathered_embeddings = lax.all_gather(embed_b, AXES, axis=0, tiled=True)
    mean_loss, embedding_gradient = contrastive(embed_b, gathered_embeddings, partner_all, me)
    grad_pooled = inv_norm * embedding_gradient - pooled * (
        inv_norm * inv_norm * inv_norm
    ) * jnp.sum(embedding_gradient * pooled, -1, keepdims=True)
    derivative_output = jnp.einsum(
        "rts,rtd->rsd",
        one_hot,
        grad_pooled.reshape(rows_dev, SEGS, width) / counts,
        precision=lax.Precision.HIGHEST,
    ).reshape(tokens_n, width)
    grad_second, gain_two_grad, shift_two_grad = layer_norm_back(
        derivative_output, normal_two, inverse_two, gain_second
    )
    lower_bias_grad = jnp.sum(grad_second, 0)
    lower_grad_b = grad_second.astype(jnp.bfloat16)
    lower_w_grad_t = lax.dot_general(
        active_b, lower_grad_b, on_tokens, preferred_element_type=jnp.float32
    )
    grad_active = jnp.dot(lower_grad_b, w_lower, preferred_element_type=jnp.float32)
    cumulative = 0.5 * (1.0 + lax.erf(upper / math.sqrt(2.0)))
    density = jnp.exp(-0.5 * upper * upper) / math.sqrt(2.0 * math.pi)
    grad_upper = grad_active * (cumulative + upper * density)
    upper_bias_grad = jnp.sum(grad_upper, 0)
    upper_grad_b = grad_upper.astype(jnp.bfloat16)
    upper_w_grad_t = lax.dot_general(
        upper_grad_b, normed_b, on_tokens, preferred_element_type=jnp.float32
    )
    ffn_grad_t = jnp.concatenate([upper_w_grad_t, lower_w_grad_t], 0)
    grad_normed = (
        lax.dot_general(upper_grad_b, w_upper, on_rows, preferred_element_type=jnp.float32)
        + grad_second
    )
    grad_first, gain_one_grad, shift_one_grad = layer_norm_back(
        grad_normed, normal_one, inverse_one, gain_first
    )
    output_bias_grad = jnp.sum(grad_first, 0)
    first_grad_b = grad_first.astype(jnp.bfloat16)
    output_w_grad_t = lax.dot_general(
        first_grad_b, mixed_flat, on_tokens, preferred_element_type=jnp.float32
    )
    grad_mixed = lax.dot_general(
        first_grad_b, w_output, on_rows, preferred_element_type=jnp.float32
    ).astype(jnp.bfloat16)
    grad_mixed = grad_mixed.reshape(rows_dev, seq_len, HEADS, HD)
    qkv_grad = attend_back(
        query_rows, key_rows, value_rows, segments, log_norm, grad_mixed
    ).reshape(tokens_n, 3 * width)
    qkv_grad_f = bf16_round(qkv_grad)
    qkv_grad_b = qkv_grad_f.astype(jnp.bfloat16)
    query_bias_grad = jnp.sum(qkv_grad_f[:, :width], 0)
    value_bias_grad = jnp.sum(qkv_grad_f[:, 2 * width :], 0)
    qkv_w_grad_t = lax.dot_general(
        qkv_grad_b, hidden_in, on_tokens, preferred_element_type=jnp.float32
    )
    input_grad = (
        lax.dot_general(qkv_grad_b, w_qkv, on_rows, preferred_element_type=jnp.float32) + grad_first
    )
    attn_grad_t = jnp.concatenate([qkv_w_grad_t, output_w_grad_t], 0)
    vector_grad = jnp.concatenate(
        [
            query_bias_grad,
            value_bias_grad,
            output_bias_grad,
            gain_one_grad,
            shift_one_grad,
            upper_bias_grad,
            lower_bias_grad,
            gain_two_grad,
            shift_two_grad,
        ]
    )
    vector_slots = small_scatter(vector_grad.reshape(n_dev, 1, -1), sizes, 1)
    vector_reduced = jnp.sum(vector_slots[:, 0, :], 0)
    attn_cols = attn_grad_t.shape[0] // n_dev
    joined = jnp.concatenate(
        [attn_grad_t.reshape(n_dev, attn_cols, width), ffn_grad_t.reshape(n_dev, -1, width)], 1
    ).reshape(-1, width)
    joined_reduced = lax.psum_scatter(joined.astype(GRAD_SEND), AXES, scatter_dimension=0, tiled=True)
    joined_reduced = joined_reduced.astype(jnp.float32)
    attn_reduced = joined_reduced[:attn_cols].T
    ffn_reduced = joined_reduced[attn_cols:].T
    attn_new, attn_moment, attn_average = apply_update(
        attn_weights, attn_reduced, attn_momentum, attn_averaged, decay_rate
    )
    ffn_new, ffn_moment, ffn_average = apply_update(
        ffn_weights, ffn_reduced, ffn_momentum, ffn_averaged, decay_rate
    )
    vector_new, vector_moment, vector_average = apply_update(
        vectors, vector_reduced, vector_momentum, vector_averaged, 0.0
    )
    return (
        mean_loss,
        input_grad,
        attn_reduced,
        ffn_reduced,
        vector_reduced,
        attn_new,
        ffn_new,
        vector_new,
        attn_moment,
        ffn_moment,
        vector_moment,
        attn_average,
        ffn_average,
        vector_average,
    )


def solution(mesh):
    in_specs = (
        P(("dp", "rep"), None),
        P(("dp", "rep"), None),
        P(("dp", "rep")),
        P(None, ("dp", "rep")),
        P(None, ("dp", "rep")),
        P(("dp", "rep")),
        P(None, ("dp", "rep")),
        P(None, ("dp", "rep")),
        P(("dp", "rep")),
        P(None, ("dp", "rep")),
        P(None, ("dp", "rep")),
        P(("dp", "rep")),
    )
    out_specs = (
        P(),
        P(("dp", "rep"), None),
        P(None, ("dp", "rep")),
        P(None, ("dp", "rep")),
        P(("dp", "rep")),
        P(None, ("dp", "rep")),
        P(None, ("dp", "rep")),
        P(("dp", "rep")),
        P(None, ("dp", "rep")),
        P(None, ("dp", "rep")),
        P(("dp", "rep")),
        P(None, ("dp", "rep")),
        P(None, ("dp", "rep")),
        P(("dp", "rep")),
    )
    return jax.shard_map(shards, mesh=mesh, in_specs=in_specs, out_specs=out_specs, check_vma=False)
```

```python
import functools
import math

import jax
import jax.numpy as jnp
from jax import lax
from jax.experimental import pallas as pl
from jax.experimental.pallas import tpu as pltpu
from jax.sharding import PartitionSpec as P

MESH = pl.DeviceIdType.MESH
GRAD_SEND = jnp.bfloat16
AXES = ("dp", "rep")

HEADS = 12
HD = 64
SEGS = 16


ln_epsilon = 1e-12
pool_epsilon = 1e-06
logit_divisor = 0.025
learn_rate = 0.01
momentum_rate = 0.9
decay_rate = 0.01
average_rate = 0.75
masked_value = -1e30


def layer_norm_parts(values, gain, shift):
    per_line_average = jnp.mean(values, -1, keepdims=True)
    centred = values - per_line_average
    inverse = lax.rsqrt(jnp.mean(centred * centred, -1, keepdims=True) + ln_epsilon)
    normal_part = centred * inverse
    return (normal_part * gain + shift, normal_part, inverse)


def layer_norm_back(grad_out, normal_part, inverse, gain):
    scaled = grad_out * gain
    grad_in = inverse * (
        scaled
        - jnp.mean(scaled, -1, keepdims=True)
        - normal_part * jnp.mean(scaled * normal_part, -1, keepdims=True)
    )
    return (grad_in, jnp.sum(grad_out * normal_part, 0), jnp.sum(grad_out, 0))


def row_scores(query_one, key_one, segment_one, scale):
    scores = (
        jnp.einsum("qhd,khd->hqk", query_one, key_one, preferred_element_type=jnp.float32) * scale
    )
    same_text = segment_one[:, None] == segment_one[None, :]
    return jnp.where(same_text[None], scores, masked_value)


def attend_rows(query_rows, key_rows, value_rows, row_segments):
    scale = 1.0 / math.sqrt(query_rows.shape[-1])

    def one_row(row_args):
        query_one, key_one, value_one, segment_one = row_args
        scores = row_scores(query_one, key_one, segment_one, scale)
        row_max = jnp.max(scores, -1, keepdims=True)
        exp_scores = jnp.exp(scores - row_max)
        sums = jnp.sum(exp_scores, -1, keepdims=True)
        attn_probs = exp_scores / sums
        mixed = jnp.einsum(
            "hqk,khd->qhd",
            attn_probs.astype(jnp.bfloat16),
            value_one,
            preferred_element_type=jnp.float32,
        )
        return (mixed.astype(jnp.bfloat16), (row_max + jnp.log(sums))[..., 0])

    return lax.map(one_row, (query_rows, key_rows, value_rows, row_segments))


def attend_back(query_rows, key_rows, value_rows, row_segments, log_norm, grad_mixed):
    scale = 1.0 / math.sqrt(query_rows.shape[-1])

    def one_row(row_args):
        query_one, key_one, value_one, segment_one, norm_one, grad_one = row_args
        scores = row_scores(query_one, key_one, segment_one, scale)
        attn_probs = jnp.exp(scores - norm_one[..., None])
        grad_value = jnp.einsum(
            "hqk,qhd->khd",
            attn_probs.astype(jnp.bfloat16),
            grad_one,
            preferred_element_type=jnp.float32,
        )
        grad_probs = jnp.einsum(
            "qhd,khd->hqk", grad_one, value_one, preferred_element_type=jnp.float32
        )
        inner = jnp.sum(attn_probs * grad_probs, -1, keepdims=True)
        grad_scores = (attn_probs * (grad_probs - inner)).astype(jnp.bfloat16)
        grad_query = (
            jnp.einsum("hqk,khd->qhd", grad_scores, key_one, preferred_element_type=jnp.float32)
            * scale
        )
        grad_key = (
            jnp.einsum("hqk,qhd->khd", grad_scores, query_one, preferred_element_type=jnp.float32)
            * scale
        )
        return jnp.concatenate([grad_query, grad_key, grad_value], axis=1)

    return lax.map(one_row, (query_rows, key_rows, value_rows, row_segments, log_norm, grad_mixed))


def apply_update(weight, grad, moment, average, decay):
    step_grad = grad + decay * weight
    new_moment = momentum_rate * moment + step_grad
    new_weight = weight - learn_rate * (step_grad + momentum_rate * new_moment)
    fresh_running_mean = average_rate * average + (1.0 - average_rate) * new_weight
    return (new_weight, new_moment, fresh_running_mean)


def bf16_round(values):
    return lax.reduce_precision(values, exponent_bits=8, mantissa_bits=7)


def flat_index(sizes):
    idx = 0
    for name, size in zip(AXES, sizes):
        idx = idx * size + lax.axis_index(name)
    return idx


def device_of(flat, sizes):
    coords = []
    for size in reversed(sizes):
        coords.append(lax.rem(flat, size))
        flat = flat // size
    return tuple(reversed(coords))


def enter_all(n, sizes, me):
    barrier = pltpu.get_barrier_semaphore()

    def greet(k, carry):
        peer = lax.rem(me + k, n)
        pl.semaphore_signal(barrier, inc=1, device_id=device_of(peer, sizes), device_id_type=MESH)
        return carry

    lax.fori_loop(1, n, greet, 0)
    pl.semaphore_wait(barrier, n - 1)


def gather_kernel(n, sizes, x_ref, out_ref, send_sem, recv_sem):
    me = flat_index(sizes)
    enter_all(n, sizes, me)

    def send(k, carry):
        peer = lax.rem(me + k, n)
        pltpu.make_async_remote_copy(
            src_ref=x_ref, dst_ref=out_ref.at[me], send_sem=send_sem.at[k], recv_sem=recv_sem.at[me],
            device_id=device_of(peer, sizes), device_id_type=MESH,
        ).start()
        return carry

    lax.fori_loop(1, n, send, 0)
    out_ref[me] = x_ref[...]

    def finish(k, carry):
        peer = lax.rem(me + k, n)
        src = lax.rem(me + n - k, n)
        pltpu.make_async_remote_copy(
            src_ref=x_ref, dst_ref=out_ref.at[me], send_sem=send_sem.at[k], recv_sem=recv_sem.at[me],
            device_id=device_of(peer, sizes), device_id_type=MESH,
        ).wait_send()
        pltpu.make_async_remote_copy(
            src_ref=x_ref, dst_ref=out_ref.at[src], send_sem=send_sem.at[k], recv_sem=recv_sem.at[src],
            device_id=device_of(src, sizes), device_id_type=MESH,
        ).wait_recv()
        return carry

    lax.fori_loop(1, n, finish, 0)


def small_gather(x, sizes, cid):
    n = math.prod(sizes)
    return pl.pallas_call(
        functools.partial(gather_kernel, n, sizes),
        out_shape=jax.ShapeDtypeStruct((n,) + x.shape, x.dtype),
        in_specs=[pl.BlockSpec(memory_space=pltpu.VMEM)],
        out_specs=pl.BlockSpec(memory_space=pltpu.VMEM),
        scratch_shapes=[pltpu.SemaphoreType.DMA((n,)), pltpu.SemaphoreType.DMA((n,))],
        compiler_params=pltpu.CompilerParams(collective_id=cid, has_side_effects=True),
    )(x)


def scatter_kernel(n, sizes, x_ref, out_ref, send_sem, recv_sem):
    me = flat_index(sizes)
    enter_all(n, sizes, me)

    def send(k, carry):
        peer = lax.rem(me + k, n)
        pltpu.make_async_remote_copy(
            src_ref=x_ref.at[peer], dst_ref=out_ref.at[me], send_sem=send_sem.at[k], recv_sem=recv_sem.at[me],
            device_id=device_of(peer, sizes), device_id_type=MESH,
        ).start()
        return carry

    lax.fori_loop(1, n, send, 0)
    out_ref[me] = x_ref[me]

    def finish(k, carry):
        peer = lax.rem(me + k, n)
        src = lax.rem(me + n - k, n)
        pltpu.make_async_remote_copy(
            src_ref=x_ref.at[peer], dst_ref=out_ref.at[me], send_sem=send_sem.at[k], recv_sem=recv_sem.at[me],
            device_id=device_of(peer, sizes), device_id_type=MESH,
        ).wait_send()
        pltpu.make_async_remote_copy(
            src_ref=x_ref.at[src], dst_ref=out_ref.at[src], send_sem=send_sem.at[k], recv_sem=recv_sem.at[src],
            device_id=device_of(src, sizes), device_id_type=MESH,
        ).wait_recv()
        return carry

    lax.fori_loop(1, n, finish, 0)


def small_scatter(x, sizes, cid):
    n = math.prod(sizes)
    return pl.pallas_call(
        functools.partial(scatter_kernel, n, sizes),
        out_shape=jax.ShapeDtypeStruct(x.shape, x.dtype),
        in_specs=[pl.BlockSpec(memory_space=pltpu.VMEM)],
        out_specs=pl.BlockSpec(memory_space=pltpu.VMEM),
        scratch_shapes=[pltpu.SemaphoreType.DMA((n,)), pltpu.SemaphoreType.DMA((n,))],
        compiler_params=pltpu.CompilerParams(collective_id=cid, has_side_effects=True),
    )(x)


def pair_gather_kernel(n, sizes, x_ref, out_ref, local_sem, send1, recv1, send2, recv2, send3, recv3):
    me = flat_index(sizes)
    chips = n // 2
    chip = me // 2
    core = lax.rem(me, 2)
    partner = me + 1 - 2 * core
    enter_all(n, sizes, me)

    local = pltpu.make_async_copy(x_ref, out_ref.at[me], local_sem)
    local.start()
    first = pltpu.make_async_remote_copy(
        src_ref=x_ref, dst_ref=out_ref.at[me], send_sem=send1, recv_sem=recv1,
        device_id=device_of(partner, sizes), device_id_type=MESH,
    )
    first.start()
    local.wait()
    first.wait_send()
    pltpu.make_async_remote_copy(
        src_ref=x_ref, dst_ref=out_ref.at[partner], send_sem=send1, recv_sem=recv1,
        device_id=device_of(partner, sizes), device_id_type=MESH,
    ).wait_recv()

    def pair(c):
        return out_ref.at[pl.ds(2 * c, 2)]

    def target(k):
        return lax.rem(chip + 2 * k - 1 + core, chips)

    def source(k):
        return lax.rem(chip + chips - (2 * k - 1 + core), chips)

    count = (chips - core) // 2

    def send_out(k, carry):
        other = target(k)
        pltpu.make_async_remote_copy(
            src_ref=pair(chip), dst_ref=pair(chip), send_sem=send2.at[other], recv_sem=recv2.at[chip],
            device_id=device_of(2 * other + core, sizes), device_id_type=MESH,
        ).start()
        return carry

    lax.fori_loop(1, count + 1, send_out, 0)

    def take_in(k, carry):
        other = source(k)
        pltpu.make_async_remote_copy(
            src_ref=pair(other), dst_ref=pair(other), send_sem=send2.at[other], recv_sem=recv2.at[other],
            device_id=device_of(2 * other + core, sizes), device_id_type=MESH,
        ).wait_recv()
        pltpu.make_async_remote_copy(
            src_ref=pair(other), dst_ref=pair(other), send_sem=send3.at[other], recv_sem=recv3.at[other],
            device_id=device_of(partner, sizes), device_id_type=MESH,
        ).start()
        return carry

    lax.fori_loop(1, count + 1, take_in, 0)

    def sent_out(k, carry):
        other = target(k)
        pltpu.make_async_remote_copy(
            src_ref=pair(chip), dst_ref=pair(chip), send_sem=send2.at[other], recv_sem=recv2.at[chip],
            device_id=device_of(2 * other + core, sizes), device_id_type=MESH,
        ).wait_send()
        return carry

    lax.fori_loop(1, count + 1, sent_out, 0)

    def forwarded(k, carry):
        other = source(k)
        pltpu.make_async_remote_copy(
            src_ref=pair(other), dst_ref=pair(other), send_sem=send3.at[other], recv_sem=recv3.at[other],
            device_id=device_of(partner, sizes), device_id_type=MESH,
        ).wait_send()
        return carry

    lax.fori_loop(1, count + 1, forwarded, 0)

    other_count = (chips - (1 - core)) // 2

    def partner_source(k):
        return lax.rem(chip + chips - (2 * k - 1 + (1 - core)), chips)

    def from_partner(k, carry):
        other = partner_source(k)
        pltpu.make_async_remote_copy(
            src_ref=pair(other), dst_ref=pair(other), send_sem=send3.at[other], recv_sem=recv3.at[other],
            device_id=device_of(partner, sizes), device_id_type=MESH,
        ).wait_recv()
        return carry

    lax.fori_loop(1, other_count + 1, from_partner, 0)


def pair_gather(x, sizes, cid):
    n = math.prod(sizes)
    chips = n // 2
    dma = pltpu.SemaphoreType.DMA
    return pl.pallas_call(
        functools.partial(pair_gather_kernel, n, sizes),
        out_shape=jax.ShapeDtypeStruct((n,) + x.shape, x.dtype),
        in_specs=[pl.BlockSpec(memory_space=pltpu.VMEM)],
        out_specs=pl.BlockSpec(memory_space=pltpu.VMEM),
        scratch_shapes=[dma(()), dma(()), dma(()), dma((chips,)), dma((chips,)), dma((chips,)), dma((chips,))],
        compiler_params=pltpu.CompilerParams(collective_id=cid, has_side_effects=True),
    )(x)


def contrastive(embed_b, gathered, partner_all, me):
    own_texts = embed_b.shape[0]
    all_texts = gathered.shape[0]
    chunk = min(all_texts, 1024)
    on_rows = (((1,), (1,)), ((), ()))

    def chunk_stats(c):
        rows_b = lax.dynamic_slice_in_dim(gathered, c * chunk, chunk)
        sim = lax.dot_general(rows_b, gathered, on_rows, preferred_element_type=jnp.float32) / logit_divisor
        column_ids = lax.broadcasted_iota(jnp.int32, sim.shape, 1)
        row_ids = lax.broadcasted_iota(jnp.int32, sim.shape, 0) + c * chunk
        masked = jnp.where(column_ids == row_ids, masked_value, sim)
        row_max = jnp.max(masked, -1, keepdims=True)
        log_sum = row_max + jnp.log(jnp.sum(jnp.exp(masked - row_max), -1, keepdims=True))
        wanted = lax.dynamic_slice_in_dim(partner_all, c * chunk, chunk)
        positive = jnp.sum(jnp.where(column_ids == wanted[:, None], sim, 0.0), -1)
        return log_sum[:, 0], positive

    if all_texts == chunk:
        log_sum_all, positive_all = chunk_stats(0)
    else:
        log_sum_all, positive_all = lax.map(chunk_stats, jnp.arange(all_texts // chunk))
        log_sum_all = log_sum_all.reshape(-1)
        positive_all = positive_all.reshape(-1)
    mean_loss = jnp.sum(log_sum_all - positive_all) / all_texts

    own_start = me * own_texts
    own_ids = lax.broadcasted_iota(jnp.int32, (own_texts,), 0) + own_start
    own_partner = lax.dynamic_slice_in_dim(partner_all, own_start, own_texts)
    own_log_sum = lax.dynamic_slice_in_dim(log_sum_all, own_start, own_texts)

    sim_rows = lax.dot_general(embed_b, gathered, on_rows, preferred_element_type=jnp.float32) / logit_divisor
    column_ids = lax.broadcasted_iota(jnp.int32, sim_rows.shape, 1)
    masked_rows = jnp.where(column_ids == own_ids[:, None], masked_value, sim_rows)
    grad_rows = (
        jnp.exp(masked_rows - own_log_sum[:, None]) - (column_ids == own_partner[:, None]).astype(jnp.float32)
    ).astype(jnp.bfloat16)

    sim_cols = lax.dot_general(gathered, embed_b, on_rows, preferred_element_type=jnp.float32) / logit_divisor
    row_ids = lax.broadcasted_iota(jnp.int32, sim_cols.shape, 0)
    masked_cols = jnp.where(row_ids == own_ids[None, :], masked_value, sim_cols)
    grad_cols = (
        jnp.exp(masked_cols - log_sum_all[:, None]) - (partner_all[:, None] == own_ids[None, :]).astype(jnp.float32)
    ).astype(jnp.bfloat16)

    on_tokens = (((0,), (0,)), ((), ()))
    embedding_gradient = (
        jnp.dot(grad_rows, gathered, preferred_element_type=jnp.float32)
        + lax.dot_general(grad_cols, gathered, on_tokens, preferred_element_type=jnp.float32)
    ) / logit_divisor
    return mean_loss, embedding_gradient


def shards(
    hidden_in,
    segments,
    partner,
    attn_weights,
    ffn_weights,
    vectors,
    attn_momentum,
    ffn_momentum,
    vector_momentum,
    attn_averaged,
    ffn_averaged,
    vector_averaged,
):
    sizes = tuple(lax.axis_size(name) for name in AXES)
    n_dev = math.prod(sizes)
    me = flat_index(sizes)
    vec_len = vectors.shape[0]
    small = jnp.concatenate([vectors, partner.astype(jnp.float32)])[None, :]
    small_all = small_gather(small, sizes, 0)[:, 0, :]
    vector_f = bf16_round(small_all[:, :vec_len].reshape(-1))
    partner_all = small_all[:, vec_len:].reshape(-1).astype(jnp.int32)
    attn_full, ffn_full = (
        lax.all_gather(attn_weights.astype(jnp.bfloat16), AXES, axis=1, tiled=True),
        lax.all_gather(ffn_weights.astype(jnp.bfloat16), AXES, axis=1, tiled=True),
    )
    width = attn_full.shape[0]
    hidden = ffn_full.shape[1] // 2
    query_bias = vector_f[0:width]
    value_bias = vector_f[width : 2 * width]
    output_bias = vector_f[2 * width : 3 * width]
    gain_first = vector_f[3 * width : 4 * width]
    shift_first = vector_f[4 * width : 5 * width]
    upper_bias = vector_f[5 * width : 5 * width + hidden]
    lower_bias = vector_f[5 * width + hidden : 6 * width + hidden]
    gain_second = vector_f[6 * width + hidden : 7 * width + hidden]
    shift_second = vector_f[7 * width + hidden : 8 * width + hidden]
    w_qkv = attn_full[:, : 3 * width]
    w_output = attn_full[:, 3 * width :]
    w_upper = ffn_full[:, :hidden]
    w_lower = ffn_full[:, hidden:]
    rows_dev, seq_len = segments.shape
    tokens_n = rows_dev * seq_len
    on_rows = (((1,), (1,)), ((), ()))
    on_tokens = (((0,), (0,)), ((), ()))
    qkv_bias = jnp.concatenate([query_bias, jnp.zeros_like(query_bias), value_bias])
    qkv_rows = (jnp.dot(hidden_in, w_qkv, preferred_element_type=jnp.float32) + qkv_bias).astype(
        jnp.bfloat16
    )
    heads = qkv_rows.reshape(rows_dev, seq_len, 3, HEADS, HD)
    query_rows = heads[:, :, 0]
    key_rows = heads[:, :, 1]
    value_rows = heads[:, :, 2]
    mixed, log_norm = attend_rows(query_rows, key_rows, value_rows, segments)
    mixed_flat = mixed.reshape(tokens_n, width)
    first_sum = (
        hidden_in.astype(jnp.float32)
        + jnp.dot(mixed_flat, w_output, preferred_element_type=jnp.float32)
        + output_bias
    )
    normed, normal_one, inverse_one = layer_norm_parts(first_sum, gain_first, shift_first)
    normed_r = bf16_round(normed)
    normed_b = normed_r.astype(jnp.bfloat16)
    upper = jnp.dot(normed_b, w_upper, preferred_element_type=jnp.float32) + upper_bias
    active_b = jax.nn.gelu(upper, approximate=False).astype(jnp.bfloat16)
    second_sum = (
        normed_r
        + lax.dot_general(active_b, w_lower, on_rows, preferred_element_type=jnp.float32)
        + lower_bias
    )
    result, normal_two, inverse_two = layer_norm_parts(second_sum, gain_second, shift_second)
    text_ids = jnp.arange(SEGS, dtype=jnp.int32)
    one_hot = (segments[:, None, :] == text_ids[None, :, None]).astype(jnp.float32)
    counts = jnp.sum(one_hot, -1, keepdims=True)
    pooled = (
        jnp.einsum(
            "rts,rsd->rtd",
            one_hot,
            result.reshape(rows_dev, seq_len, width),
            precision=lax.Precision.HIGHEST,
        )
        / counts
    ).reshape(-1, width)
    inv_norm = lax.rsqrt(jnp.sum(pooled * pooled, -1, keepdims=True) + pool_epsilon)
    embed_b = (pooled * inv_norm).astype(jnp.bfloat16)
    gathered_embeddings = pair_gather(embed_b, sizes, 2).reshape(-1, width)
    mean_loss, embedding_gradient = contrastive(embed_b, gathered_embeddings, partner_all, me)
    grad_pooled = inv_norm * embedding_gradient - pooled * (
        inv_norm * inv_norm * inv_norm
    ) * jnp.sum(embedding_gradient * pooled, -1, keepdims=True)
    derivative_output = jnp.einsum(
        "rts,rtd->rsd",
        one_hot,
        grad_pooled.reshape(rows_dev, SEGS, width) / counts,
        precision=lax.Precision.HIGHEST,
    ).reshape(tokens_n, width)
    grad_second, gain_two_grad, shift_two_grad = layer_norm_back(
        derivative_output, normal_two, inverse_two, gain_second
    )
    lower_bias_grad = jnp.sum(grad_second, 0)
    lower_grad_b = grad_second.astype(jnp.bfloat16)
    lower_w_grad_t = lax.dot_general(
        active_b, lower_grad_b, on_tokens, preferred_element_type=jnp.float32
    )
    grad_active = jnp.dot(lower_grad_b, w_lower, preferred_element_type=jnp.float32)
    cumulative = 0.5 * (1.0 + lax.erf(upper / math.sqrt(2.0)))
    density = jnp.exp(-0.5 * upper * upper) / math.sqrt(2.0 * math.pi)
    grad_upper = grad_active * (cumulative + upper * density)
    upper_bias_grad = jnp.sum(grad_upper, 0)
    upper_grad_b = grad_upper.astype(jnp.bfloat16)
    upper_w_grad_t = lax.dot_general(
        upper_grad_b, normed_b, on_tokens, preferred_element_type=jnp.float32
    )
    ffn_grad_t = jnp.concatenate([upper_w_grad_t, lower_w_grad_t], 0)
    grad_normed = (
        lax.dot_general(upper_grad_b, w_upper, on_rows, preferred_element_type=jnp.float32)
        + grad_second
    )
    grad_first, gain_one_grad, shift_one_grad = layer_norm_back(
        grad_normed, normal_one, inverse_one, gain_first
    )
    output_bias_grad = jnp.sum(grad_first, 0)
    first_grad_b = grad_first.astype(jnp.bfloat16)
    output_w_grad_t = lax.dot_general(
        first_grad_b, mixed_flat, on_tokens, preferred_element_type=jnp.float32
    )
    grad_mixed = lax.dot_general(
        first_grad_b, w_output, on_rows, preferred_element_type=jnp.float32
    ).astype(jnp.bfloat16)
    grad_mixed = grad_mixed.reshape(rows_dev, seq_len, HEADS, HD)
    qkv_grad = attend_back(
        query_rows, key_rows, value_rows, segments, log_norm, grad_mixed
    ).reshape(tokens_n, 3 * width)
    qkv_grad_f = bf16_round(qkv_grad)
    qkv_grad_b = qkv_grad_f.astype(jnp.bfloat16)
    query_bias_grad = jnp.sum(qkv_grad_f[:, :width], 0)
    value_bias_grad = jnp.sum(qkv_grad_f[:, 2 * width :], 0)
    qkv_w_grad_t = lax.dot_general(
        qkv_grad_b, hidden_in, on_tokens, preferred_element_type=jnp.float32
    )
    input_grad = (
        lax.dot_general(qkv_grad_b, w_qkv, on_rows, preferred_element_type=jnp.float32) + grad_first
    )
    attn_grad_t = jnp.concatenate([qkv_w_grad_t, output_w_grad_t], 0)
    vector_grad = jnp.concatenate(
        [
            query_bias_grad,
            value_bias_grad,
            output_bias_grad,
            gain_one_grad,
            shift_one_grad,
            upper_bias_grad,
            lower_bias_grad,
            gain_two_grad,
            shift_two_grad,
        ]
    )
    vector_slots = small_scatter(vector_grad.reshape(n_dev, 1, -1), sizes, 1)
    vector_reduced = jnp.sum(vector_slots[:, 0, :], 0)
    attn_cols = attn_grad_t.shape[0] // n_dev
    joined = jnp.concatenate(
        [attn_grad_t.reshape(n_dev, attn_cols, width), ffn_grad_t.reshape(n_dev, -1, width)], 1
    ).reshape(-1, width)
    joined_reduced = lax.psum_scatter(joined.astype(GRAD_SEND), AXES, scatter_dimension=0, tiled=True)
    joined_reduced = joined_reduced.astype(jnp.float32)
    attn_reduced = joined_reduced[:attn_cols].T
    ffn_reduced = joined_reduced[attn_cols:].T
    attn_new, attn_moment, attn_average = apply_update(
        attn_weights, attn_reduced, attn_momentum, attn_averaged, decay_rate
    )
    ffn_new, ffn_moment, ffn_average = apply_update(
        ffn_weights, ffn_reduced, ffn_momentum, ffn_averaged, decay_rate
    )
    vector_new, vector_moment, vector_average = apply_update(
        vectors, vector_reduced, vector_momentum, vector_averaged, 0.0
    )
    return (
        mean_loss,
        input_grad,
        attn_reduced,
        ffn_reduced,
        vector_reduced,
        attn_new,
        ffn_new,
        vector_new,
        attn_moment,
        ffn_moment,
        vector_moment,
        attn_average,
        ffn_average,
        vector_average,
    )


def solution(mesh):
    in_specs = (
        P(("dp", "rep"), None),
        P(("dp", "rep"), None),
        P(("dp", "rep")),
        P(None, ("dp", "rep")),
        P(None, ("dp", "rep")),
        P(("dp", "rep")),
        P(None, ("dp", "rep")),
        P(None, ("dp", "rep")),
        P(("dp", "rep")),
        P(None, ("dp", "rep")),
        P(None, ("dp", "rep")),
        P(("dp", "rep")),
    )
    out_specs = (
        P(),
        P(("dp", "rep"), None),
        P(None, ("dp", "rep")),
        P(None, ("dp", "rep")),
        P(("dp", "rep")),
        P(None, ("dp", "rep")),
        P(None, ("dp", "rep")),
        P(("dp", "rep")),
        P(None, ("dp", "rep")),
        P(None, ("dp", "rep")),
        P(("dp", "rep")),
        P(None, ("dp", "rep")),
        P(None, ("dp", "rep")),
        P(("dp", "rep")),
    )
    return jax.shard_map(shards, mesh=mesh, in_specs=in_specs, out_specs=out_specs, check_vma=False)
```

```python
import functools
import math

import jax
import jax.numpy as jnp
from jax import lax
from jax.experimental import pallas as pl
from jax.experimental.pallas import tpu as pltpu
from jax.sharding import PartitionSpec as P

MESH = pl.DeviceIdType.MESH
GRAD_SEND = jnp.bfloat16
AXES = ("dp", "rep")

HEADS = 12
HD = 64
SEGS = 16


ln_epsilon = 1e-12
pool_epsilon = 1e-06
logit_divisor = 0.025
learn_rate = 0.01
momentum_rate = 0.9
decay_rate = 0.01
average_rate = 0.75
masked_value = -1e30


def layer_norm_parts(values, gain, shift):
    per_line_average = jnp.mean(values, -1, keepdims=True)
    centred = values - per_line_average
    inverse = lax.rsqrt(jnp.mean(centred * centred, -1, keepdims=True) + ln_epsilon)
    normal_part = centred * inverse
    return (normal_part * gain + shift, normal_part, inverse)


def layer_norm_back(grad_out, normal_part, inverse, gain):
    scaled = grad_out * gain
    grad_in = inverse * (
        scaled
        - jnp.mean(scaled, -1, keepdims=True)
        - normal_part * jnp.mean(scaled * normal_part, -1, keepdims=True)
    )
    return (grad_in, jnp.sum(grad_out * normal_part, 0), jnp.sum(grad_out, 0))


def row_scores(query_one, key_one, segment_one, scale):
    scores = (
        jnp.einsum("qhd,khd->hqk", query_one, key_one, preferred_element_type=jnp.float32) * scale
    )
    same_text = segment_one[:, None] == segment_one[None, :]
    return jnp.where(same_text[None], scores, masked_value)


def attend_rows(query_rows, key_rows, value_rows, row_segments):
    scale = 1.0 / math.sqrt(query_rows.shape[-1])

    def one_row(row_args):
        query_one, key_one, value_one, segment_one = row_args
        scores = row_scores(query_one, key_one, segment_one, scale)
        row_max = jnp.max(scores, -1, keepdims=True)
        exp_scores = jnp.exp(scores - row_max)
        sums = jnp.sum(exp_scores, -1, keepdims=True)
        attn_probs = exp_scores / sums
        mixed = jnp.einsum(
            "hqk,khd->qhd",
            attn_probs.astype(jnp.bfloat16),
            value_one,
            preferred_element_type=jnp.float32,
        )
        return (mixed.astype(jnp.bfloat16), (row_max + jnp.log(sums))[..., 0])

    return lax.map(one_row, (query_rows, key_rows, value_rows, row_segments))


def attend_back(query_rows, key_rows, value_rows, row_segments, log_norm, grad_mixed):
    scale = 1.0 / math.sqrt(query_rows.shape[-1])

    def one_row(row_args):
        query_one, key_one, value_one, segment_one, norm_one, grad_one = row_args
        scores = row_scores(query_one, key_one, segment_one, scale)
        attn_probs = jnp.exp(scores - norm_one[..., None])
        grad_value = jnp.einsum(
            "hqk,qhd->khd",
            attn_probs.astype(jnp.bfloat16),
            grad_one,
            preferred_element_type=jnp.float32,
        )
        grad_probs = jnp.einsum(
            "qhd,khd->hqk", grad_one, value_one, preferred_element_type=jnp.float32
        )
        inner = jnp.sum(attn_probs * grad_probs, -1, keepdims=True)
        grad_scores = (attn_probs * (grad_probs - inner)).astype(jnp.bfloat16)
        grad_query = (
            jnp.einsum("hqk,khd->qhd", grad_scores, key_one, preferred_element_type=jnp.float32)
            * scale
        )
        grad_key = (
            jnp.einsum("hqk,qhd->khd", grad_scores, query_one, preferred_element_type=jnp.float32)
            * scale
        )
        return jnp.concatenate([grad_query, grad_key, grad_value], axis=1)

    return lax.map(one_row, (query_rows, key_rows, value_rows, row_segments, log_norm, grad_mixed))


def attention_back_kernel(scale, q_ref, k_ref, v_ref, g_ref, norm_ref, seg_col_ref, seg_row_ref, dq_ref, dk_ref, dv_ref):
    pair = pl.program_id(1)
    width = q_ref.shape[1]
    half = width // 2
    lane = lax.broadcasted_iota(jnp.int32, (1, width), 1)
    same = seg_col_ref[...] == seg_row_ref[0]
    norms = norm_ref[...]
    norm_lane = lax.broadcasted_iota(jnp.int32, norms.shape, 1)
    q = q_ref[...]
    k = k_ref[...]
    v = v_ref[...]
    g = g_ref[...]
    zero_b = jnp.zeros_like(q)
    on_last = (((1,), (1,)), ((), ()))
    on_first = (((0,), (0,)), ((), ()))
    dq = jnp.zeros(q.shape, jnp.float32)
    dk = jnp.zeros(q.shape, jnp.float32)
    dv = jnp.zeros(q.shape, jnp.float32)
    for head in range(2):
        mine = (lane >= head * half) & (lane < (head + 1) * half)
        q_h = jnp.where(mine, q, zero_b)
        g_h = jnp.where(mine, g, zero_b)
        norm_h = jnp.sum(jnp.where(norm_lane == 2 * pair + head, norms, 0.0), 1, keepdims=True)
        scores = lax.dot_general(q_h, k, on_last, preferred_element_type=jnp.float32) * scale
        scores = jnp.where(same, scores, masked_value)
        probs = jnp.exp(scores - norm_h)
        grad_v = lax.dot_general(probs.astype(jnp.bfloat16), g, on_first, preferred_element_type=jnp.float32)
        grad_p = lax.dot_general(g_h, v, on_last, preferred_element_type=jnp.float32)
        inner = jnp.sum(probs * grad_p, -1, keepdims=True)
        grad_s = (probs * (grad_p - inner)).astype(jnp.bfloat16)
        grad_q = jnp.dot(grad_s, k, preferred_element_type=jnp.float32) * scale
        grad_k = lax.dot_general(grad_s, q, on_first, preferred_element_type=jnp.float32) * scale
        dq = jnp.where(mine, grad_q, dq)
        dk = jnp.where(mine, grad_k, dk)
        dv = jnp.where(mine, grad_v, dv)
    dq_ref[...] = dq.astype(dq_ref.dtype)
    dk_ref[...] = dk.astype(dk_ref.dtype)
    dv_ref[...] = dv.astype(dv_ref.dtype)


def attention_back(qkv_rows, grad_mixed_flat, norm_tokens, segments, heads, head_dim):
    tokens, three_width = qkv_rows.shape
    width = three_width // 3
    rows, seq_len = segments.shape
    pair_width = 2 * head_dim
    pairs = heads // 2
    seg_col = segments.reshape(tokens, 1)
    seg_row = segments.reshape(rows, 1, seq_len)
    scale = 1.0 / math.sqrt(head_dim)
    out = jax.ShapeDtypeStruct((tokens, width), jnp.bfloat16)
    return pl.pallas_call(
        functools.partial(attention_back_kernel, scale),
        grid=(rows, pairs),
        in_specs=[
            pl.BlockSpec((seq_len, pair_width), lambda r, p: (r, p)),
            pl.BlockSpec((seq_len, pair_width), lambda r, p: (r, pairs + p)),
            pl.BlockSpec((seq_len, pair_width), lambda r, p: (r, 2 * pairs + p)),
            pl.BlockSpec((seq_len, pair_width), lambda r, p: (r, p)),
            pl.BlockSpec((seq_len, heads), lambda r, p: (r, 0)),
            pl.BlockSpec((seq_len, 1), lambda r, p: (r, 0)),
            pl.BlockSpec((1, 1, seq_len), lambda r, p: (r, 0, 0)),
        ],
        out_specs=[pl.BlockSpec((seq_len, pair_width), lambda r, p: (r, p))] * 3,
        out_shape=[out, out, out],
        compiler_params=pltpu.CompilerParams(vmem_limit_bytes=48 * 1024 * 1024),
        cost_estimate=pl.CostEstimate(
            flops=10 * rows * heads * seq_len * seq_len * pair_width,
            transcendentals=rows * heads * seq_len * seq_len,
            bytes_accessed=tokens * (three_width + 4 * width) * 2,
        ),
    )(qkv_rows, qkv_rows, qkv_rows, grad_mixed_flat, norm_tokens, seg_col, seg_row)


def apply_update(weight, grad, moment, average, decay):
    step_grad = grad + decay * weight
    new_moment = momentum_rate * moment + step_grad
    new_weight = weight - learn_rate * (step_grad + momentum_rate * new_moment)
    fresh_running_mean = average_rate * average + (1.0 - average_rate) * new_weight
    return (new_weight, new_moment, fresh_running_mean)


def bf16_round(values):
    return lax.reduce_precision(values, exponent_bits=8, mantissa_bits=7)


def flat_index(sizes):
    idx = 0
    for name, size in zip(AXES, sizes):
        idx = idx * size + lax.axis_index(name)
    return idx


def device_of(flat, sizes):
    coords = []
    for size in reversed(sizes):
        coords.append(lax.rem(flat, size))
        flat = flat // size
    return tuple(reversed(coords))


def enter_all(n, sizes, me):
    barrier = pltpu.get_barrier_semaphore()

    def greet(k, carry):
        peer = lax.rem(me + k, n)
        pl.semaphore_signal(barrier, inc=1, device_id=device_of(peer, sizes), device_id_type=MESH)
        return carry

    lax.fori_loop(1, n, greet, 0)
    pl.semaphore_wait(barrier, n - 1)


def gather_kernel(n, sizes, x_ref, out_ref, send_sem, recv_sem):
    me = flat_index(sizes)
    enter_all(n, sizes, me)

    def send(k, carry):
        peer = lax.rem(me + k, n)
        pltpu.make_async_remote_copy(
            src_ref=x_ref, dst_ref=out_ref.at[me], send_sem=send_sem.at[k], recv_sem=recv_sem.at[me],
            device_id=device_of(peer, sizes), device_id_type=MESH,
        ).start()
        return carry

    lax.fori_loop(1, n, send, 0)
    out_ref[me] = x_ref[...]

    def finish(k, carry):
        peer = lax.rem(me + k, n)
        src = lax.rem(me + n - k, n)
        pltpu.make_async_remote_copy(
            src_ref=x_ref, dst_ref=out_ref.at[me], send_sem=send_sem.at[k], recv_sem=recv_sem.at[me],
            device_id=device_of(peer, sizes), device_id_type=MESH,
        ).wait_send()
        pltpu.make_async_remote_copy(
            src_ref=x_ref, dst_ref=out_ref.at[src], send_sem=send_sem.at[k], recv_sem=recv_sem.at[src],
            device_id=device_of(src, sizes), device_id_type=MESH,
        ).wait_recv()
        return carry

    lax.fori_loop(1, n, finish, 0)


def small_gather(x, sizes, cid):
    n = math.prod(sizes)
    return pl.pallas_call(
        functools.partial(gather_kernel, n, sizes),
        out_shape=jax.ShapeDtypeStruct((n,) + x.shape, x.dtype),
        in_specs=[pl.BlockSpec(memory_space=pltpu.VMEM)],
        out_specs=pl.BlockSpec(memory_space=pltpu.VMEM),
        scratch_shapes=[pltpu.SemaphoreType.DMA((n,)), pltpu.SemaphoreType.DMA((n,))],
        compiler_params=pltpu.CompilerParams(collective_id=cid, has_side_effects=True),
    )(x)


def scatter_kernel(n, sizes, x_ref, out_ref, send_sem, recv_sem):
    me = flat_index(sizes)
    enter_all(n, sizes, me)

    def send(k, carry):
        peer = lax.rem(me + k, n)
        pltpu.make_async_remote_copy(
            src_ref=x_ref.at[peer], dst_ref=out_ref.at[me], send_sem=send_sem.at[k], recv_sem=recv_sem.at[me],
            device_id=device_of(peer, sizes), device_id_type=MESH,
        ).start()
        return carry

    lax.fori_loop(1, n, send, 0)
    out_ref[me] = x_ref[me]

    def finish(k, carry):
        peer = lax.rem(me + k, n)
        src = lax.rem(me + n - k, n)
        pltpu.make_async_remote_copy(
            src_ref=x_ref.at[peer], dst_ref=out_ref.at[me], send_sem=send_sem.at[k], recv_sem=recv_sem.at[me],
            device_id=device_of(peer, sizes), device_id_type=MESH,
        ).wait_send()
        pltpu.make_async_remote_copy(
            src_ref=x_ref.at[src], dst_ref=out_ref.at[src], send_sem=send_sem.at[k], recv_sem=recv_sem.at[src],
            device_id=device_of(src, sizes), device_id_type=MESH,
        ).wait_recv()
        return carry

    lax.fori_loop(1, n, finish, 0)


def small_scatter(x, sizes, cid):
    n = math.prod(sizes)
    return pl.pallas_call(
        functools.partial(scatter_kernel, n, sizes),
        out_shape=jax.ShapeDtypeStruct(x.shape, x.dtype),
        in_specs=[pl.BlockSpec(memory_space=pltpu.VMEM)],
        out_specs=pl.BlockSpec(memory_space=pltpu.VMEM),
        scratch_shapes=[pltpu.SemaphoreType.DMA((n,)), pltpu.SemaphoreType.DMA((n,))],
        compiler_params=pltpu.CompilerParams(collective_id=cid, has_side_effects=True),
    )(x)


def pair_gather_kernel(n, sizes, x_ref, out_ref, local_sem, send1, recv1, send2, recv2, send3, recv3):
    me = flat_index(sizes)
    chips = n // 2
    chip = me // 2
    core = lax.rem(me, 2)
    partner = me + 1 - 2 * core
    enter_all(n, sizes, me)

    local = pltpu.make_async_copy(x_ref, out_ref.at[me], local_sem)
    local.start()
    first = pltpu.make_async_remote_copy(
        src_ref=x_ref, dst_ref=out_ref.at[me], send_sem=send1, recv_sem=recv1,
        device_id=device_of(partner, sizes), device_id_type=MESH,
    )
    first.start()
    local.wait()
    first.wait_send()
    pltpu.make_async_remote_copy(
        src_ref=x_ref, dst_ref=out_ref.at[partner], send_sem=send1, recv_sem=recv1,
        device_id=device_of(partner, sizes), device_id_type=MESH,
    ).wait_recv()

    def pair(c):
        return out_ref.at[pl.ds(2 * c, 2)]

    def target(k):
        return lax.rem(chip + 2 * k - 1 + core, chips)

    def source(k):
        return lax.rem(chip + chips - (2 * k - 1 + core), chips)

    count = (chips - core) // 2

    def send_out(k, carry):
        other = target(k)
        pltpu.make_async_remote_copy(
            src_ref=pair(chip), dst_ref=pair(chip), send_sem=send2.at[other], recv_sem=recv2.at[chip],
            device_id=device_of(2 * other + core, sizes), device_id_type=MESH,
        ).start()
        return carry

    lax.fori_loop(1, count + 1, send_out, 0)

    def take_in(k, carry):
        other = source(k)
        pltpu.make_async_remote_copy(
            src_ref=pair(other), dst_ref=pair(other), send_sem=send2.at[other], recv_sem=recv2.at[other],
            device_id=device_of(2 * other + core, sizes), device_id_type=MESH,
        ).wait_recv()
        pltpu.make_async_remote_copy(
            src_ref=pair(other), dst_ref=pair(other), send_sem=send3.at[other], recv_sem=recv3.at[other],
            device_id=device_of(partner, sizes), device_id_type=MESH,
        ).start()
        return carry

    lax.fori_loop(1, count + 1, take_in, 0)

    def sent_out(k, carry):
        other = target(k)
        pltpu.make_async_remote_copy(
            src_ref=pair(chip), dst_ref=pair(chip), send_sem=send2.at[other], recv_sem=recv2.at[chip],
            device_id=device_of(2 * other + core, sizes), device_id_type=MESH,
        ).wait_send()
        return carry

    lax.fori_loop(1, count + 1, sent_out, 0)

    def forwarded(k, carry):
        other = source(k)
        pltpu.make_async_remote_copy(
            src_ref=pair(other), dst_ref=pair(other), send_sem=send3.at[other], recv_sem=recv3.at[other],
            device_id=device_of(partner, sizes), device_id_type=MESH,
        ).wait_send()
        return carry

    lax.fori_loop(1, count + 1, forwarded, 0)

    other_count = (chips - (1 - core)) // 2

    def partner_source(k):
        return lax.rem(chip + chips - (2 * k - 1 + (1 - core)), chips)

    def from_partner(k, carry):
        other = partner_source(k)
        pltpu.make_async_remote_copy(
            src_ref=pair(other), dst_ref=pair(other), send_sem=send3.at[other], recv_sem=recv3.at[other],
            device_id=device_of(partner, sizes), device_id_type=MESH,
        ).wait_recv()
        return carry

    lax.fori_loop(1, other_count + 1, from_partner, 0)


def pair_gather(x, sizes, cid):
    n = math.prod(sizes)
    chips = n // 2
    dma = pltpu.SemaphoreType.DMA
    return pl.pallas_call(
        functools.partial(pair_gather_kernel, n, sizes),
        out_shape=jax.ShapeDtypeStruct((n,) + x.shape, x.dtype),
        in_specs=[pl.BlockSpec(memory_space=pltpu.VMEM)],
        out_specs=pl.BlockSpec(memory_space=pltpu.VMEM),
        scratch_shapes=[dma(()), dma(()), dma(()), dma((chips,)), dma((chips,)), dma((chips,)), dma((chips,))],
        compiler_params=pltpu.CompilerParams(collective_id=cid, has_side_effects=True),
    )(x)


def contrastive(embed_b, gathered, partner_all, me):
    own_texts = embed_b.shape[0]
    all_texts = gathered.shape[0]
    chunk = min(all_texts, 1024)
    on_rows = (((1,), (1,)), ((), ()))

    def chunk_stats(c):
        rows_b = lax.dynamic_slice_in_dim(gathered, c * chunk, chunk)
        sim = lax.dot_general(rows_b, gathered, on_rows, preferred_element_type=jnp.float32) / logit_divisor
        column_ids = lax.broadcasted_iota(jnp.int32, sim.shape, 1)
        row_ids = lax.broadcasted_iota(jnp.int32, sim.shape, 0) + c * chunk
        masked = jnp.where(column_ids == row_ids, masked_value, sim)
        row_max = jnp.max(masked, -1, keepdims=True)
        log_sum = row_max + jnp.log(jnp.sum(jnp.exp(masked - row_max), -1, keepdims=True))
        wanted = lax.dynamic_slice_in_dim(partner_all, c * chunk, chunk)
        positive = jnp.sum(jnp.where(column_ids == wanted[:, None], sim, 0.0), -1)
        return log_sum[:, 0], positive

    if all_texts == chunk:
        log_sum_all, positive_all = chunk_stats(0)
    else:
        log_sum_all, positive_all = lax.map(chunk_stats, jnp.arange(all_texts // chunk))
        log_sum_all = log_sum_all.reshape(-1)
        positive_all = positive_all.reshape(-1)
    mean_loss = jnp.sum(log_sum_all - positive_all) / all_texts

    own_start = me * own_texts
    own_ids = lax.broadcasted_iota(jnp.int32, (own_texts,), 0) + own_start
    own_partner = lax.dynamic_slice_in_dim(partner_all, own_start, own_texts)
    own_log_sum = lax.dynamic_slice_in_dim(log_sum_all, own_start, own_texts)

    sim_rows = lax.dot_general(embed_b, gathered, on_rows, preferred_element_type=jnp.float32) / logit_divisor
    column_ids = lax.broadcasted_iota(jnp.int32, sim_rows.shape, 1)
    masked_rows = jnp.where(column_ids == own_ids[:, None], masked_value, sim_rows)
    grad_rows = (
        jnp.exp(masked_rows - own_log_sum[:, None]) - (column_ids == own_partner[:, None]).astype(jnp.float32)
    ).astype(jnp.bfloat16)

    sim_cols = lax.dot_general(gathered, embed_b, on_rows, preferred_element_type=jnp.float32) / logit_divisor
    row_ids = lax.broadcasted_iota(jnp.int32, sim_cols.shape, 0)
    masked_cols = jnp.where(row_ids == own_ids[None, :], masked_value, sim_cols)
    grad_cols = (
        jnp.exp(masked_cols - log_sum_all[:, None]) - (partner_all[:, None] == own_ids[None, :]).astype(jnp.float32)
    ).astype(jnp.bfloat16)

    on_tokens = (((0,), (0,)), ((), ()))
    embedding_gradient = (
        jnp.dot(grad_rows, gathered, preferred_element_type=jnp.float32)
        + lax.dot_general(grad_cols, gathered, on_tokens, preferred_element_type=jnp.float32)
    ) / logit_divisor
    return mean_loss, embedding_gradient


def shards(
    hidden_in,
    segments,
    partner,
    attn_weights,
    ffn_weights,
    vectors,
    attn_momentum,
    ffn_momentum,
    vector_momentum,
    attn_averaged,
    ffn_averaged,
    vector_averaged,
):
    sizes = tuple(lax.axis_size(name) for name in AXES)
    n_dev = math.prod(sizes)
    me = flat_index(sizes)
    vec_len = vectors.shape[0]
    small = jnp.concatenate([vectors, partner.astype(jnp.float32)])[None, :]
    small_all = small_gather(small, sizes, 0)[:, 0, :]
    vector_f = bf16_round(small_all[:, :vec_len].reshape(-1))
    partner_all = small_all[:, vec_len:].reshape(-1).astype(jnp.int32)
    attn_full, ffn_full = (
        lax.all_gather(attn_weights.astype(jnp.bfloat16), AXES, axis=1, tiled=True),
        lax.all_gather(ffn_weights.astype(jnp.bfloat16), AXES, axis=1, tiled=True),
    )
    width = attn_full.shape[0]
    hidden = ffn_full.shape[1] // 2
    query_bias = vector_f[0:width]
    value_bias = vector_f[width : 2 * width]
    output_bias = vector_f[2 * width : 3 * width]
    gain_first = vector_f[3 * width : 4 * width]
    shift_first = vector_f[4 * width : 5 * width]
    upper_bias = vector_f[5 * width : 5 * width + hidden]
    lower_bias = vector_f[5 * width + hidden : 6 * width + hidden]
    gain_second = vector_f[6 * width + hidden : 7 * width + hidden]
    shift_second = vector_f[7 * width + hidden : 8 * width + hidden]
    w_qkv = attn_full[:, : 3 * width]
    w_output = attn_full[:, 3 * width :]
    w_upper = ffn_full[:, :hidden]
    w_lower = ffn_full[:, hidden:]
    rows_dev, seq_len = segments.shape
    tokens_n = rows_dev * seq_len
    on_rows = (((1,), (1,)), ((), ()))
    on_tokens = (((0,), (0,)), ((), ()))
    qkv_bias = jnp.concatenate([query_bias, jnp.zeros_like(query_bias), value_bias])
    qkv_rows = (jnp.dot(hidden_in, w_qkv, preferred_element_type=jnp.float32) + qkv_bias).astype(
        jnp.bfloat16
    )
    heads = qkv_rows.reshape(rows_dev, seq_len, 3, HEADS, HD)
    query_rows = heads[:, :, 0]
    key_rows = heads[:, :, 1]
    value_rows = heads[:, :, 2]
    mixed, log_norm = attend_rows(query_rows, key_rows, value_rows, segments)
    mixed_flat = mixed.reshape(tokens_n, width)
    first_sum = (
        hidden_in.astype(jnp.float32)
        + jnp.dot(mixed_flat, w_output, preferred_element_type=jnp.float32)
        + output_bias
    )
    normed, normal_one, inverse_one = layer_norm_parts(first_sum, gain_first, shift_first)
    normed_r = bf16_round(normed)
    normed_b = normed_r.astype(jnp.bfloat16)
    upper = jnp.dot(normed_b, w_upper, preferred_element_type=jnp.float32) + upper_bias
    active_b = jax.nn.gelu(upper, approximate=False).astype(jnp.bfloat16)
    second_sum = (
        normed_r
        + lax.dot_general(active_b, w_lower, on_rows, preferred_element_type=jnp.float32)
        + lower_bias
    )
    result, normal_two, inverse_two = layer_norm_parts(second_sum, gain_second, shift_second)
    text_ids = jnp.arange(SEGS, dtype=jnp.int32)
    one_hot = (segments[:, None, :] == text_ids[None, :, None]).astype(jnp.float32)
    counts = jnp.sum(one_hot, -1, keepdims=True)
    pooled = (
        jnp.einsum(
            "rts,rsd->rtd",
            one_hot,
            result.reshape(rows_dev, seq_len, width),
            precision=lax.Precision.HIGHEST,
        )
        / counts
    ).reshape(-1, width)
    inv_norm = lax.rsqrt(jnp.sum(pooled * pooled, -1, keepdims=True) + pool_epsilon)
    embed_b = (pooled * inv_norm).astype(jnp.bfloat16)
    gathered_embeddings = pair_gather(embed_b, sizes, 2).reshape(-1, width)
    mean_loss, embedding_gradient = contrastive(embed_b, gathered_embeddings, partner_all, me)
    grad_pooled = inv_norm * embedding_gradient - pooled * (
        inv_norm * inv_norm * inv_norm
    ) * jnp.sum(embedding_gradient * pooled, -1, keepdims=True)
    derivative_output = jnp.einsum(
        "rts,rtd->rsd",
        one_hot,
        grad_pooled.reshape(rows_dev, SEGS, width) / counts,
        precision=lax.Precision.HIGHEST,
    ).reshape(tokens_n, width)
    grad_second, gain_two_grad, shift_two_grad = layer_norm_back(
        derivative_output, normal_two, inverse_two, gain_second
    )
    lower_bias_grad = jnp.sum(grad_second, 0)
    lower_grad_b = grad_second.astype(jnp.bfloat16)
    lower_w_grad_t = lax.dot_general(
        active_b, lower_grad_b, on_tokens, preferred_element_type=jnp.float32
    )
    grad_active = jnp.dot(lower_grad_b, w_lower, preferred_element_type=jnp.float32)
    cumulative = 0.5 * (1.0 + lax.erf(upper / math.sqrt(2.0)))
    density = jnp.exp(-0.5 * upper * upper) / math.sqrt(2.0 * math.pi)
    grad_upper = grad_active * (cumulative + upper * density)
    upper_bias_grad = jnp.sum(grad_upper, 0)
    upper_grad_b = grad_upper.astype(jnp.bfloat16)
    upper_w_grad_t = lax.dot_general(
        upper_grad_b, normed_b, on_tokens, preferred_element_type=jnp.float32
    )
    ffn_grad_t = jnp.concatenate([upper_w_grad_t, lower_w_grad_t], 0)
    grad_normed = (
        lax.dot_general(upper_grad_b, w_upper, on_rows, preferred_element_type=jnp.float32)
        + grad_second
    )
    grad_first, gain_one_grad, shift_one_grad = layer_norm_back(
        grad_normed, normal_one, inverse_one, gain_first
    )
    output_bias_grad = jnp.sum(grad_first, 0)
    first_grad_b = grad_first.astype(jnp.bfloat16)
    output_w_grad_t = lax.dot_general(
        first_grad_b, mixed_flat, on_tokens, preferred_element_type=jnp.float32
    )
    grad_mixed = lax.dot_general(
        first_grad_b, w_output, on_rows, preferred_element_type=jnp.float32
    ).astype(jnp.bfloat16)
    grad_mixed = grad_mixed.reshape(rows_dev, seq_len, HEADS, HD)
    norm_tokens = jnp.swapaxes(log_norm, 1, 2).reshape(tokens_n, HEADS)
    qkv_grad = jnp.concatenate(
        attention_back(qkv_rows, grad_mixed.reshape(tokens_n, width), norm_tokens, segments, HEADS, HD), 1
    ).astype(jnp.float32)
    qkv_grad_f = bf16_round(qkv_grad)
    qkv_grad_b = qkv_grad_f.astype(jnp.bfloat16)
    query_bias_grad = jnp.sum(qkv_grad_f[:, :width], 0)
    value_bias_grad = jnp.sum(qkv_grad_f[:, 2 * width :], 0)
    qkv_w_grad_t = lax.dot_general(
        qkv_grad_b, hidden_in, on_tokens, preferred_element_type=jnp.float32
    )
    input_grad = (
        lax.dot_general(qkv_grad_b, w_qkv, on_rows, preferred_element_type=jnp.float32) + grad_first
    )
    attn_grad_t = jnp.concatenate([qkv_w_grad_t, output_w_grad_t], 0)
    vector_grad = jnp.concatenate(
        [
            query_bias_grad,
            value_bias_grad,
            output_bias_grad,
            gain_one_grad,
            shift_one_grad,
            upper_bias_grad,
            lower_bias_grad,
            gain_two_grad,
            shift_two_grad,
        ]
    )
    vector_slots = small_scatter(vector_grad.reshape(n_dev, 1, -1), sizes, 1)
    vector_reduced = jnp.sum(vector_slots[:, 0, :], 0)
    attn_cols = attn_grad_t.shape[0] // n_dev
    joined = jnp.concatenate(
        [attn_grad_t.reshape(n_dev, attn_cols, width), ffn_grad_t.reshape(n_dev, -1, width)], 1
    ).reshape(-1, width)
    joined_reduced = lax.psum_scatter(joined.astype(GRAD_SEND), AXES, scatter_dimension=0, tiled=True)
    joined_reduced = joined_reduced.astype(jnp.float32)
    attn_reduced = joined_reduced[:attn_cols].T
    ffn_reduced = joined_reduced[attn_cols:].T
    attn_new, attn_moment, attn_average = apply_update(
        attn_weights, attn_reduced, attn_momentum, attn_averaged, decay_rate
    )
    ffn_new, ffn_moment, ffn_average = apply_update(
        ffn_weights, ffn_reduced, ffn_momentum, ffn_averaged, decay_rate
    )
    vector_new, vector_moment, vector_average = apply_update(
        vectors, vector_reduced, vector_momentum, vector_averaged, 0.0
    )
    return (
        mean_loss,
        input_grad,
        attn_reduced,
        ffn_reduced,
        vector_reduced,
        attn_new,
        ffn_new,
        vector_new,
        attn_moment,
        ffn_moment,
        vector_moment,
        attn_average,
        ffn_average,
        vector_average,
    )


def solution(mesh):
    in_specs = (
        P(("dp", "rep"), None),
        P(("dp", "rep"), None),
        P(("dp", "rep")),
        P(None, ("dp", "rep")),
        P(None, ("dp", "rep")),
        P(("dp", "rep")),
        P(None, ("dp", "rep")),
        P(None, ("dp", "rep")),
        P(("dp", "rep")),
        P(None, ("dp", "rep")),
        P(None, ("dp", "rep")),
        P(("dp", "rep")),
    )
    out_specs = (
        P(),
        P(("dp", "rep"), None),
        P(None, ("dp", "rep")),
        P(None, ("dp", "rep")),
        P(("dp", "rep")),
        P(None, ("dp", "rep")),
        P(None, ("dp", "rep")),
        P(("dp", "rep")),
        P(None, ("dp", "rep")),
        P(None, ("dp", "rep")),
        P(("dp", "rep")),
        P(None, ("dp", "rep")),
        P(None, ("dp", "rep")),
        P(("dp", "rep")),
    )
    return jax.shard_map(shards, mesh=mesh, in_specs=in_specs, out_specs=out_specs, check_vma=False)
```

```python
import functools
import math

import jax
import jax.numpy as jnp
from jax import lax
from jax.experimental import pallas as pl
from jax.experimental.pallas import tpu as pltpu
from jax.sharding import PartitionSpec as P

MESH = pl.DeviceIdType.MESH
GRAD_SEND = jnp.bfloat16
AXES = ("dp", "rep")

HEADS = 12
HD = 64
SEGS = 16


ln_epsilon = 1e-12
pool_epsilon = 1e-06
logit_divisor = 0.025
learn_rate = 0.01
momentum_rate = 0.9
decay_rate = 0.01
average_rate = 0.75
masked_value = -1e30


def layer_norm_parts(values, gain, shift):
    per_line_average = jnp.mean(values, -1, keepdims=True)
    centred = values - per_line_average
    inverse = lax.rsqrt(jnp.mean(centred * centred, -1, keepdims=True) + ln_epsilon)
    normal_part = centred * inverse
    return (normal_part * gain + shift, normal_part, inverse)


def layer_norm_back(grad_out, normal_part, inverse, gain):
    scaled = grad_out * gain
    grad_in = inverse * (
        scaled
        - jnp.mean(scaled, -1, keepdims=True)
        - normal_part * jnp.mean(scaled * normal_part, -1, keepdims=True)
    )
    return (grad_in, jnp.sum(grad_out * normal_part, 0), jnp.sum(grad_out, 0))


def row_scores(query_one, key_one, segment_one, scale):
    scores = (
        jnp.einsum("qhd,khd->hqk", query_one, key_one, preferred_element_type=jnp.float32) * scale
    )
    same_text = segment_one[:, None] == segment_one[None, :]
    return jnp.where(same_text[None], scores, masked_value)


def attend_rows(query_rows, key_rows, value_rows, row_segments):
    scale = 1.0 / math.sqrt(query_rows.shape[-1])

    def one_row(row_args):
        query_one, key_one, value_one, segment_one = row_args
        scores = row_scores(query_one, key_one, segment_one, scale)
        row_max = jnp.max(scores, -1, keepdims=True)
        exp_scores = jnp.exp(scores - row_max)
        sums = jnp.sum(exp_scores, -1, keepdims=True)
        attn_probs = exp_scores / sums
        mixed = jnp.einsum(
            "hqk,khd->qhd",
            attn_probs.astype(jnp.bfloat16),
            value_one,
            preferred_element_type=jnp.float32,
        )
        return (mixed.astype(jnp.bfloat16), (row_max + jnp.log(sums))[..., 0])

    return lax.map(one_row, (query_rows, key_rows, value_rows, row_segments))


def attend_back(query_rows, key_rows, value_rows, row_segments, log_norm, grad_mixed):
    scale = 1.0 / math.sqrt(query_rows.shape[-1])

    def one_row(row_args):
        query_one, key_one, value_one, segment_one, norm_one, grad_one = row_args
        scores = row_scores(query_one, key_one, segment_one, scale)
        attn_probs = jnp.exp(scores - norm_one[..., None])
        grad_value = jnp.einsum(
            "hqk,qhd->khd",
            attn_probs.astype(jnp.bfloat16),
            grad_one,
            preferred_element_type=jnp.float32,
        )
        grad_probs = jnp.einsum(
            "qhd,khd->hqk", grad_one, value_one, preferred_element_type=jnp.float32
        )
        inner = jnp.sum(attn_probs * grad_probs, -1, keepdims=True)
        grad_scores = (attn_probs * (grad_probs - inner)).astype(jnp.bfloat16)
        grad_query = (
            jnp.einsum("hqk,khd->qhd", grad_scores, key_one, preferred_element_type=jnp.float32)
            * scale
        )
        grad_key = (
            jnp.einsum("hqk,qhd->khd", grad_scores, query_one, preferred_element_type=jnp.float32)
            * scale
        )
        return jnp.concatenate([grad_query, grad_key, grad_value], axis=1)

    return lax.map(one_row, (query_rows, key_rows, value_rows, row_segments, log_norm, grad_mixed))


def attention_back_kernel(scale, q_ref, k_ref, v_ref, g_ref, norm_ref, seg_col_ref, seg_row_ref, dq_ref, dk_ref, dv_ref):
    pair = pl.program_id(1)
    width = q_ref.shape[1]
    half = width // 2
    lane = lax.broadcasted_iota(jnp.int32, (1, width), 1)
    same = seg_col_ref[...] == seg_row_ref[0]
    norms = norm_ref[...]
    norm_lane = lax.broadcasted_iota(jnp.int32, norms.shape, 1)
    q = q_ref[...]
    k = k_ref[...]
    v = v_ref[...]
    g = g_ref[...]
    zero_b = jnp.zeros_like(q)
    on_last = (((1,), (1,)), ((), ()))
    on_first = (((0,), (0,)), ((), ()))
    dq = jnp.zeros(q.shape, jnp.float32)
    dk = jnp.zeros(q.shape, jnp.float32)
    dv = jnp.zeros(q.shape, jnp.float32)
    for head in range(2):
        mine = (lane >= head * half) & (lane < (head + 1) * half)
        q_h = jnp.where(mine, q, zero_b)
        g_h = jnp.where(mine, g, zero_b)
        norm_h = jnp.sum(jnp.where(norm_lane == 2 * pair + head, norms, 0.0), 1, keepdims=True)
        scores = lax.dot_general(q_h, k, on_last, preferred_element_type=jnp.float32) * scale
        scores = jnp.where(same, scores, masked_value)
        probs = jnp.exp(scores - norm_h)
        grad_v = lax.dot_general(probs.astype(jnp.bfloat16), g, on_first, preferred_element_type=jnp.float32)
        grad_p = lax.dot_general(g_h, v, on_last, preferred_element_type=jnp.float32)
        inner = jnp.sum(probs * grad_p, -1, keepdims=True)
        grad_s = (probs * (grad_p - inner)).astype(jnp.bfloat16)
        grad_q = jnp.dot(grad_s, k, preferred_element_type=jnp.float32) * scale
        grad_k = lax.dot_general(grad_s, q, on_first, preferred_element_type=jnp.float32) * scale
        dq = jnp.where(mine, grad_q, dq)
        dk = jnp.where(mine, grad_k, dk)
        dv = jnp.where(mine, grad_v, dv)
    dq_ref[...] = dq.astype(dq_ref.dtype)
    dk_ref[...] = dk.astype(dk_ref.dtype)
    dv_ref[...] = dv.astype(dv_ref.dtype)


def attention_back(qkv_rows, grad_mixed_flat, norm_tokens, segments, heads, head_dim):
    tokens, three_width = qkv_rows.shape
    width = three_width // 3
    rows, seq_len = segments.shape
    pair_width = 2 * head_dim
    pairs = heads // 2
    seg_col = segments.reshape(tokens, 1)
    seg_row = segments.reshape(rows, 1, seq_len)
    scale = 1.0 / math.sqrt(head_dim)
    out = jax.ShapeDtypeStruct((tokens, width), jnp.bfloat16)
    return pl.pallas_call(
        functools.partial(attention_back_kernel, scale),
        grid=(rows, pairs),
        in_specs=[
            pl.BlockSpec((seq_len, pair_width), lambda r, p: (r, p)),
            pl.BlockSpec((seq_len, pair_width), lambda r, p: (r, pairs + p)),
            pl.BlockSpec((seq_len, pair_width), lambda r, p: (r, 2 * pairs + p)),
            pl.BlockSpec((seq_len, pair_width), lambda r, p: (r, p)),
            pl.BlockSpec((seq_len, heads), lambda r, p: (r, 0)),
            pl.BlockSpec((seq_len, 1), lambda r, p: (r, 0)),
            pl.BlockSpec((1, 1, seq_len), lambda r, p: (r, 0, 0)),
        ],
        out_specs=[pl.BlockSpec((seq_len, pair_width), lambda r, p: (r, p))] * 3,
        out_shape=[out, out, out],
        compiler_params=pltpu.CompilerParams(vmem_limit_bytes=48 * 1024 * 1024),
        cost_estimate=pl.CostEstimate(
            flops=10 * rows * heads * seq_len * seq_len * pair_width,
            transcendentals=rows * heads * seq_len * seq_len,
            bytes_accessed=tokens * (three_width + 4 * width) * 2,
        ),
    )(qkv_rows, qkv_rows, qkv_rows, grad_mixed_flat, norm_tokens, seg_col, seg_row)


def apply_update(weight, grad, moment, average, decay):
    step_grad = grad + decay * weight
    new_moment = momentum_rate * moment + step_grad
    new_weight = weight - learn_rate * (step_grad + momentum_rate * new_moment)
    fresh_running_mean = average_rate * average + (1.0 - average_rate) * new_weight
    return (new_weight, new_moment, fresh_running_mean)


def bf16_round(values):
    return lax.reduce_precision(values, exponent_bits=8, mantissa_bits=7)


def flat_index(sizes):
    idx = 0
    for name, size in zip(AXES, sizes):
        idx = idx * size + lax.axis_index(name)
    return idx


def device_of(flat, sizes):
    coords = []
    for size in reversed(sizes):
        coords.append(lax.rem(flat, size))
        flat = flat // size
    return tuple(reversed(coords))


def enter_all(n, sizes, me):
    barrier = pltpu.get_barrier_semaphore()

    def greet(k, carry):
        peer = lax.rem(me + k, n)
        pl.semaphore_signal(barrier, inc=1, device_id=device_of(peer, sizes), device_id_type=MESH)
        return carry

    lax.fori_loop(1, n, greet, 0)
    pl.semaphore_wait(barrier, n - 1)


def gather_kernel(n, sizes, x_ref, out_ref, send_sem, recv_sem):
    me = flat_index(sizes)
    enter_all(n, sizes, me)

    def send(k, carry):
        peer = lax.rem(me + k, n)
        pltpu.make_async_remote_copy(
            src_ref=x_ref, dst_ref=out_ref.at[me], send_sem=send_sem.at[k], recv_sem=recv_sem.at[me],
            device_id=device_of(peer, sizes), device_id_type=MESH,
        ).start()
        return carry

    lax.fori_loop(1, n, send, 0)
    out_ref[me] = x_ref[...]

    def finish(k, carry):
        peer = lax.rem(me + k, n)
        src = lax.rem(me + n - k, n)
        pltpu.make_async_remote_copy(
            src_ref=x_ref, dst_ref=out_ref.at[me], send_sem=send_sem.at[k], recv_sem=recv_sem.at[me],
            device_id=device_of(peer, sizes), device_id_type=MESH,
        ).wait_send()
        pltpu.make_async_remote_copy(
            src_ref=x_ref, dst_ref=out_ref.at[src], send_sem=send_sem.at[k], recv_sem=recv_sem.at[src],
            device_id=device_of(src, sizes), device_id_type=MESH,
        ).wait_recv()
        return carry

    lax.fori_loop(1, n, finish, 0)


def small_gather(x, sizes, cid):
    n = math.prod(sizes)
    return pl.pallas_call(
        functools.partial(gather_kernel, n, sizes),
        out_shape=jax.ShapeDtypeStruct((n,) + x.shape, x.dtype),
        in_specs=[pl.BlockSpec(memory_space=pltpu.VMEM)],
        out_specs=pl.BlockSpec(memory_space=pltpu.VMEM),
        scratch_shapes=[pltpu.SemaphoreType.DMA((n,)), pltpu.SemaphoreType.DMA((n,))],
        compiler_params=pltpu.CompilerParams(collective_id=cid, has_side_effects=True),
    )(x)


def scatter_kernel(n, sizes, x_ref, out_ref, send_sem, recv_sem):
    me = flat_index(sizes)
    enter_all(n, sizes, me)

    def send(k, carry):
        peer = lax.rem(me + k, n)
        pltpu.make_async_remote_copy(
            src_ref=x_ref.at[peer], dst_ref=out_ref.at[me], send_sem=send_sem.at[k], recv_sem=recv_sem.at[me],
            device_id=device_of(peer, sizes), device_id_type=MESH,
        ).start()
        return carry

    lax.fori_loop(1, n, send, 0)
    out_ref[me] = x_ref[me]

    def finish(k, carry):
        peer = lax.rem(me + k, n)
        src = lax.rem(me + n - k, n)
        pltpu.make_async_remote_copy(
            src_ref=x_ref.at[peer], dst_ref=out_ref.at[me], send_sem=send_sem.at[k], recv_sem=recv_sem.at[me],
            device_id=device_of(peer, sizes), device_id_type=MESH,
        ).wait_send()
        pltpu.make_async_remote_copy(
            src_ref=x_ref.at[src], dst_ref=out_ref.at[src], send_sem=send_sem.at[k], recv_sem=recv_sem.at[src],
            device_id=device_of(src, sizes), device_id_type=MESH,
        ).wait_recv()
        return carry

    lax.fori_loop(1, n, finish, 0)


def small_scatter(x, sizes, cid):
    n = math.prod(sizes)
    return pl.pallas_call(
        functools.partial(scatter_kernel, n, sizes),
        out_shape=jax.ShapeDtypeStruct(x.shape, x.dtype),
        in_specs=[pl.BlockSpec(memory_space=pltpu.VMEM)],
        out_specs=pl.BlockSpec(memory_space=pltpu.VMEM),
        scratch_shapes=[pltpu.SemaphoreType.DMA((n,)), pltpu.SemaphoreType.DMA((n,))],
        compiler_params=pltpu.CompilerParams(collective_id=cid, has_side_effects=True),
    )(x)


def pair_gather_kernel(n, sizes, x_ref, out_ref, local_sem, send1, recv1, send2, recv2, send3, recv3):
    me = flat_index(sizes)
    chips = n // 2
    chip = me // 2
    core = lax.rem(me, 2)
    partner = me + 1 - 2 * core
    enter_all(n, sizes, me)

    local = pltpu.make_async_copy(x_ref, out_ref.at[me], local_sem)
    local.start()
    first = pltpu.make_async_remote_copy(
        src_ref=x_ref, dst_ref=out_ref.at[me], send_sem=send1, recv_sem=recv1,
        device_id=device_of(partner, sizes), device_id_type=MESH,
    )
    first.start()
    local.wait()
    first.wait_send()
    pltpu.make_async_remote_copy(
        src_ref=x_ref, dst_ref=out_ref.at[partner], send_sem=send1, recv_sem=recv1,
        device_id=device_of(partner, sizes), device_id_type=MESH,
    ).wait_recv()

    def pair(c):
        return out_ref.at[pl.ds(2 * c, 2)]

    def target(k):
        return lax.rem(chip + 2 * k - 1 + core, chips)

    def source(k):
        return lax.rem(chip + chips - (2 * k - 1 + core), chips)

    count = (chips - core) // 2

    def send_out(k, carry):
        other = target(k)
        pltpu.make_async_remote_copy(
            src_ref=pair(chip), dst_ref=pair(chip), send_sem=send2.at[other], recv_sem=recv2.at[chip],
            device_id=device_of(2 * other + core, sizes), device_id_type=MESH,
        ).start()
        return carry

    lax.fori_loop(1, count + 1, send_out, 0)

    def take_in(k, carry):
        other = source(k)
        pltpu.make_async_remote_copy(
            src_ref=pair(other), dst_ref=pair(other), send_sem=send2.at[other], recv_sem=recv2.at[other],
            device_id=device_of(2 * other + core, sizes), device_id_type=MESH,
        ).wait_recv()
        pltpu.make_async_remote_copy(
            src_ref=pair(other), dst_ref=pair(other), send_sem=send3.at[other], recv_sem=recv3.at[other],
            device_id=device_of(partner, sizes), device_id_type=MESH,
        ).start()
        return carry

    lax.fori_loop(1, count + 1, take_in, 0)

    def sent_out(k, carry):
        other = target(k)
        pltpu.make_async_remote_copy(
            src_ref=pair(chip), dst_ref=pair(chip), send_sem=send2.at[other], recv_sem=recv2.at[chip],
            device_id=device_of(2 * other + core, sizes), device_id_type=MESH,
        ).wait_send()
        return carry

    lax.fori_loop(1, count + 1, sent_out, 0)

    def forwarded(k, carry):
        other = source(k)
        pltpu.make_async_remote_copy(
            src_ref=pair(other), dst_ref=pair(other), send_sem=send3.at[other], recv_sem=recv3.at[other],
            device_id=device_of(partner, sizes), device_id_type=MESH,
        ).wait_send()
        return carry

    lax.fori_loop(1, count + 1, forwarded, 0)

    other_count = (chips - (1 - core)) // 2

    def partner_source(k):
        return lax.rem(chip + chips - (2 * k - 1 + (1 - core)), chips)

    def from_partner(k, carry):
        other = partner_source(k)
        pltpu.make_async_remote_copy(
            src_ref=pair(other), dst_ref=pair(other), send_sem=send3.at[other], recv_sem=recv3.at[other],
            device_id=device_of(partner, sizes), device_id_type=MESH,
        ).wait_recv()
        return carry

    lax.fori_loop(1, other_count + 1, from_partner, 0)


def pair_gather(x, sizes, cid):
    n = math.prod(sizes)
    chips = n // 2
    dma = pltpu.SemaphoreType.DMA
    return pl.pallas_call(
        functools.partial(pair_gather_kernel, n, sizes),
        out_shape=jax.ShapeDtypeStruct((n,) + x.shape, x.dtype),
        in_specs=[pl.BlockSpec(memory_space=pltpu.VMEM)],
        out_specs=pl.BlockSpec(memory_space=pltpu.VMEM),
        scratch_shapes=[dma(()), dma(()), dma(()), dma((chips,)), dma((chips,)), dma((chips,)), dma((chips,))],
        compiler_params=pltpu.CompilerParams(collective_id=cid, has_side_effects=True),
    )(x)


def contrastive(embed_b, gathered, partner_all, me):
    own_texts = embed_b.shape[0]
    all_texts = gathered.shape[0]
    chunk = min(all_texts, 1024)
    on_rows = (((1,), (1,)), ((), ()))

    def chunk_stats(c):
        rows_b = lax.dynamic_slice_in_dim(gathered, c * chunk, chunk)
        sim = lax.dot_general(rows_b, gathered, on_rows, preferred_element_type=jnp.float32) / logit_divisor
        column_ids = lax.broadcasted_iota(jnp.int32, sim.shape, 1)
        row_ids = lax.broadcasted_iota(jnp.int32, sim.shape, 0) + c * chunk
        masked = jnp.where(column_ids == row_ids, masked_value, sim)
        row_max = jnp.max(masked, -1, keepdims=True)
        log_sum = row_max + jnp.log(jnp.sum(jnp.exp(masked - row_max), -1, keepdims=True))
        wanted = lax.dynamic_slice_in_dim(partner_all, c * chunk, chunk)
        positive = jnp.sum(jnp.where(column_ids == wanted[:, None], sim, 0.0), -1)
        return log_sum[:, 0], positive

    if all_texts == chunk:
        log_sum_all, positive_all = chunk_stats(0)
    else:
        log_sum_all, positive_all = lax.map(chunk_stats, jnp.arange(all_texts // chunk))
        log_sum_all = log_sum_all.reshape(-1)
        positive_all = positive_all.reshape(-1)
    mean_loss = jnp.sum(log_sum_all - positive_all) / all_texts

    own_start = me * own_texts
    own_ids = lax.broadcasted_iota(jnp.int32, (own_texts,), 0) + own_start
    own_partner = lax.dynamic_slice_in_dim(partner_all, own_start, own_texts)
    own_log_sum = lax.dynamic_slice_in_dim(log_sum_all, own_start, own_texts)

    sim_rows = lax.dot_general(embed_b, gathered, on_rows, preferred_element_type=jnp.float32) / logit_divisor
    column_ids = lax.broadcasted_iota(jnp.int32, sim_rows.shape, 1)
    masked_rows = jnp.where(column_ids == own_ids[:, None], masked_value, sim_rows)
    grad_rows = (
        jnp.exp(masked_rows - own_log_sum[:, None]) - (column_ids == own_partner[:, None]).astype(jnp.float32)
    ).astype(jnp.bfloat16)

    sim_cols = lax.dot_general(gathered, embed_b, on_rows, preferred_element_type=jnp.float32) / logit_divisor
    row_ids = lax.broadcasted_iota(jnp.int32, sim_cols.shape, 0)
    masked_cols = jnp.where(row_ids == own_ids[None, :], masked_value, sim_cols)
    grad_cols = (
        jnp.exp(masked_cols - log_sum_all[:, None]) - (partner_all[:, None] == own_ids[None, :]).astype(jnp.float32)
    ).astype(jnp.bfloat16)

    on_tokens = (((0,), (0,)), ((), ()))
    embedding_gradient = (
        jnp.dot(grad_rows, gathered, preferred_element_type=jnp.float32)
        + lax.dot_general(grad_cols, gathered, on_tokens, preferred_element_type=jnp.float32)
    ) / logit_divisor
    return mean_loss, embedding_gradient


def shards(
    hidden_in,
    segments,
    partner,
    attn_weights,
    ffn_weights,
    vectors,
    attn_momentum,
    ffn_momentum,
    vector_momentum,
    attn_averaged,
    ffn_averaged,
    vector_averaged,
):
    sizes = tuple(lax.axis_size(name) for name in AXES)
    n_dev = math.prod(sizes)
    me = flat_index(sizes)
    vec_len = vectors.shape[0]
    small = jnp.concatenate([vectors, partner.astype(jnp.float32)])[None, :]
    small_all = small_gather(small, sizes, 0)[:, 0, :]
    vector_f = bf16_round(small_all[:, :vec_len].reshape(-1))
    partner_all = small_all[:, vec_len:].reshape(-1).astype(jnp.int32)
    attn_full, ffn_full = (
        lax.all_gather(attn_weights.astype(jnp.bfloat16), AXES, axis=1, tiled=True),
        lax.all_gather(ffn_weights.astype(jnp.bfloat16), AXES, axis=1, tiled=True),
    )
    width = attn_full.shape[0]
    hidden = ffn_full.shape[1] // 2
    query_bias = vector_f[0:width]
    value_bias = vector_f[width : 2 * width]
    output_bias = vector_f[2 * width : 3 * width]
    gain_first = vector_f[3 * width : 4 * width]
    shift_first = vector_f[4 * width : 5 * width]
    upper_bias = vector_f[5 * width : 5 * width + hidden]
    lower_bias = vector_f[5 * width + hidden : 6 * width + hidden]
    gain_second = vector_f[6 * width + hidden : 7 * width + hidden]
    shift_second = vector_f[7 * width + hidden : 8 * width + hidden]
    w_qkv = attn_full[:, : 3 * width]
    w_output = attn_full[:, 3 * width :]
    w_upper = ffn_full[:, :hidden]
    w_lower = ffn_full[:, hidden:]
    rows_dev, seq_len = segments.shape
    tokens_n = rows_dev * seq_len
    on_rows = (((1,), (1,)), ((), ()))
    on_tokens = (((0,), (0,)), ((), ()))
    qkv_bias = jnp.concatenate([query_bias, jnp.zeros_like(query_bias), value_bias])
    qkv_rows = (jnp.dot(hidden_in, w_qkv, preferred_element_type=jnp.float32) + qkv_bias).astype(
        jnp.bfloat16
    )
    heads = qkv_rows.reshape(rows_dev, seq_len, 3, HEADS, HD)
    query_rows = heads[:, :, 0]
    key_rows = heads[:, :, 1]
    value_rows = heads[:, :, 2]
    mixed, log_norm = attend_rows(query_rows, key_rows, value_rows, segments)
    mixed_flat = mixed.reshape(tokens_n, width)
    first_sum = (
        hidden_in.astype(jnp.float32)
        + jnp.dot(mixed_flat, w_output, preferred_element_type=jnp.float32)
        + output_bias
    )
    normed, normal_one, inverse_one = layer_norm_parts(first_sum, gain_first, shift_first)
    normed_r = bf16_round(normed)
    normed_b = normed_r.astype(jnp.bfloat16)
    upper = jnp.dot(normed_b, w_upper, preferred_element_type=jnp.float32) + upper_bias
    active_b = jax.nn.gelu(upper, approximate=False).astype(jnp.bfloat16)
    second_sum = (
        normed_r
        + lax.dot_general(active_b, w_lower, on_rows, preferred_element_type=jnp.float32)
        + lower_bias
    )
    result, normal_two, inverse_two = layer_norm_parts(second_sum, gain_second, shift_second)
    text_ids = jnp.arange(SEGS, dtype=jnp.int32)
    one_hot = (segments[:, None, :] == text_ids[None, :, None]).astype(jnp.float32)
    counts = jnp.sum(one_hot, -1, keepdims=True)
    pooled = (
        jnp.einsum(
            "rts,rsd->rtd",
            one_hot,
            result.reshape(rows_dev, seq_len, width),
            precision=lax.Precision.HIGHEST,
        )
        / counts
    ).reshape(-1, width)
    inv_norm = lax.rsqrt(jnp.sum(pooled * pooled, -1, keepdims=True) + pool_epsilon)
    embed_b = (pooled * inv_norm).astype(jnp.bfloat16)
    gathered_embeddings = pair_gather(embed_b, sizes, 2).reshape(-1, width)
    mean_loss, embedding_gradient = contrastive(embed_b, gathered_embeddings, partner_all, me)
    grad_pooled = inv_norm * embedding_gradient - pooled * (
        inv_norm * inv_norm * inv_norm
    ) * jnp.sum(embedding_gradient * pooled, -1, keepdims=True)
    derivative_output = jnp.einsum(
        "rts,rtd->rsd",
        one_hot,
        grad_pooled.reshape(rows_dev, SEGS, width) / counts,
        precision=lax.Precision.HIGHEST,
    ).reshape(tokens_n, width)
    grad_second, gain_two_grad, shift_two_grad = layer_norm_back(
        derivative_output, normal_two, inverse_two, gain_second
    )
    lower_bias_grad = jnp.sum(grad_second, 0)
    lower_grad_b = grad_second.astype(jnp.bfloat16)
    lower_w_grad_t = lax.dot_general(
        active_b, lower_grad_b, on_tokens, preferred_element_type=jnp.float32
    )
    grad_active = jnp.dot(lower_grad_b, w_lower, preferred_element_type=jnp.float32)
    cumulative = 0.5 * (1.0 + lax.erf(upper / math.sqrt(2.0)))
    density = jnp.exp(-0.5 * upper * upper) / math.sqrt(2.0 * math.pi)
    grad_upper = grad_active * (cumulative + upper * density)
    upper_bias_grad = jnp.sum(grad_upper, 0)
    upper_grad_b = grad_upper.astype(jnp.bfloat16)
    upper_w_grad_t = lax.dot_general(
        upper_grad_b, normed_b, on_tokens, preferred_element_type=jnp.float32
    )
    grad_normed = (
        lax.dot_general(upper_grad_b, w_upper, on_rows, preferred_element_type=jnp.float32)
        + grad_second
    )
    grad_first, gain_one_grad, shift_one_grad = layer_norm_back(
        grad_normed, normal_one, inverse_one, gain_first
    )
    output_bias_grad = jnp.sum(grad_first, 0)
    first_grad_b = grad_first.astype(jnp.bfloat16)
    output_w_grad_t = lax.dot_general(
        first_grad_b, mixed_flat, on_tokens, preferred_element_type=jnp.float32
    )
    grad_mixed = lax.dot_general(
        first_grad_b, w_output, on_rows, preferred_element_type=jnp.float32
    ).astype(jnp.bfloat16)
    grad_mixed = grad_mixed.reshape(rows_dev, seq_len, HEADS, HD)
    norm_tokens = jnp.swapaxes(log_norm, 1, 2).reshape(tokens_n, HEADS)
    qkv_grad = jnp.concatenate(
        attention_back(qkv_rows, grad_mixed.reshape(tokens_n, width), norm_tokens, segments, HEADS, HD), 1
    ).astype(jnp.float32)
    qkv_grad_f = bf16_round(qkv_grad)
    qkv_grad_b = qkv_grad_f.astype(jnp.bfloat16)
    query_bias_grad = jnp.sum(qkv_grad_f[:, :width], 0)
    value_bias_grad = jnp.sum(qkv_grad_f[:, 2 * width :], 0)
    qkv_w_grad_t = lax.dot_general(
        qkv_grad_b, hidden_in, on_tokens, preferred_element_type=jnp.float32
    )
    input_grad = (
        lax.dot_general(qkv_grad_b, w_qkv, on_rows, preferred_element_type=jnp.float32) + grad_first
    )
    vector_grad = jnp.concatenate(
        [
            query_bias_grad,
            value_bias_grad,
            output_bias_grad,
            gain_one_grad,
            shift_one_grad,
            upper_bias_grad,
            lower_bias_grad,
            gain_two_grad,
            shift_two_grad,
        ]
    )
    vector_slots = small_scatter(vector_grad.reshape(n_dev, 1, -1), sizes, 1)
    vector_reduced = jnp.sum(vector_slots[:, 0, :], 0)
    attn_cols = (qkv_w_grad_t.shape[0] + output_w_grad_t.shape[0]) // n_dev
    ffn_cols = (upper_w_grad_t.shape[0] + lower_w_grad_t.shape[0]) // n_dev
    attn_blocks = jnp.concatenate(
        [qkv_w_grad_t.reshape(-1, attn_cols, width), output_w_grad_t.reshape(-1, attn_cols, width)], 0
    )
    ffn_blocks = jnp.concatenate(
        [upper_w_grad_t.reshape(-1, ffn_cols, width), lower_w_grad_t.reshape(-1, ffn_cols, width)], 0
    )
    joined = jnp.concatenate([attn_blocks, ffn_blocks], 1).astype(GRAD_SEND).reshape(-1, width)
    joined_reduced = lax.psum_scatter(joined, AXES, scatter_dimension=0, tiled=True)
    joined_reduced = joined_reduced.astype(jnp.float32)
    attn_reduced = joined_reduced[:attn_cols].T
    ffn_reduced = joined_reduced[attn_cols:].T
    attn_new, attn_moment, attn_average = apply_update(
        attn_weights, attn_reduced, attn_momentum, attn_averaged, decay_rate
    )
    ffn_new, ffn_moment, ffn_average = apply_update(
        ffn_weights, ffn_reduced, ffn_momentum, ffn_averaged, decay_rate
    )
    vector_new, vector_moment, vector_average = apply_update(
        vectors, vector_reduced, vector_momentum, vector_averaged, 0.0
    )
    return (
        mean_loss,
        input_grad,
        attn_reduced,
        ffn_reduced,
        vector_reduced,
        attn_new,
        ffn_new,
        vector_new,
        attn_moment,
        ffn_moment,
        vector_moment,
        attn_average,
        ffn_average,
        vector_average,
    )


def solution(mesh):
    in_specs = (
        P(("dp", "rep"), None),
        P(("dp", "rep"), None),
        P(("dp", "rep")),
        P(None, ("dp", "rep")),
        P(None, ("dp", "rep")),
        P(("dp", "rep")),
        P(None, ("dp", "rep")),
        P(None, ("dp", "rep")),
        P(("dp", "rep")),
        P(None, ("dp", "rep")),
        P(None, ("dp", "rep")),
        P(("dp", "rep")),
    )
    out_specs = (
        P(),
        P(("dp", "rep"), None),
        P(None, ("dp", "rep")),
        P(None, ("dp", "rep")),
        P(("dp", "rep")),
        P(None, ("dp", "rep")),
        P(None, ("dp", "rep")),
        P(("dp", "rep")),
        P(None, ("dp", "rep")),
        P(None, ("dp", "rep")),
        P(("dp", "rep")),
        P(None, ("dp", "rep")),
        P(None, ("dp", "rep")),
        P(("dp", "rep")),
    )
    return jax.shard_map(shards, mesh=mesh, in_specs=in_specs, out_specs=out_specs, check_vma=False)
```

```python
import functools
import math

import jax
import jax.numpy as jnp
from jax import lax
from jax.experimental import pallas as pl
from jax.experimental.pallas import tpu as pltpu
from jax.sharding import PartitionSpec as P

MESH = pl.DeviceIdType.MESH
GRAD_SEND = jnp.bfloat16
AXES = ("dp", "rep")

HEADS = 12
HD = 64
SEGS = 16


ln_epsilon = 1e-12
pool_epsilon = 1e-06
logit_divisor = 0.025
learn_rate = 0.01
momentum_rate = 0.9
decay_rate = 0.01
average_rate = 0.75
masked_value = -1e30


def layer_norm_parts(values, gain, shift):
    per_line_average = jnp.mean(values, -1, keepdims=True)
    centred = values - per_line_average
    inverse = lax.rsqrt(jnp.mean(centred * centred, -1, keepdims=True) + ln_epsilon)
    normal_part = centred * inverse
    return (normal_part * gain + shift, normal_part, inverse)


def layer_norm_back(grad_out, normal_part, inverse, gain):
    scaled = grad_out * gain
    grad_in = inverse * (
        scaled
        - jnp.mean(scaled, -1, keepdims=True)
        - normal_part * jnp.mean(scaled * normal_part, -1, keepdims=True)
    )
    return (grad_in, jnp.sum(grad_out * normal_part, 0), jnp.sum(grad_out, 0))


def row_scores(query_one, key_one, segment_one, scale):
    scores = (
        jnp.einsum("qhd,khd->hqk", query_one, key_one, preferred_element_type=jnp.float32) * scale
    )
    same_text = segment_one[:, None] == segment_one[None, :]
    return jnp.where(same_text[None], scores, masked_value)


def attend_rows(query_rows, key_rows, value_rows, row_segments):
    scale = 1.0 / math.sqrt(query_rows.shape[-1])

    def one_row(row_args):
        query_one, key_one, value_one, segment_one = row_args
        scores = row_scores(query_one, key_one, segment_one, scale)
        row_max = jnp.max(scores, -1, keepdims=True)
        exp_scores = jnp.exp(scores - row_max)
        sums = jnp.sum(exp_scores, -1, keepdims=True)
        attn_probs = exp_scores / sums
        mixed = jnp.einsum(
            "hqk,khd->qhd",
            attn_probs.astype(jnp.bfloat16),
            value_one,
            preferred_element_type=jnp.float32,
        )
        return (mixed.astype(jnp.bfloat16), (row_max + jnp.log(sums))[..., 0])

    return lax.map(one_row, (query_rows, key_rows, value_rows, row_segments))


def attend_back(query_rows, key_rows, value_rows, row_segments, log_norm, grad_mixed):
    scale = 1.0 / math.sqrt(query_rows.shape[-1])

    def one_row(row_args):
        query_one, key_one, value_one, segment_one, norm_one, grad_one = row_args
        scores = row_scores(query_one, key_one, segment_one, scale)
        attn_probs = jnp.exp(scores - norm_one[..., None])
        grad_value = jnp.einsum(
            "hqk,qhd->khd",
            attn_probs.astype(jnp.bfloat16),
            grad_one,
            preferred_element_type=jnp.float32,
        )
        grad_probs = jnp.einsum(
            "qhd,khd->hqk", grad_one, value_one, preferred_element_type=jnp.float32
        )
        inner = jnp.sum(attn_probs * grad_probs, -1, keepdims=True)
        grad_scores = (attn_probs * (grad_probs - inner)).astype(jnp.bfloat16)
        grad_query = (
            jnp.einsum("hqk,khd->qhd", grad_scores, key_one, preferred_element_type=jnp.float32)
            * scale
        )
        grad_key = (
            jnp.einsum("hqk,qhd->khd", grad_scores, query_one, preferred_element_type=jnp.float32)
            * scale
        )
        return jnp.concatenate([grad_query, grad_key, grad_value], axis=1)

    return lax.map(one_row, (query_rows, key_rows, value_rows, row_segments, log_norm, grad_mixed))


def attention_back_kernel(scale, q_ref, k_ref, v_ref, g_ref, norm_ref, seg_col_ref, seg_row_ref, dq_ref, dk_ref, dv_ref):
    pair = pl.program_id(1)
    width = q_ref.shape[1]
    half = width // 2
    lane = lax.broadcasted_iota(jnp.int32, (1, width), 1)
    same = seg_col_ref[...] == seg_row_ref[0]
    norms = norm_ref[...]
    norm_lane = lax.broadcasted_iota(jnp.int32, norms.shape, 1)
    q = q_ref[...]
    k = k_ref[...]
    v = v_ref[...]
    g = g_ref[...]
    zero_b = jnp.zeros_like(q)
    on_last = (((1,), (1,)), ((), ()))
    on_first = (((0,), (0,)), ((), ()))
    dq = jnp.zeros(q.shape, jnp.float32)
    dk = jnp.zeros(q.shape, jnp.float32)
    dv = jnp.zeros(q.shape, jnp.float32)
    for head in range(2):
        mine = (lane >= head * half) & (lane < (head + 1) * half)
        q_h = jnp.where(mine, q, zero_b)
        g_h = jnp.where(mine, g, zero_b)
        norm_h = jnp.sum(jnp.where(norm_lane == 2 * pair + head, norms, 0.0), 1, keepdims=True)
        scores = lax.dot_general(q_h, k, on_last, preferred_element_type=jnp.float32) * scale
        scores = jnp.where(same, scores, masked_value)
        probs = jnp.exp(scores - norm_h)
        grad_v = lax.dot_general(probs.astype(jnp.bfloat16), g, on_first, preferred_element_type=jnp.float32)
        grad_p = lax.dot_general(g_h, v, on_last, preferred_element_type=jnp.float32)
        inner = jnp.sum(probs * grad_p, -1, keepdims=True)
        grad_s = (probs * (grad_p - inner)).astype(jnp.bfloat16)
        grad_q = jnp.dot(grad_s, k, preferred_element_type=jnp.float32) * scale
        grad_k = lax.dot_general(grad_s, q, on_first, preferred_element_type=jnp.float32) * scale
        dq = jnp.where(mine, grad_q, dq)
        dk = jnp.where(mine, grad_k, dk)
        dv = jnp.where(mine, grad_v, dv)
    dq_ref[...] = dq.astype(dq_ref.dtype)
    dk_ref[...] = dk.astype(dk_ref.dtype)
    dv_ref[...] = dv.astype(dv_ref.dtype)


def attention_back(qkv_rows, grad_mixed_flat, norm_tokens, segments, heads, head_dim):
    tokens, three_width = qkv_rows.shape
    width = three_width // 3
    rows, seq_len = segments.shape
    pair_width = 2 * head_dim
    pairs = heads // 2
    seg_col = segments.reshape(tokens, 1)
    seg_row = segments.reshape(rows, 1, seq_len)
    scale = 1.0 / math.sqrt(head_dim)
    out = jax.ShapeDtypeStruct((tokens, width), jnp.bfloat16)
    return pl.pallas_call(
        functools.partial(attention_back_kernel, scale),
        grid=(rows, pairs),
        in_specs=[
            pl.BlockSpec((seq_len, pair_width), lambda r, p: (r, p)),
            pl.BlockSpec((seq_len, pair_width), lambda r, p: (r, pairs + p)),
            pl.BlockSpec((seq_len, pair_width), lambda r, p: (r, 2 * pairs + p)),
            pl.BlockSpec((seq_len, pair_width), lambda r, p: (r, p)),
            pl.BlockSpec((seq_len, heads), lambda r, p: (r, 0)),
            pl.BlockSpec((seq_len, 1), lambda r, p: (r, 0)),
            pl.BlockSpec((1, 1, seq_len), lambda r, p: (r, 0, 0)),
        ],
        out_specs=[pl.BlockSpec((seq_len, pair_width), lambda r, p: (r, p))] * 3,
        out_shape=[out, out, out],
        compiler_params=pltpu.CompilerParams(vmem_limit_bytes=48 * 1024 * 1024),
        cost_estimate=pl.CostEstimate(
            flops=10 * rows * heads * seq_len * seq_len * pair_width,
            transcendentals=rows * heads * seq_len * seq_len,
            bytes_accessed=tokens * (three_width + 4 * width) * 2,
        ),
    )(qkv_rows, qkv_rows, qkv_rows, grad_mixed_flat, norm_tokens, seg_col, seg_row)


def apply_update(weight, grad, moment, average, decay):
    step_grad = grad + decay * weight
    new_moment = momentum_rate * moment + step_grad
    new_weight = weight - learn_rate * (step_grad + momentum_rate * new_moment)
    fresh_running_mean = average_rate * average + (1.0 - average_rate) * new_weight
    return (new_weight, new_moment, fresh_running_mean)


def bf16_round(values):
    return lax.reduce_precision(values, exponent_bits=8, mantissa_bits=7)


def flat_index(sizes):
    idx = 0
    for name, size in zip(AXES, sizes):
        idx = idx * size + lax.axis_index(name)
    return idx


def device_of(flat, sizes):
    coords = []
    for size in reversed(sizes):
        coords.append(lax.rem(flat, size))
        flat = flat // size
    return tuple(reversed(coords))


def enter_all(n, sizes, me):
    barrier = pltpu.get_barrier_semaphore()

    def greet(k, carry):
        peer = lax.rem(me + k, n)
        pl.semaphore_signal(barrier, inc=1, device_id=device_of(peer, sizes), device_id_type=MESH)
        return carry

    lax.fori_loop(1, n, greet, 0)
    pl.semaphore_wait(barrier, n - 1)


def gather_kernel(n, sizes, x_ref, out_ref, send_sem, recv_sem):
    me = flat_index(sizes)
    enter_all(n, sizes, me)

    def send(k, carry):
        peer = lax.rem(me + k, n)
        pltpu.make_async_remote_copy(
            src_ref=x_ref, dst_ref=out_ref.at[me], send_sem=send_sem.at[k], recv_sem=recv_sem.at[me],
            device_id=device_of(peer, sizes), device_id_type=MESH,
        ).start()
        return carry

    lax.fori_loop(1, n, send, 0)
    out_ref[me] = x_ref[...]

    def finish(k, carry):
        peer = lax.rem(me + k, n)
        src = lax.rem(me + n - k, n)
        pltpu.make_async_remote_copy(
            src_ref=x_ref, dst_ref=out_ref.at[me], send_sem=send_sem.at[k], recv_sem=recv_sem.at[me],
            device_id=device_of(peer, sizes), device_id_type=MESH,
        ).wait_send()
        pltpu.make_async_remote_copy(
            src_ref=x_ref, dst_ref=out_ref.at[src], send_sem=send_sem.at[k], recv_sem=recv_sem.at[src],
            device_id=device_of(src, sizes), device_id_type=MESH,
        ).wait_recv()
        return carry

    lax.fori_loop(1, n, finish, 0)


def small_gather(x, sizes, cid):
    n = math.prod(sizes)
    return pl.pallas_call(
        functools.partial(gather_kernel, n, sizes),
        out_shape=jax.ShapeDtypeStruct((n,) + x.shape, x.dtype),
        in_specs=[pl.BlockSpec(memory_space=pltpu.VMEM)],
        out_specs=pl.BlockSpec(memory_space=pltpu.VMEM),
        scratch_shapes=[pltpu.SemaphoreType.DMA((n,)), pltpu.SemaphoreType.DMA((n,))],
        compiler_params=pltpu.CompilerParams(collective_id=cid, has_side_effects=True),
    )(x)


def scatter_kernel(n, sizes, x_ref, out_ref, send_sem, recv_sem):
    me = flat_index(sizes)
    enter_all(n, sizes, me)

    def send(k, carry):
        peer = lax.rem(me + k, n)
        pltpu.make_async_remote_copy(
            src_ref=x_ref.at[peer], dst_ref=out_ref.at[me], send_sem=send_sem.at[k], recv_sem=recv_sem.at[me],
            device_id=device_of(peer, sizes), device_id_type=MESH,
        ).start()
        return carry

    lax.fori_loop(1, n, send, 0)
    out_ref[me] = x_ref[me]

    def finish(k, carry):
        peer = lax.rem(me + k, n)
        src = lax.rem(me + n - k, n)
        pltpu.make_async_remote_copy(
            src_ref=x_ref.at[peer], dst_ref=out_ref.at[me], send_sem=send_sem.at[k], recv_sem=recv_sem.at[me],
            device_id=device_of(peer, sizes), device_id_type=MESH,
        ).wait_send()
        pltpu.make_async_remote_copy(
            src_ref=x_ref.at[src], dst_ref=out_ref.at[src], send_sem=send_sem.at[k], recv_sem=recv_sem.at[src],
            device_id=device_of(src, sizes), device_id_type=MESH,
        ).wait_recv()
        return carry

    lax.fori_loop(1, n, finish, 0)


def small_scatter(x, sizes, cid):
    n = math.prod(sizes)
    return pl.pallas_call(
        functools.partial(scatter_kernel, n, sizes),
        out_shape=jax.ShapeDtypeStruct(x.shape, x.dtype),
        in_specs=[pl.BlockSpec(memory_space=pltpu.VMEM)],
        out_specs=pl.BlockSpec(memory_space=pltpu.VMEM),
        scratch_shapes=[pltpu.SemaphoreType.DMA((n,)), pltpu.SemaphoreType.DMA((n,))],
        compiler_params=pltpu.CompilerParams(collective_id=cid, has_side_effects=True),
    )(x)


def pair_gather_kernel(n, sizes, x_ref, out_ref, local_sem, send1, recv1, send2, recv2, send3, recv3):
    me = flat_index(sizes)
    chips = n // 2
    chip = me // 2
    core = lax.rem(me, 2)
    partner = me + 1 - 2 * core
    enter_all(n, sizes, me)

    local = pltpu.make_async_copy(x_ref, out_ref.at[me], local_sem)
    local.start()
    first = pltpu.make_async_remote_copy(
        src_ref=x_ref, dst_ref=out_ref.at[me], send_sem=send1, recv_sem=recv1,
        device_id=device_of(partner, sizes), device_id_type=MESH,
    )
    first.start()
    local.wait()
    first.wait_send()
    pltpu.make_async_remote_copy(
        src_ref=x_ref, dst_ref=out_ref.at[partner], send_sem=send1, recv_sem=recv1,
        device_id=device_of(partner, sizes), device_id_type=MESH,
    ).wait_recv()

    def pair(c):
        return out_ref.at[pl.ds(2 * c, 2)]

    def target(k):
        return lax.rem(chip + 2 * k - 1 + core, chips)

    def source(k):
        return lax.rem(chip + chips - (2 * k - 1 + core), chips)

    count = (chips - core) // 2

    def send_out(k, carry):
        other = target(k)
        pltpu.make_async_remote_copy(
            src_ref=pair(chip), dst_ref=pair(chip), send_sem=send2.at[other], recv_sem=recv2.at[chip],
            device_id=device_of(2 * other + core, sizes), device_id_type=MESH,
        ).start()
        return carry

    lax.fori_loop(1, count + 1, send_out, 0)

    def take_in(k, carry):
        other = source(k)
        pltpu.make_async_remote_copy(
            src_ref=pair(other), dst_ref=pair(other), send_sem=send2.at[other], recv_sem=recv2.at[other],
            device_id=device_of(2 * other + core, sizes), device_id_type=MESH,
        ).wait_recv()
        pltpu.make_async_remote_copy(
            src_ref=pair(other), dst_ref=pair(other), send_sem=send3.at[other], recv_sem=recv3.at[other],
            device_id=device_of(partner, sizes), device_id_type=MESH,
        ).start()
        return carry

    lax.fori_loop(1, count + 1, take_in, 0)

    def sent_out(k, carry):
        other = target(k)
        pltpu.make_async_remote_copy(
            src_ref=pair(chip), dst_ref=pair(chip), send_sem=send2.at[other], recv_sem=recv2.at[chip],
            device_id=device_of(2 * other + core, sizes), device_id_type=MESH,
        ).wait_send()
        return carry

    lax.fori_loop(1, count + 1, sent_out, 0)

    def forwarded(k, carry):
        other = source(k)
        pltpu.make_async_remote_copy(
            src_ref=pair(other), dst_ref=pair(other), send_sem=send3.at[other], recv_sem=recv3.at[other],
            device_id=device_of(partner, sizes), device_id_type=MESH,
        ).wait_send()
        return carry

    lax.fori_loop(1, count + 1, forwarded, 0)

    other_count = (chips - (1 - core)) // 2

    def partner_source(k):
        return lax.rem(chip + chips - (2 * k - 1 + (1 - core)), chips)

    def from_partner(k, carry):
        other = partner_source(k)
        pltpu.make_async_remote_copy(
            src_ref=pair(other), dst_ref=pair(other), send_sem=send3.at[other], recv_sem=recv3.at[other],
            device_id=device_of(partner, sizes), device_id_type=MESH,
        ).wait_recv()
        return carry

    lax.fori_loop(1, other_count + 1, from_partner, 0)


def pair_gather(x, sizes, cid):
    n = math.prod(sizes)
    chips = n // 2
    dma = pltpu.SemaphoreType.DMA
    return pl.pallas_call(
        functools.partial(pair_gather_kernel, n, sizes),
        out_shape=jax.ShapeDtypeStruct((n,) + x.shape, x.dtype),
        in_specs=[pl.BlockSpec(memory_space=pltpu.VMEM)],
        out_specs=pl.BlockSpec(memory_space=pltpu.VMEM),
        scratch_shapes=[dma(()), dma(()), dma(()), dma((chips,)), dma((chips,)), dma((chips,)), dma((chips,))],
        compiler_params=pltpu.CompilerParams(collective_id=cid, has_side_effects=True),
    )(x)


def contrastive(embed_b, gathered, partner_all, me):
    own_texts = embed_b.shape[0]
    all_texts = gathered.shape[0]
    chunk = min(all_texts, 1024)
    on_rows = (((1,), (1,)), ((), ()))

    def chunk_stats(c):
        rows_b = lax.dynamic_slice_in_dim(gathered, c * chunk, chunk)
        sim = lax.dot_general(rows_b, gathered, on_rows, preferred_element_type=jnp.float32) / logit_divisor
        column_ids = lax.broadcasted_iota(jnp.int32, sim.shape, 1)
        row_ids = lax.broadcasted_iota(jnp.int32, sim.shape, 0) + c * chunk
        masked = jnp.where(column_ids == row_ids, masked_value, sim)
        row_max = jnp.max(masked, -1, keepdims=True)
        log_sum = row_max + jnp.log(jnp.sum(jnp.exp(masked - row_max), -1, keepdims=True))
        wanted = lax.dynamic_slice_in_dim(partner_all, c * chunk, chunk)
        positive = jnp.sum(jnp.where(column_ids == wanted[:, None], sim, 0.0), -1)
        return log_sum[:, 0], positive

    if all_texts == chunk:
        log_sum_all, positive_all = chunk_stats(0)
    else:
        log_sum_all, positive_all = lax.map(chunk_stats, jnp.arange(all_texts // chunk))
        log_sum_all = log_sum_all.reshape(-1)
        positive_all = positive_all.reshape(-1)
    mean_loss = jnp.sum(log_sum_all - positive_all) / all_texts

    own_start = me * own_texts
    own_ids = lax.broadcasted_iota(jnp.int32, (own_texts,), 0) + own_start
    own_partner = lax.dynamic_slice_in_dim(partner_all, own_start, own_texts)
    own_log_sum = lax.dynamic_slice_in_dim(log_sum_all, own_start, own_texts)

    sim_rows = lax.dot_general(embed_b, gathered, on_rows, preferred_element_type=jnp.float32) / logit_divisor
    column_ids = lax.broadcasted_iota(jnp.int32, sim_rows.shape, 1)
    masked_rows = jnp.where(column_ids == own_ids[:, None], masked_value, sim_rows)
    grad_rows = (
        jnp.exp(masked_rows - own_log_sum[:, None]) - (column_ids == own_partner[:, None]).astype(jnp.float32)
    ).astype(jnp.bfloat16)

    sim_cols = lax.dot_general(gathered, embed_b, on_rows, preferred_element_type=jnp.float32) / logit_divisor
    row_ids = lax.broadcasted_iota(jnp.int32, sim_cols.shape, 0)
    masked_cols = jnp.where(row_ids == own_ids[None, :], masked_value, sim_cols)
    grad_cols = (
        jnp.exp(masked_cols - log_sum_all[:, None]) - (partner_all[:, None] == own_ids[None, :]).astype(jnp.float32)
    ).astype(jnp.bfloat16)

    on_tokens = (((0,), (0,)), ((), ()))
    embedding_gradient = (
        jnp.dot(grad_rows, gathered, preferred_element_type=jnp.float32)
        + lax.dot_general(grad_cols, gathered, on_tokens, preferred_element_type=jnp.float32)
    ) / logit_divisor
    return mean_loss, embedding_gradient


def shards(
    hidden_in,
    segments,
    partner,
    attn_weights,
    ffn_weights,
    vectors,
    attn_momentum,
    ffn_momentum,
    vector_momentum,
    attn_averaged,
    ffn_averaged,
    vector_averaged,
):
    sizes = tuple(lax.axis_size(name) for name in AXES)
    n_dev = math.prod(sizes)
    me = flat_index(sizes)
    vec_len = vectors.shape[0]
    own_texts_n = partner.shape[0]
    width = attn_weights.shape[0]
    attn_local_t = attn_weights.T.astype(jnp.bfloat16)
    digit = 64
    extra = jnp.concatenate(
        [
            vectors.astype(jnp.bfloat16),
            (partner // digit).astype(jnp.bfloat16),
            (partner % digit).astype(jnp.bfloat16),
        ]
    )
    extra = jnp.pad(extra, (0, width - extra.shape[0]))[None, :]
    attn_block = jnp.concatenate([attn_local_t, extra], 0)
    attn_gathered = pair_gather(attn_block, sizes, 0)
    local_cols = attn_local_t.shape[0]
    attn_full_t = attn_gathered[:, :local_cols, :].reshape(-1, width)
    extra_all = attn_gathered[:, local_cols, :]
    vector_f = extra_all[:, :vec_len].reshape(-1).astype(jnp.float32)
    partner_all = (
        extra_all[:, vec_len : vec_len + own_texts_n].astype(jnp.int32) * digit
        + extra_all[:, vec_len + own_texts_n : vec_len + 2 * own_texts_n].astype(jnp.int32)
    ).reshape(-1)
    ffn_full = lax.all_gather(ffn_weights.astype(jnp.bfloat16), AXES, axis=1, tiled=True)
    hidden = ffn_full.shape[1] // 2
    query_bias = vector_f[0:width]
    value_bias = vector_f[width : 2 * width]
    output_bias = vector_f[2 * width : 3 * width]
    gain_first = vector_f[3 * width : 4 * width]
    shift_first = vector_f[4 * width : 5 * width]
    upper_bias = vector_f[5 * width : 5 * width + hidden]
    lower_bias = vector_f[5 * width + hidden : 6 * width + hidden]
    gain_second = vector_f[6 * width + hidden : 7 * width + hidden]
    shift_second = vector_f[7 * width + hidden : 8 * width + hidden]
    w_qkv_t = attn_full_t[: 3 * width]
    w_output_t = attn_full_t[3 * width :]
    w_upper = ffn_full[:, :hidden]
    w_lower = ffn_full[:, hidden:]
    rows_dev, seq_len = segments.shape
    tokens_n = rows_dev * seq_len
    on_rows = (((1,), (1,)), ((), ()))
    on_tokens = (((0,), (0,)), ((), ()))
    qkv_bias = jnp.concatenate([query_bias, jnp.zeros_like(query_bias), value_bias])
    qkv_rows = (lax.dot_general(hidden_in, w_qkv_t, (((1,), (1,)), ((), ())), preferred_element_type=jnp.float32) + qkv_bias).astype(
        jnp.bfloat16
    )
    heads = qkv_rows.reshape(rows_dev, seq_len, 3, HEADS, HD)
    query_rows = heads[:, :, 0]
    key_rows = heads[:, :, 1]
    value_rows = heads[:, :, 2]
    mixed, log_norm = attend_rows(query_rows, key_rows, value_rows, segments)
    mixed_flat = mixed.reshape(tokens_n, width)
    first_sum = (
        hidden_in.astype(jnp.float32)
        + lax.dot_general(mixed_flat, w_output_t, (((1,), (1,)), ((), ())), preferred_element_type=jnp.float32)
        + output_bias
    )
    normed, normal_one, inverse_one = layer_norm_parts(first_sum, gain_first, shift_first)
    normed_r = bf16_round(normed)
    normed_b = normed_r.astype(jnp.bfloat16)
    upper = jnp.dot(normed_b, w_upper, preferred_element_type=jnp.float32) + upper_bias
    active_b = jax.nn.gelu(upper, approximate=False).astype(jnp.bfloat16)
    second_sum = (
        normed_r
        + lax.dot_general(active_b, w_lower, on_rows, preferred_element_type=jnp.float32)
        + lower_bias
    )
    result, normal_two, inverse_two = layer_norm_parts(second_sum, gain_second, shift_second)
    text_ids = jnp.arange(SEGS, dtype=jnp.int32)
    one_hot = (segments[:, None, :] == text_ids[None, :, None]).astype(jnp.float32)
    counts = jnp.sum(one_hot, -1, keepdims=True)
    pooled = (
        jnp.einsum(
            "rts,rsd->rtd",
            one_hot,
            result.reshape(rows_dev, seq_len, width),
            precision=lax.Precision.HIGHEST,
        )
        / counts
    ).reshape(-1, width)
    inv_norm = lax.rsqrt(jnp.sum(pooled * pooled, -1, keepdims=True) + pool_epsilon)
    embed_b = (pooled * inv_norm).astype(jnp.bfloat16)
    gathered_embeddings = pair_gather(embed_b, sizes, 2).reshape(-1, width)
    mean_loss, embedding_gradient = contrastive(embed_b, gathered_embeddings, partner_all, me)
    grad_pooled = inv_norm * embedding_gradient - pooled * (
        inv_norm * inv_norm * inv_norm
    ) * jnp.sum(embedding_gradient * pooled, -1, keepdims=True)
    derivative_output = jnp.einsum(
        "rts,rtd->rsd",
        one_hot,
        grad_pooled.reshape(rows_dev, SEGS, width) / counts,
        precision=lax.Precision.HIGHEST,
    ).reshape(tokens_n, width)
    grad_second, gain_two_grad, shift_two_grad = layer_norm_back(
        derivative_output, normal_two, inverse_two, gain_second
    )
    lower_bias_grad = jnp.sum(grad_second, 0)
    lower_grad_b = grad_second.astype(jnp.bfloat16)
    lower_w_grad_t = lax.dot_general(
        active_b, lower_grad_b, on_tokens, preferred_element_type=jnp.float32
    )
    grad_active = jnp.dot(lower_grad_b, w_lower, preferred_element_type=jnp.float32)
    cumulative = 0.5 * (1.0 + lax.erf(upper / math.sqrt(2.0)))
    density = jnp.exp(-0.5 * upper * upper) / math.sqrt(2.0 * math.pi)
    grad_upper = grad_active * (cumulative + upper * density)
    upper_bias_grad = jnp.sum(grad_upper, 0)
    upper_grad_b = grad_upper.astype(jnp.bfloat16)
    upper_w_grad_t = lax.dot_general(
        upper_grad_b, normed_b, on_tokens, preferred_element_type=jnp.float32
    )
    grad_normed = (
        lax.dot_general(upper_grad_b, w_upper, on_rows, preferred_element_type=jnp.float32)
        + grad_second
    )
    grad_first, gain_one_grad, shift_one_grad = layer_norm_back(
        grad_normed, normal_one, inverse_one, gain_first
    )
    output_bias_grad = jnp.sum(grad_first, 0)
    first_grad_b = grad_first.astype(jnp.bfloat16)
    output_w_grad_t = lax.dot_general(
        first_grad_b, mixed_flat, on_tokens, preferred_element_type=jnp.float32
    )
    grad_mixed = jnp.dot(
        first_grad_b, w_output_t, preferred_element_type=jnp.float32
    ).astype(jnp.bfloat16)
    grad_mixed = grad_mixed.reshape(rows_dev, seq_len, HEADS, HD)
    norm_tokens = jnp.swapaxes(log_norm, 1, 2).reshape(tokens_n, HEADS)
    qkv_grad = jnp.concatenate(
        attention_back(qkv_rows, grad_mixed.reshape(tokens_n, width), norm_tokens, segments, HEADS, HD), 1
    ).astype(jnp.float32)
    qkv_grad_f = bf16_round(qkv_grad)
    qkv_grad_b = qkv_grad_f.astype(jnp.bfloat16)
    query_bias_grad = jnp.sum(qkv_grad_f[:, :width], 0)
    value_bias_grad = jnp.sum(qkv_grad_f[:, 2 * width :], 0)
    qkv_w_grad_t = lax.dot_general(
        qkv_grad_b, hidden_in, on_tokens, preferred_element_type=jnp.float32
    )
    input_grad = (
        jnp.dot(qkv_grad_b, w_qkv_t, preferred_element_type=jnp.float32) + grad_first
    )
    vector_grad = jnp.concatenate(
        [
            query_bias_grad,
            value_bias_grad,
            output_bias_grad,
            gain_one_grad,
            shift_one_grad,
            upper_bias_grad,
            lower_bias_grad,
            gain_two_grad,
            shift_two_grad,
        ]
    )
    vector_slots = small_scatter(vector_grad.reshape(n_dev, 1, -1), sizes, 1)
    vector_reduced = jnp.sum(vector_slots[:, 0, :], 0)
    attn_cols = (qkv_w_grad_t.shape[0] + output_w_grad_t.shape[0]) // n_dev
    ffn_cols = (upper_w_grad_t.shape[0] + lower_w_grad_t.shape[0]) // n_dev
    attn_blocks = jnp.concatenate(
        [qkv_w_grad_t.reshape(-1, attn_cols, width), output_w_grad_t.reshape(-1, attn_cols, width)], 0
    )
    ffn_blocks = jnp.concatenate(
        [upper_w_grad_t.reshape(-1, ffn_cols, width), lower_w_grad_t.reshape(-1, ffn_cols, width)], 0
    )
    joined = jnp.concatenate([attn_blocks, ffn_blocks], 1).astype(GRAD_SEND).reshape(-1, width)
    joined_reduced = lax.psum_scatter(joined, AXES, scatter_dimension=0, tiled=True)
    joined_reduced = joined_reduced.astype(jnp.float32)
    attn_reduced = joined_reduced[:attn_cols].T
    ffn_reduced = joined_reduced[attn_cols:].T
    attn_new, attn_moment, attn_average = apply_update(
        attn_weights, attn_reduced, attn_momentum, attn_averaged, decay_rate
    )
    ffn_new, ffn_moment, ffn_average = apply_update(
        ffn_weights, ffn_reduced, ffn_momentum, ffn_averaged, decay_rate
    )
    vector_new, vector_moment, vector_average = apply_update(
        vectors, vector_reduced, vector_momentum, vector_averaged, 0.0
    )
    return (
        mean_loss,
        input_grad,
        attn_reduced,
        ffn_reduced,
        vector_reduced,
        attn_new,
        ffn_new,
        vector_new,
        attn_moment,
        ffn_moment,
        vector_moment,
        attn_average,
        ffn_average,
        vector_average,
    )


def solution(mesh):
    in_specs = (
        P(("dp", "rep"), None),
        P(("dp", "rep"), None),
        P(("dp", "rep")),
        P(None, ("dp", "rep")),
        P(None, ("dp", "rep")),
        P(("dp", "rep")),
        P(None, ("dp", "rep")),
        P(None, ("dp", "rep")),
        P(("dp", "rep")),
        P(None, ("dp", "rep")),
        P(None, ("dp", "rep")),
        P(("dp", "rep")),
    )
    out_specs = (
        P(),
        P(("dp", "rep"), None),
        P(None, ("dp", "rep")),
        P(None, ("dp", "rep")),
        P(("dp", "rep")),
        P(None, ("dp", "rep")),
        P(None, ("dp", "rep")),
        P(("dp", "rep")),
        P(None, ("dp", "rep")),
        P(None, ("dp", "rep")),
        P(("dp", "rep")),
        P(None, ("dp", "rep")),
        P(None, ("dp", "rep")),
        P(("dp", "rep")),
    )
    return jax.shard_map(shards, mesh=mesh, in_specs=in_specs, out_specs=out_specs, check_vma=False)
```

```python
import functools
import math

import jax
import jax.numpy as jnp
from jax import lax
from jax.experimental import pallas as pl
from jax.experimental.pallas import tpu as pltpu
from jax.sharding import PartitionSpec as P

MESH = pl.DeviceIdType.MESH
GRAD_SEND = jnp.bfloat16
AXES = ("dp", "rep")

HEADS = 12
HD = 64
SEGS = 16


ln_epsilon = 1e-12
pool_epsilon = 1e-06
logit_divisor = 0.025
learn_rate = 0.01
momentum_rate = 0.9
decay_rate = 0.01
average_rate = 0.75
masked_value = -1e30


def layer_norm_parts(values, gain, shift):
    per_line_average = jnp.mean(values, -1, keepdims=True)
    centred = values - per_line_average
    inverse = lax.rsqrt(jnp.mean(centred * centred, -1, keepdims=True) + ln_epsilon)
    normal_part = centred * inverse
    return (normal_part * gain + shift, normal_part, inverse)


def layer_norm_back(grad_out, normal_part, inverse, gain):
    scaled = grad_out * gain
    grad_in = inverse * (
        scaled
        - jnp.mean(scaled, -1, keepdims=True)
        - normal_part * jnp.mean(scaled * normal_part, -1, keepdims=True)
    )
    return (grad_in, jnp.sum(grad_out * normal_part, 0), jnp.sum(grad_out, 0))


def row_scores(query_one, key_one, segment_one, scale):
    scores = (
        jnp.einsum("qhd,khd->hqk", query_one, key_one, preferred_element_type=jnp.float32) * scale
    )
    same_text = segment_one[:, None] == segment_one[None, :]
    return jnp.where(same_text[None], scores, masked_value)


def attend_rows(query_rows, key_rows, value_rows, row_segments):
    scale = 1.0 / math.sqrt(query_rows.shape[-1])

    def one_row(row_args):
        query_one, key_one, value_one, segment_one = row_args
        scores = row_scores(query_one, key_one, segment_one, scale)
        row_max = jnp.max(scores, -1, keepdims=True)
        exp_scores = jnp.exp(scores - row_max)
        sums = jnp.sum(exp_scores, -1, keepdims=True)
        attn_probs = exp_scores / sums
        mixed = jnp.einsum(
            "hqk,khd->qhd",
            attn_probs.astype(jnp.bfloat16),
            value_one,
            preferred_element_type=jnp.float32,
        )
        return (mixed.astype(jnp.bfloat16), (row_max + jnp.log(sums))[..., 0])

    return lax.map(one_row, (query_rows, key_rows, value_rows, row_segments))


def attend_back(query_rows, key_rows, value_rows, row_segments, log_norm, grad_mixed):
    scale = 1.0 / math.sqrt(query_rows.shape[-1])

    def one_row(row_args):
        query_one, key_one, value_one, segment_one, norm_one, grad_one = row_args
        scores = row_scores(query_one, key_one, segment_one, scale)
        attn_probs = jnp.exp(scores - norm_one[..., None])
        grad_value = jnp.einsum(
            "hqk,qhd->khd",
            attn_probs.astype(jnp.bfloat16),
            grad_one,
            preferred_element_type=jnp.float32,
        )
        grad_probs = jnp.einsum(
            "qhd,khd->hqk", grad_one, value_one, preferred_element_type=jnp.float32
        )
        inner = jnp.sum(attn_probs * grad_probs, -1, keepdims=True)
        grad_scores = (attn_probs * (grad_probs - inner)).astype(jnp.bfloat16)
        grad_query = (
            jnp.einsum("hqk,khd->qhd", grad_scores, key_one, preferred_element_type=jnp.float32)
            * scale
        )
        grad_key = (
            jnp.einsum("hqk,qhd->khd", grad_scores, query_one, preferred_element_type=jnp.float32)
            * scale
        )
        return jnp.concatenate([grad_query, grad_key, grad_value], axis=1)

    return lax.map(one_row, (query_rows, key_rows, value_rows, row_segments, log_norm, grad_mixed))


def attention_back_kernel(scale, q_ref, k_ref, v_ref, g_ref, norm_ref, seg_col_ref, seg_row_ref, dq_ref, dk_ref, dv_ref):
    pair = pl.program_id(1)
    width = q_ref.shape[1]
    half = width // 2
    lane = lax.broadcasted_iota(jnp.int32, (1, width), 1)
    same = seg_col_ref[...] == seg_row_ref[0]
    norms = norm_ref[...]
    norm_lane = lax.broadcasted_iota(jnp.int32, norms.shape, 1)
    q = q_ref[...]
    k = k_ref[...]
    v = v_ref[...]
    g = g_ref[...]
    zero_b = jnp.zeros_like(q)
    on_last = (((1,), (1,)), ((), ()))
    on_first = (((0,), (0,)), ((), ()))
    dq = jnp.zeros(q.shape, jnp.float32)
    dk = jnp.zeros(q.shape, jnp.float32)
    dv = jnp.zeros(q.shape, jnp.float32)
    for head in range(2):
        mine = (lane >= head * half) & (lane < (head + 1) * half)
        q_h = jnp.where(mine, q, zero_b)
        g_h = jnp.where(mine, g, zero_b)
        norm_h = jnp.sum(jnp.where(norm_lane == 2 * pair + head, norms, 0.0), 1, keepdims=True)
        scores = lax.dot_general(q_h, k, on_last, preferred_element_type=jnp.float32) * scale
        scores = jnp.where(same, scores, masked_value)
        probs = jnp.exp(scores - norm_h)
        grad_v = lax.dot_general(probs.astype(jnp.bfloat16), g, on_first, preferred_element_type=jnp.float32)
        grad_p = lax.dot_general(g_h, v, on_last, preferred_element_type=jnp.float32)
        inner = jnp.sum(probs * grad_p, -1, keepdims=True)
        grad_s = (probs * (grad_p - inner)).astype(jnp.bfloat16)
        grad_q = jnp.dot(grad_s, k, preferred_element_type=jnp.float32) * scale
        grad_k = lax.dot_general(grad_s, q, on_first, preferred_element_type=jnp.float32) * scale
        dq = jnp.where(mine, grad_q, dq)
        dk = jnp.where(mine, grad_k, dk)
        dv = jnp.where(mine, grad_v, dv)
    dq_ref[...] = dq.astype(dq_ref.dtype)
    dk_ref[...] = dk.astype(dk_ref.dtype)
    dv_ref[...] = dv.astype(dv_ref.dtype)


def attention_back(qkv_rows, grad_mixed_flat, norm_tokens, segments, heads, head_dim):
    tokens, three_width = qkv_rows.shape
    width = three_width // 3
    rows, seq_len = segments.shape
    pair_width = 2 * head_dim
    pairs = heads // 2
    seg_col = segments.reshape(tokens, 1)
    seg_row = segments.reshape(rows, 1, seq_len)
    scale = 1.0 / math.sqrt(head_dim)
    out = jax.ShapeDtypeStruct((tokens, width), jnp.bfloat16)
    return pl.pallas_call(
        functools.partial(attention_back_kernel, scale),
        grid=(rows, pairs),
        in_specs=[
            pl.BlockSpec((seq_len, pair_width), lambda r, p: (r, p)),
            pl.BlockSpec((seq_len, pair_width), lambda r, p: (r, pairs + p)),
            pl.BlockSpec((seq_len, pair_width), lambda r, p: (r, 2 * pairs + p)),
            pl.BlockSpec((seq_len, pair_width), lambda r, p: (r, p)),
            pl.BlockSpec((seq_len, heads), lambda r, p: (r, 0)),
            pl.BlockSpec((seq_len, 1), lambda r, p: (r, 0)),
            pl.BlockSpec((1, 1, seq_len), lambda r, p: (r, 0, 0)),
        ],
        out_specs=[pl.BlockSpec((seq_len, pair_width), lambda r, p: (r, p))] * 3,
        out_shape=[out, out, out],
        compiler_params=pltpu.CompilerParams(vmem_limit_bytes=48 * 1024 * 1024),
        cost_estimate=pl.CostEstimate(
            flops=10 * rows * heads * seq_len * seq_len * pair_width,
            transcendentals=rows * heads * seq_len * seq_len,
            bytes_accessed=tokens * (three_width + 4 * width) * 2,
        ),
    )(qkv_rows, qkv_rows, qkv_rows, grad_mixed_flat, norm_tokens, seg_col, seg_row)


def apply_update(weight, grad, moment, average, decay):
    step_grad = grad + decay * weight
    new_moment = momentum_rate * moment + step_grad
    new_weight = weight - learn_rate * (step_grad + momentum_rate * new_moment)
    fresh_running_mean = average_rate * average + (1.0 - average_rate) * new_weight
    return (new_weight, new_moment, fresh_running_mean)


def bf16_round(values):
    return lax.reduce_precision(values, exponent_bits=8, mantissa_bits=7)


def flat_index(sizes):
    idx = 0
    for name, size in zip(AXES, sizes):
        idx = idx * size + lax.axis_index(name)
    return idx


def device_of(flat, sizes):
    coords = []
    for size in reversed(sizes):
        coords.append(lax.rem(flat, size))
        flat = flat // size
    return tuple(reversed(coords))


def enter_all(n, sizes, me):
    barrier = pltpu.get_barrier_semaphore()

    def greet(k, carry):
        peer = lax.rem(me + k, n)
        pl.semaphore_signal(barrier, inc=1, device_id=device_of(peer, sizes), device_id_type=MESH)
        return carry

    lax.fori_loop(1, n, greet, 0)
    pl.semaphore_wait(barrier, n - 1)


def gather_kernel(n, sizes, x_ref, out_ref, send_sem, recv_sem):
    me = flat_index(sizes)
    enter_all(n, sizes, me)

    def send(k, carry):
        peer = lax.rem(me + k, n)
        pltpu.make_async_remote_copy(
            src_ref=x_ref, dst_ref=out_ref.at[me], send_sem=send_sem.at[k], recv_sem=recv_sem.at[me],
            device_id=device_of(peer, sizes), device_id_type=MESH,
        ).start()
        return carry

    lax.fori_loop(1, n, send, 0)
    out_ref[me] = x_ref[...]

    def finish(k, carry):
        peer = lax.rem(me + k, n)
        src = lax.rem(me + n - k, n)
        pltpu.make_async_remote_copy(
            src_ref=x_ref, dst_ref=out_ref.at[me], send_sem=send_sem.at[k], recv_sem=recv_sem.at[me],
            device_id=device_of(peer, sizes), device_id_type=MESH,
        ).wait_send()
        pltpu.make_async_remote_copy(
            src_ref=x_ref, dst_ref=out_ref.at[src], send_sem=send_sem.at[k], recv_sem=recv_sem.at[src],
            device_id=device_of(src, sizes), device_id_type=MESH,
        ).wait_recv()
        return carry

    lax.fori_loop(1, n, finish, 0)


def small_gather(x, sizes, cid):
    n = math.prod(sizes)
    return pl.pallas_call(
        functools.partial(gather_kernel, n, sizes),
        out_shape=jax.ShapeDtypeStruct((n,) + x.shape, x.dtype),
        in_specs=[pl.BlockSpec(memory_space=pltpu.VMEM)],
        out_specs=pl.BlockSpec(memory_space=pltpu.VMEM),
        scratch_shapes=[pltpu.SemaphoreType.DMA((n,)), pltpu.SemaphoreType.DMA((n,))],
        compiler_params=pltpu.CompilerParams(collective_id=cid, has_side_effects=True),
    )(x)


def scatter_kernel(n, sizes, x_ref, out_ref, send_sem, recv_sem):
    me = flat_index(sizes)
    enter_all(n, sizes, me)

    def send(k, carry):
        peer = lax.rem(me + k, n)
        pltpu.make_async_remote_copy(
            src_ref=x_ref.at[peer], dst_ref=out_ref.at[me], send_sem=send_sem.at[k], recv_sem=recv_sem.at[me],
            device_id=device_of(peer, sizes), device_id_type=MESH,
        ).start()
        return carry

    lax.fori_loop(1, n, send, 0)
    out_ref[me] = x_ref[me]

    def finish(k, carry):
        peer = lax.rem(me + k, n)
        src = lax.rem(me + n - k, n)
        pltpu.make_async_remote_copy(
            src_ref=x_ref.at[peer], dst_ref=out_ref.at[me], send_sem=send_sem.at[k], recv_sem=recv_sem.at[me],
            device_id=device_of(peer, sizes), device_id_type=MESH,
        ).wait_send()
        pltpu.make_async_remote_copy(
            src_ref=x_ref.at[src], dst_ref=out_ref.at[src], send_sem=send_sem.at[k], recv_sem=recv_sem.at[src],
            device_id=device_of(src, sizes), device_id_type=MESH,
        ).wait_recv()
        return carry

    lax.fori_loop(1, n, finish, 0)


def small_scatter(x, sizes, cid):
    n = math.prod(sizes)
    return pl.pallas_call(
        functools.partial(scatter_kernel, n, sizes),
        out_shape=jax.ShapeDtypeStruct(x.shape, x.dtype),
        in_specs=[pl.BlockSpec(memory_space=pltpu.VMEM)],
        out_specs=pl.BlockSpec(memory_space=pltpu.VMEM),
        scratch_shapes=[pltpu.SemaphoreType.DMA((n,)), pltpu.SemaphoreType.DMA((n,))],
        compiler_params=pltpu.CompilerParams(collective_id=cid, has_side_effects=True),
    )(x)


def pair_gather_kernel(n, sizes, x_ref, out_ref, local_sem, send1, recv1, send2, recv2, send3, recv3):
    me = flat_index(sizes)
    chips = n // 2
    chip = me // 2
    core = lax.rem(me, 2)
    partner = me + 1 - 2 * core
    enter_all(n, sizes, me)

    local = pltpu.make_async_copy(x_ref, out_ref.at[me], local_sem)
    local.start()
    first = pltpu.make_async_remote_copy(
        src_ref=x_ref, dst_ref=out_ref.at[me], send_sem=send1, recv_sem=recv1,
        device_id=device_of(partner, sizes), device_id_type=MESH,
    )
    first.start()
    local.wait()
    first.wait_send()
    pltpu.make_async_remote_copy(
        src_ref=x_ref, dst_ref=out_ref.at[partner], send_sem=send1, recv_sem=recv1,
        device_id=device_of(partner, sizes), device_id_type=MESH,
    ).wait_recv()

    def pair(c):
        return out_ref.at[pl.ds(2 * c, 2)]

    def target(k):
        return lax.rem(chip + 2 * k - 1 + core, chips)

    def source(k):
        return lax.rem(chip + chips - (2 * k - 1 + core), chips)

    count = (chips - core) // 2

    def send_out(k, carry):
        other = target(k)
        pltpu.make_async_remote_copy(
            src_ref=pair(chip), dst_ref=pair(chip), send_sem=send2.at[other], recv_sem=recv2.at[chip],
            device_id=device_of(2 * other + core, sizes), device_id_type=MESH,
        ).start()
        return carry

    lax.fori_loop(1, count + 1, send_out, 0)

    def take_in(k, carry):
        other = source(k)
        pltpu.make_async_remote_copy(
            src_ref=pair(other), dst_ref=pair(other), send_sem=send2.at[other], recv_sem=recv2.at[other],
            device_id=device_of(2 * other + core, sizes), device_id_type=MESH,
        ).wait_recv()
        pltpu.make_async_remote_copy(
            src_ref=pair(other), dst_ref=pair(other), send_sem=send3.at[other], recv_sem=recv3.at[other],
            device_id=device_of(partner, sizes), device_id_type=MESH,
        ).start()
        return carry

    lax.fori_loop(1, count + 1, take_in, 0)

    def sent_out(k, carry):
        other = target(k)
        pltpu.make_async_remote_copy(
            src_ref=pair(chip), dst_ref=pair(chip), send_sem=send2.at[other], recv_sem=recv2.at[chip],
            device_id=device_of(2 * other + core, sizes), device_id_type=MESH,
        ).wait_send()
        return carry

    lax.fori_loop(1, count + 1, sent_out, 0)

    def forwarded(k, carry):
        other = source(k)
        pltpu.make_async_remote_copy(
            src_ref=pair(other), dst_ref=pair(other), send_sem=send3.at[other], recv_sem=recv3.at[other],
            device_id=device_of(partner, sizes), device_id_type=MESH,
        ).wait_send()
        return carry

    lax.fori_loop(1, count + 1, forwarded, 0)

    other_count = (chips - (1 - core)) // 2

    def partner_source(k):
        return lax.rem(chip + chips - (2 * k - 1 + (1 - core)), chips)

    def from_partner(k, carry):
        other = partner_source(k)
        pltpu.make_async_remote_copy(
            src_ref=pair(other), dst_ref=pair(other), send_sem=send3.at[other], recv_sem=recv3.at[other],
            device_id=device_of(partner, sizes), device_id_type=MESH,
        ).wait_recv()
        return carry

    lax.fori_loop(1, other_count + 1, from_partner, 0)


def pair_gather(x, sizes, cid):
    n = math.prod(sizes)
    chips = n // 2
    dma = pltpu.SemaphoreType.DMA
    return pl.pallas_call(
        functools.partial(pair_gather_kernel, n, sizes),
        out_shape=jax.ShapeDtypeStruct((n,) + x.shape, x.dtype),
        in_specs=[pl.BlockSpec(memory_space=pltpu.VMEM)],
        out_specs=pl.BlockSpec(memory_space=pltpu.VMEM),
        scratch_shapes=[dma(()), dma(()), dma(()), dma((chips,)), dma((chips,)), dma((chips,)), dma((chips,))],
        compiler_params=pltpu.CompilerParams(collective_id=cid, has_side_effects=True),
    )(x)


def halving_orders(n, parts):
    bits = n.bit_length() - 1
    middle = list(range(1, bits - 1))
    orders = []
    for p in range(parts):
        shift = p % len(middle) if middle else 0
        orders.append(tuple([0] + middle[shift:] + middle[:shift] + [bits - 1]))
    return tuple(orders)


def halving_kernel(n, sizes, orders, x_hbm, out_ref, work, *rest):
    steps = len(orders[0])
    parts = len(orders)
    recvs = rest[:steps]
    local_sem, send_sems, recv_sems = rest[steps:]
    me = flat_index(sizes)

    def partner_of(bit):
        mine = lax.rem(me // (2**bit), 2)
        return mine, me + (1 - 2 * mine) * (2**bit)

    barrier = pltpu.get_barrier_semaphore()
    for bit in range(steps):
        _, other = partner_of(bit)
        pl.semaphore_signal(barrier, inc=1, device_id=device_of(other, sizes), device_id_type=MESH)
    pl.semaphore_wait(barrier, steps)

    for step in range(steps):
        half = n >> (step + 1)
        copies = []
        for p in range(parts):
            mine, other = partner_of(orders[p][step])
            source = x_hbm if step == 0 else work
            send = pltpu.make_async_remote_copy(
                src_ref=source.at[p, pl.ds((1 - mine) * half, half)], dst_ref=recvs[step].at[p],
                send_sem=send_sems.at[p, step], recv_sem=recv_sems.at[p, step],
                device_id=device_of(other, sizes), device_id_type=MESH,
            )
            send.start()
            local = None
            if step == 0:
                local = pltpu.make_async_copy(
                    x_hbm.at[p, pl.ds(mine * half, half)], work.at[p, pl.ds(0, half)], local_sem.at[p]
                )
                local.start()
            copies.append((mine, send, local))
        for p in range(parts):
            mine, send, local = copies[p]
            if local is not None:
                local.wait()
            send.wait_recv()
            send.wait_send()
            start = 0 if step == 0 else mine * half

            def accumulate(i, carry, p=p, start=start, step=step):
                total = work[p, start + i].astype(jnp.float32) + recvs[step][p, i].astype(jnp.float32)
                work[p, i] = total.astype(work.dtype)
                return carry

            lax.fori_loop(0, half, accumulate, 0)
    for p in range(parts):
        out_ref[p] = work[p, 0]


def halving_scatter(x, sizes, cid):
    parts, n, rows, cols = x.shape
    orders = halving_orders(n, parts)
    steps = len(orders[0])
    dma = pltpu.SemaphoreType.DMA
    scratch = [pltpu.VMEM((parts, n // 2, rows, cols), x.dtype)]
    scratch += [pltpu.VMEM((parts, n >> (k + 1), rows, cols), x.dtype) for k in range(steps)]
    scratch += [dma((parts,)), dma((parts, steps)), dma((parts, steps))]
    return pl.pallas_call(
        functools.partial(halving_kernel, n, sizes, orders),
        out_shape=jax.ShapeDtypeStruct((parts, rows, cols), x.dtype),
        in_specs=[pl.BlockSpec(memory_space=pl.ANY)],
        out_specs=pl.BlockSpec(memory_space=pltpu.VMEM),
        scratch_shapes=scratch,
        compiler_params=pltpu.CompilerParams(
            collective_id=cid, has_side_effects=True, vmem_limit_bytes=56 * 1024 * 1024
        ),
    )(x)


def owner_permuted(joined, parts):
    n, rows, width = joined.shape
    bits = n.bit_length() - 1
    orders = halving_orders(n, parts)
    cols = width // parts
    view = joined.reshape([2] * bits + [rows, parts, cols])
    pieces = []
    for p in range(parts):
        piece = view[..., p, :]
        axes = [bits - 1 - b for b in orders[p]] + [bits, bits + 1]
        pieces.append(jnp.transpose(piece, axes).reshape(n, rows, cols))
    return jnp.stack(pieces)


def contrastive(embed_b, gathered, partner_all, me):
    own_texts = embed_b.shape[0]
    all_texts = gathered.shape[0]
    chunk = min(all_texts, 1024)
    on_rows = (((1,), (1,)), ((), ()))

    def chunk_stats(c):
        rows_b = lax.dynamic_slice_in_dim(gathered, c * chunk, chunk)
        sim = lax.dot_general(rows_b, gathered, on_rows, preferred_element_type=jnp.float32) / logit_divisor
        column_ids = lax.broadcasted_iota(jnp.int32, sim.shape, 1)
        row_ids = lax.broadcasted_iota(jnp.int32, sim.shape, 0) + c * chunk
        masked = jnp.where(column_ids == row_ids, masked_value, sim)
        row_max = jnp.max(masked, -1, keepdims=True)
        log_sum = row_max + jnp.log(jnp.sum(jnp.exp(masked - row_max), -1, keepdims=True))
        wanted = lax.dynamic_slice_in_dim(partner_all, c * chunk, chunk)
        positive = jnp.sum(jnp.where(column_ids == wanted[:, None], sim, 0.0), -1)
        return log_sum[:, 0], positive

    if all_texts == chunk:
        log_sum_all, positive_all = chunk_stats(0)
    else:
        log_sum_all, positive_all = lax.map(chunk_stats, jnp.arange(all_texts // chunk))
        log_sum_all = log_sum_all.reshape(-1)
        positive_all = positive_all.reshape(-1)
    mean_loss = jnp.sum(log_sum_all - positive_all) / all_texts

    own_start = me * own_texts
    own_ids = lax.broadcasted_iota(jnp.int32, (own_texts,), 0) + own_start
    own_partner = lax.dynamic_slice_in_dim(partner_all, own_start, own_texts)
    own_log_sum = lax.dynamic_slice_in_dim(log_sum_all, own_start, own_texts)

    sim_rows = lax.dot_general(embed_b, gathered, on_rows, preferred_element_type=jnp.float32) / logit_divisor
    column_ids = lax.broadcasted_iota(jnp.int32, sim_rows.shape, 1)
    masked_rows = jnp.where(column_ids == own_ids[:, None], masked_value, sim_rows)
    grad_rows = (
        jnp.exp(masked_rows - own_log_sum[:, None]) - (column_ids == own_partner[:, None]).astype(jnp.float32)
    ).astype(jnp.bfloat16)

    sim_cols = lax.dot_general(gathered, embed_b, on_rows, preferred_element_type=jnp.float32) / logit_divisor
    row_ids = lax.broadcasted_iota(jnp.int32, sim_cols.shape, 0)
    masked_cols = jnp.where(row_ids == own_ids[None, :], masked_value, sim_cols)
    grad_cols = (
        jnp.exp(masked_cols - log_sum_all[:, None]) - (partner_all[:, None] == own_ids[None, :]).astype(jnp.float32)
    ).astype(jnp.bfloat16)

    on_tokens = (((0,), (0,)), ((), ()))
    embedding_gradient = (
        jnp.dot(grad_rows, gathered, preferred_element_type=jnp.float32)
        + lax.dot_general(grad_cols, gathered, on_tokens, preferred_element_type=jnp.float32)
    ) / logit_divisor
    return mean_loss, embedding_gradient


def shards(
    hidden_in,
    segments,
    partner,
    attn_weights,
    ffn_weights,
    vectors,
    attn_momentum,
    ffn_momentum,
    vector_momentum,
    attn_averaged,
    ffn_averaged,
    vector_averaged,
):
    sizes = tuple(lax.axis_size(name) for name in AXES)
    n_dev = math.prod(sizes)
    me = flat_index(sizes)
    vec_len = vectors.shape[0]
    small = jnp.concatenate([vectors, partner.astype(jnp.float32)])[None, :]
    small_all = small_gather(small, sizes, 0)[:, 0, :]
    vector_f = bf16_round(small_all[:, :vec_len].reshape(-1))
    partner_all = small_all[:, vec_len:].reshape(-1).astype(jnp.int32)
    attn_full, ffn_full = (
        lax.all_gather(attn_weights.astype(jnp.bfloat16), AXES, axis=1, tiled=True),
        lax.all_gather(ffn_weights.astype(jnp.bfloat16), AXES, axis=1, tiled=True),
    )
    width = attn_full.shape[0]
    hidden = ffn_full.shape[1] // 2
    query_bias = vector_f[0:width]
    value_bias = vector_f[width : 2 * width]
    output_bias = vector_f[2 * width : 3 * width]
    gain_first = vector_f[3 * width : 4 * width]
    shift_first = vector_f[4 * width : 5 * width]
    upper_bias = vector_f[5 * width : 5 * width + hidden]
    lower_bias = vector_f[5 * width + hidden : 6 * width + hidden]
    gain_second = vector_f[6 * width + hidden : 7 * width + hidden]
    shift_second = vector_f[7 * width + hidden : 8 * width + hidden]
    w_qkv = attn_full[:, : 3 * width]
    w_output = attn_full[:, 3 * width :]
    w_upper = ffn_full[:, :hidden]
    w_lower = ffn_full[:, hidden:]
    rows_dev, seq_len = segments.shape
    tokens_n = rows_dev * seq_len
    on_rows = (((1,), (1,)), ((), ()))
    on_tokens = (((0,), (0,)), ((), ()))
    qkv_bias = jnp.concatenate([query_bias, jnp.zeros_like(query_bias), value_bias])
    qkv_rows = (jnp.dot(hidden_in, w_qkv, preferred_element_type=jnp.float32) + qkv_bias).astype(
        jnp.bfloat16
    )
    heads = qkv_rows.reshape(rows_dev, seq_len, 3, HEADS, HD)
    query_rows = heads[:, :, 0]
    key_rows = heads[:, :, 1]
    value_rows = heads[:, :, 2]
    mixed, log_norm = attend_rows(query_rows, key_rows, value_rows, segments)
    mixed_flat = mixed.reshape(tokens_n, width)
    first_sum = (
        hidden_in.astype(jnp.float32)
        + jnp.dot(mixed_flat, w_output, preferred_element_type=jnp.float32)
        + output_bias
    )
    normed, normal_one, inverse_one = layer_norm_parts(first_sum, gain_first, shift_first)
    normed_r = bf16_round(normed)
    normed_b = normed_r.astype(jnp.bfloat16)
    upper = jnp.dot(normed_b, w_upper, preferred_element_type=jnp.float32) + upper_bias
    active_b = jax.nn.gelu(upper, approximate=False).astype(jnp.bfloat16)
    second_sum = (
        normed_r
        + lax.dot_general(active_b, w_lower, on_rows, preferred_element_type=jnp.float32)
        + lower_bias
    )
    result, normal_two, inverse_two = layer_norm_parts(second_sum, gain_second, shift_second)
    text_ids = jnp.arange(SEGS, dtype=jnp.int32)
    one_hot = (segments[:, None, :] == text_ids[None, :, None]).astype(jnp.float32)
    counts = jnp.sum(one_hot, -1, keepdims=True)
    pooled = (
        jnp.einsum(
            "rts,rsd->rtd",
            one_hot,
            result.reshape(rows_dev, seq_len, width),
            precision=lax.Precision.HIGHEST,
        )
        / counts
    ).reshape(-1, width)
    inv_norm = lax.rsqrt(jnp.sum(pooled * pooled, -1, keepdims=True) + pool_epsilon)
    embed_b = (pooled * inv_norm).astype(jnp.bfloat16)
    gathered_embeddings = pair_gather(embed_b, sizes, 2).reshape(-1, width)
    mean_loss, embedding_gradient = contrastive(embed_b, gathered_embeddings, partner_all, me)
    grad_pooled = inv_norm * embedding_gradient - pooled * (
        inv_norm * inv_norm * inv_norm
    ) * jnp.sum(embedding_gradient * pooled, -1, keepdims=True)
    derivative_output = jnp.einsum(
        "rts,rtd->rsd",
        one_hot,
        grad_pooled.reshape(rows_dev, SEGS, width) / counts,
        precision=lax.Precision.HIGHEST,
    ).reshape(tokens_n, width)
    grad_second, gain_two_grad, shift_two_grad = layer_norm_back(
        derivative_output, normal_two, inverse_two, gain_second
    )
    lower_bias_grad = jnp.sum(grad_second, 0)
    lower_grad_b = grad_second.astype(jnp.bfloat16)
    lower_w_grad_t = lax.dot_general(
        active_b, lower_grad_b, on_tokens, preferred_element_type=jnp.float32
    )
    grad_active = jnp.dot(lower_grad_b, w_lower, preferred_element_type=jnp.float32)
    cumulative = 0.5 * (1.0 + lax.erf(upper / math.sqrt(2.0)))
    density = jnp.exp(-0.5 * upper * upper) / math.sqrt(2.0 * math.pi)
    grad_upper = grad_active * (cumulative + upper * density)
    upper_bias_grad = jnp.sum(grad_upper, 0)
    upper_grad_b = grad_upper.astype(jnp.bfloat16)
    upper_w_grad_t = lax.dot_general(
        upper_grad_b, normed_b, on_tokens, preferred_element_type=jnp.float32
    )
    grad_normed = (
        lax.dot_general(upper_grad_b, w_upper, on_rows, preferred_element_type=jnp.float32)
        + grad_second
    )
    grad_first, gain_one_grad, shift_one_grad = layer_norm_back(
        grad_normed, normal_one, inverse_one, gain_first
    )
    output_bias_grad = jnp.sum(grad_first, 0)
    first_grad_b = grad_first.astype(jnp.bfloat16)
    output_w_grad_t = lax.dot_general(
        first_grad_b, mixed_flat, on_tokens, preferred_element_type=jnp.float32
    )
    grad_mixed = lax.dot_general(
        first_grad_b, w_output, on_rows, preferred_element_type=jnp.float32
    ).astype(jnp.bfloat16)
    grad_mixed = grad_mixed.reshape(rows_dev, seq_len, HEADS, HD)
    norm_tokens = jnp.swapaxes(log_norm, 1, 2).reshape(tokens_n, HEADS)
    qkv_grad = jnp.concatenate(
        attention_back(qkv_rows, grad_mixed.reshape(tokens_n, width), norm_tokens, segments, HEADS, HD), 1
    ).astype(jnp.float32)
    qkv_grad_f = bf16_round(qkv_grad)
    qkv_grad_b = qkv_grad_f.astype(jnp.bfloat16)
    query_bias_grad = jnp.sum(qkv_grad_f[:, :width], 0)
    value_bias_grad = jnp.sum(qkv_grad_f[:, 2 * width :], 0)
    qkv_w_grad_t = lax.dot_general(
        qkv_grad_b, hidden_in, on_tokens, preferred_element_type=jnp.float32
    )
    input_grad = (
        lax.dot_general(qkv_grad_b, w_qkv, on_rows, preferred_element_type=jnp.float32) + grad_first
    )
    vector_grad = jnp.concatenate(
        [
            query_bias_grad,
            value_bias_grad,
            output_bias_grad,
            gain_one_grad,
            shift_one_grad,
            upper_bias_grad,
            lower_bias_grad,
            gain_two_grad,
            shift_two_grad,
        ]
    )
    vector_slots = small_scatter(vector_grad.reshape(n_dev, 1, -1), sizes, 1)
    vector_reduced = jnp.sum(vector_slots[:, 0, :], 0)
    attn_cols = (qkv_w_grad_t.shape[0] + output_w_grad_t.shape[0]) // n_dev
    ffn_cols = (upper_w_grad_t.shape[0] + lower_w_grad_t.shape[0]) // n_dev
    attn_blocks = jnp.concatenate(
        [qkv_w_grad_t.reshape(-1, attn_cols, width), output_w_grad_t.reshape(-1, attn_cols, width)], 0
    )
    ffn_blocks = jnp.concatenate(
        [upper_w_grad_t.reshape(-1, ffn_cols, width), lower_w_grad_t.reshape(-1, ffn_cols, width)], 0
    )
    joined = jnp.concatenate([attn_blocks, ffn_blocks], 1).astype(GRAD_SEND)
    parts = 3
    mine_parts = halving_scatter(owner_permuted(joined, parts), sizes, 3)
    joined_reduced = jnp.transpose(mine_parts, (1, 0, 2)).reshape(-1, width).astype(jnp.float32)
    attn_reduced = joined_reduced[:attn_cols].T
    ffn_reduced = joined_reduced[attn_cols:].T
    attn_new, attn_moment, attn_average = apply_update(
        attn_weights, attn_reduced, attn_momentum, attn_averaged, decay_rate
    )
    ffn_new, ffn_moment, ffn_average = apply_update(
        ffn_weights, ffn_reduced, ffn_momentum, ffn_averaged, decay_rate
    )
    vector_new, vector_moment, vector_average = apply_update(
        vectors, vector_reduced, vector_momentum, vector_averaged, 0.0
    )
    return (
        mean_loss,
        input_grad,
        attn_reduced,
        ffn_reduced,
        vector_reduced,
        attn_new,
        ffn_new,
        vector_new,
        attn_moment,
        ffn_moment,
        vector_moment,
        attn_average,
        ffn_average,
        vector_average,
    )


def solution(mesh):
    in_specs = (
        P(("dp", "rep"), None),
        P(("dp", "rep"), None),
        P(("dp", "rep")),
        P(None, ("dp", "rep")),
        P(None, ("dp", "rep")),
        P(("dp", "rep")),
        P(None, ("dp", "rep")),
        P(None, ("dp", "rep")),
        P(("dp", "rep")),
        P(None, ("dp", "rep")),
        P(None, ("dp", "rep")),
        P(("dp", "rep")),
    )
    out_specs = (
        P(),
        P(("dp", "rep"), None),
        P(None, ("dp", "rep")),
        P(None, ("dp", "rep")),
        P(("dp", "rep")),
        P(None, ("dp", "rep")),
        P(None, ("dp", "rep")),
        P(("dp", "rep")),
        P(None, ("dp", "rep")),
        P(None, ("dp", "rep")),
        P(("dp", "rep")),
        P(None, ("dp", "rep")),
        P(None, ("dp", "rep")),
        P(("dp", "rep")),
    )
    return jax.shard_map(shards, mesh=mesh, in_specs=in_specs, out_specs=out_specs, check_vma=False)
```

```python
import functools
import math

import jax
import jax.numpy as jnp
from jax import lax
from jax.experimental import pallas as pl
from jax.experimental.pallas import tpu as pltpu
from jax.sharding import PartitionSpec as P

MESH = pl.DeviceIdType.MESH
GRAD_SEND = jnp.bfloat16
AXES = ("dp", "rep")

HEADS = 12
HD = 64
SEGS = 16


ln_epsilon = 1e-12
pool_epsilon = 1e-06
logit_divisor = 0.025
learn_rate = 0.01
momentum_rate = 0.9
decay_rate = 0.01
average_rate = 0.75
masked_value = -1e30


def layer_norm_parts(values, gain, shift):
    per_line_average = jnp.mean(values, -1, keepdims=True)
    centred = values - per_line_average
    inverse = lax.rsqrt(jnp.mean(centred * centred, -1, keepdims=True) + ln_epsilon)
    normal_part = centred * inverse
    return (normal_part * gain + shift, normal_part, inverse)


def layer_norm_back(grad_out, normal_part, inverse, gain):
    scaled = grad_out * gain
    grad_in = inverse * (
        scaled
        - jnp.mean(scaled, -1, keepdims=True)
        - normal_part * jnp.mean(scaled * normal_part, -1, keepdims=True)
    )
    return (grad_in, jnp.sum(grad_out * normal_part, 0), jnp.sum(grad_out, 0))


def row_scores(query_one, key_one, segment_one, scale):
    scores = (
        jnp.einsum("qhd,khd->hqk", query_one, key_one, preferred_element_type=jnp.float32) * scale
    )
    same_text = segment_one[:, None] == segment_one[None, :]
    return jnp.where(same_text[None], scores, masked_value)


def attend_rows(query_rows, key_rows, value_rows, row_segments):
    scale = 1.0 / math.sqrt(query_rows.shape[-1])

    def one_row(row_args):
        query_one, key_one, value_one, segment_one = row_args
        scores = row_scores(query_one, key_one, segment_one, scale)
        row_max = jnp.max(scores, -1, keepdims=True)
        exp_scores = jnp.exp(scores - row_max)
        sums = jnp.sum(exp_scores, -1, keepdims=True)
        attn_probs = exp_scores / sums
        mixed = jnp.einsum(
            "hqk,khd->qhd",
            attn_probs.astype(jnp.bfloat16),
            value_one,
            preferred_element_type=jnp.float32,
        )
        return (mixed.astype(jnp.bfloat16), (row_max + jnp.log(sums))[..., 0])

    return lax.map(one_row, (query_rows, key_rows, value_rows, row_segments))


def attend_back(query_rows, key_rows, value_rows, row_segments, log_norm, grad_mixed):
    scale = 1.0 / math.sqrt(query_rows.shape[-1])

    def one_row(row_args):
        query_one, key_one, value_one, segment_one, norm_one, grad_one = row_args
        scores = row_scores(query_one, key_one, segment_one, scale)
        attn_probs = jnp.exp(scores - norm_one[..., None])
        grad_value = jnp.einsum(
            "hqk,qhd->khd",
            attn_probs.astype(jnp.bfloat16),
            grad_one,
            preferred_element_type=jnp.float32,
        )
        grad_probs = jnp.einsum(
            "qhd,khd->hqk", grad_one, value_one, preferred_element_type=jnp.float32
        )
        inner = jnp.sum(attn_probs * grad_probs, -1, keepdims=True)
        grad_scores = (attn_probs * (grad_probs - inner)).astype(jnp.bfloat16)
        grad_query = (
            jnp.einsum("hqk,khd->qhd", grad_scores, key_one, preferred_element_type=jnp.float32)
            * scale
        )
        grad_key = (
            jnp.einsum("hqk,qhd->khd", grad_scores, query_one, preferred_element_type=jnp.float32)
            * scale
        )
        return jnp.concatenate([grad_query, grad_key, grad_value], axis=1)

    return lax.map(one_row, (query_rows, key_rows, value_rows, row_segments, log_norm, grad_mixed))


def attention_back_kernel(scale, q_ref, k_ref, v_ref, g_ref, norm_ref, seg_col_ref, seg_row_ref, dq_ref, dk_ref, dv_ref):
    pair = pl.program_id(1)
    width = q_ref.shape[1]
    half = width // 2
    lane = lax.broadcasted_iota(jnp.int32, (1, width), 1)
    same = seg_col_ref[...] == seg_row_ref[0]
    norms = norm_ref[...]
    norm_lane = lax.broadcasted_iota(jnp.int32, norms.shape, 1)
    q = q_ref[...]
    k = k_ref[...]
    v = v_ref[...]
    g = g_ref[...]
    zero_b = jnp.zeros_like(q)
    on_last = (((1,), (1,)), ((), ()))
    on_first = (((0,), (0,)), ((), ()))
    dq = jnp.zeros(q.shape, jnp.float32)
    dk = jnp.zeros(q.shape, jnp.float32)
    dv = jnp.zeros(q.shape, jnp.float32)
    for head in range(2):
        mine = (lane >= head * half) & (lane < (head + 1) * half)
        q_h = jnp.where(mine, q, zero_b)
        g_h = jnp.where(mine, g, zero_b)
        norm_h = jnp.sum(jnp.where(norm_lane == 2 * pair + head, norms, 0.0), 1, keepdims=True)
        scores = lax.dot_general(q_h, k, on_last, preferred_element_type=jnp.float32) * scale
        scores = jnp.where(same, scores, masked_value)
        probs = jnp.exp(scores - norm_h)
        grad_v = lax.dot_general(probs.astype(jnp.bfloat16), g, on_first, preferred_element_type=jnp.float32)
        grad_p = lax.dot_general(g_h, v, on_last, preferred_element_type=jnp.float32)
        inner = jnp.sum(probs * grad_p, -1, keepdims=True)
        grad_s = (probs * (grad_p - inner)).astype(jnp.bfloat16)
        grad_q = jnp.dot(grad_s, k, preferred_element_type=jnp.float32) * scale
        grad_k = lax.dot_general(grad_s, q, on_first, preferred_element_type=jnp.float32) * scale
        dq = jnp.where(mine, grad_q, dq)
        dk = jnp.where(mine, grad_k, dk)
        dv = jnp.where(mine, grad_v, dv)
    dq_ref[...] = dq.astype(dq_ref.dtype)
    dk_ref[...] = dk.astype(dk_ref.dtype)
    dv_ref[...] = dv.astype(dv_ref.dtype)


def attention_back(qkv_rows, grad_mixed_flat, norm_tokens, segments, heads, head_dim):
    tokens, three_width = qkv_rows.shape
    width = three_width // 3
    rows, seq_len = segments.shape
    pair_width = 2 * head_dim
    pairs = heads // 2
    seg_col = segments.reshape(tokens, 1)
    seg_row = segments.reshape(rows, 1, seq_len)
    scale = 1.0 / math.sqrt(head_dim)
    out = jax.ShapeDtypeStruct((tokens, width), jnp.bfloat16)
    return pl.pallas_call(
        functools.partial(attention_back_kernel, scale),
        grid=(rows, pairs),
        in_specs=[
            pl.BlockSpec((seq_len, pair_width), lambda r, p: (r, p)),
            pl.BlockSpec((seq_len, pair_width), lambda r, p: (r, pairs + p)),
            pl.BlockSpec((seq_len, pair_width), lambda r, p: (r, 2 * pairs + p)),
            pl.BlockSpec((seq_len, pair_width), lambda r, p: (r, p)),
            pl.BlockSpec((seq_len, heads), lambda r, p: (r, 0)),
            pl.BlockSpec((seq_len, 1), lambda r, p: (r, 0)),
            pl.BlockSpec((1, 1, seq_len), lambda r, p: (r, 0, 0)),
        ],
        out_specs=[pl.BlockSpec((seq_len, pair_width), lambda r, p: (r, p))] * 3,
        out_shape=[out, out, out],
        compiler_params=pltpu.CompilerParams(vmem_limit_bytes=48 * 1024 * 1024),
        cost_estimate=pl.CostEstimate(
            flops=10 * rows * heads * seq_len * seq_len * pair_width,
            transcendentals=rows * heads * seq_len * seq_len,
            bytes_accessed=tokens * (three_width + 4 * width) * 2,
        ),
    )(qkv_rows, qkv_rows, qkv_rows, grad_mixed_flat, norm_tokens, seg_col, seg_row)


def apply_update(weight, grad, moment, average, decay):
    step_grad = grad + decay * weight
    new_moment = momentum_rate * moment + step_grad
    new_weight = weight - learn_rate * (step_grad + momentum_rate * new_moment)
    fresh_running_mean = average_rate * average + (1.0 - average_rate) * new_weight
    return (new_weight, new_moment, fresh_running_mean)


def bf16_round(values):
    return lax.reduce_precision(values, exponent_bits=8, mantissa_bits=7)


def flat_index(sizes):
    idx = 0
    for name, size in zip(AXES, sizes):
        idx = idx * size + lax.axis_index(name)
    return idx


def device_of(flat, sizes):
    coords = []
    for size in reversed(sizes):
        coords.append(lax.rem(flat, size))
        flat = flat // size
    return tuple(reversed(coords))


def enter_all(n, sizes, me):
    barrier = pltpu.get_barrier_semaphore()

    def greet(k, carry):
        peer = lax.rem(me + k, n)
        pl.semaphore_signal(barrier, inc=1, device_id=device_of(peer, sizes), device_id_type=MESH)
        return carry

    lax.fori_loop(1, n, greet, 0)
    pl.semaphore_wait(barrier, n - 1)


def gather_kernel(n, sizes, x_ref, out_ref, send_sem, recv_sem):
    me = flat_index(sizes)
    enter_all(n, sizes, me)

    def send(k, carry):
        peer = lax.rem(me + k, n)
        pltpu.make_async_remote_copy(
            src_ref=x_ref, dst_ref=out_ref.at[me], send_sem=send_sem.at[k], recv_sem=recv_sem.at[me],
            device_id=device_of(peer, sizes), device_id_type=MESH,
        ).start()
        return carry

    lax.fori_loop(1, n, send, 0)
    out_ref[me] = x_ref[...]

    def finish(k, carry):
        peer = lax.rem(me + k, n)
        src = lax.rem(me + n - k, n)
        pltpu.make_async_remote_copy(
            src_ref=x_ref, dst_ref=out_ref.at[me], send_sem=send_sem.at[k], recv_sem=recv_sem.at[me],
            device_id=device_of(peer, sizes), device_id_type=MESH,
        ).wait_send()
        pltpu.make_async_remote_copy(
            src_ref=x_ref, dst_ref=out_ref.at[src], send_sem=send_sem.at[k], recv_sem=recv_sem.at[src],
            device_id=device_of(src, sizes), device_id_type=MESH,
        ).wait_recv()
        return carry

    lax.fori_loop(1, n, finish, 0)


def small_gather(x, sizes, cid):
    n = math.prod(sizes)
    return pl.pallas_call(
        functools.partial(gather_kernel, n, sizes),
        out_shape=jax.ShapeDtypeStruct((n,) + x.shape, x.dtype),
        in_specs=[pl.BlockSpec(memory_space=pltpu.VMEM)],
        out_specs=pl.BlockSpec(memory_space=pltpu.VMEM),
        scratch_shapes=[pltpu.SemaphoreType.DMA((n,)), pltpu.SemaphoreType.DMA((n,))],
        compiler_params=pltpu.CompilerParams(collective_id=cid, has_side_effects=True),
    )(x)


def scatter_kernel(n, sizes, x_ref, out_ref, send_sem, recv_sem):
    me = flat_index(sizes)
    enter_all(n, sizes, me)

    def send(k, carry):
        peer = lax.rem(me + k, n)
        pltpu.make_async_remote_copy(
            src_ref=x_ref.at[peer], dst_ref=out_ref.at[me], send_sem=send_sem.at[k], recv_sem=recv_sem.at[me],
            device_id=device_of(peer, sizes), device_id_type=MESH,
        ).start()
        return carry

    lax.fori_loop(1, n, send, 0)
    out_ref[me] = x_ref[me]

    def finish(k, carry):
        peer = lax.rem(me + k, n)
        src = lax.rem(me + n - k, n)
        pltpu.make_async_remote_copy(
            src_ref=x_ref.at[peer], dst_ref=out_ref.at[me], send_sem=send_sem.at[k], recv_sem=recv_sem.at[me],
            device_id=device_of(peer, sizes), device_id_type=MESH,
        ).wait_send()
        pltpu.make_async_remote_copy(
            src_ref=x_ref.at[src], dst_ref=out_ref.at[src], send_sem=send_sem.at[k], recv_sem=recv_sem.at[src],
            device_id=device_of(src, sizes), device_id_type=MESH,
        ).wait_recv()
        return carry

    lax.fori_loop(1, n, finish, 0)


def small_scatter(x, sizes, cid):
    n = math.prod(sizes)
    return pl.pallas_call(
        functools.partial(scatter_kernel, n, sizes),
        out_shape=jax.ShapeDtypeStruct(x.shape, x.dtype),
        in_specs=[pl.BlockSpec(memory_space=pltpu.VMEM)],
        out_specs=pl.BlockSpec(memory_space=pltpu.VMEM),
        scratch_shapes=[pltpu.SemaphoreType.DMA((n,)), pltpu.SemaphoreType.DMA((n,))],
        compiler_params=pltpu.CompilerParams(collective_id=cid, has_side_effects=True),
    )(x)


def pair_gather_kernel(n, sizes, x_ref, out_ref, local_sem, send1, recv1, send2, recv2, send3, recv3):
    me = flat_index(sizes)
    chips = n // 2
    chip = me // 2
    core = lax.rem(me, 2)
    partner = me + 1 - 2 * core
    enter_all(n, sizes, me)

    local = pltpu.make_async_copy(x_ref, out_ref.at[me], local_sem)
    local.start()
    first = pltpu.make_async_remote_copy(
        src_ref=x_ref, dst_ref=out_ref.at[me], send_sem=send1, recv_sem=recv1,
        device_id=device_of(partner, sizes), device_id_type=MESH,
    )
    first.start()
    local.wait()
    first.wait_send()
    pltpu.make_async_remote_copy(
        src_ref=x_ref, dst_ref=out_ref.at[partner], send_sem=send1, recv_sem=recv1,
        device_id=device_of(partner, sizes), device_id_type=MESH,
    ).wait_recv()

    def pair(c):
        return out_ref.at[pl.ds(2 * c, 2)]

    def target(k):
        return lax.rem(chip + 2 * k - 1 + core, chips)

    def source(k):
        return lax.rem(chip + chips - (2 * k - 1 + core), chips)

    count = (chips - core) // 2

    def send_out(k, carry):
        other = target(k)
        pltpu.make_async_remote_copy(
            src_ref=pair(chip), dst_ref=pair(chip), send_sem=send2.at[other], recv_sem=recv2.at[chip],
            device_id=device_of(2 * other + core, sizes), device_id_type=MESH,
        ).start()
        return carry

    lax.fori_loop(1, count + 1, send_out, 0)

    def take_in(k, carry):
        other = source(k)
        pltpu.make_async_remote_copy(
            src_ref=pair(other), dst_ref=pair(other), send_sem=send2.at[other], recv_sem=recv2.at[other],
            device_id=device_of(2 * other + core, sizes), device_id_type=MESH,
        ).wait_recv()
        pltpu.make_async_remote_copy(
            src_ref=pair(other), dst_ref=pair(other), send_sem=send3.at[other], recv_sem=recv3.at[other],
            device_id=device_of(partner, sizes), device_id_type=MESH,
        ).start()
        return carry

    lax.fori_loop(1, count + 1, take_in, 0)

    def sent_out(k, carry):
        other = target(k)
        pltpu.make_async_remote_copy(
            src_ref=pair(chip), dst_ref=pair(chip), send_sem=send2.at[other], recv_sem=recv2.at[chip],
            device_id=device_of(2 * other + core, sizes), device_id_type=MESH,
        ).wait_send()
        return carry

    lax.fori_loop(1, count + 1, sent_out, 0)

    def forwarded(k, carry):
        other = source(k)
        pltpu.make_async_remote_copy(
            src_ref=pair(other), dst_ref=pair(other), send_sem=send3.at[other], recv_sem=recv3.at[other],
            device_id=device_of(partner, sizes), device_id_type=MESH,
        ).wait_send()
        return carry

    lax.fori_loop(1, count + 1, forwarded, 0)

    other_count = (chips - (1 - core)) // 2

    def partner_source(k):
        return lax.rem(chip + chips - (2 * k - 1 + (1 - core)), chips)

    def from_partner(k, carry):
        other = partner_source(k)
        pltpu.make_async_remote_copy(
            src_ref=pair(other), dst_ref=pair(other), send_sem=send3.at[other], recv_sem=recv3.at[other],
            device_id=device_of(partner, sizes), device_id_type=MESH,
        ).wait_recv()
        return carry

    lax.fori_loop(1, other_count + 1, from_partner, 0)


def pair_gather(x, sizes, cid):
    n = math.prod(sizes)
    chips = n // 2
    dma = pltpu.SemaphoreType.DMA
    return pl.pallas_call(
        functools.partial(pair_gather_kernel, n, sizes),
        out_shape=jax.ShapeDtypeStruct((n,) + x.shape, x.dtype),
        in_specs=[pl.BlockSpec(memory_space=pltpu.VMEM)],
        out_specs=pl.BlockSpec(memory_space=pltpu.VMEM),
        scratch_shapes=[dma(()), dma(()), dma(()), dma((chips,)), dma((chips,)), dma((chips,)), dma((chips,))],
        compiler_params=pltpu.CompilerParams(collective_id=cid, has_side_effects=True),
    )(x)


def halving_orders(n, parts):
    bits = n.bit_length() - 1
    middle = list(range(1, bits - 1))
    orders = []
    for p in range(parts):
        shift = p % len(middle) if middle else 0
        orders.append(tuple([0] + middle[shift:] + middle[:shift] + [bits - 1]))
    return tuple(orders)


def halving_kernel(n, sizes, orders, cols, x_hbm, out_ref, work, *rest):
    steps = len(orders[0])
    parts = len(orders)
    recvs = rest[:steps]
    local_sem, send_sems, recv_sems = rest[steps:]
    me = flat_index(sizes)

    def partner_of(bit):
        mine = lax.rem(me // (2**bit), 2)
        return mine, me + (1 - 2 * mine) * (2**bit)

    barrier = pltpu.get_barrier_semaphore()
    for bit in range(steps):
        _, other = partner_of(bit)
        pl.semaphore_signal(barrier, inc=1, device_id=device_of(other, sizes), device_id_type=MESH)
    pl.semaphore_wait(barrier, steps)

    half = n // 2
    first = []
    for p in range(parts):
        order = orders[p]
        mine, other = partner_of(order[0])
        column = pl.ds(p * cols, cols)

        def owner(j, side, order=order):
            o = side * (2 ** order[0])
            for m, bit in enumerate(order[1:]):
                o = o + lax.rem(j // (2 ** (steps - 2 - m)), 2) * (2**bit)
            return o

        def issue(j, carry, p=p, owner=owner, mine=mine, other=other, column=column):
            pltpu.make_async_remote_copy(
                src_ref=x_hbm.at[owner(j, 1 - mine), :, column], dst_ref=recvs[0].at[p, j],
                send_sem=send_sems.at[p, 0], recv_sem=recv_sems.at[p, 0],
                device_id=device_of(other, sizes), device_id_type=MESH,
            ).start()
            pltpu.make_async_copy(x_hbm.at[owner(j, mine), :, column], work.at[p, j], local_sem.at[p]).start()
            return carry

        lax.fori_loop(0, half, issue, 0)
        first.append(other)
    for p in range(parts):
        whole = pltpu.make_async_remote_copy(
            src_ref=work.at[p, pl.ds(0, half)], dst_ref=recvs[0].at[p],
            send_sem=send_sems.at[p, 0], recv_sem=recv_sems.at[p, 0],
            device_id=device_of(first[p], sizes), device_id_type=MESH,
        )
        pltpu.make_async_copy(work.at[p, pl.ds(0, half)], work.at[p, pl.ds(0, half)], local_sem.at[p]).wait()
        whole.wait_recv()
        whole.wait_send()

        def accumulate0(i, carry, p=p):
            total = work[p, i].astype(jnp.float32) + recvs[0][p, i].astype(jnp.float32)
            work[p, i] = total.astype(work.dtype)
            return carry

        lax.fori_loop(0, half, accumulate0, 0)

    for step in range(1, steps):
        half = n >> (step + 1)
        copies = []
        for p in range(parts):
            mine, other = partner_of(orders[p][step])
            send = pltpu.make_async_remote_copy(
                src_ref=work.at[p, pl.ds((1 - mine) * half, half)], dst_ref=recvs[step].at[p],
                send_sem=send_sems.at[p, step], recv_sem=recv_sems.at[p, step],
                device_id=device_of(other, sizes), device_id_type=MESH,
            )
            send.start()
            copies.append((mine, send))
        for p in range(parts):
            mine, send = copies[p]
            send.wait_recv()
            send.wait_send()

            def accumulate(i, carry, p=p, mine=mine, half=half, step=step):
                total = work[p, mine * half + i].astype(jnp.float32) + recvs[step][p, i].astype(jnp.float32)
                work[p, i] = total.astype(work.dtype)
                return carry

            lax.fori_loop(0, half, accumulate, 0)
    for p in range(parts):
        out_ref[p] = work[p, 0]


def halving_scatter(x, sizes, parts, cid):
    n, rows, width = x.shape
    cols = width // parts
    orders = halving_orders(n, parts)
    steps = len(orders[0])
    dma = pltpu.SemaphoreType.DMA
    scratch = [pltpu.VMEM((parts, n // 2, rows, cols), x.dtype)]
    scratch += [pltpu.VMEM((parts, n >> (k + 1), rows, cols), x.dtype) for k in range(steps)]
    scratch += [dma((parts,)), dma((parts, steps)), dma((parts, steps))]
    return pl.pallas_call(
        functools.partial(halving_kernel, n, sizes, orders, cols),
        out_shape=jax.ShapeDtypeStruct((parts, rows, cols), x.dtype),
        in_specs=[pl.BlockSpec(memory_space=pl.ANY)],
        out_specs=pl.BlockSpec(memory_space=pltpu.VMEM),
        scratch_shapes=scratch,
        compiler_params=pltpu.CompilerParams(
            collective_id=cid, has_side_effects=True, vmem_limit_bytes=56 * 1024 * 1024
        ),
    )(x)


def contrastive(embed_b, gathered, partner_all, me):
    own_texts = embed_b.shape[0]
    all_texts = gathered.shape[0]
    chunk = min(all_texts, 1024)
    on_rows = (((1,), (1,)), ((), ()))

    def chunk_stats(c):
        rows_b = lax.dynamic_slice_in_dim(gathered, c * chunk, chunk)
        sim = lax.dot_general(rows_b, gathered, on_rows, preferred_element_type=jnp.float32) / logit_divisor
        column_ids = lax.broadcasted_iota(jnp.int32, sim.shape, 1)
        row_ids = lax.broadcasted_iota(jnp.int32, sim.shape, 0) + c * chunk
        masked = jnp.where(column_ids == row_ids, masked_value, sim)
        row_max = jnp.max(masked, -1, keepdims=True)
        log_sum = row_max + jnp.log(jnp.sum(jnp.exp(masked - row_max), -1, keepdims=True))
        wanted = lax.dynamic_slice_in_dim(partner_all, c * chunk, chunk)
        positive = jnp.sum(jnp.where(column_ids == wanted[:, None], sim, 0.0), -1)
        return log_sum[:, 0], positive

    if all_texts == chunk:
        log_sum_all, positive_all = chunk_stats(0)
    else:
        log_sum_all, positive_all = lax.map(chunk_stats, jnp.arange(all_texts // chunk))
        log_sum_all = log_sum_all.reshape(-1)
        positive_all = positive_all.reshape(-1)
    mean_loss = jnp.sum(log_sum_all - positive_all) / all_texts

    own_start = me * own_texts
    own_ids = lax.broadcasted_iota(jnp.int32, (own_texts,), 0) + own_start
    own_partner = lax.dynamic_slice_in_dim(partner_all, own_start, own_texts)
    own_log_sum = lax.dynamic_slice_in_dim(log_sum_all, own_start, own_texts)

    sim_rows = lax.dot_general(embed_b, gathered, on_rows, preferred_element_type=jnp.float32) / logit_divisor
    column_ids = lax.broadcasted_iota(jnp.int32, sim_rows.shape, 1)
    masked_rows = jnp.where(column_ids == own_ids[:, None], masked_value, sim_rows)
    grad_rows = (
        jnp.exp(masked_rows - own_log_sum[:, None]) - (column_ids == own_partner[:, None]).astype(jnp.float32)
    ).astype(jnp.bfloat16)

    sim_cols = lax.dot_general(gathered, embed_b, on_rows, preferred_element_type=jnp.float32) / logit_divisor
    row_ids = lax.broadcasted_iota(jnp.int32, sim_cols.shape, 0)
    masked_cols = jnp.where(row_ids == own_ids[None, :], masked_value, sim_cols)
    grad_cols = (
        jnp.exp(masked_cols - log_sum_all[:, None]) - (partner_all[:, None] == own_ids[None, :]).astype(jnp.float32)
    ).astype(jnp.bfloat16)

    on_tokens = (((0,), (0,)), ((), ()))
    embedding_gradient = (
        jnp.dot(grad_rows, gathered, preferred_element_type=jnp.float32)
        + lax.dot_general(grad_cols, gathered, on_tokens, preferred_element_type=jnp.float32)
    ) / logit_divisor
    return mean_loss, embedding_gradient


def shards(
    hidden_in,
    segments,
    partner,
    attn_weights,
    ffn_weights,
    vectors,
    attn_momentum,
    ffn_momentum,
    vector_momentum,
    attn_averaged,
    ffn_averaged,
    vector_averaged,
):
    sizes = tuple(lax.axis_size(name) for name in AXES)
    n_dev = math.prod(sizes)
    me = flat_index(sizes)
    vec_len = vectors.shape[0]
    small = jnp.concatenate([vectors, partner.astype(jnp.float32)])[None, :]
    small_all = small_gather(small, sizes, 0)[:, 0, :]
    vector_f = bf16_round(small_all[:, :vec_len].reshape(-1))
    partner_all = small_all[:, vec_len:].reshape(-1).astype(jnp.int32)
    attn_full, ffn_full = (
        lax.all_gather(attn_weights.astype(jnp.bfloat16), AXES, axis=1, tiled=True),
        lax.all_gather(ffn_weights.astype(jnp.bfloat16), AXES, axis=1, tiled=True),
    )
    width = attn_full.shape[0]
    hidden = ffn_full.shape[1] // 2
    query_bias = vector_f[0:width]
    value_bias = vector_f[width : 2 * width]
    output_bias = vector_f[2 * width : 3 * width]
    gain_first = vector_f[3 * width : 4 * width]
    shift_first = vector_f[4 * width : 5 * width]
    upper_bias = vector_f[5 * width : 5 * width + hidden]
    lower_bias = vector_f[5 * width + hidden : 6 * width + hidden]
    gain_second = vector_f[6 * width + hidden : 7 * width + hidden]
    shift_second = vector_f[7 * width + hidden : 8 * width + hidden]
    w_qkv = attn_full[:, : 3 * width]
    w_output = attn_full[:, 3 * width :]
    w_upper = ffn_full[:, :hidden]
    w_lower = ffn_full[:, hidden:]
    rows_dev, seq_len = segments.shape
    tokens_n = rows_dev * seq_len
    on_rows = (((1,), (1,)), ((), ()))
    on_tokens = (((0,), (0,)), ((), ()))
    qkv_bias = jnp.concatenate([query_bias, jnp.zeros_like(query_bias), value_bias])
    qkv_rows = (jnp.dot(hidden_in, w_qkv, preferred_element_type=jnp.float32) + qkv_bias).astype(
        jnp.bfloat16
    )
    heads = qkv_rows.reshape(rows_dev, seq_len, 3, HEADS, HD)
    query_rows = heads[:, :, 0]
    key_rows = heads[:, :, 1]
    value_rows = heads[:, :, 2]
    mixed, log_norm = attend_rows(query_rows, key_rows, value_rows, segments)
    mixed_flat = mixed.reshape(tokens_n, width)
    first_sum = (
        hidden_in.astype(jnp.float32)
        + jnp.dot(mixed_flat, w_output, preferred_element_type=jnp.float32)
        + output_bias
    )
    normed, normal_one, inverse_one = layer_norm_parts(first_sum, gain_first, shift_first)
    normed_r = bf16_round(normed)
    normed_b = normed_r.astype(jnp.bfloat16)
    upper = jnp.dot(normed_b, w_upper, preferred_element_type=jnp.float32) + upper_bias
    active_b = jax.nn.gelu(upper, approximate=False).astype(jnp.bfloat16)
    second_sum = (
        normed_r
        + lax.dot_general(active_b, w_lower, on_rows, preferred_element_type=jnp.float32)
        + lower_bias
    )
    result, normal_two, inverse_two = layer_norm_parts(second_sum, gain_second, shift_second)
    text_ids = jnp.arange(SEGS, dtype=jnp.int32)
    one_hot = (segments[:, None, :] == text_ids[None, :, None]).astype(jnp.float32)
    counts = jnp.sum(one_hot, -1, keepdims=True)
    pooled = (
        jnp.einsum(
            "rts,rsd->rtd",
            one_hot,
            result.reshape(rows_dev, seq_len, width),
            precision=lax.Precision.HIGHEST,
        )
        / counts
    ).reshape(-1, width)
    inv_norm = lax.rsqrt(jnp.sum(pooled * pooled, -1, keepdims=True) + pool_epsilon)
    embed_b = (pooled * inv_norm).astype(jnp.bfloat16)
    gathered_embeddings = pair_gather(embed_b, sizes, 2).reshape(-1, width)
    mean_loss, embedding_gradient = contrastive(embed_b, gathered_embeddings, partner_all, me)
    grad_pooled = inv_norm * embedding_gradient - pooled * (
        inv_norm * inv_norm * inv_norm
    ) * jnp.sum(embedding_gradient * pooled, -1, keepdims=True)
    derivative_output = jnp.einsum(
        "rts,rtd->rsd",
        one_hot,
        grad_pooled.reshape(rows_dev, SEGS, width) / counts,
        precision=lax.Precision.HIGHEST,
    ).reshape(tokens_n, width)
    grad_second, gain_two_grad, shift_two_grad = layer_norm_back(
        derivative_output, normal_two, inverse_two, gain_second
    )
    lower_bias_grad = jnp.sum(grad_second, 0)
    lower_grad_b = grad_second.astype(jnp.bfloat16)
    lower_w_grad_t = lax.dot_general(
        active_b, lower_grad_b, on_tokens, preferred_element_type=jnp.float32
    )
    grad_active = jnp.dot(lower_grad_b, w_lower, preferred_element_type=jnp.float32)
    cumulative = 0.5 * (1.0 + lax.erf(upper / math.sqrt(2.0)))
    density = jnp.exp(-0.5 * upper * upper) / math.sqrt(2.0 * math.pi)
    grad_upper = grad_active * (cumulative + upper * density)
    upper_bias_grad = jnp.sum(grad_upper, 0)
    upper_grad_b = grad_upper.astype(jnp.bfloat16)
    upper_w_grad_t = lax.dot_general(
        upper_grad_b, normed_b, on_tokens, preferred_element_type=jnp.float32
    )
    grad_normed = (
        lax.dot_general(upper_grad_b, w_upper, on_rows, preferred_element_type=jnp.float32)
        + grad_second
    )
    grad_first, gain_one_grad, shift_one_grad = layer_norm_back(
        grad_normed, normal_one, inverse_one, gain_first
    )
    output_bias_grad = jnp.sum(grad_first, 0)
    first_grad_b = grad_first.astype(jnp.bfloat16)
    output_w_grad_t = lax.dot_general(
        first_grad_b, mixed_flat, on_tokens, preferred_element_type=jnp.float32
    )
    grad_mixed = lax.dot_general(
        first_grad_b, w_output, on_rows, preferred_element_type=jnp.float32
    ).astype(jnp.bfloat16)
    grad_mixed = grad_mixed.reshape(rows_dev, seq_len, HEADS, HD)
    norm_tokens = jnp.swapaxes(log_norm, 1, 2).reshape(tokens_n, HEADS)
    qkv_grad = jnp.concatenate(
        attention_back(qkv_rows, grad_mixed.reshape(tokens_n, width), norm_tokens, segments, HEADS, HD), 1
    ).astype(jnp.float32)
    qkv_grad_f = bf16_round(qkv_grad)
    qkv_grad_b = qkv_grad_f.astype(jnp.bfloat16)
    query_bias_grad = jnp.sum(qkv_grad_f[:, :width], 0)
    value_bias_grad = jnp.sum(qkv_grad_f[:, 2 * width :], 0)
    qkv_w_grad_t = lax.dot_general(
        qkv_grad_b, hidden_in, on_tokens, preferred_element_type=jnp.float32
    )
    input_grad = (
        lax.dot_general(qkv_grad_b, w_qkv, on_rows, preferred_element_type=jnp.float32) + grad_first
    )
    vector_grad = jnp.concatenate(
        [
            query_bias_grad,
            value_bias_grad,
            output_bias_grad,
            gain_one_grad,
            shift_one_grad,
            upper_bias_grad,
            lower_bias_grad,
            gain_two_grad,
            shift_two_grad,
        ]
    )
    vector_slots = small_scatter(vector_grad.reshape(n_dev, 1, -1), sizes, 1)
    vector_reduced = jnp.sum(vector_slots[:, 0, :], 0)
    attn_cols = (qkv_w_grad_t.shape[0] + output_w_grad_t.shape[0]) // n_dev
    ffn_cols = (upper_w_grad_t.shape[0] + lower_w_grad_t.shape[0]) // n_dev
    attn_blocks = jnp.concatenate(
        [qkv_w_grad_t.reshape(-1, attn_cols, width), output_w_grad_t.reshape(-1, attn_cols, width)], 0
    )
    ffn_blocks = jnp.concatenate(
        [upper_w_grad_t.reshape(-1, ffn_cols, width), lower_w_grad_t.reshape(-1, ffn_cols, width)], 0
    )
    joined = jnp.concatenate([attn_blocks, ffn_blocks], 1).astype(GRAD_SEND)
    parts = 3
    mine_parts = halving_scatter(joined, sizes, parts, 3)
    joined_reduced = jnp.transpose(mine_parts, (1, 0, 2)).reshape(-1, width).astype(jnp.float32)
    attn_reduced = joined_reduced[:attn_cols].T
    ffn_reduced = joined_reduced[attn_cols:].T
    attn_new, attn_moment, attn_average = apply_update(
        attn_weights, attn_reduced, attn_momentum, attn_averaged, decay_rate
    )
    ffn_new, ffn_moment, ffn_average = apply_update(
        ffn_weights, ffn_reduced, ffn_momentum, ffn_averaged, decay_rate
    )
    vector_new, vector_moment, vector_average = apply_update(
        vectors, vector_reduced, vector_momentum, vector_averaged, 0.0
    )
    return (
        mean_loss,
        input_grad,
        attn_reduced,
        ffn_reduced,
        vector_reduced,
        attn_new,
        ffn_new,
        vector_new,
        attn_moment,
        ffn_moment,
        vector_moment,
        attn_average,
        ffn_average,
        vector_average,
    )


def solution(mesh):
    in_specs = (
        P(("dp", "rep"), None),
        P(("dp", "rep"), None),
        P(("dp", "rep")),
        P(None, ("dp", "rep")),
        P(None, ("dp", "rep")),
        P(("dp", "rep")),
        P(None, ("dp", "rep")),
        P(None, ("dp", "rep")),
        P(("dp", "rep")),
        P(None, ("dp", "rep")),
        P(None, ("dp", "rep")),
        P(("dp", "rep")),
    )
    out_specs = (
        P(),
        P(("dp", "rep"), None),
        P(None, ("dp", "rep")),
        P(None, ("dp", "rep")),
        P(("dp", "rep")),
        P(None, ("dp", "rep")),
        P(None, ("dp", "rep")),
        P(("dp", "rep")),
        P(None, ("dp", "rep")),
        P(None, ("dp", "rep")),
        P(("dp", "rep")),
        P(None, ("dp", "rep")),
        P(None, ("dp", "rep")),
        P(("dp", "rep")),
    )
    return jax.shard_map(shards, mesh=mesh, in_specs=in_specs, out_specs=out_specs, check_vma=False)
```

```python
import functools
import math

import jax
import jax.numpy as jnp
from jax import lax
from jax.experimental import pallas as pl
from jax.experimental.pallas import tpu as pltpu
from jax.sharding import PartitionSpec as P

MESH = pl.DeviceIdType.MESH
GRAD_SEND = jnp.bfloat16
AXES = ("dp", "rep")

HEADS = 12
HD = 64
SEGS = 16


ln_epsilon = 1e-12
pool_epsilon = 1e-06
logit_divisor = 0.025
learn_rate = 0.01
momentum_rate = 0.9
decay_rate = 0.01
average_rate = 0.75
masked_value = -1e30


def layer_norm_parts(values, gain, shift):
    per_line_average = jnp.mean(values, -1, keepdims=True)
    centred = values - per_line_average
    inverse = lax.rsqrt(jnp.mean(centred * centred, -1, keepdims=True) + ln_epsilon)
    normal_part = centred * inverse
    return (normal_part * gain + shift, normal_part, inverse)


def layer_norm_back(grad_out, normal_part, inverse, gain):
    scaled = grad_out * gain
    grad_in = inverse * (
        scaled
        - jnp.mean(scaled, -1, keepdims=True)
        - normal_part * jnp.mean(scaled * normal_part, -1, keepdims=True)
    )
    return (grad_in, jnp.sum(grad_out * normal_part, 0), jnp.sum(grad_out, 0))


def row_scores(query_one, key_one, segment_one, scale):
    scores = (
        jnp.einsum("qhd,khd->hqk", query_one, key_one, preferred_element_type=jnp.float32) * scale
    )
    same_text = segment_one[:, None] == segment_one[None, :]
    return jnp.where(same_text[None], scores, masked_value)


def attend_rows(query_rows, key_rows, value_rows, row_segments):
    scale = 1.0 / math.sqrt(query_rows.shape[-1])

    def one_row(row_args):
        query_one, key_one, value_one, segment_one = row_args
        scores = row_scores(query_one, key_one, segment_one, scale)
        row_max = jnp.max(scores, -1, keepdims=True)
        exp_scores = jnp.exp(scores - row_max)
        sums = jnp.sum(exp_scores, -1, keepdims=True)
        attn_probs = exp_scores / sums
        mixed = jnp.einsum(
            "hqk,khd->qhd",
            attn_probs.astype(jnp.bfloat16),
            value_one,
            preferred_element_type=jnp.float32,
        )
        return (mixed.astype(jnp.bfloat16), (row_max + jnp.log(sums))[..., 0])

    return lax.map(one_row, (query_rows, key_rows, value_rows, row_segments))


def attend_back(query_rows, key_rows, value_rows, row_segments, log_norm, grad_mixed):
    scale = 1.0 / math.sqrt(query_rows.shape[-1])

    def one_row(row_args):
        query_one, key_one, value_one, segment_one, norm_one, grad_one = row_args
        scores = row_scores(query_one, key_one, segment_one, scale)
        attn_probs = jnp.exp(scores - norm_one[..., None])
        grad_value = jnp.einsum(
            "hqk,qhd->khd",
            attn_probs.astype(jnp.bfloat16),
            grad_one,
            preferred_element_type=jnp.float32,
        )
        grad_probs = jnp.einsum(
            "qhd,khd->hqk", grad_one, value_one, preferred_element_type=jnp.float32
        )
        inner = jnp.sum(attn_probs * grad_probs, -1, keepdims=True)
        grad_scores = (attn_probs * (grad_probs - inner)).astype(jnp.bfloat16)
        grad_query = (
            jnp.einsum("hqk,khd->qhd", grad_scores, key_one, preferred_element_type=jnp.float32)
            * scale
        )
        grad_key = (
            jnp.einsum("hqk,qhd->khd", grad_scores, query_one, preferred_element_type=jnp.float32)
            * scale
        )
        return jnp.concatenate([grad_query, grad_key, grad_value], axis=1)

    return lax.map(one_row, (query_rows, key_rows, value_rows, row_segments, log_norm, grad_mixed))


def attention_back_kernel(scale, q_ref, k_ref, v_ref, g_ref, norm_ref, seg_col_ref, seg_row_ref, dq_ref, dk_ref, dv_ref):
    pair = pl.program_id(1)
    width = q_ref.shape[1]
    half = width // 2
    lane = lax.broadcasted_iota(jnp.int32, (1, width), 1)
    same = seg_col_ref[...] == seg_row_ref[0]
    norms = norm_ref[...]
    norm_lane = lax.broadcasted_iota(jnp.int32, norms.shape, 1)
    q = q_ref[...]
    k = k_ref[...]
    v = v_ref[...]
    g = g_ref[...]
    zero_b = jnp.zeros_like(q)
    on_last = (((1,), (1,)), ((), ()))
    on_first = (((0,), (0,)), ((), ()))
    dq = jnp.zeros(q.shape, jnp.float32)
    dk = jnp.zeros(q.shape, jnp.float32)
    dv = jnp.zeros(q.shape, jnp.float32)
    for head in range(2):
        mine = (lane >= head * half) & (lane < (head + 1) * half)
        q_h = jnp.where(mine, q, zero_b)
        g_h = jnp.where(mine, g, zero_b)
        norm_h = jnp.sum(jnp.where(norm_lane == 2 * pair + head, norms, 0.0), 1, keepdims=True)
        scores = lax.dot_general(q_h, k, on_last, preferred_element_type=jnp.float32) * scale
        scores = jnp.where(same, scores, masked_value)
        probs = jnp.exp(scores - norm_h)
        grad_v = lax.dot_general(probs.astype(jnp.bfloat16), g, on_first, preferred_element_type=jnp.float32)
        grad_p = lax.dot_general(g_h, v, on_last, preferred_element_type=jnp.float32)
        inner = jnp.sum(probs * grad_p, -1, keepdims=True)
        grad_s = (probs * (grad_p - inner)).astype(jnp.bfloat16)
        grad_q = jnp.dot(grad_s, k, preferred_element_type=jnp.float32) * scale
        grad_k = lax.dot_general(grad_s, q, on_first, preferred_element_type=jnp.float32) * scale
        dq = jnp.where(mine, grad_q, dq)
        dk = jnp.where(mine, grad_k, dk)
        dv = jnp.where(mine, grad_v, dv)
    dq_ref[...] = dq.astype(dq_ref.dtype)
    dk_ref[...] = dk.astype(dk_ref.dtype)
    dv_ref[...] = dv.astype(dv_ref.dtype)


def attention_back(qkv_rows, grad_mixed_flat, norm_tokens, segments, heads, head_dim):
    tokens, three_width = qkv_rows.shape
    width = three_width // 3
    rows, seq_len = segments.shape
    pair_width = 2 * head_dim
    pairs = heads // 2
    seg_col = segments.reshape(tokens, 1)
    seg_row = segments.reshape(rows, 1, seq_len)
    scale = 1.0 / math.sqrt(head_dim)
    out = jax.ShapeDtypeStruct((tokens, width), jnp.bfloat16)
    return pl.pallas_call(
        functools.partial(attention_back_kernel, scale),
        grid=(rows, pairs),
        in_specs=[
            pl.BlockSpec((seq_len, pair_width), lambda r, p: (r, p)),
            pl.BlockSpec((seq_len, pair_width), lambda r, p: (r, pairs + p)),
            pl.BlockSpec((seq_len, pair_width), lambda r, p: (r, 2 * pairs + p)),
            pl.BlockSpec((seq_len, pair_width), lambda r, p: (r, p)),
            pl.BlockSpec((seq_len, heads), lambda r, p: (r, 0)),
            pl.BlockSpec((seq_len, 1), lambda r, p: (r, 0)),
            pl.BlockSpec((1, 1, seq_len), lambda r, p: (r, 0, 0)),
        ],
        out_specs=[pl.BlockSpec((seq_len, pair_width), lambda r, p: (r, p))] * 3,
        out_shape=[out, out, out],
        compiler_params=pltpu.CompilerParams(vmem_limit_bytes=48 * 1024 * 1024),
        cost_estimate=pl.CostEstimate(
            flops=10 * rows * heads * seq_len * seq_len * pair_width,
            transcendentals=rows * heads * seq_len * seq_len,
            bytes_accessed=tokens * (three_width + 4 * width) * 2,
        ),
    )(qkv_rows, qkv_rows, qkv_rows, grad_mixed_flat, norm_tokens, seg_col, seg_row)


def apply_update(weight, grad, moment, average, decay):
    step_grad = grad + decay * weight
    new_moment = momentum_rate * moment + step_grad
    new_weight = weight - learn_rate * (step_grad + momentum_rate * new_moment)
    fresh_running_mean = average_rate * average + (1.0 - average_rate) * new_weight
    return (new_weight, new_moment, fresh_running_mean)


def bf16_round(values):
    return lax.reduce_precision(values, exponent_bits=8, mantissa_bits=7)


def flat_index(sizes):
    idx = 0
    for name, size in zip(AXES, sizes):
        idx = idx * size + lax.axis_index(name)
    return idx


def device_of(flat, sizes):
    coords = []
    for size in reversed(sizes):
        coords.append(lax.rem(flat, size))
        flat = flat // size
    return tuple(reversed(coords))


def enter_all(n, sizes, me):
    barrier = pltpu.get_barrier_semaphore()

    def greet(k, carry):
        peer = lax.rem(me + k, n)
        pl.semaphore_signal(barrier, inc=1, device_id=device_of(peer, sizes), device_id_type=MESH)
        return carry

    lax.fori_loop(1, n, greet, 0)
    pl.semaphore_wait(barrier, n - 1)


def gather_kernel(n, sizes, x_ref, out_ref, send_sem, recv_sem):
    me = flat_index(sizes)
    enter_all(n, sizes, me)

    def send(k, carry):
        peer = lax.rem(me + k, n)
        pltpu.make_async_remote_copy(
            src_ref=x_ref, dst_ref=out_ref.at[me], send_sem=send_sem.at[k], recv_sem=recv_sem.at[me],
            device_id=device_of(peer, sizes), device_id_type=MESH,
        ).start()
        return carry

    lax.fori_loop(1, n, send, 0)
    out_ref[me] = x_ref[...]

    def finish(k, carry):
        peer = lax.rem(me + k, n)
        src = lax.rem(me + n - k, n)
        pltpu.make_async_remote_copy(
            src_ref=x_ref, dst_ref=out_ref.at[me], send_sem=send_sem.at[k], recv_sem=recv_sem.at[me],
            device_id=device_of(peer, sizes), device_id_type=MESH,
        ).wait_send()
        pltpu.make_async_remote_copy(
            src_ref=x_ref, dst_ref=out_ref.at[src], send_sem=send_sem.at[k], recv_sem=recv_sem.at[src],
            device_id=device_of(src, sizes), device_id_type=MESH,
        ).wait_recv()
        return carry

    lax.fori_loop(1, n, finish, 0)


def small_gather(x, sizes, cid):
    n = math.prod(sizes)
    return pl.pallas_call(
        functools.partial(gather_kernel, n, sizes),
        out_shape=jax.ShapeDtypeStruct((n,) + x.shape, x.dtype),
        in_specs=[pl.BlockSpec(memory_space=pltpu.VMEM)],
        out_specs=pl.BlockSpec(memory_space=pltpu.VMEM),
        scratch_shapes=[pltpu.SemaphoreType.DMA((n,)), pltpu.SemaphoreType.DMA((n,))],
        compiler_params=pltpu.CompilerParams(collective_id=cid, has_side_effects=True),
    )(x)


def scatter_kernel(n, sizes, x_ref, out_ref, send_sem, recv_sem):
    me = flat_index(sizes)
    enter_all(n, sizes, me)

    def send(k, carry):
        peer = lax.rem(me + k, n)
        pltpu.make_async_remote_copy(
            src_ref=x_ref.at[peer], dst_ref=out_ref.at[me], send_sem=send_sem.at[k], recv_sem=recv_sem.at[me],
            device_id=device_of(peer, sizes), device_id_type=MESH,
        ).start()
        return carry

    lax.fori_loop(1, n, send, 0)
    out_ref[me] = x_ref[me]

    def finish(k, carry):
        peer = lax.rem(me + k, n)
        src = lax.rem(me + n - k, n)
        pltpu.make_async_remote_copy(
            src_ref=x_ref.at[peer], dst_ref=out_ref.at[me], send_sem=send_sem.at[k], recv_sem=recv_sem.at[me],
            device_id=device_of(peer, sizes), device_id_type=MESH,
        ).wait_send()
        pltpu.make_async_remote_copy(
            src_ref=x_ref.at[src], dst_ref=out_ref.at[src], send_sem=send_sem.at[k], recv_sem=recv_sem.at[src],
            device_id=device_of(src, sizes), device_id_type=MESH,
        ).wait_recv()
        return carry

    lax.fori_loop(1, n, finish, 0)


def small_scatter(x, sizes, cid):
    n = math.prod(sizes)
    return pl.pallas_call(
        functools.partial(scatter_kernel, n, sizes),
        out_shape=jax.ShapeDtypeStruct(x.shape, x.dtype),
        in_specs=[pl.BlockSpec(memory_space=pltpu.VMEM)],
        out_specs=pl.BlockSpec(memory_space=pltpu.VMEM),
        scratch_shapes=[pltpu.SemaphoreType.DMA((n,)), pltpu.SemaphoreType.DMA((n,))],
        compiler_params=pltpu.CompilerParams(collective_id=cid, has_side_effects=True),
    )(x)


def pair_gather_kernel(n, sizes, x_ref, out_ref, local_sem, send1, recv1, send2, recv2, send3, recv3):
    me = flat_index(sizes)
    chips = n // 2
    chip = me // 2
    core = lax.rem(me, 2)
    partner = me + 1 - 2 * core
    enter_all(n, sizes, me)

    local = pltpu.make_async_copy(x_ref, out_ref.at[me], local_sem)
    local.start()
    first = pltpu.make_async_remote_copy(
        src_ref=x_ref, dst_ref=out_ref.at[me], send_sem=send1, recv_sem=recv1,
        device_id=device_of(partner, sizes), device_id_type=MESH,
    )
    first.start()
    local.wait()
    first.wait_send()
    pltpu.make_async_remote_copy(
        src_ref=x_ref, dst_ref=out_ref.at[partner], send_sem=send1, recv_sem=recv1,
        device_id=device_of(partner, sizes), device_id_type=MESH,
    ).wait_recv()

    def pair(c):
        return out_ref.at[pl.ds(2 * c, 2)]

    def target(k):
        return lax.rem(chip + 2 * k - 1 + core, chips)

    def source(k):
        return lax.rem(chip + chips - (2 * k - 1 + core), chips)

    count = (chips - core) // 2

    def send_out(k, carry):
        other = target(k)
        pltpu.make_async_remote_copy(
            src_ref=pair(chip), dst_ref=pair(chip), send_sem=send2.at[other], recv_sem=recv2.at[chip],
            device_id=device_of(2 * other + core, sizes), device_id_type=MESH,
        ).start()
        return carry

    lax.fori_loop(1, count + 1, send_out, 0)

    def take_in(k, carry):
        other = source(k)
        pltpu.make_async_remote_copy(
            src_ref=pair(other), dst_ref=pair(other), send_sem=send2.at[other], recv_sem=recv2.at[other],
            device_id=device_of(2 * other + core, sizes), device_id_type=MESH,
        ).wait_recv()
        pltpu.make_async_remote_copy(
            src_ref=pair(other), dst_ref=pair(other), send_sem=send3.at[other], recv_sem=recv3.at[other],
            device_id=device_of(partner, sizes), device_id_type=MESH,
        ).start()
        return carry

    lax.fori_loop(1, count + 1, take_in, 0)

    def sent_out(k, carry):
        other = target(k)
        pltpu.make_async_remote_copy(
            src_ref=pair(chip), dst_ref=pair(chip), send_sem=send2.at[other], recv_sem=recv2.at[chip],
            device_id=device_of(2 * other + core, sizes), device_id_type=MESH,
        ).wait_send()
        return carry

    lax.fori_loop(1, count + 1, sent_out, 0)

    def forwarded(k, carry):
        other = source(k)
        pltpu.make_async_remote_copy(
            src_ref=pair(other), dst_ref=pair(other), send_sem=send3.at[other], recv_sem=recv3.at[other],
            device_id=device_of(partner, sizes), device_id_type=MESH,
        ).wait_send()
        return carry

    lax.fori_loop(1, count + 1, forwarded, 0)

    other_count = (chips - (1 - core)) // 2

    def partner_source(k):
        return lax.rem(chip + chips - (2 * k - 1 + (1 - core)), chips)

    def from_partner(k, carry):
        other = partner_source(k)
        pltpu.make_async_remote_copy(
            src_ref=pair(other), dst_ref=pair(other), send_sem=send3.at[other], recv_sem=recv3.at[other],
            device_id=device_of(partner, sizes), device_id_type=MESH,
        ).wait_recv()
        return carry

    lax.fori_loop(1, other_count + 1, from_partner, 0)


def pair_gather(x, sizes, cid):
    n = math.prod(sizes)
    chips = n // 2
    dma = pltpu.SemaphoreType.DMA
    return pl.pallas_call(
        functools.partial(pair_gather_kernel, n, sizes),
        out_shape=jax.ShapeDtypeStruct((n,) + x.shape, x.dtype),
        in_specs=[pl.BlockSpec(memory_space=pltpu.VMEM)],
        out_specs=pl.BlockSpec(memory_space=pltpu.VMEM),
        scratch_shapes=[dma(()), dma(()), dma(()), dma((chips,)), dma((chips,)), dma((chips,)), dma((chips,))],
        compiler_params=pltpu.CompilerParams(collective_id=cid, has_side_effects=True),
    )(x)


def halving_orders(n, parts):
    bits = n.bit_length() - 1
    middle = list(range(1, bits - 1))
    orders = []
    for p in range(parts):
        shift = p % len(middle) if middle else 0
        orders.append(tuple([0] + middle[shift:] + middle[:shift] + [bits - 1]))
    return tuple(orders)


def halving_kernel(n, sizes, orders, cols, x_hbm, out_ref, work, *rest):
    steps = len(orders[0])
    parts = len(orders)
    recvs = rest[:steps]
    local_sem, send_sems, recv_sems = rest[steps:]
    me = flat_index(sizes)

    def partner_of(bit):
        mine = lax.rem(me // (2**bit), 2)
        return mine, me + (1 - 2 * mine) * (2**bit)

    barrier = pltpu.get_barrier_semaphore()
    for bit in range(steps):
        _, other = partner_of(bit)
        pl.semaphore_signal(barrier, inc=1, device_id=device_of(other, sizes), device_id_type=MESH)
    pl.semaphore_wait(barrier, steps)

    half = n // 2
    first = []
    for p in range(parts):
        order = orders[p]
        mine, other = partner_of(order[0])
        column = pl.ds(p * cols, cols)

        def owner(j, side, order=order):
            o = side * (2 ** order[0])
            for m, bit in enumerate(order[1:]):
                o = o + lax.rem(j // (2 ** (steps - 2 - m)), 2) * (2**bit)
            return o

        def issue(j, carry, p=p, owner=owner, mine=mine, other=other, column=column):
            pltpu.make_async_remote_copy(
                src_ref=x_hbm.at[owner(j, 1 - mine), :, column], dst_ref=recvs[0].at[p, j],
                send_sem=send_sems.at[p, 0], recv_sem=recv_sems.at[p, 0],
                device_id=device_of(other, sizes), device_id_type=MESH,
            ).start()
            pltpu.make_async_copy(x_hbm.at[owner(j, mine), :, column], work.at[p, j], local_sem.at[p]).start()
            return carry

        lax.fori_loop(0, half, issue, 0)
        first.append(other)
    for p in range(parts):
        whole = pltpu.make_async_remote_copy(
            src_ref=work.at[p, pl.ds(0, half)], dst_ref=recvs[0].at[p],
            send_sem=send_sems.at[p, 0], recv_sem=recv_sems.at[p, 0],
            device_id=device_of(first[p], sizes), device_id_type=MESH,
        )
        pltpu.make_async_copy(work.at[p, pl.ds(0, half)], work.at[p, pl.ds(0, half)], local_sem.at[p]).wait()
        whole.wait_recv()
        whole.wait_send()

        def accumulate0(i, carry, p=p):
            total = work[p, i].astype(jnp.float32) + recvs[0][p, i].astype(jnp.float32)
            work[p, i] = total.astype(work.dtype)
            return carry

        lax.fori_loop(0, half, accumulate0, 0)

    for step in range(1, steps):
        half = n >> (step + 1)
        copies = []
        for p in range(parts):
            mine, other = partner_of(orders[p][step])
            send = pltpu.make_async_remote_copy(
                src_ref=work.at[p, pl.ds((1 - mine) * half, half)], dst_ref=recvs[step].at[p],
                send_sem=send_sems.at[p, step], recv_sem=recv_sems.at[p, step],
                device_id=device_of(other, sizes), device_id_type=MESH,
            )
            send.start()
            copies.append((mine, send))
        for p in range(parts):
            mine, send = copies[p]
            send.wait_recv()
            send.wait_send()

            def accumulate(i, carry, p=p, mine=mine, half=half, step=step):
                total = work[p, mine * half + i].astype(jnp.float32) + recvs[step][p, i].astype(jnp.float32)
                work[p, i] = total.astype(work.dtype)
                return carry

            lax.fori_loop(0, half, accumulate, 0)
    for p in range(parts):
        out_ref[p] = work[p, 0]


def halving_scatter(x, sizes, parts, cid):
    n, rows, width = x.shape
    cols = width // parts
    orders = halving_orders(n, parts)
    steps = len(orders[0])
    dma = pltpu.SemaphoreType.DMA
    scratch = [pltpu.VMEM((parts, n // 2, rows, cols), x.dtype)]
    scratch += [pltpu.VMEM((parts, n >> (k + 1), rows, cols), x.dtype) for k in range(steps)]
    scratch += [dma((parts,)), dma((parts, steps)), dma((parts, steps))]
    return pl.pallas_call(
        functools.partial(halving_kernel, n, sizes, orders, cols),
        out_shape=jax.ShapeDtypeStruct((parts, rows, cols), x.dtype),
        in_specs=[pl.BlockSpec(memory_space=pl.ANY)],
        out_specs=pl.BlockSpec(memory_space=pltpu.VMEM),
        scratch_shapes=scratch,
        compiler_params=pltpu.CompilerParams(
            collective_id=cid, has_side_effects=True, vmem_limit_bytes=56 * 1024 * 1024
        ),
    )(x)


def contrastive(embed_b, gathered, partner_all, me):
    own_texts = embed_b.shape[0]
    all_texts = gathered.shape[0]
    chunk = min(all_texts, 1024)
    on_rows = (((1,), (1,)), ((), ()))

    def chunk_stats(c):
        rows_b = lax.dynamic_slice_in_dim(gathered, c * chunk, chunk)
        sim = lax.dot_general(rows_b, gathered, on_rows, preferred_element_type=jnp.float32) / logit_divisor
        column_ids = lax.broadcasted_iota(jnp.int32, sim.shape, 1)
        row_ids = lax.broadcasted_iota(jnp.int32, sim.shape, 0) + c * chunk
        masked = jnp.where(column_ids == row_ids, masked_value, sim)
        row_max = jnp.max(masked, -1, keepdims=True)
        log_sum = row_max + jnp.log(jnp.sum(jnp.exp(masked - row_max), -1, keepdims=True))
        wanted = lax.dynamic_slice_in_dim(partner_all, c * chunk, chunk)
        positive = jnp.sum(jnp.where(column_ids == wanted[:, None], sim, 0.0), -1)
        return log_sum[:, 0], positive

    if all_texts == chunk:
        log_sum_all, positive_all = chunk_stats(0)
    else:
        log_sum_all, positive_all = lax.map(chunk_stats, jnp.arange(all_texts // chunk))
        log_sum_all = log_sum_all.reshape(-1)
        positive_all = positive_all.reshape(-1)
    mean_loss = jnp.sum(log_sum_all - positive_all) / all_texts

    own_start = me * own_texts
    own_ids = lax.broadcasted_iota(jnp.int32, (own_texts,), 0) + own_start
    own_partner = lax.dynamic_slice_in_dim(partner_all, own_start, own_texts)
    own_log_sum = lax.dynamic_slice_in_dim(log_sum_all, own_start, own_texts)

    sim_rows = lax.dot_general(embed_b, gathered, on_rows, preferred_element_type=jnp.float32) / logit_divisor
    column_ids = lax.broadcasted_iota(jnp.int32, sim_rows.shape, 1)
    masked_rows = jnp.where(column_ids == own_ids[:, None], masked_value, sim_rows)
    grad_rows = (
        jnp.exp(masked_rows - own_log_sum[:, None]) - (column_ids == own_partner[:, None]).astype(jnp.float32)
    ).astype(jnp.bfloat16)

    sim_cols = lax.dot_general(gathered, embed_b, on_rows, preferred_element_type=jnp.float32) / logit_divisor
    row_ids = lax.broadcasted_iota(jnp.int32, sim_cols.shape, 0)
    masked_cols = jnp.where(row_ids == own_ids[None, :], masked_value, sim_cols)
    grad_cols = (
        jnp.exp(masked_cols - log_sum_all[:, None]) - (partner_all[:, None] == own_ids[None, :]).astype(jnp.float32)
    ).astype(jnp.bfloat16)

    on_tokens = (((0,), (0,)), ((), ()))
    embedding_gradient = (
        jnp.dot(grad_rows, gathered, preferred_element_type=jnp.float32)
        + lax.dot_general(grad_cols, gathered, on_tokens, preferred_element_type=jnp.float32)
    ) / logit_divisor
    return mean_loss, embedding_gradient


def shards(
    hidden_in,
    segments,
    partner,
    attn_weights,
    ffn_weights,
    vectors,
    attn_momentum,
    ffn_momentum,
    vector_momentum,
    attn_averaged,
    ffn_averaged,
    vector_averaged,
):
    sizes = tuple(lax.axis_size(name) for name in AXES)
    n_dev = math.prod(sizes)
    me = flat_index(sizes)
    vec_len = vectors.shape[0]
    own_texts_n = partner.shape[0]
    width = attn_weights.shape[0]
    attn_local_t = attn_weights.T.astype(jnp.bfloat16)
    digit = 64
    extra = jnp.concatenate(
        [
            vectors.astype(jnp.bfloat16),
            (partner // digit).astype(jnp.bfloat16),
            (partner % digit).astype(jnp.bfloat16),
        ]
    )
    extra = jnp.pad(extra, (0, width - extra.shape[0]))[None, :]
    attn_block = jnp.concatenate([attn_local_t, extra], 0)
    attn_gathered = pair_gather(attn_block, sizes, 0)
    local_cols = attn_local_t.shape[0]
    attn_full_t = attn_gathered[:, :local_cols, :].reshape(-1, width)
    extra_all = attn_gathered[:, local_cols, :]
    vector_f = extra_all[:, :vec_len].reshape(-1).astype(jnp.float32)
    partner_all = (
        extra_all[:, vec_len : vec_len + own_texts_n].astype(jnp.int32) * digit
        + extra_all[:, vec_len + own_texts_n : vec_len + 2 * own_texts_n].astype(jnp.int32)
    ).reshape(-1)
    ffn_local, attn_gathered = lax.optimization_barrier((ffn_weights.astype(jnp.bfloat16), attn_gathered))
    ffn_full = lax.all_gather(ffn_local, AXES, axis=1, tiled=True)
    hidden = ffn_full.shape[1] // 2
    query_bias = vector_f[0:width]
    value_bias = vector_f[width : 2 * width]
    output_bias = vector_f[2 * width : 3 * width]
    gain_first = vector_f[3 * width : 4 * width]
    shift_first = vector_f[4 * width : 5 * width]
    upper_bias = vector_f[5 * width : 5 * width + hidden]
    lower_bias = vector_f[5 * width + hidden : 6 * width + hidden]
    gain_second = vector_f[6 * width + hidden : 7 * width + hidden]
    shift_second = vector_f[7 * width + hidden : 8 * width + hidden]
    w_qkv_t = attn_full_t[: 3 * width]
    w_output_t = attn_full_t[3 * width :]
    w_upper = ffn_full[:, :hidden]
    w_lower = ffn_full[:, hidden:]
    rows_dev, seq_len = segments.shape
    tokens_n = rows_dev * seq_len
    on_rows = (((1,), (1,)), ((), ()))
    on_tokens = (((0,), (0,)), ((), ()))
    qkv_bias = jnp.concatenate([query_bias, jnp.zeros_like(query_bias), value_bias])
    qkv_rows = (lax.dot_general(hidden_in, w_qkv_t, (((1,), (1,)), ((), ())), preferred_element_type=jnp.float32) + qkv_bias).astype(
        jnp.bfloat16
    )
    heads = qkv_rows.reshape(rows_dev, seq_len, 3, HEADS, HD)
    query_rows = heads[:, :, 0]
    key_rows = heads[:, :, 1]
    value_rows = heads[:, :, 2]
    mixed, log_norm = attend_rows(query_rows, key_rows, value_rows, segments)
    mixed_flat = mixed.reshape(tokens_n, width)
    first_sum = (
        hidden_in.astype(jnp.float32)
        + lax.dot_general(mixed_flat, w_output_t, (((1,), (1,)), ((), ())), preferred_element_type=jnp.float32)
        + output_bias
    )
    normed, normal_one, inverse_one = layer_norm_parts(first_sum, gain_first, shift_first)
    normed_r = bf16_round(normed)
    normed_b = normed_r.astype(jnp.bfloat16)
    upper = jnp.dot(normed_b, w_upper, preferred_element_type=jnp.float32) + upper_bias
    active_b = jax.nn.gelu(upper, approximate=False).astype(jnp.bfloat16)
    second_sum = (
        normed_r
        + lax.dot_general(active_b, w_lower, on_rows, preferred_element_type=jnp.float32)
        + lower_bias
    )
    result, normal_two, inverse_two = layer_norm_parts(second_sum, gain_second, shift_second)
    text_ids = jnp.arange(SEGS, dtype=jnp.int32)
    one_hot = (segments[:, None, :] == text_ids[None, :, None]).astype(jnp.float32)
    counts = jnp.sum(one_hot, -1, keepdims=True)
    pooled = (
        jnp.einsum(
            "rts,rsd->rtd",
            one_hot,
            result.reshape(rows_dev, seq_len, width),
            precision=lax.Precision.HIGHEST,
        )
        / counts
    ).reshape(-1, width)
    inv_norm = lax.rsqrt(jnp.sum(pooled * pooled, -1, keepdims=True) + pool_epsilon)
    embed_b = (pooled * inv_norm).astype(jnp.bfloat16)
    gathered_embeddings = pair_gather(embed_b, sizes, 2).reshape(-1, width)
    mean_loss, embedding_gradient = contrastive(embed_b, gathered_embeddings, partner_all, me)
    grad_pooled = inv_norm * embedding_gradient - pooled * (
        inv_norm * inv_norm * inv_norm
    ) * jnp.sum(embedding_gradient * pooled, -1, keepdims=True)
    derivative_output = jnp.einsum(
        "rts,rtd->rsd",
        one_hot,
        grad_pooled.reshape(rows_dev, SEGS, width) / counts,
        precision=lax.Precision.HIGHEST,
    ).reshape(tokens_n, width)
    grad_second, gain_two_grad, shift_two_grad = layer_norm_back(
        derivative_output, normal_two, inverse_two, gain_second
    )
    lower_bias_grad = jnp.sum(grad_second, 0)
    lower_grad_b = grad_second.astype(jnp.bfloat16)
    lower_w_grad_t = lax.dot_general(
        active_b, lower_grad_b, on_tokens, preferred_element_type=jnp.float32
    )
    grad_active = jnp.dot(lower_grad_b, w_lower, preferred_element_type=jnp.float32)
    cumulative = 0.5 * (1.0 + lax.erf(upper / math.sqrt(2.0)))
    density = jnp.exp(-0.5 * upper * upper) / math.sqrt(2.0 * math.pi)
    grad_upper = grad_active * (cumulative + upper * density)
    upper_bias_grad = jnp.sum(grad_upper, 0)
    upper_grad_b = grad_upper.astype(jnp.bfloat16)
    upper_w_grad_t = lax.dot_general(
        upper_grad_b, normed_b, on_tokens, preferred_element_type=jnp.float32
    )
    grad_normed = (
        lax.dot_general(upper_grad_b, w_upper, on_rows, preferred_element_type=jnp.float32)
        + grad_second
    )
    grad_first, gain_one_grad, shift_one_grad = layer_norm_back(
        grad_normed, normal_one, inverse_one, gain_first
    )
    output_bias_grad = jnp.sum(grad_first, 0)
    first_grad_b = grad_first.astype(jnp.bfloat16)
    output_w_grad_t = lax.dot_general(
        first_grad_b, mixed_flat, on_tokens, preferred_element_type=jnp.float32
    )
    grad_mixed = jnp.dot(
        first_grad_b, w_output_t, preferred_element_type=jnp.float32
    ).astype(jnp.bfloat16)
    grad_mixed = grad_mixed.reshape(rows_dev, seq_len, HEADS, HD)
    norm_tokens = jnp.swapaxes(log_norm, 1, 2).reshape(tokens_n, HEADS)
    qkv_grad = jnp.concatenate(
        attention_back(qkv_rows, grad_mixed.reshape(tokens_n, width), norm_tokens, segments, HEADS, HD), 1
    ).astype(jnp.float32)
    qkv_grad_f = bf16_round(qkv_grad)
    qkv_grad_b = qkv_grad_f.astype(jnp.bfloat16)
    query_bias_grad = jnp.sum(qkv_grad_f[:, :width], 0)
    value_bias_grad = jnp.sum(qkv_grad_f[:, 2 * width :], 0)
    qkv_w_grad_t = lax.dot_general(
        qkv_grad_b, hidden_in, on_tokens, preferred_element_type=jnp.float32
    )
    input_grad = (
        jnp.dot(qkv_grad_b, w_qkv_t, preferred_element_type=jnp.float32) + grad_first
    )
    vector_grad = jnp.concatenate(
        [
            query_bias_grad,
            value_bias_grad,
            output_bias_grad,
            gain_one_grad,
            shift_one_grad,
            upper_bias_grad,
            lower_bias_grad,
            gain_two_grad,
            shift_two_grad,
        ]
    )
    vector_slots = small_scatter(vector_grad.reshape(n_dev, 1, -1), sizes, 1)
    vector_reduced = jnp.sum(vector_slots[:, 0, :], 0)
    attn_cols = (qkv_w_grad_t.shape[0] + output_w_grad_t.shape[0]) // n_dev
    ffn_cols = (upper_w_grad_t.shape[0] + lower_w_grad_t.shape[0]) // n_dev
    attn_blocks = jnp.concatenate(
        [qkv_w_grad_t.reshape(-1, attn_cols, width), output_w_grad_t.reshape(-1, attn_cols, width)], 0
    )
    ffn_blocks = jnp.concatenate(
        [upper_w_grad_t.reshape(-1, ffn_cols, width), lower_w_grad_t.reshape(-1, ffn_cols, width)], 0
    )
    joined = jnp.concatenate([attn_blocks, ffn_blocks], 1).astype(GRAD_SEND)
    parts = 3
    mine_parts = halving_scatter(joined, sizes, parts, 3)
    joined_reduced = jnp.transpose(mine_parts, (1, 0, 2)).reshape(-1, width).astype(jnp.float32)
    attn_reduced = joined_reduced[:attn_cols].T
    ffn_reduced = joined_reduced[attn_cols:].T
    attn_new, attn_moment, attn_average = apply_update(
        attn_weights, attn_reduced, attn_momentum, attn_averaged, decay_rate
    )
    ffn_new, ffn_moment, ffn_average = apply_update(
        ffn_weights, ffn_reduced, ffn_momentum, ffn_averaged, decay_rate
    )
    vector_new, vector_moment, vector_average = apply_update(
        vectors, vector_reduced, vector_momentum, vector_averaged, 0.0
    )
    return (
        mean_loss,
        input_grad,
        attn_reduced,
        ffn_reduced,
        vector_reduced,
        attn_new,
        ffn_new,
        vector_new,
        attn_moment,
        ffn_moment,
        vector_moment,
        attn_average,
        ffn_average,
        vector_average,
    )


def solution(mesh):
    in_specs = (
        P(("dp", "rep"), None),
        P(("dp", "rep"), None),
        P(("dp", "rep")),
        P(None, ("dp", "rep")),
        P(None, ("dp", "rep")),
        P(("dp", "rep")),
        P(None, ("dp", "rep")),
        P(None, ("dp", "rep")),
        P(("dp", "rep")),
        P(None, ("dp", "rep")),
        P(None, ("dp", "rep")),
        P(("dp", "rep")),
    )
    out_specs = (
        P(),
        P(("dp", "rep"), None),
        P(None, ("dp", "rep")),
        P(None, ("dp", "rep")),
        P(("dp", "rep")),
        P(None, ("dp", "rep")),
        P(None, ("dp", "rep")),
        P(("dp", "rep")),
        P(None, ("dp", "rep")),
        P(None, ("dp", "rep")),
        P(("dp", "rep")),
        P(None, ("dp", "rep")),
        P(None, ("dp", "rep")),
        P(("dp", "rep")),
    )
    return jax.shard_map(shards, mesh=mesh, in_specs=in_specs, out_specs=out_specs, check_vma=False)
```

```python
import functools
import math

import jax
import jax.numpy as jnp
from jax import lax
from jax.experimental import pallas as pl
from jax.experimental.pallas import tpu as pltpu
from jax.sharding import PartitionSpec as P

MESH = pl.DeviceIdType.MESH
GRAD_SEND = jnp.bfloat16
AXES = ("dp", "rep")

HEADS = 12
HD = 64
SEGS = 16


ln_epsilon = 1e-12
pool_epsilon = 1e-06
logit_divisor = 0.025
learn_rate = 0.01
momentum_rate = 0.9
decay_rate = 0.01
average_rate = 0.75
masked_value = -1e30


def layer_norm_parts(values, gain, shift):
    per_line_average = jnp.mean(values, -1, keepdims=True)
    centred = values - per_line_average
    inverse = lax.rsqrt(jnp.mean(centred * centred, -1, keepdims=True) + ln_epsilon)
    normal_part = centred * inverse
    return (normal_part * gain + shift, normal_part, inverse)


def layer_norm_back(grad_out, normal_part, inverse, gain):
    scaled = grad_out * gain
    grad_in = inverse * (
        scaled
        - jnp.mean(scaled, -1, keepdims=True)
        - normal_part * jnp.mean(scaled * normal_part, -1, keepdims=True)
    )
    return (grad_in, jnp.sum(grad_out * normal_part, 0), jnp.sum(grad_out, 0))


def row_scores(query_one, key_one, segment_one, scale):
    scores = (
        jnp.einsum("qhd,khd->hqk", query_one, key_one, preferred_element_type=jnp.float32) * scale
    )
    same_text = segment_one[:, None] == segment_one[None, :]
    return jnp.where(same_text[None], scores, masked_value)


def attend_rows(query_rows, key_rows, value_rows, row_segments):
    scale = 1.0 / math.sqrt(query_rows.shape[-1])

    def one_row(row_args):
        query_one, key_one, value_one, segment_one = row_args
        scores = row_scores(query_one, key_one, segment_one, scale)
        row_max = jnp.max(scores, -1, keepdims=True)
        exp_scores = jnp.exp(scores - row_max)
        sums = jnp.sum(exp_scores, -1, keepdims=True)
        attn_probs = exp_scores / sums
        mixed = jnp.einsum(
            "hqk,khd->qhd",
            attn_probs.astype(jnp.bfloat16),
            value_one,
            preferred_element_type=jnp.float32,
        )
        return (mixed.astype(jnp.bfloat16), (row_max + jnp.log(sums))[..., 0])

    return lax.map(one_row, (query_rows, key_rows, value_rows, row_segments))


def attend_back(query_rows, key_rows, value_rows, row_segments, log_norm, grad_mixed):
    scale = 1.0 / math.sqrt(query_rows.shape[-1])

    def one_row(row_args):
        query_one, key_one, value_one, segment_one, norm_one, grad_one = row_args
        scores = row_scores(query_one, key_one, segment_one, scale)
        attn_probs = jnp.exp(scores - norm_one[..., None])
        grad_value = jnp.einsum(
            "hqk,qhd->khd",
            attn_probs.astype(jnp.bfloat16),
            grad_one,
            preferred_element_type=jnp.float32,
        )
        grad_probs = jnp.einsum(
            "qhd,khd->hqk", grad_one, value_one, preferred_element_type=jnp.float32
        )
        inner = jnp.sum(attn_probs * grad_probs, -1, keepdims=True)
        grad_scores = (attn_probs * (grad_probs - inner)).astype(jnp.bfloat16)
        grad_query = (
            jnp.einsum("hqk,khd->qhd", grad_scores, key_one, preferred_element_type=jnp.float32)
            * scale
        )
        grad_key = (
            jnp.einsum("hqk,qhd->khd", grad_scores, query_one, preferred_element_type=jnp.float32)
            * scale
        )
        return jnp.concatenate([grad_query, grad_key, grad_value], axis=1)

    return lax.map(one_row, (query_rows, key_rows, value_rows, row_segments, log_norm, grad_mixed))


def attention_back_kernel(scale, q_ref, k_ref, v_ref, g_ref, norm_ref, seg_col_ref, seg_row_ref, dq_ref, dk_ref, dv_ref):
    pair = pl.program_id(1)
    width = q_ref.shape[1]
    half = width // 2
    lane = lax.broadcasted_iota(jnp.int32, (1, width), 1)
    same = seg_col_ref[...] == seg_row_ref[0]
    norms = norm_ref[...]
    norm_lane = lax.broadcasted_iota(jnp.int32, norms.shape, 1)
    q = q_ref[...]
    k = k_ref[...]
    v = v_ref[...]
    g = g_ref[...]
    zero_b = jnp.zeros_like(q)
    on_last = (((1,), (1,)), ((), ()))
    on_first = (((0,), (0,)), ((), ()))
    dq = jnp.zeros(q.shape, jnp.float32)
    dk = jnp.zeros(q.shape, jnp.float32)
    dv = jnp.zeros(q.shape, jnp.float32)
    for head in range(2):
        mine = (lane >= head * half) & (lane < (head + 1) * half)
        q_h = jnp.where(mine, q, zero_b)
        g_h = jnp.where(mine, g, zero_b)
        norm_h = jnp.sum(jnp.where(norm_lane == 2 * pair + head, norms, 0.0), 1, keepdims=True)
        scores = lax.dot_general(q_h, k, on_last, preferred_element_type=jnp.float32) * scale
        scores = jnp.where(same, scores, masked_value)
        probs = jnp.exp(scores - norm_h)
        grad_v = lax.dot_general(probs.astype(jnp.bfloat16), g, on_first, preferred_element_type=jnp.float32)
        grad_p = lax.dot_general(g_h, v, on_last, preferred_element_type=jnp.float32)
        inner = jnp.sum(probs * grad_p, -1, keepdims=True)
        grad_s = (probs * (grad_p - inner)).astype(jnp.bfloat16)
        grad_q = jnp.dot(grad_s, k, preferred_element_type=jnp.float32) * scale
        grad_k = lax.dot_general(grad_s, q, on_first, preferred_element_type=jnp.float32) * scale
        dq = jnp.where(mine, grad_q, dq)
        dk = jnp.where(mine, grad_k, dk)
        dv = jnp.where(mine, grad_v, dv)
    dq_ref[...] = dq.astype(dq_ref.dtype)
    dk_ref[...] = dk.astype(dk_ref.dtype)
    dv_ref[...] = dv.astype(dv_ref.dtype)


def attention_back(qkv_rows, grad_mixed_flat, norm_tokens, segments, heads, head_dim):
    tokens, three_width = qkv_rows.shape
    width = three_width // 3
    rows, seq_len = segments.shape
    pair_width = 2 * head_dim
    pairs = heads // 2
    seg_col = segments.reshape(tokens, 1)
    seg_row = segments.reshape(rows, 1, seq_len)
    scale = 1.0 / math.sqrt(head_dim)
    out = jax.ShapeDtypeStruct((tokens, width), jnp.bfloat16)
    return pl.pallas_call(
        functools.partial(attention_back_kernel, scale),
        grid=(rows, pairs),
        in_specs=[
            pl.BlockSpec((seq_len, pair_width), lambda r, p: (r, p)),
            pl.BlockSpec((seq_len, pair_width), lambda r, p: (r, pairs + p)),
            pl.BlockSpec((seq_len, pair_width), lambda r, p: (r, 2 * pairs + p)),
            pl.BlockSpec((seq_len, pair_width), lambda r, p: (r, p)),
            pl.BlockSpec((seq_len, heads), lambda r, p: (r, 0)),
            pl.BlockSpec((seq_len, 1), lambda r, p: (r, 0)),
            pl.BlockSpec((1, 1, seq_len), lambda r, p: (r, 0, 0)),
        ],
        out_specs=[pl.BlockSpec((seq_len, pair_width), lambda r, p: (r, p))] * 3,
        out_shape=[out, out, out],
        compiler_params=pltpu.CompilerParams(vmem_limit_bytes=48 * 1024 * 1024),
        cost_estimate=pl.CostEstimate(
            flops=10 * rows * heads * seq_len * seq_len * pair_width,
            transcendentals=rows * heads * seq_len * seq_len,
            bytes_accessed=tokens * (three_width + 4 * width) * 2,
        ),
    )(qkv_rows, qkv_rows, qkv_rows, grad_mixed_flat, norm_tokens, seg_col, seg_row)


def apply_update(weight, grad, moment, average, decay):
    step_grad = grad + decay * weight
    new_moment = momentum_rate * moment + step_grad
    new_weight = weight - learn_rate * (step_grad + momentum_rate * new_moment)
    fresh_running_mean = average_rate * average + (1.0 - average_rate) * new_weight
    return (new_weight, new_moment, fresh_running_mean)


def bf16_round(values):
    return lax.reduce_precision(values, exponent_bits=8, mantissa_bits=7)


def flat_index(sizes):
    idx = 0
    for name, size in zip(AXES, sizes):
        idx = idx * size + lax.axis_index(name)
    return idx


def device_of(flat, sizes):
    coords = []
    for size in reversed(sizes):
        coords.append(lax.rem(flat, size))
        flat = flat // size
    return tuple(reversed(coords))


def enter_all(n, sizes, me):
    barrier = pltpu.get_barrier_semaphore()

    def greet(k, carry):
        peer = lax.rem(me + k, n)
        pl.semaphore_signal(barrier, inc=1, device_id=device_of(peer, sizes), device_id_type=MESH)
        return carry

    lax.fori_loop(1, n, greet, 0)
    pl.semaphore_wait(barrier, n - 1)


def gather_kernel(n, sizes, x_ref, out_ref, send_sem, recv_sem):
    me = flat_index(sizes)
    enter_all(n, sizes, me)

    def send(k, carry):
        peer = lax.rem(me + k, n)
        pltpu.make_async_remote_copy(
            src_ref=x_ref, dst_ref=out_ref.at[me], send_sem=send_sem.at[k], recv_sem=recv_sem.at[me],
            device_id=device_of(peer, sizes), device_id_type=MESH,
        ).start()
        return carry

    lax.fori_loop(1, n, send, 0)
    out_ref[me] = x_ref[...]

    def finish(k, carry):
        peer = lax.rem(me + k, n)
        src = lax.rem(me + n - k, n)
        pltpu.make_async_remote_copy(
            src_ref=x_ref, dst_ref=out_ref.at[me], send_sem=send_sem.at[k], recv_sem=recv_sem.at[me],
            device_id=device_of(peer, sizes), device_id_type=MESH,
        ).wait_send()
        pltpu.make_async_remote_copy(
            src_ref=x_ref, dst_ref=out_ref.at[src], send_sem=send_sem.at[k], recv_sem=recv_sem.at[src],
            device_id=device_of(src, sizes), device_id_type=MESH,
        ).wait_recv()
        return carry

    lax.fori_loop(1, n, finish, 0)


def small_gather(x, sizes, cid):
    n = math.prod(sizes)
    return pl.pallas_call(
        functools.partial(gather_kernel, n, sizes),
        out_shape=jax.ShapeDtypeStruct((n,) + x.shape, x.dtype),
        in_specs=[pl.BlockSpec(memory_space=pltpu.VMEM)],
        out_specs=pl.BlockSpec(memory_space=pltpu.VMEM),
        scratch_shapes=[pltpu.SemaphoreType.DMA((n,)), pltpu.SemaphoreType.DMA((n,))],
        compiler_params=pltpu.CompilerParams(collective_id=cid, has_side_effects=True),
    )(x)


def scatter_kernel(n, sizes, x_ref, out_ref, send_sem, recv_sem):
    me = flat_index(sizes)
    enter_all(n, sizes, me)

    def send(k, carry):
        peer = lax.rem(me + k, n)
        pltpu.make_async_remote_copy(
            src_ref=x_ref.at[peer], dst_ref=out_ref.at[me], send_sem=send_sem.at[k], recv_sem=recv_sem.at[me],
            device_id=device_of(peer, sizes), device_id_type=MESH,
        ).start()
        return carry

    lax.fori_loop(1, n, send, 0)
    out_ref[me] = x_ref[me]

    def finish(k, carry):
        peer = lax.rem(me + k, n)
        src = lax.rem(me + n - k, n)
        pltpu.make_async_remote_copy(
            src_ref=x_ref.at[peer], dst_ref=out_ref.at[me], send_sem=send_sem.at[k], recv_sem=recv_sem.at[me],
            device_id=device_of(peer, sizes), device_id_type=MESH,
        ).wait_send()
        pltpu.make_async_remote_copy(
            src_ref=x_ref.at[src], dst_ref=out_ref.at[src], send_sem=send_sem.at[k], recv_sem=recv_sem.at[src],
            device_id=device_of(src, sizes), device_id_type=MESH,
        ).wait_recv()
        return carry

    lax.fori_loop(1, n, finish, 0)


def small_scatter(x, sizes, cid):
    n = math.prod(sizes)
    return pl.pallas_call(
        functools.partial(scatter_kernel, n, sizes),
        out_shape=jax.ShapeDtypeStruct(x.shape, x.dtype),
        in_specs=[pl.BlockSpec(memory_space=pltpu.VMEM)],
        out_specs=pl.BlockSpec(memory_space=pltpu.VMEM),
        scratch_shapes=[pltpu.SemaphoreType.DMA((n,)), pltpu.SemaphoreType.DMA((n,))],
        compiler_params=pltpu.CompilerParams(collective_id=cid, has_side_effects=True),
    )(x)


def pair_gather_kernel(n, sizes, x_ref, out_ref, local_sem, send1, recv1, send2, recv2, send3, recv3):
    me = flat_index(sizes)
    chips = n // 2
    chip = me // 2
    core = lax.rem(me, 2)
    partner = me + 1 - 2 * core
    enter_all(n, sizes, me)

    local = pltpu.make_async_copy(x_ref, out_ref.at[me], local_sem)
    local.start()
    first = pltpu.make_async_remote_copy(
        src_ref=x_ref, dst_ref=out_ref.at[me], send_sem=send1, recv_sem=recv1,
        device_id=device_of(partner, sizes), device_id_type=MESH,
    )
    first.start()
    local.wait()
    first.wait_send()
    pltpu.make_async_remote_copy(
        src_ref=x_ref, dst_ref=out_ref.at[partner], send_sem=send1, recv_sem=recv1,
        device_id=device_of(partner, sizes), device_id_type=MESH,
    ).wait_recv()

    def pair(c):
        return out_ref.at[pl.ds(2 * c, 2)]

    def target(k):
        return lax.rem(chip + 2 * k - 1 + core, chips)

    def source(k):
        return lax.rem(chip + chips - (2 * k - 1 + core), chips)

    count = (chips - core) // 2

    def send_out(k, carry):
        other = target(k)
        pltpu.make_async_remote_copy(
            src_ref=pair(chip), dst_ref=pair(chip), send_sem=send2.at[other], recv_sem=recv2.at[chip],
            device_id=device_of(2 * other + core, sizes), device_id_type=MESH,
        ).start()
        return carry

    lax.fori_loop(1, count + 1, send_out, 0)

    def take_in(k, carry):
        other = source(k)
        pltpu.make_async_remote_copy(
            src_ref=pair(other), dst_ref=pair(other), send_sem=send2.at[other], recv_sem=recv2.at[other],
            device_id=device_of(2 * other + core, sizes), device_id_type=MESH,
        ).wait_recv()
        pltpu.make_async_remote_copy(
            src_ref=pair(other), dst_ref=pair(other), send_sem=send3.at[other], recv_sem=recv3.at[other],
            device_id=device_of(partner, sizes), device_id_type=MESH,
        ).start()
        return carry

    lax.fori_loop(1, count + 1, take_in, 0)

    def sent_out(k, carry):
        other = target(k)
        pltpu.make_async_remote_copy(
            src_ref=pair(chip), dst_ref=pair(chip), send_sem=send2.at[other], recv_sem=recv2.at[chip],
            device_id=device_of(2 * other + core, sizes), device_id_type=MESH,
        ).wait_send()
        return carry

    lax.fori_loop(1, count + 1, sent_out, 0)

    def forwarded(k, carry):
        other = source(k)
        pltpu.make_async_remote_copy(
            src_ref=pair(other), dst_ref=pair(other), send_sem=send3.at[other], recv_sem=recv3.at[other],
            device_id=device_of(partner, sizes), device_id_type=MESH,
        ).wait_send()
        return carry

    lax.fori_loop(1, count + 1, forwarded, 0)

    other_count = (chips - (1 - core)) // 2

    def partner_source(k):
        return lax.rem(chip + chips - (2 * k - 1 + (1 - core)), chips)

    def from_partner(k, carry):
        other = partner_source(k)
        pltpu.make_async_remote_copy(
            src_ref=pair(other), dst_ref=pair(other), send_sem=send3.at[other], recv_sem=recv3.at[other],
            device_id=device_of(partner, sizes), device_id_type=MESH,
        ).wait_recv()
        return carry

    lax.fori_loop(1, other_count + 1, from_partner, 0)


def pair_gather(x, sizes, cid):
    n = math.prod(sizes)
    chips = n // 2
    dma = pltpu.SemaphoreType.DMA
    return pl.pallas_call(
        functools.partial(pair_gather_kernel, n, sizes),
        out_shape=jax.ShapeDtypeStruct((n,) + x.shape, x.dtype),
        in_specs=[pl.BlockSpec(memory_space=pltpu.VMEM)],
        out_specs=pl.BlockSpec(memory_space=pltpu.VMEM),
        scratch_shapes=[dma(()), dma(()), dma(()), dma((chips,)), dma((chips,)), dma((chips,)), dma((chips,))],
        compiler_params=pltpu.CompilerParams(collective_id=cid, has_side_effects=True),
    )(x)


def halving_orders(n, parts):
    bits = n.bit_length() - 1
    middle = list(range(1, bits - 1))
    orders = []
    for p in range(parts):
        shift = p % len(middle) if middle else 0
        orders.append(tuple([0] + middle[shift:] + middle[:shift] + [bits - 1]))
    return tuple(orders)


def halving_kernel(n, sizes, orders, cols, tile, x_hbm, vec_ref, dq_ref, w_ref, res_ref,
                   out_ref, vec_out, grad_out, work, *rest):
    steps = len(orders[0])
    parts = len(orders)
    recvs = rest[:steps]
    local_sem, send_sems, recv_sems, vec_send, vec_recv = rest[steps:]
    me = flat_index(sizes)

    def partner_of(bit):
        mine = lax.rem(me // (2**bit), 2)
        return mine, me + (1 - 2 * mine) * (2**bit)

    enter_all(n, sizes, me)

    def vec_copy(k):
        peer = lax.rem(me + k, n)
        return pltpu.make_async_remote_copy(
            src_ref=vec_ref.at[peer], dst_ref=vec_out.at[me], send_sem=vec_send.at[k], recv_sem=vec_recv.at[me],
            device_id=device_of(peer, sizes), device_id_type=MESH,
        )

    def vec_start(k, carry):
        vec_copy(k).start()
        return carry

    lax.fori_loop(1, n, vec_start, 0)
    vec_out[me] = vec_ref[me]

    half = n // 2
    first = []
    for p in range(parts):
        order = orders[p]
        mine, other = partner_of(order[0])
        column = pl.ds(p * cols, cols)

        def owner(j, side, order=order):
            o = side * (2 ** order[0])
            for m, bit in enumerate(order[1:]):
                o = o + lax.rem(j // (2 ** (steps - 2 - m)), 2) * (2**bit)
            return o

        def issue(j, carry, p=p, owner=owner, mine=mine, other=other, column=column):
            pltpu.make_async_remote_copy(
                src_ref=x_hbm.at[owner(j, 1 - mine), :, column], dst_ref=recvs[0].at[p, j],
                send_sem=send_sems.at[p, 0], recv_sem=recv_sems.at[p, 0],
                device_id=device_of(other, sizes), device_id_type=MESH,
            ).start()
            pltpu.make_async_copy(x_hbm.at[owner(j, mine), :, column], work.at[p, j], local_sem.at[p]).start()
            return carry

        lax.fori_loop(0, half, issue, 0)
        first.append(other)
    for p in range(parts):
        whole = pltpu.make_async_remote_copy(
            src_ref=work.at[p, pl.ds(0, half)], dst_ref=recvs[0].at[p],
            send_sem=send_sems.at[p, 0], recv_sem=recv_sems.at[p, 0],
            device_id=device_of(first[p], sizes), device_id_type=MESH,
        )
        pltpu.make_async_copy(work.at[p, pl.ds(0, half)], work.at[p, pl.ds(0, half)], local_sem.at[p]).wait()
        whole.wait_recv()
        whole.wait_send()

        def accumulate0(i, carry, p=p):
            total = work[p, i].astype(jnp.float32) + recvs[0][p, i].astype(jnp.float32)
            work[p, i] = total.astype(work.dtype)
            return carry

        lax.fori_loop(0, half, accumulate0, 0)

    for step in range(1, steps):
        half = n >> (step + 1)
        copies = []
        for p in range(parts):
            mine, other = partner_of(orders[p][step])
            send = pltpu.make_async_remote_copy(
                src_ref=work.at[p, pl.ds((1 - mine) * half, half)], dst_ref=recvs[step].at[p],
                send_sem=send_sems.at[p, step], recv_sem=recv_sems.at[p, step],
                device_id=device_of(other, sizes), device_id_type=MESH,
            )
            send.start()
            copies.append((mine, send))
        if step == 1:
            def product(t, carry):
                rows = pl.ds(pl.multiple_of(t * tile, tile), tile)
                grad_out[rows, :] = (
                    jnp.dot(dq_ref[rows, :], w_ref[...], preferred_element_type=jnp.float32) + res_ref[rows, :]
                )
                return carry

            lax.fori_loop(0, grad_out.shape[0] // tile, product, 0)
        for p in range(parts):
            mine, send = copies[p]
            send.wait_recv()
            send.wait_send()

            def accumulate(i, carry, p=p, mine=mine, half=half, step=step):
                total = work[p, mine * half + i].astype(jnp.float32) + recvs[step][p, i].astype(jnp.float32)
                work[p, i] = total.astype(work.dtype)
                return carry

            lax.fori_loop(0, half, accumulate, 0)
    for p in range(parts):
        out_ref[p] = work[p, 0]

    def vec_finish(k, carry):
        vec_copy(k).wait_send()
        src = lax.rem(me + n - k, n)
        pltpu.make_async_remote_copy(
            src_ref=vec_ref.at[src], dst_ref=vec_out.at[src], send_sem=vec_send.at[k], recv_sem=vec_recv.at[src],
            device_id=device_of(src, sizes), device_id_type=MESH,
        ).wait_recv()
        return carry

    lax.fori_loop(1, n, vec_finish, 0)


def halving_scatter(x, vec, grad_b, weight_t, residual, sizes, parts, cid):
    n, rows, width = x.shape
    cols = width // parts
    orders = halving_orders(n, parts)
    steps = len(orders[0])
    tile = 128
    dma = pltpu.SemaphoreType.DMA
    vmem = pl.BlockSpec(memory_space=pltpu.VMEM)
    scratch = [pltpu.VMEM((parts, n // 2, rows, cols), x.dtype)]
    scratch += [pltpu.VMEM((parts, n >> (k + 1), rows, cols), x.dtype) for k in range(steps)]
    scratch += [dma((parts,)), dma((parts, steps)), dma((parts, steps)), dma((n,)), dma((n,))]
    return pl.pallas_call(
        functools.partial(halving_kernel, n, sizes, orders, cols, tile),
        out_shape=(
            jax.ShapeDtypeStruct((parts, rows, cols), x.dtype),
            jax.ShapeDtypeStruct(vec.shape, vec.dtype),
            jax.ShapeDtypeStruct(residual.shape, jnp.float32),
        ),
        in_specs=[pl.BlockSpec(memory_space=pl.ANY), vmem, vmem, vmem, vmem],
        out_specs=(vmem, vmem, vmem),
        scratch_shapes=scratch,
        compiler_params=pltpu.CompilerParams(
            collective_id=cid, has_side_effects=True, vmem_limit_bytes=60 * 1024 * 1024
        ),
    )(x, vec, grad_b, weight_t, residual)


def contrastive(embed_b, gathered, partner_all, me):
    own_texts = embed_b.shape[0]
    all_texts = gathered.shape[0]
    chunk = min(all_texts, 1024)
    on_rows = (((1,), (1,)), ((), ()))

    def chunk_stats(c):
        rows_b = lax.dynamic_slice_in_dim(gathered, c * chunk, chunk)
        sim = lax.dot_general(rows_b, gathered, on_rows, preferred_element_type=jnp.float32) / logit_divisor
        column_ids = lax.broadcasted_iota(jnp.int32, sim.shape, 1)
        row_ids = lax.broadcasted_iota(jnp.int32, sim.shape, 0) + c * chunk
        masked = jnp.where(column_ids == row_ids, masked_value, sim)
        row_max = jnp.max(masked, -1, keepdims=True)
        log_sum = row_max + jnp.log(jnp.sum(jnp.exp(masked - row_max), -1, keepdims=True))
        wanted = lax.dynamic_slice_in_dim(partner_all, c * chunk, chunk)
        positive = jnp.sum(jnp.where(column_ids == wanted[:, None], sim, 0.0), -1)
        return log_sum[:, 0], positive

    if all_texts == chunk:
        log_sum_all, positive_all = chunk_stats(0)
    else:
        log_sum_all, positive_all = lax.map(chunk_stats, jnp.arange(all_texts // chunk))
        log_sum_all = log_sum_all.reshape(-1)
        positive_all = positive_all.reshape(-1)
    mean_loss = jnp.sum(log_sum_all - positive_all) / all_texts

    own_start = me * own_texts
    own_ids = lax.broadcasted_iota(jnp.int32, (own_texts,), 0) + own_start
    own_partner = lax.dynamic_slice_in_dim(partner_all, own_start, own_texts)
    own_log_sum = lax.dynamic_slice_in_dim(log_sum_all, own_start, own_texts)

    sim_rows = lax.dot_general(embed_b, gathered, on_rows, preferred_element_type=jnp.float32) / logit_divisor
    column_ids = lax.broadcasted_iota(jnp.int32, sim_rows.shape, 1)
    masked_rows = jnp.where(column_ids == own_ids[:, None], masked_value, sim_rows)
    grad_rows = (
        jnp.exp(masked_rows - own_log_sum[:, None]) - (column_ids == own_partner[:, None]).astype(jnp.float32)
    ).astype(jnp.bfloat16)

    sim_cols = lax.dot_general(gathered, embed_b, on_rows, preferred_element_type=jnp.float32) / logit_divisor
    row_ids = lax.broadcasted_iota(jnp.int32, sim_cols.shape, 0)
    masked_cols = jnp.where(row_ids == own_ids[None, :], masked_value, sim_cols)
    grad_cols = (
        jnp.exp(masked_cols - log_sum_all[:, None]) - (partner_all[:, None] == own_ids[None, :]).astype(jnp.float32)
    ).astype(jnp.bfloat16)

    on_tokens = (((0,), (0,)), ((), ()))
    embedding_gradient = (
        jnp.dot(grad_rows, gathered, preferred_element_type=jnp.float32)
        + lax.dot_general(grad_cols, gathered, on_tokens, preferred_element_type=jnp.float32)
    ) / logit_divisor
    return mean_loss, embedding_gradient


def shards(
    hidden_in,
    segments,
    partner,
    attn_weights,
    ffn_weights,
    vectors,
    attn_momentum,
    ffn_momentum,
    vector_momentum,
    attn_averaged,
    ffn_averaged,
    vector_averaged,
):
    sizes = tuple(lax.axis_size(name) for name in AXES)
    n_dev = math.prod(sizes)
    me = flat_index(sizes)
    vec_len = vectors.shape[0]
    small = jnp.concatenate([vectors, partner.astype(jnp.float32)])[None, :]
    small_all = small_gather(small, sizes, 0)[:, 0, :]
    vector_f = bf16_round(small_all[:, :vec_len].reshape(-1))
    partner_all = small_all[:, vec_len:].reshape(-1).astype(jnp.int32)
    attn_full, ffn_full = (
        lax.all_gather(attn_weights.astype(jnp.bfloat16), AXES, axis=1, tiled=True),
        lax.all_gather(ffn_weights.astype(jnp.bfloat16), AXES, axis=1, tiled=True),
    )
    width = attn_full.shape[0]
    hidden = ffn_full.shape[1] // 2
    query_bias = vector_f[0:width]
    value_bias = vector_f[width : 2 * width]
    output_bias = vector_f[2 * width : 3 * width]
    gain_first = vector_f[3 * width : 4 * width]
    shift_first = vector_f[4 * width : 5 * width]
    upper_bias = vector_f[5 * width : 5 * width + hidden]
    lower_bias = vector_f[5 * width + hidden : 6 * width + hidden]
    gain_second = vector_f[6 * width + hidden : 7 * width + hidden]
    shift_second = vector_f[7 * width + hidden : 8 * width + hidden]
    w_qkv = attn_full[:, : 3 * width]
    w_output = attn_full[:, 3 * width :]
    w_upper = ffn_full[:, :hidden]
    w_lower = ffn_full[:, hidden:]
    rows_dev, seq_len = segments.shape
    tokens_n = rows_dev * seq_len
    on_rows = (((1,), (1,)), ((), ()))
    on_tokens = (((0,), (0,)), ((), ()))
    qkv_bias = jnp.concatenate([query_bias, jnp.zeros_like(query_bias), value_bias])
    qkv_rows = (jnp.dot(hidden_in, w_qkv, preferred_element_type=jnp.float32) + qkv_bias).astype(
        jnp.bfloat16
    )
    heads = qkv_rows.reshape(rows_dev, seq_len, 3, HEADS, HD)
    query_rows = heads[:, :, 0]
    key_rows = heads[:, :, 1]
    value_rows = heads[:, :, 2]
    mixed, log_norm = attend_rows(query_rows, key_rows, value_rows, segments)
    mixed_flat = mixed.reshape(tokens_n, width)
    first_sum = (
        hidden_in.astype(jnp.float32)
        + jnp.dot(mixed_flat, w_output, preferred_element_type=jnp.float32)
        + output_bias
    )
    normed, normal_one, inverse_one = layer_norm_parts(first_sum, gain_first, shift_first)
    normed_r = bf16_round(normed)
    normed_b = normed_r.astype(jnp.bfloat16)
    upper = jnp.dot(normed_b, w_upper, preferred_element_type=jnp.float32) + upper_bias
    active_b = jax.nn.gelu(upper, approximate=False).astype(jnp.bfloat16)
    second_sum = (
        normed_r
        + lax.dot_general(active_b, w_lower, on_rows, preferred_element_type=jnp.float32)
        + lower_bias
    )
    result, normal_two, inverse_two = layer_norm_parts(second_sum, gain_second, shift_second)
    text_ids = jnp.arange(SEGS, dtype=jnp.int32)
    one_hot = (segments[:, None, :] == text_ids[None, :, None]).astype(jnp.float32)
    counts = jnp.sum(one_hot, -1, keepdims=True)
    pooled = (
        jnp.einsum(
            "rts,rsd->rtd",
            one_hot,
            result.reshape(rows_dev, seq_len, width),
            precision=lax.Precision.HIGHEST,
        )
        / counts
    ).reshape(-1, width)
    inv_norm = lax.rsqrt(jnp.sum(pooled * pooled, -1, keepdims=True) + pool_epsilon)
    embed_b = (pooled * inv_norm).astype(jnp.bfloat16)
    gathered_embeddings = pair_gather(embed_b, sizes, 2).reshape(-1, width)
    mean_loss, embedding_gradient = contrastive(embed_b, gathered_embeddings, partner_all, me)
    grad_pooled = inv_norm * embedding_gradient - pooled * (
        inv_norm * inv_norm * inv_norm
    ) * jnp.sum(embedding_gradient * pooled, -1, keepdims=True)
    derivative_output = jnp.einsum(
        "rts,rtd->rsd",
        one_hot,
        grad_pooled.reshape(rows_dev, SEGS, width) / counts,
        precision=lax.Precision.HIGHEST,
    ).reshape(tokens_n, width)
    grad_second, gain_two_grad, shift_two_grad = layer_norm_back(
        derivative_output, normal_two, inverse_two, gain_second
    )
    lower_bias_grad = jnp.sum(grad_second, 0)
    lower_grad_b = grad_second.astype(jnp.bfloat16)
    lower_w_grad_t = lax.dot_general(
        active_b, lower_grad_b, on_tokens, preferred_element_type=jnp.float32
    )
    grad_active = jnp.dot(lower_grad_b, w_lower, preferred_element_type=jnp.float32)
    cumulative = 0.5 * (1.0 + lax.erf(upper / math.sqrt(2.0)))
    density = jnp.exp(-0.5 * upper * upper) / math.sqrt(2.0 * math.pi)
    grad_upper = grad_active * (cumulative + upper * density)
    upper_bias_grad = jnp.sum(grad_upper, 0)
    upper_grad_b = grad_upper.astype(jnp.bfloat16)
    upper_w_grad_t = lax.dot_general(
        upper_grad_b, normed_b, on_tokens, preferred_element_type=jnp.float32
    )
    grad_normed = (
        lax.dot_general(upper_grad_b, w_upper, on_rows, preferred_element_type=jnp.float32)
        + grad_second
    )
    grad_first, gain_one_grad, shift_one_grad = layer_norm_back(
        grad_normed, normal_one, inverse_one, gain_first
    )
    output_bias_grad = jnp.sum(grad_first, 0)
    first_grad_b = grad_first.astype(jnp.bfloat16)
    output_w_grad_t = lax.dot_general(
        first_grad_b, mixed_flat, on_tokens, preferred_element_type=jnp.float32
    )
    grad_mixed = lax.dot_general(
        first_grad_b, w_output, on_rows, preferred_element_type=jnp.float32
    ).astype(jnp.bfloat16)
    grad_mixed = grad_mixed.reshape(rows_dev, seq_len, HEADS, HD)
    norm_tokens = jnp.swapaxes(log_norm, 1, 2).reshape(tokens_n, HEADS)
    qkv_grad = jnp.concatenate(
        attention_back(qkv_rows, grad_mixed.reshape(tokens_n, width), norm_tokens, segments, HEADS, HD), 1
    ).astype(jnp.float32)
    qkv_grad_f = bf16_round(qkv_grad)
    qkv_grad_b = qkv_grad_f.astype(jnp.bfloat16)
    query_bias_grad = jnp.sum(qkv_grad_f[:, :width], 0)
    value_bias_grad = jnp.sum(qkv_grad_f[:, 2 * width :], 0)
    qkv_w_grad_t = lax.dot_general(
        qkv_grad_b, hidden_in, on_tokens, preferred_element_type=jnp.float32
    )
    vector_grad = jnp.concatenate(
        [
            query_bias_grad,
            value_bias_grad,
            output_bias_grad,
            gain_one_grad,
            shift_one_grad,
            upper_bias_grad,
            lower_bias_grad,
            gain_two_grad,
            shift_two_grad,
        ]
    )
    attn_cols = (qkv_w_grad_t.shape[0] + output_w_grad_t.shape[0]) // n_dev
    ffn_cols = (upper_w_grad_t.shape[0] + lower_w_grad_t.shape[0]) // n_dev
    attn_blocks = jnp.concatenate(
        [qkv_w_grad_t.reshape(-1, attn_cols, width), output_w_grad_t.reshape(-1, attn_cols, width)], 0
    )
    ffn_blocks = jnp.concatenate(
        [upper_w_grad_t.reshape(-1, ffn_cols, width), lower_w_grad_t.reshape(-1, ffn_cols, width)], 0
    )
    joined = jnp.concatenate([attn_blocks, ffn_blocks], 1).astype(GRAD_SEND)
    parts = 3
    mine_parts, vector_slots, input_grad = halving_scatter(
        joined, vector_grad.reshape(n_dev, 1, -1), qkv_grad_b, w_qkv.T, grad_first, sizes, parts, 3
    )
    vector_reduced = jnp.sum(vector_slots[:, 0, :], 0)
    joined_reduced = jnp.transpose(mine_parts, (1, 0, 2)).reshape(-1, width).astype(jnp.float32)
    attn_reduced = joined_reduced[:attn_cols].T
    ffn_reduced = joined_reduced[attn_cols:].T
    attn_new, attn_moment, attn_average = apply_update(
        attn_weights, attn_reduced, attn_momentum, attn_averaged, decay_rate
    )
    ffn_new, ffn_moment, ffn_average = apply_update(
        ffn_weights, ffn_reduced, ffn_momentum, ffn_averaged, decay_rate
    )
    vector_new, vector_moment, vector_average = apply_update(
        vectors, vector_reduced, vector_momentum, vector_averaged, 0.0
    )
    return (
        mean_loss,
        input_grad,
        attn_reduced,
        ffn_reduced,
        vector_reduced,
        attn_new,
        ffn_new,
        vector_new,
        attn_moment,
        ffn_moment,
        vector_moment,
        attn_average,
        ffn_average,
        vector_average,
    )


def solution(mesh):
    in_specs = (
        P(("dp", "rep"), None),
        P(("dp", "rep"), None),
        P(("dp", "rep")),
        P(None, ("dp", "rep")),
        P(None, ("dp", "rep")),
        P(("dp", "rep")),
        P(None, ("dp", "rep")),
        P(None, ("dp", "rep")),
        P(("dp", "rep")),
        P(None, ("dp", "rep")),
        P(None, ("dp", "rep")),
        P(("dp", "rep")),
    )
    out_specs = (
        P(),
        P(("dp", "rep"), None),
        P(None, ("dp", "rep")),
        P(None, ("dp", "rep")),
        P(("dp", "rep")),
        P(None, ("dp", "rep")),
        P(None, ("dp", "rep")),
        P(("dp", "rep")),
        P(None, ("dp", "rep")),
        P(None, ("dp", "rep")),
        P(("dp", "rep")),
        P(None, ("dp", "rep")),
        P(None, ("dp", "rep")),
        P(("dp", "rep")),
    )
    return jax.shard_map(shards, mesh=mesh, in_specs=in_specs, out_specs=out_specs, check_vma=False)
```

```python
import functools
import math

import jax
import jax.numpy as jnp
from jax import lax
from jax.experimental import pallas as pl
from jax.experimental.pallas import tpu as pltpu
from jax.sharding import PartitionSpec as P

MESH = pl.DeviceIdType.MESH
GRAD_SEND = jnp.bfloat16
AXES = ("dp", "rep")

HEADS = 12
HD = 64
SEGS = 16


ln_epsilon = 1e-12
pool_epsilon = 1e-06
logit_divisor = 0.025
learn_rate = 0.01
momentum_rate = 0.9
decay_rate = 0.01
average_rate = 0.75
masked_value = -1e30


def layer_norm_parts(values, gain, shift):
    per_line_average = jnp.mean(values, -1, keepdims=True)
    centred = values - per_line_average
    inverse = lax.rsqrt(jnp.mean(centred * centred, -1, keepdims=True) + ln_epsilon)
    normal_part = centred * inverse
    return (normal_part * gain + shift, normal_part, inverse)


def layer_norm_back(grad_out, normal_part, inverse, gain):
    scaled = grad_out * gain
    grad_in = inverse * (
        scaled
        - jnp.mean(scaled, -1, keepdims=True)
        - normal_part * jnp.mean(scaled * normal_part, -1, keepdims=True)
    )
    return (grad_in, jnp.sum(grad_out * normal_part, 0), jnp.sum(grad_out, 0))


def row_scores(query_one, key_one, segment_one, scale):
    scores = (
        jnp.einsum("qhd,khd->hqk", query_one, key_one, preferred_element_type=jnp.float32) * scale
    )
    same_text = segment_one[:, None] == segment_one[None, :]
    return jnp.where(same_text[None], scores, masked_value)


def attend_rows(query_rows, key_rows, value_rows, row_segments):
    scale = 1.0 / math.sqrt(query_rows.shape[-1])

    def one_row(row_args):
        query_one, key_one, value_one, segment_one = row_args
        scores = row_scores(query_one, key_one, segment_one, scale)
        row_max = jnp.max(scores, -1, keepdims=True)
        exp_scores = jnp.exp(scores - row_max)
        sums = jnp.sum(exp_scores, -1, keepdims=True)
        attn_probs = exp_scores / sums
        mixed = jnp.einsum(
            "hqk,khd->qhd",
            attn_probs.astype(jnp.bfloat16),
            value_one,
            preferred_element_type=jnp.float32,
        )
        return (mixed.astype(jnp.bfloat16), (row_max + jnp.log(sums))[..., 0])

    return lax.map(one_row, (query_rows, key_rows, value_rows, row_segments))


def attend_back(query_rows, key_rows, value_rows, row_segments, log_norm, grad_mixed):
    scale = 1.0 / math.sqrt(query_rows.shape[-1])

    def one_row(row_args):
        query_one, key_one, value_one, segment_one, norm_one, grad_one = row_args
        scores = row_scores(query_one, key_one, segment_one, scale)
        attn_probs = jnp.exp(scores - norm_one[..., None])
        grad_value = jnp.einsum(
            "hqk,qhd->khd",
            attn_probs.astype(jnp.bfloat16),
            grad_one,
            preferred_element_type=jnp.float32,
        )
        grad_probs = jnp.einsum(
            "qhd,khd->hqk", grad_one, value_one, preferred_element_type=jnp.float32
        )
        inner = jnp.sum(attn_probs * grad_probs, -1, keepdims=True)
        grad_scores = (attn_probs * (grad_probs - inner)).astype(jnp.bfloat16)
        grad_query = (
            jnp.einsum("hqk,khd->qhd", grad_scores, key_one, preferred_element_type=jnp.float32)
            * scale
        )
        grad_key = (
            jnp.einsum("hqk,qhd->khd", grad_scores, query_one, preferred_element_type=jnp.float32)
            * scale
        )
        return jnp.concatenate([grad_query, grad_key, grad_value], axis=1)

    return lax.map(one_row, (query_rows, key_rows, value_rows, row_segments, log_norm, grad_mixed))


def attention_back_kernel(scale, q_ref, k_ref, v_ref, g_ref, norm_ref, seg_col_ref, seg_row_ref, dq_ref, dk_ref, dv_ref):
    pair = pl.program_id(1)
    width = q_ref.shape[1]
    half = width // 2
    lane = lax.broadcasted_iota(jnp.int32, (1, width), 1)
    same = seg_col_ref[...] == seg_row_ref[0]
    norms = norm_ref[...]
    norm_lane = lax.broadcasted_iota(jnp.int32, norms.shape, 1)
    q = q_ref[...]
    k = k_ref[...]
    v = v_ref[...]
    g = g_ref[...]
    zero_b = jnp.zeros_like(q)
    on_last = (((1,), (1,)), ((), ()))
    on_first = (((0,), (0,)), ((), ()))
    dq = jnp.zeros(q.shape, jnp.float32)
    dk = jnp.zeros(q.shape, jnp.float32)
    dv = jnp.zeros(q.shape, jnp.float32)
    for head in range(2):
        mine = (lane >= head * half) & (lane < (head + 1) * half)
        q_h = jnp.where(mine, q, zero_b)
        g_h = jnp.where(mine, g, zero_b)
        norm_h = jnp.sum(jnp.where(norm_lane == 2 * pair + head, norms, 0.0), 1, keepdims=True)
        scores = lax.dot_general(q_h, k, on_last, preferred_element_type=jnp.float32) * scale
        scores = jnp.where(same, scores, masked_value)
        probs = jnp.exp(scores - norm_h)
        grad_v = lax.dot_general(probs.astype(jnp.bfloat16), g, on_first, preferred_element_type=jnp.float32)
        grad_p = lax.dot_general(g_h, v, on_last, preferred_element_type=jnp.float32)
        inner = jnp.sum(probs * grad_p, -1, keepdims=True)
        grad_s = (probs * (grad_p - inner)).astype(jnp.bfloat16)
        grad_q = jnp.dot(grad_s, k, preferred_element_type=jnp.float32) * scale
        grad_k = lax.dot_general(grad_s, q, on_first, preferred_element_type=jnp.float32) * scale
        dq = jnp.where(mine, grad_q, dq)
        dk = jnp.where(mine, grad_k, dk)
        dv = jnp.where(mine, grad_v, dv)
    dq_ref[...] = dq.astype(dq_ref.dtype)
    dk_ref[...] = dk.astype(dk_ref.dtype)
    dv_ref[...] = dv.astype(dv_ref.dtype)


def attention_back(qkv_rows, grad_mixed_flat, norm_tokens, segments, heads, head_dim):
    tokens, three_width = qkv_rows.shape
    width = three_width // 3
    rows, seq_len = segments.shape
    pair_width = 2 * head_dim
    pairs = heads // 2
    seg_col = segments.reshape(tokens, 1)
    seg_row = segments.reshape(rows, 1, seq_len)
    scale = 1.0 / math.sqrt(head_dim)
    out = jax.ShapeDtypeStruct((tokens, width), jnp.bfloat16)
    return pl.pallas_call(
        functools.partial(attention_back_kernel, scale),
        grid=(rows, pairs),
        in_specs=[
            pl.BlockSpec((seq_len, pair_width), lambda r, p: (r, p)),
            pl.BlockSpec((seq_len, pair_width), lambda r, p: (r, pairs + p)),
            pl.BlockSpec((seq_len, pair_width), lambda r, p: (r, 2 * pairs + p)),
            pl.BlockSpec((seq_len, pair_width), lambda r, p: (r, p)),
            pl.BlockSpec((seq_len, heads), lambda r, p: (r, 0)),
            pl.BlockSpec((seq_len, 1), lambda r, p: (r, 0)),
            pl.BlockSpec((1, 1, seq_len), lambda r, p: (r, 0, 0)),
        ],
        out_specs=[pl.BlockSpec((seq_len, pair_width), lambda r, p: (r, p))] * 3,
        out_shape=[out, out, out],
        compiler_params=pltpu.CompilerParams(vmem_limit_bytes=48 * 1024 * 1024),
        cost_estimate=pl.CostEstimate(
            flops=10 * rows * heads * seq_len * seq_len * pair_width,
            transcendentals=rows * heads * seq_len * seq_len,
            bytes_accessed=tokens * (three_width + 4 * width) * 2,
        ),
    )(qkv_rows, qkv_rows, qkv_rows, grad_mixed_flat, norm_tokens, seg_col, seg_row)


def apply_update(weight, grad, moment, average, decay):
    step_grad = grad + decay * weight
    new_moment = momentum_rate * moment + step_grad
    new_weight = weight - learn_rate * (step_grad + momentum_rate * new_moment)
    fresh_running_mean = average_rate * average + (1.0 - average_rate) * new_weight
    return (new_weight, new_moment, fresh_running_mean)


def bf16_round(values):
    return lax.reduce_precision(values, exponent_bits=8, mantissa_bits=7)


def flat_index(sizes):
    idx = 0
    for name, size in zip(AXES, sizes):
        idx = idx * size + lax.axis_index(name)
    return idx


def device_of(flat, sizes):
    coords = []
    for size in reversed(sizes):
        coords.append(lax.rem(flat, size))
        flat = flat // size
    return tuple(reversed(coords))


def enter_all(n, sizes, me):
    barrier = pltpu.get_barrier_semaphore()

    def greet(k, carry):
        peer = lax.rem(me + k, n)
        pl.semaphore_signal(barrier, inc=1, device_id=device_of(peer, sizes), device_id_type=MESH)
        return carry

    lax.fori_loop(1, n, greet, 0)
    pl.semaphore_wait(barrier, n - 1)


def gather_kernel(n, sizes, x_ref, out_ref, send_sem, recv_sem):
    me = flat_index(sizes)
    enter_all(n, sizes, me)

    def send(k, carry):
        peer = lax.rem(me + k, n)
        pltpu.make_async_remote_copy(
            src_ref=x_ref, dst_ref=out_ref.at[me], send_sem=send_sem.at[k], recv_sem=recv_sem.at[me],
            device_id=device_of(peer, sizes), device_id_type=MESH,
        ).start()
        return carry

    lax.fori_loop(1, n, send, 0)
    out_ref[me] = x_ref[...]

    def finish(k, carry):
        peer = lax.rem(me + k, n)
        src = lax.rem(me + n - k, n)
        pltpu.make_async_remote_copy(
            src_ref=x_ref, dst_ref=out_ref.at[me], send_sem=send_sem.at[k], recv_sem=recv_sem.at[me],
            device_id=device_of(peer, sizes), device_id_type=MESH,
        ).wait_send()
        pltpu.make_async_remote_copy(
            src_ref=x_ref, dst_ref=out_ref.at[src], send_sem=send_sem.at[k], recv_sem=recv_sem.at[src],
            device_id=device_of(src, sizes), device_id_type=MESH,
        ).wait_recv()
        return carry

    lax.fori_loop(1, n, finish, 0)


def small_gather(x, sizes, cid):
    n = math.prod(sizes)
    return pl.pallas_call(
        functools.partial(gather_kernel, n, sizes),
        out_shape=jax.ShapeDtypeStruct((n,) + x.shape, x.dtype),
        in_specs=[pl.BlockSpec(memory_space=pltpu.VMEM)],
        out_specs=pl.BlockSpec(memory_space=pltpu.VMEM),
        scratch_shapes=[pltpu.SemaphoreType.DMA((n,)), pltpu.SemaphoreType.DMA((n,))],
        compiler_params=pltpu.CompilerParams(collective_id=cid, has_side_effects=True),
    )(x)


def scatter_kernel(n, sizes, x_ref, out_ref, send_sem, recv_sem):
    me = flat_index(sizes)
    enter_all(n, sizes, me)

    def send(k, carry):
        peer = lax.rem(me + k, n)
        pltpu.make_async_remote_copy(
            src_ref=x_ref.at[peer], dst_ref=out_ref.at[me], send_sem=send_sem.at[k], recv_sem=recv_sem.at[me],
            device_id=device_of(peer, sizes), device_id_type=MESH,
        ).start()
        return carry

    lax.fori_loop(1, n, send, 0)
    out_ref[me] = x_ref[me]

    def finish(k, carry):
        peer = lax.rem(me + k, n)
        src = lax.rem(me + n - k, n)
        pltpu.make_async_remote_copy(
            src_ref=x_ref.at[peer], dst_ref=out_ref.at[me], send_sem=send_sem.at[k], recv_sem=recv_sem.at[me],
            device_id=device_of(peer, sizes), device_id_type=MESH,
        ).wait_send()
        pltpu.make_async_remote_copy(
            src_ref=x_ref.at[src], dst_ref=out_ref.at[src], send_sem=send_sem.at[k], recv_sem=recv_sem.at[src],
            device_id=device_of(src, sizes), device_id_type=MESH,
        ).wait_recv()
        return carry

    lax.fori_loop(1, n, finish, 0)


def small_scatter(x, sizes, cid):
    n = math.prod(sizes)
    return pl.pallas_call(
        functools.partial(scatter_kernel, n, sizes),
        out_shape=jax.ShapeDtypeStruct(x.shape, x.dtype),
        in_specs=[pl.BlockSpec(memory_space=pltpu.VMEM)],
        out_specs=pl.BlockSpec(memory_space=pltpu.VMEM),
        scratch_shapes=[pltpu.SemaphoreType.DMA((n,)), pltpu.SemaphoreType.DMA((n,))],
        compiler_params=pltpu.CompilerParams(collective_id=cid, has_side_effects=True),
    )(x)


def pair_gather_kernel(n, sizes, x_ref, out_ref, local_sem, send1, recv1, send2, recv2, send3, recv3):
    me = flat_index(sizes)
    chips = n // 2
    chip = me // 2
    core = lax.rem(me, 2)
    partner = me + 1 - 2 * core
    enter_all(n, sizes, me)

    local = pltpu.make_async_copy(x_ref, out_ref.at[me], local_sem)
    local.start()
    first = pltpu.make_async_remote_copy(
        src_ref=x_ref, dst_ref=out_ref.at[me], send_sem=send1, recv_sem=recv1,
        device_id=device_of(partner, sizes), device_id_type=MESH,
    )
    first.start()
    local.wait()
    first.wait_send()
    pltpu.make_async_remote_copy(
        src_ref=x_ref, dst_ref=out_ref.at[partner], send_sem=send1, recv_sem=recv1,
        device_id=device_of(partner, sizes), device_id_type=MESH,
    ).wait_recv()

    def pair(c):
        return out_ref.at[pl.ds(2 * c, 2)]

    def target(k):
        return lax.rem(chip + 2 * k - 1 + core, chips)

    def source(k):
        return lax.rem(chip + chips - (2 * k - 1 + core), chips)

    count = (chips - core) // 2

    def send_out(k, carry):
        other = target(k)
        pltpu.make_async_remote_copy(
            src_ref=pair(chip), dst_ref=pair(chip), send_sem=send2.at[other], recv_sem=recv2.at[chip],
            device_id=device_of(2 * other + core, sizes), device_id_type=MESH,
        ).start()
        return carry

    lax.fori_loop(1, count + 1, send_out, 0)

    def take_in(k, carry):
        other = source(k)
        pltpu.make_async_remote_copy(
            src_ref=pair(other), dst_ref=pair(other), send_sem=send2.at[other], recv_sem=recv2.at[other],
            device_id=device_of(2 * other + core, sizes), device_id_type=MESH,
        ).wait_recv()
        pltpu.make_async_remote_copy(
            src_ref=pair(other), dst_ref=pair(other), send_sem=send3.at[other], recv_sem=recv3.at[other],
            device_id=device_of(partner, sizes), device_id_type=MESH,
        ).start()
        return carry

    lax.fori_loop(1, count + 1, take_in, 0)

    def sent_out(k, carry):
        other = target(k)
        pltpu.make_async_remote_copy(
            src_ref=pair(chip), dst_ref=pair(chip), send_sem=send2.at[other], recv_sem=recv2.at[chip],
            device_id=device_of(2 * other + core, sizes), device_id_type=MESH,
        ).wait_send()
        return carry

    lax.fori_loop(1, count + 1, sent_out, 0)

    def forwarded(k, carry):
        other = source(k)
        pltpu.make_async_remote_copy(
            src_ref=pair(other), dst_ref=pair(other), send_sem=send3.at[other], recv_sem=recv3.at[other],
            device_id=device_of(partner, sizes), device_id_type=MESH,
        ).wait_send()
        return carry

    lax.fori_loop(1, count + 1, forwarded, 0)

    other_count = (chips - (1 - core)) // 2

    def partner_source(k):
        return lax.rem(chip + chips - (2 * k - 1 + (1 - core)), chips)

    def from_partner(k, carry):
        other = partner_source(k)
        pltpu.make_async_remote_copy(
            src_ref=pair(other), dst_ref=pair(other), send_sem=send3.at[other], recv_sem=recv3.at[other],
            device_id=device_of(partner, sizes), device_id_type=MESH,
        ).wait_recv()
        return carry

    lax.fori_loop(1, other_count + 1, from_partner, 0)


def pair_gather(x, sizes, cid):
    n = math.prod(sizes)
    chips = n // 2
    dma = pltpu.SemaphoreType.DMA
    return pl.pallas_call(
        functools.partial(pair_gather_kernel, n, sizes),
        out_shape=jax.ShapeDtypeStruct((n,) + x.shape, x.dtype),
        in_specs=[pl.BlockSpec(memory_space=pltpu.VMEM)],
        out_specs=pl.BlockSpec(memory_space=pltpu.VMEM),
        scratch_shapes=[dma(()), dma(()), dma(()), dma((chips,)), dma((chips,)), dma((chips,)), dma((chips,))],
        compiler_params=pltpu.CompilerParams(collective_id=cid, has_side_effects=True),
    )(x)


def halving_orders(n, parts):
    bits = n.bit_length() - 1
    middle = list(range(1, bits - 1))
    orders = []
    for p in range(parts):
        shift = p % len(middle) if middle else 0
        orders.append(tuple([0] + middle[shift:] + middle[:shift] + [bits - 1]))
    return tuple(orders)


def halving_kernel(n, sizes, orders, cols, tile, groups, *refs):
    count = sum(groups)
    sources = refs[:count]
    vec_ref, dq_ref, w_ref, res_ref, out_ref, vec_out, grad_out, work = refs[count : count + 8]
    rest = refs[count + 8 :]
    grouped = []
    at = 0
    for g in groups:
        grouped.append(sources[at : at + g])
        at += g
    steps = len(orders[0])
    parts = len(orders)
    layout = []
    head = 0
    for group in grouped:
        size = sum(math.prod(s.shape[:-1]) for s in group) // n
        layout.append((group, size, head))
        head += size
    recvs = rest[:steps]
    local_sem, send_sems, recv_sems, vec_send, vec_recv = rest[steps:]
    me = flat_index(sizes)

    def partner_of(bit):
        mine = lax.rem(me // (2**bit), 2)
        return mine, me + (1 - 2 * mine) * (2**bit)

    enter_all(n, sizes, me)

    def vec_copy(k):
        peer = lax.rem(me + k, n)
        return pltpu.make_async_remote_copy(
            src_ref=vec_ref.at[peer], dst_ref=vec_out.at[me], send_sem=vec_send.at[k], recv_sem=vec_recv.at[me],
            device_id=device_of(peer, sizes), device_id_type=MESH,
        )

    def vec_start(k, carry):
        vec_copy(k).start()
        return carry

    lax.fori_loop(1, n, vec_start, 0)
    vec_out[me] = vec_ref[me]

    half = n // 2
    first = []
    for p in range(parts):
        order = orders[p]
        mine, other = partner_of(order[0])
        column = pl.ds(p * cols, cols)

        def owner(j, side, order=order):
            o = side * (2 ** order[0])
            for m, bit in enumerate(order[1:]):
                o = o + lax.rem(j // (2 ** (steps - 2 - m)), 2) * (2**bit)
            return o

        def issue(j, carry, p=p, owner=owner, mine=mine, other=other, column=column):
            for o, dst, remote in ((owner(j, 1 - mine), recvs[0].at[p, j], True), (owner(j, mine), work.at[p, j], False)):
                for group, size, head in layout:
                    offset = 0
                    for chosen in group:
                        split = math.prod(chosen.shape[:-1]) // size

                        def move(chosen=chosen, offset=offset, o=o, dst=dst, remote=remote, size=size, head=head):
                            if len(chosen.shape) == 3:
                                src_ref = chosen.at[o - offset, :, column]
                            else:
                                src_ref = chosen.at[pl.ds((o - offset) * size, size), column]
                            dst_ref = dst.at[pl.ds(head, size)]
                            if remote:
                                pltpu.make_async_remote_copy(
                                    src_ref=src_ref, dst_ref=dst_ref,
                                    send_sem=send_sems.at[p, 0], recv_sem=recv_sems.at[p, 0],
                                    device_id=device_of(other, sizes), device_id_type=MESH,
                                ).start()
                            else:
                                pltpu.make_async_copy(src_ref, dst_ref, local_sem.at[p]).start()

                        if len(group) == 1:
                            move()
                        else:
                            pl.when((o >= offset) & (o < offset + split))(move)
                        offset += split

            return carry

        lax.fori_loop(0, half, issue, 0)
        first.append(other)
    for p in range(parts):
        whole = pltpu.make_async_remote_copy(
            src_ref=work.at[p, pl.ds(0, half)], dst_ref=recvs[0].at[p],
            send_sem=send_sems.at[p, 0], recv_sem=recv_sems.at[p, 0],
            device_id=device_of(first[p], sizes), device_id_type=MESH,
        )
        pltpu.make_async_copy(work.at[p, pl.ds(0, half)], work.at[p, pl.ds(0, half)], local_sem.at[p]).wait()
        whole.wait_recv()
        whole.wait_send()

        def accumulate0(i, carry, p=p):
            total = work[p, i].astype(jnp.float32) + recvs[0][p, i].astype(jnp.float32)
            work[p, i] = total.astype(work.dtype)
            return carry

        lax.fori_loop(0, half, accumulate0, 0)

    for step in range(1, steps):
        half = n >> (step + 1)
        copies = []
        for p in range(parts):
            mine, other = partner_of(orders[p][step])
            send = pltpu.make_async_remote_copy(
                src_ref=work.at[p, pl.ds((1 - mine) * half, half)], dst_ref=recvs[step].at[p],
                send_sem=send_sems.at[p, step], recv_sem=recv_sems.at[p, step],
                device_id=device_of(other, sizes), device_id_type=MESH,
            )
            send.start()
            copies.append((mine, send))
        if step == 1:
            def product(t, carry):
                rows = pl.ds(pl.multiple_of(t * tile, tile), tile)
                grad_out[rows, :] = (
                    jnp.dot(dq_ref[rows, :], w_ref[...], preferred_element_type=jnp.float32) + res_ref[rows, :]
                )
                return carry

            lax.fori_loop(0, grad_out.shape[0] // tile, product, 0)
        for p in range(parts):
            mine, send = copies[p]
            send.wait_recv()
            send.wait_send()

            def accumulate(i, carry, p=p, mine=mine, half=half, step=step):
                total = work[p, mine * half + i].astype(jnp.float32) + recvs[step][p, i].astype(jnp.float32)
                work[p, i] = total.astype(work.dtype)
                return carry

            lax.fori_loop(0, half, accumulate, 0)
    for p in range(parts):
        out_ref[p] = work[p, 0]

    def vec_finish(k, carry):
        vec_copy(k).wait_send()
        src = lax.rem(me + n - k, n)
        pltpu.make_async_remote_copy(
            src_ref=vec_ref.at[src], dst_ref=vec_out.at[src], send_sem=vec_send.at[k], recv_sem=vec_recv.at[src],
            device_id=device_of(src, sizes), device_id_type=MESH,
        ).wait_recv()
        return carry

    lax.fori_loop(1, n, vec_finish, 0)


def halving_scatter(grouped, vec, grad_b, weight_t, residual, sizes, parts, cid):
    n = math.prod(sizes)
    groups = tuple(len(g) for g in grouped)
    grads = [s for g in grouped for s in g]
    width = grads[0].shape[-1]
    rows = sum(math.prod(g.shape[:-1]) for g in grads) // n
    cols = width // parts
    orders = halving_orders(n, parts)
    steps = len(orders[0])
    dtype = grads[0].dtype
    tile = 128
    dma = pltpu.SemaphoreType.DMA
    vmem = pl.BlockSpec(memory_space=pltpu.VMEM)
    scratch = [pltpu.VMEM((parts, n // 2, rows, cols), dtype)]
    scratch += [pltpu.VMEM((parts, n >> (k + 1), rows, cols), dtype) for k in range(steps)]
    scratch += [dma((parts,)), dma((parts, steps)), dma((parts, steps)), dma((n,)), dma((n,))]
    return pl.pallas_call(
        functools.partial(halving_kernel, n, sizes, orders, cols, tile, groups),
        out_shape=(
            jax.ShapeDtypeStruct((parts, rows, cols), dtype),
            jax.ShapeDtypeStruct(vec.shape, vec.dtype),
            jax.ShapeDtypeStruct(residual.shape, jnp.float32),
        ),
        in_specs=[pl.BlockSpec(memory_space=pl.ANY)] * len(grads) + [vmem, vmem, vmem, vmem],
        out_specs=(vmem, vmem, vmem),
        scratch_shapes=scratch,
        compiler_params=pltpu.CompilerParams(
            collective_id=cid, has_side_effects=True, vmem_limit_bytes=60 * 1024 * 1024
        ),
    )(*grads, vec, grad_b, weight_t, residual)


def contrastive(embed_b, gathered, partner_all, me):
    own_texts = embed_b.shape[0]
    all_texts = gathered.shape[0]
    chunk = min(all_texts, 1024)
    on_rows = (((1,), (1,)), ((), ()))

    def chunk_stats(c):
        rows_b = lax.dynamic_slice_in_dim(gathered, c * chunk, chunk)
        sim = lax.dot_general(rows_b, gathered, on_rows, preferred_element_type=jnp.float32) / logit_divisor
        column_ids = lax.broadcasted_iota(jnp.int32, sim.shape, 1)
        row_ids = lax.broadcasted_iota(jnp.int32, sim.shape, 0) + c * chunk
        masked = jnp.where(column_ids == row_ids, masked_value, sim)
        row_max = jnp.max(masked, -1, keepdims=True)
        log_sum = row_max + jnp.log(jnp.sum(jnp.exp(masked - row_max), -1, keepdims=True))
        wanted = lax.dynamic_slice_in_dim(partner_all, c * chunk, chunk)
        positive = jnp.sum(jnp.where(column_ids == wanted[:, None], sim, 0.0), -1)
        return log_sum[:, 0], positive

    if all_texts == chunk:
        log_sum_all, positive_all = chunk_stats(0)
    else:
        log_sum_all, positive_all = lax.map(chunk_stats, jnp.arange(all_texts // chunk))
        log_sum_all = log_sum_all.reshape(-1)
        positive_all = positive_all.reshape(-1)
    mean_loss = jnp.sum(log_sum_all - positive_all) / all_texts

    own_start = me * own_texts
    own_ids = lax.broadcasted_iota(jnp.int32, (own_texts,), 0) + own_start
    own_partner = lax.dynamic_slice_in_dim(partner_all, own_start, own_texts)
    own_log_sum = lax.dynamic_slice_in_dim(log_sum_all, own_start, own_texts)

    sim_rows = lax.dot_general(embed_b, gathered, on_rows, preferred_element_type=jnp.float32) / logit_divisor
    column_ids = lax.broadcasted_iota(jnp.int32, sim_rows.shape, 1)
    masked_rows = jnp.where(column_ids == own_ids[:, None], masked_value, sim_rows)
    grad_rows = (
        jnp.exp(masked_rows - own_log_sum[:, None]) - (column_ids == own_partner[:, None]).astype(jnp.float32)
    ).astype(jnp.bfloat16)

    sim_cols = lax.dot_general(gathered, embed_b, on_rows, preferred_element_type=jnp.float32) / logit_divisor
    row_ids = lax.broadcasted_iota(jnp.int32, sim_cols.shape, 0)
    masked_cols = jnp.where(row_ids == own_ids[None, :], masked_value, sim_cols)
    grad_cols = (
        jnp.exp(masked_cols - log_sum_all[:, None]) - (partner_all[:, None] == own_ids[None, :]).astype(jnp.float32)
    ).astype(jnp.bfloat16)

    on_tokens = (((0,), (0,)), ((), ()))
    embedding_gradient = (
        jnp.dot(grad_rows, gathered, preferred_element_type=jnp.float32)
        + lax.dot_general(grad_cols, gathered, on_tokens, preferred_element_type=jnp.float32)
    ) / logit_divisor
    return mean_loss, embedding_gradient


def shards(
    hidden_in,
    segments,
    partner,
    attn_weights,
    ffn_weights,
    vectors,
    attn_momentum,
    ffn_momentum,
    vector_momentum,
    attn_averaged,
    ffn_averaged,
    vector_averaged,
):
    sizes = tuple(lax.axis_size(name) for name in AXES)
    n_dev = math.prod(sizes)
    me = flat_index(sizes)
    vec_len = vectors.shape[0]
    small = jnp.concatenate([vectors, partner.astype(jnp.float32)])[None, :]
    small_all = small_gather(small, sizes, 0)[:, 0, :]
    vector_f = bf16_round(small_all[:, :vec_len].reshape(-1))
    partner_all = small_all[:, vec_len:].reshape(-1).astype(jnp.int32)
    attn_full, ffn_full = (
        lax.all_gather(attn_weights.astype(jnp.bfloat16), AXES, axis=1, tiled=True),
        lax.all_gather(ffn_weights.astype(jnp.bfloat16), AXES, axis=1, tiled=True),
    )
    width = attn_full.shape[0]
    hidden = ffn_full.shape[1] // 2
    query_bias = vector_f[0:width]
    value_bias = vector_f[width : 2 * width]
    output_bias = vector_f[2 * width : 3 * width]
    gain_first = vector_f[3 * width : 4 * width]
    shift_first = vector_f[4 * width : 5 * width]
    upper_bias = vector_f[5 * width : 5 * width + hidden]
    lower_bias = vector_f[5 * width + hidden : 6 * width + hidden]
    gain_second = vector_f[6 * width + hidden : 7 * width + hidden]
    shift_second = vector_f[7 * width + hidden : 8 * width + hidden]
    w_qkv = attn_full[:, : 3 * width]
    w_output = attn_full[:, 3 * width :]
    w_upper = ffn_full[:, :hidden]
    w_lower = ffn_full[:, hidden:]
    rows_dev, seq_len = segments.shape
    tokens_n = rows_dev * seq_len
    on_rows = (((1,), (1,)), ((), ()))
    on_tokens = (((0,), (0,)), ((), ()))
    qkv_bias = jnp.concatenate([query_bias, jnp.zeros_like(query_bias), value_bias])
    qkv_rows = (jnp.dot(hidden_in, w_qkv, preferred_element_type=jnp.float32) + qkv_bias).astype(
        jnp.bfloat16
    )
    heads = qkv_rows.reshape(rows_dev, seq_len, 3, HEADS, HD)
    query_rows = heads[:, :, 0]
    key_rows = heads[:, :, 1]
    value_rows = heads[:, :, 2]
    mixed, log_norm = attend_rows(query_rows, key_rows, value_rows, segments)
    mixed_flat = mixed.reshape(tokens_n, width)
    first_sum = (
        hidden_in.astype(jnp.float32)
        + jnp.dot(mixed_flat, w_output, preferred_element_type=jnp.float32)
        + output_bias
    )
    normed, normal_one, inverse_one = layer_norm_parts(first_sum, gain_first, shift_first)
    normed_r = bf16_round(normed)
    normed_b = normed_r.astype(jnp.bfloat16)
    upper = jnp.dot(normed_b, w_upper, preferred_element_type=jnp.float32) + upper_bias
    active_b = jax.nn.gelu(upper, approximate=False).astype(jnp.bfloat16)
    second_sum = (
        normed_r
        + lax.dot_general(active_b, w_lower, on_rows, preferred_element_type=jnp.float32)
        + lower_bias
    )
    result, normal_two, inverse_two = layer_norm_parts(second_sum, gain_second, shift_second)
    text_ids = jnp.arange(SEGS, dtype=jnp.int32)
    one_hot = (segments[:, None, :] == text_ids[None, :, None]).astype(jnp.float32)
    counts = jnp.sum(one_hot, -1, keepdims=True)
    pooled = (
        jnp.einsum(
            "rts,rsd->rtd",
            one_hot,
            result.reshape(rows_dev, seq_len, width),
            precision=lax.Precision.HIGHEST,
        )
        / counts
    ).reshape(-1, width)
    inv_norm = lax.rsqrt(jnp.sum(pooled * pooled, -1, keepdims=True) + pool_epsilon)
    embed_b = (pooled * inv_norm).astype(jnp.bfloat16)
    gathered_embeddings = pair_gather(embed_b, sizes, 2).reshape(-1, width)
    mean_loss, embedding_gradient = contrastive(embed_b, gathered_embeddings, partner_all, me)
    grad_pooled = inv_norm * embedding_gradient - pooled * (
        inv_norm * inv_norm * inv_norm
    ) * jnp.sum(embedding_gradient * pooled, -1, keepdims=True)
    derivative_output = jnp.einsum(
        "rts,rtd->rsd",
        one_hot,
        grad_pooled.reshape(rows_dev, SEGS, width) / counts,
        precision=lax.Precision.HIGHEST,
    ).reshape(tokens_n, width)
    grad_second, gain_two_grad, shift_two_grad = layer_norm_back(
        derivative_output, normal_two, inverse_two, gain_second
    )
    lower_bias_grad = jnp.sum(grad_second, 0)
    lower_grad_b = grad_second.astype(jnp.bfloat16)
    lower_w_grad_t = lax.dot_general(
        active_b, lower_grad_b, on_tokens, preferred_element_type=jnp.float32
    )
    grad_active = jnp.dot(lower_grad_b, w_lower, preferred_element_type=jnp.float32)
    cumulative = 0.5 * (1.0 + lax.erf(upper / math.sqrt(2.0)))
    density = jnp.exp(-0.5 * upper * upper) / math.sqrt(2.0 * math.pi)
    grad_upper = grad_active * (cumulative + upper * density)
    upper_bias_grad = jnp.sum(grad_upper, 0)
    upper_grad_b = grad_upper.astype(jnp.bfloat16)
    upper_w_grad_t = lax.dot_general(
        upper_grad_b, normed_b, on_tokens, preferred_element_type=jnp.float32
    )
    grad_normed = (
        lax.dot_general(upper_grad_b, w_upper, on_rows, preferred_element_type=jnp.float32)
        + grad_second
    )
    grad_first, gain_one_grad, shift_one_grad = layer_norm_back(
        grad_normed, normal_one, inverse_one, gain_first
    )
    output_bias_grad = jnp.sum(grad_first, 0)
    first_grad_b = grad_first.astype(jnp.bfloat16)
    output_w_grad_t = lax.dot_general(
        first_grad_b, mixed_flat, on_tokens, preferred_element_type=jnp.float32
    )
    grad_mixed = lax.dot_general(
        first_grad_b, w_output, on_rows, preferred_element_type=jnp.float32
    ).astype(jnp.bfloat16)
    grad_mixed = grad_mixed.reshape(rows_dev, seq_len, HEADS, HD)
    norm_tokens = jnp.swapaxes(log_norm, 1, 2).reshape(tokens_n, HEADS)
    qkv_grad = jnp.concatenate(
        attention_back(qkv_rows, grad_mixed.reshape(tokens_n, width), norm_tokens, segments, HEADS, HD), 1
    ).astype(jnp.float32)
    qkv_grad_f = bf16_round(qkv_grad)
    qkv_grad_b = qkv_grad_f.astype(jnp.bfloat16)
    query_bias_grad = jnp.sum(qkv_grad_f[:, :width], 0)
    value_bias_grad = jnp.sum(qkv_grad_f[:, 2 * width :], 0)
    qkv_w_grad_t = lax.dot_general(
        qkv_grad_b, hidden_in, on_tokens, preferred_element_type=jnp.float32
    )
    vector_grad = jnp.concatenate(
        [
            query_bias_grad,
            value_bias_grad,
            output_bias_grad,
            gain_one_grad,
            shift_one_grad,
            upper_bias_grad,
            lower_bias_grad,
            gain_two_grad,
            shift_two_grad,
        ]
    )
    attn_cols = (qkv_w_grad_t.shape[0] + output_w_grad_t.shape[0]) // n_dev
    ffn_cols = (upper_w_grad_t.shape[0] + lower_w_grad_t.shape[0]) // n_dev
    if attn_cols % 16 == 0 and ffn_cols % 16 == 0:
        grads = (
            (qkv_w_grad_t.astype(GRAD_SEND), output_w_grad_t.astype(GRAD_SEND)),
            (upper_w_grad_t.astype(GRAD_SEND), lower_w_grad_t.astype(GRAD_SEND)),
        )
    else:
        attn_blocks = jnp.concatenate(
            [qkv_w_grad_t.reshape(-1, attn_cols, width), output_w_grad_t.reshape(-1, attn_cols, width)], 0
        )
        ffn_blocks = jnp.concatenate(
            [upper_w_grad_t.reshape(-1, ffn_cols, width), lower_w_grad_t.reshape(-1, ffn_cols, width)], 0
        )
        grads = ((jnp.concatenate([attn_blocks, ffn_blocks], 1).astype(GRAD_SEND),),)
    parts = 3
    mine_parts, vector_slots, input_grad = halving_scatter(
        grads, vector_grad.reshape(n_dev, 1, -1), qkv_grad_b, w_qkv.T, grad_first, sizes, parts, 3
    )
    vector_reduced = jnp.sum(vector_slots[:, 0, :], 0)
    joined_reduced = jnp.transpose(mine_parts, (1, 0, 2)).reshape(-1, width).astype(jnp.float32)
    attn_reduced = joined_reduced[:attn_cols].T
    ffn_reduced = joined_reduced[attn_cols:].T
    attn_new, attn_moment, attn_average = apply_update(
        attn_weights, attn_reduced, attn_momentum, attn_averaged, decay_rate
    )
    ffn_new, ffn_moment, ffn_average = apply_update(
        ffn_weights, ffn_reduced, ffn_momentum, ffn_averaged, decay_rate
    )
    vector_new, vector_moment, vector_average = apply_update(
        vectors, vector_reduced, vector_momentum, vector_averaged, 0.0
    )
    return (
        mean_loss,
        input_grad,
        attn_reduced,
        ffn_reduced,
        vector_reduced,
        attn_new,
        ffn_new,
        vector_new,
        attn_moment,
        ffn_moment,
        vector_moment,
        attn_average,
        ffn_average,
        vector_average,
    )


def solution(mesh):
    in_specs = (
        P(("dp", "rep"), None),
        P(("dp", "rep"), None),
        P(("dp", "rep")),
        P(None, ("dp", "rep")),
        P(None, ("dp", "rep")),
        P(("dp", "rep")),
        P(None, ("dp", "rep")),
        P(None, ("dp", "rep")),
        P(("dp", "rep")),
        P(None, ("dp", "rep")),
        P(None, ("dp", "rep")),
        P(("dp", "rep")),
    )
    out_specs = (
        P(),
        P(("dp", "rep"), None),
        P(None, ("dp", "rep")),
        P(None, ("dp", "rep")),
        P(("dp", "rep")),
        P(None, ("dp", "rep")),
        P(None, ("dp", "rep")),
        P(("dp", "rep")),
        P(None, ("dp", "rep")),
        P(None, ("dp", "rep")),
        P(("dp", "rep")),
        P(None, ("dp", "rep")),
        P(None, ("dp", "rep")),
        P(("dp", "rep")),
    )
    return jax.shard_map(shards, mesh=mesh, in_specs=in_specs, out_specs=out_specs, check_vma=False)
```

```python
import functools
import math

import jax
import jax.numpy as jnp
from jax import lax
from jax.experimental import pallas as pl
from jax.experimental.pallas import tpu as pltpu
from jax.sharding import PartitionSpec as P

MESH = pl.DeviceIdType.MESH
GRAD_SEND = jnp.bfloat16
AXES = ("dp", "rep")

HEADS = 12
HD = 64
SEGS = 16


ln_epsilon = 1e-12
pool_epsilon = 1e-06
logit_divisor = 0.025
learn_rate = 0.01
momentum_rate = 0.9
decay_rate = 0.01
average_rate = 0.75
masked_value = -1e30


def layer_norm_parts(values, gain, shift):
    per_line_average = jnp.mean(values, -1, keepdims=True)
    centred = values - per_line_average
    inverse = lax.rsqrt(jnp.mean(centred * centred, -1, keepdims=True) + ln_epsilon)
    normal_part = centred * inverse
    return (normal_part * gain + shift, normal_part, inverse)


def layer_norm_back(grad_out, normal_part, inverse, gain):
    scaled = grad_out * gain
    grad_in = inverse * (
        scaled
        - jnp.mean(scaled, -1, keepdims=True)
        - normal_part * jnp.mean(scaled * normal_part, -1, keepdims=True)
    )
    return (grad_in, jnp.sum(grad_out * normal_part, 0), jnp.sum(grad_out, 0))


def row_scores(query_one, key_one, segment_one, scale):
    scores = (
        jnp.einsum("qhd,khd->hqk", query_one, key_one, preferred_element_type=jnp.float32) * scale
    )
    same_text = segment_one[:, None] == segment_one[None, :]
    return jnp.where(same_text[None], scores, masked_value)


def attend_rows(query_rows, key_rows, value_rows, row_segments):
    scale = 1.0 / math.sqrt(query_rows.shape[-1])

    def one_row(row_args):
        query_one, key_one, value_one, segment_one = row_args
        scores = row_scores(query_one, key_one, segment_one, scale)
        row_max = jnp.max(scores, -1, keepdims=True)
        exp_scores = jnp.exp(scores - row_max)
        sums = jnp.sum(exp_scores, -1, keepdims=True)
        attn_probs = exp_scores / sums
        mixed = jnp.einsum(
            "hqk,khd->qhd",
            attn_probs.astype(jnp.bfloat16),
            value_one,
            preferred_element_type=jnp.float32,
        )
        return (mixed.astype(jnp.bfloat16), (row_max + jnp.log(sums))[..., 0])

    return lax.map(one_row, (query_rows, key_rows, value_rows, row_segments))


def attend_back(query_rows, key_rows, value_rows, row_segments, log_norm, grad_mixed):
    scale = 1.0 / math.sqrt(query_rows.shape[-1])

    def one_row(row_args):
        query_one, key_one, value_one, segment_one, norm_one, grad_one = row_args
        scores = row_scores(query_one, key_one, segment_one, scale)
        attn_probs = jnp.exp(scores - norm_one[..., None])
        grad_value = jnp.einsum(
            "hqk,qhd->khd",
            attn_probs.astype(jnp.bfloat16),
            grad_one,
            preferred_element_type=jnp.float32,
        )
        grad_probs = jnp.einsum(
            "qhd,khd->hqk", grad_one, value_one, preferred_element_type=jnp.float32
        )
        inner = jnp.sum(attn_probs * grad_probs, -1, keepdims=True)
        grad_scores = (attn_probs * (grad_probs - inner)).astype(jnp.bfloat16)
        grad_query = (
            jnp.einsum("hqk,khd->qhd", grad_scores, key_one, preferred_element_type=jnp.float32)
            * scale
        )
        grad_key = (
            jnp.einsum("hqk,qhd->khd", grad_scores, query_one, preferred_element_type=jnp.float32)
            * scale
        )
        return jnp.concatenate([grad_query, grad_key, grad_value], axis=1)

    return lax.map(one_row, (query_rows, key_rows, value_rows, row_segments, log_norm, grad_mixed))


def attention_back_kernel(scale, q_ref, k_ref, v_ref, g_ref, norm_ref, seg_col_ref, seg_row_ref, dq_ref, dk_ref, dv_ref):
    pair = pl.program_id(1)
    width = q_ref.shape[1]
    half = width // 2
    lane = lax.broadcasted_iota(jnp.int32, (1, width), 1)
    same = seg_col_ref[...] == seg_row_ref[0]
    norms = norm_ref[...]
    norm_lane = lax.broadcasted_iota(jnp.int32, norms.shape, 1)
    q = q_ref[...]
    k = k_ref[...]
    v = v_ref[...]
    g = g_ref[...]
    zero_b = jnp.zeros_like(q)
    on_last = (((1,), (1,)), ((), ()))
    on_first = (((0,), (0,)), ((), ()))
    dq = jnp.zeros(q.shape, jnp.float32)
    dk = jnp.zeros(q.shape, jnp.float32)
    dv = jnp.zeros(q.shape, jnp.float32)
    for head in range(2):
        mine = (lane >= head * half) & (lane < (head + 1) * half)
        q_h = jnp.where(mine, q, zero_b)
        g_h = jnp.where(mine, g, zero_b)
        norm_h = jnp.sum(jnp.where(norm_lane == 2 * pair + head, norms, 0.0), 1, keepdims=True)
        scores = lax.dot_general(q_h, k, on_last, preferred_element_type=jnp.float32) * scale
        scores = jnp.where(same, scores, masked_value)
        probs = jnp.exp(scores - norm_h)
        grad_v = lax.dot_general(probs.astype(jnp.bfloat16), g, on_first, preferred_element_type=jnp.float32)
        grad_p = lax.dot_general(g_h, v, on_last, preferred_element_type=jnp.float32)
        inner = jnp.sum(probs * grad_p, -1, keepdims=True)
        grad_s = (probs * (grad_p - inner)).astype(jnp.bfloat16)
        grad_q = jnp.dot(grad_s, k, preferred_element_type=jnp.float32) * scale
        grad_k = lax.dot_general(grad_s, q, on_first, preferred_element_type=jnp.float32) * scale
        dq = jnp.where(mine, grad_q, dq)
        dk = jnp.where(mine, grad_k, dk)
        dv = jnp.where(mine, grad_v, dv)
    dq_ref[...] = dq.astype(dq_ref.dtype)
    dk_ref[...] = dk.astype(dk_ref.dtype)
    dv_ref[...] = dv.astype(dv_ref.dtype)


def attention_back(qkv_rows, grad_mixed_flat, norm_tokens, segments, heads, head_dim):
    tokens, three_width = qkv_rows.shape
    width = three_width // 3
    rows, seq_len = segments.shape
    pair_width = 2 * head_dim
    pairs = heads // 2
    seg_col = segments.reshape(tokens, 1)
    seg_row = segments.reshape(rows, 1, seq_len)
    scale = 1.0 / math.sqrt(head_dim)
    out = jax.ShapeDtypeStruct((tokens, width), jnp.bfloat16)
    return pl.pallas_call(
        functools.partial(attention_back_kernel, scale),
        grid=(rows, pairs),
        in_specs=[
            pl.BlockSpec((seq_len, pair_width), lambda r, p: (r, p)),
            pl.BlockSpec((seq_len, pair_width), lambda r, p: (r, pairs + p)),
            pl.BlockSpec((seq_len, pair_width), lambda r, p: (r, 2 * pairs + p)),
            pl.BlockSpec((seq_len, pair_width), lambda r, p: (r, p)),
            pl.BlockSpec((seq_len, heads), lambda r, p: (r, 0)),
            pl.BlockSpec((seq_len, 1), lambda r, p: (r, 0)),
            pl.BlockSpec((1, 1, seq_len), lambda r, p: (r, 0, 0)),
        ],
        out_specs=[pl.BlockSpec((seq_len, pair_width), lambda r, p: (r, p))] * 3,
        out_shape=[out, out, out],
        compiler_params=pltpu.CompilerParams(vmem_limit_bytes=48 * 1024 * 1024),
        cost_estimate=pl.CostEstimate(
            flops=10 * rows * heads * seq_len * seq_len * pair_width,
            transcendentals=rows * heads * seq_len * seq_len,
            bytes_accessed=tokens * (three_width + 4 * width) * 2,
        ),
    )(qkv_rows, qkv_rows, qkv_rows, grad_mixed_flat, norm_tokens, seg_col, seg_row)


def apply_update(weight, grad, moment, average, decay):
    step_grad = grad + decay * weight
    new_moment = momentum_rate * moment + step_grad
    new_weight = weight - learn_rate * (step_grad + momentum_rate * new_moment)
    fresh_running_mean = average_rate * average + (1.0 - average_rate) * new_weight
    return (new_weight, new_moment, fresh_running_mean)


def bf16_round(values):
    return lax.reduce_precision(values, exponent_bits=8, mantissa_bits=7)


def flat_index(sizes):
    idx = 0
    for name, size in zip(AXES, sizes):
        idx = idx * size + lax.axis_index(name)
    return idx


def device_of(flat, sizes):
    coords = []
    for size in reversed(sizes):
        coords.append(lax.rem(flat, size))
        flat = flat // size
    return tuple(reversed(coords))


def enter_all(n, sizes, me):
    barrier = pltpu.get_barrier_semaphore()

    def greet(k, carry):
        peer = lax.rem(me + k, n)
        pl.semaphore_signal(barrier, inc=1, device_id=device_of(peer, sizes), device_id_type=MESH)
        return carry

    lax.fori_loop(1, n, greet, 0)
    pl.semaphore_wait(barrier, n - 1)


def gather_kernel(n, sizes, x_ref, out_ref, send_sem, recv_sem):
    me = flat_index(sizes)
    enter_all(n, sizes, me)

    def send(k, carry):
        peer = lax.rem(me + k, n)
        pltpu.make_async_remote_copy(
            src_ref=x_ref, dst_ref=out_ref.at[me], send_sem=send_sem.at[k], recv_sem=recv_sem.at[me],
            device_id=device_of(peer, sizes), device_id_type=MESH,
        ).start()
        return carry

    lax.fori_loop(1, n, send, 0)
    out_ref[me] = x_ref[...]

    def finish(k, carry):
        peer = lax.rem(me + k, n)
        src = lax.rem(me + n - k, n)
        pltpu.make_async_remote_copy(
            src_ref=x_ref, dst_ref=out_ref.at[me], send_sem=send_sem.at[k], recv_sem=recv_sem.at[me],
            device_id=device_of(peer, sizes), device_id_type=MESH,
        ).wait_send()
        pltpu.make_async_remote_copy(
            src_ref=x_ref, dst_ref=out_ref.at[src], send_sem=send_sem.at[k], recv_sem=recv_sem.at[src],
            device_id=device_of(src, sizes), device_id_type=MESH,
        ).wait_recv()
        return carry

    lax.fori_loop(1, n, finish, 0)


def small_gather(x, sizes, cid):
    n = math.prod(sizes)
    return pl.pallas_call(
        functools.partial(gather_kernel, n, sizes),
        out_shape=jax.ShapeDtypeStruct((n,) + x.shape, x.dtype),
        in_specs=[pl.BlockSpec(memory_space=pltpu.VMEM)],
        out_specs=pl.BlockSpec(memory_space=pltpu.VMEM),
        scratch_shapes=[pltpu.SemaphoreType.DMA((n,)), pltpu.SemaphoreType.DMA((n,))],
        compiler_params=pltpu.CompilerParams(collective_id=cid, has_side_effects=True),
    )(x)


def scatter_kernel(n, sizes, x_ref, out_ref, send_sem, recv_sem):
    me = flat_index(sizes)
    enter_all(n, sizes, me)

    def send(k, carry):
        peer = lax.rem(me + k, n)
        pltpu.make_async_remote_copy(
            src_ref=x_ref.at[peer], dst_ref=out_ref.at[me], send_sem=send_sem.at[k], recv_sem=recv_sem.at[me],
            device_id=device_of(peer, sizes), device_id_type=MESH,
        ).start()
        return carry

    lax.fori_loop(1, n, send, 0)
    out_ref[me] = x_ref[me]

    def finish(k, carry):
        peer = lax.rem(me + k, n)
        src = lax.rem(me + n - k, n)
        pltpu.make_async_remote_copy(
            src_ref=x_ref.at[peer], dst_ref=out_ref.at[me], send_sem=send_sem.at[k], recv_sem=recv_sem.at[me],
            device_id=device_of(peer, sizes), device_id_type=MESH,
        ).wait_send()
        pltpu.make_async_remote_copy(
            src_ref=x_ref.at[src], dst_ref=out_ref.at[src], send_sem=send_sem.at[k], recv_sem=recv_sem.at[src],
            device_id=device_of(src, sizes), device_id_type=MESH,
        ).wait_recv()
        return carry

    lax.fori_loop(1, n, finish, 0)


def small_scatter(x, sizes, cid):
    n = math.prod(sizes)
    return pl.pallas_call(
        functools.partial(scatter_kernel, n, sizes),
        out_shape=jax.ShapeDtypeStruct(x.shape, x.dtype),
        in_specs=[pl.BlockSpec(memory_space=pltpu.VMEM)],
        out_specs=pl.BlockSpec(memory_space=pltpu.VMEM),
        scratch_shapes=[pltpu.SemaphoreType.DMA((n,)), pltpu.SemaphoreType.DMA((n,))],
        compiler_params=pltpu.CompilerParams(collective_id=cid, has_side_effects=True),
    )(x)


def pair_gather_kernel(n, sizes, x_ref, out_ref, local_sem, send1, recv1, send2, recv2, send3, recv3):
    me = flat_index(sizes)
    chips = n // 2
    chip = me // 2
    core = lax.rem(me, 2)
    partner = me + 1 - 2 * core
    enter_all(n, sizes, me)

    local = pltpu.make_async_copy(x_ref, out_ref.at[me], local_sem)
    local.start()
    first = pltpu.make_async_remote_copy(
        src_ref=x_ref, dst_ref=out_ref.at[me], send_sem=send1, recv_sem=recv1,
        device_id=device_of(partner, sizes), device_id_type=MESH,
    )
    first.start()
    local.wait()
    first.wait_send()
    pltpu.make_async_remote_copy(
        src_ref=x_ref, dst_ref=out_ref.at[partner], send_sem=send1, recv_sem=recv1,
        device_id=device_of(partner, sizes), device_id_type=MESH,
    ).wait_recv()

    def pair(c):
        return out_ref.at[pl.ds(2 * c, 2)]

    def target(k):
        return lax.rem(chip + 2 * k - 1 + core, chips)

    def source(k):
        return lax.rem(chip + chips - (2 * k - 1 + core), chips)

    count = (chips - core) // 2

    def send_out(k, carry):
        other = target(k)
        pltpu.make_async_remote_copy(
            src_ref=pair(chip), dst_ref=pair(chip), send_sem=send2.at[other], recv_sem=recv2.at[chip],
            device_id=device_of(2 * other + core, sizes), device_id_type=MESH,
        ).start()
        return carry

    lax.fori_loop(1, count + 1, send_out, 0)

    def take_in(k, carry):
        other = source(k)
        pltpu.make_async_remote_copy(
            src_ref=pair(other), dst_ref=pair(other), send_sem=send2.at[other], recv_sem=recv2.at[other],
            device_id=device_of(2 * other + core, sizes), device_id_type=MESH,
        ).wait_recv()
        pltpu.make_async_remote_copy(
            src_ref=pair(other), dst_ref=pair(other), send_sem=send3.at[other], recv_sem=recv3.at[other],
            device_id=device_of(partner, sizes), device_id_type=MESH,
        ).start()
        return carry

    lax.fori_loop(1, count + 1, take_in, 0)

    def sent_out(k, carry):
        other = target(k)
        pltpu.make_async_remote_copy(
            src_ref=pair(chip), dst_ref=pair(chip), send_sem=send2.at[other], recv_sem=recv2.at[chip],
            device_id=device_of(2 * other + core, sizes), device_id_type=MESH,
        ).wait_send()
        return carry

    lax.fori_loop(1, count + 1, sent_out, 0)

    def forwarded(k, carry):
        other = source(k)
        pltpu.make_async_remote_copy(
            src_ref=pair(other), dst_ref=pair(other), send_sem=send3.at[other], recv_sem=recv3.at[other],
            device_id=device_of(partner, sizes), device_id_type=MESH,
        ).wait_send()
        return carry

    lax.fori_loop(1, count + 1, forwarded, 0)

    other_count = (chips - (1 - core)) // 2

    def partner_source(k):
        return lax.rem(chip + chips - (2 * k - 1 + (1 - core)), chips)

    def from_partner(k, carry):
        other = partner_source(k)
        pltpu.make_async_remote_copy(
            src_ref=pair(other), dst_ref=pair(other), send_sem=send3.at[other], recv_sem=recv3.at[other],
            device_id=device_of(partner, sizes), device_id_type=MESH,
        ).wait_recv()
        return carry

    lax.fori_loop(1, other_count + 1, from_partner, 0)


def pair_gather(x, sizes, cid):
    n = math.prod(sizes)
    chips = n // 2
    dma = pltpu.SemaphoreType.DMA
    return pl.pallas_call(
        functools.partial(pair_gather_kernel, n, sizes),
        out_shape=jax.ShapeDtypeStruct((n,) + x.shape, x.dtype),
        in_specs=[pl.BlockSpec(memory_space=pltpu.VMEM)],
        out_specs=pl.BlockSpec(memory_space=pltpu.VMEM),
        scratch_shapes=[dma(()), dma(()), dma(()), dma((chips,)), dma((chips,)), dma((chips,)), dma((chips,))],
        compiler_params=pltpu.CompilerParams(collective_id=cid, has_side_effects=True),
    )(x)


def halving_orders(n, parts):
    bits = n.bit_length() - 1
    middle = list(range(1, bits - 1))
    orders = []
    for p in range(parts):
        shift = p % len(middle) if middle else 0
        orders.append(tuple([0] + middle[shift:] + middle[:shift] + [bits - 1]))
    return tuple(orders)


def halving_kernel(n, sizes, orders, cols, tile, groups, *refs):
    count = sum(groups)
    sources = refs[:count]
    vec_ref, dq_ref, w_ref, res_ref, out_ref, vec_out, grad_out, work = refs[count : count + 8]
    rest = refs[count + 8 :]
    grouped = []
    at = 0
    for g in groups:
        grouped.append(sources[at : at + g])
        at += g
    steps = len(orders[0])
    parts = len(orders)
    layout = []
    head = 0
    for group in grouped:
        size = sum(math.prod(s.shape[:-1]) for s in group) // n
        layout.append((group, size, head))
        head += size
    recvs = rest[:steps]
    local_sem, send_sems, recv_sems, vec_send, vec_recv = rest[steps:]
    me = flat_index(sizes)

    def partner_of(bit):
        mine = lax.rem(me // (2**bit), 2)
        return mine, me + (1 - 2 * mine) * (2**bit)

    enter_all(n, sizes, me)

    def vec_copy(k):
        peer = lax.rem(me + k, n)
        return pltpu.make_async_remote_copy(
            src_ref=vec_ref.at[peer], dst_ref=vec_out.at[me], send_sem=vec_send.at[k], recv_sem=vec_recv.at[me],
            device_id=device_of(peer, sizes), device_id_type=MESH,
        )

    def vec_start(k, carry):
        vec_copy(k).start()
        return carry

    lax.fori_loop(1, n, vec_start, 0)
    vec_out[me] = vec_ref[me]

    half = n // 2
    first = []
    for p in range(parts):
        order = orders[p]
        mine, other = partner_of(order[0])
        column = pl.ds(p * cols, cols)

        def owner(j, side, order=order):
            o = side * (2 ** order[0])
            for m, bit in enumerate(order[1:]):
                o = o + lax.rem(j // (2 ** (steps - 2 - m)), 2) * (2**bit)
            return o

        def issue(j, carry, p=p, owner=owner, mine=mine, other=other, column=column):
            for o, dst, remote in ((owner(j, 1 - mine), recvs[0].at[p, j], True), (owner(j, mine), work.at[p, j], False)):
                for group, size, head in layout:
                    offset = 0
                    for chosen in group:
                        split = math.prod(chosen.shape[:-1]) // size

                        def move(chosen=chosen, offset=offset, o=o, dst=dst, remote=remote, size=size, head=head):
                            if len(chosen.shape) == 3:
                                src_ref = chosen.at[o - offset, :, column]
                            else:
                                src_ref = chosen.at[pl.ds((o - offset) * size, size), column]
                            dst_ref = dst.at[pl.ds(head, size)]
                            if remote:
                                pltpu.make_async_remote_copy(
                                    src_ref=src_ref, dst_ref=dst_ref,
                                    send_sem=send_sems.at[p, 0], recv_sem=recv_sems.at[p, 0],
                                    device_id=device_of(other, sizes), device_id_type=MESH,
                                ).start()
                            else:
                                pltpu.make_async_copy(src_ref, dst_ref, local_sem.at[p]).start()

                        if len(group) == 1:
                            move()
                        else:
                            pl.when((o >= offset) & (o < offset + split))(move)
                        offset += split

            return carry

        lax.fori_loop(0, half, issue, 0)
        first.append(other)
    for p in range(parts):
        whole = pltpu.make_async_remote_copy(
            src_ref=work.at[p, pl.ds(0, half)], dst_ref=recvs[0].at[p],
            send_sem=send_sems.at[p, 0], recv_sem=recv_sems.at[p, 0],
            device_id=device_of(first[p], sizes), device_id_type=MESH,
        )
        pltpu.make_async_copy(work.at[p, pl.ds(0, half)], work.at[p, pl.ds(0, half)], local_sem.at[p]).wait()
        whole.wait_recv()
        whole.wait_send()

        def accumulate0(i, carry, p=p):
            total = work[p, i].astype(jnp.float32) + recvs[0][p, i].astype(jnp.float32)
            work[p, i] = total.astype(work.dtype)
            return carry

        lax.fori_loop(0, half, accumulate0, 0)

    for step in range(1, steps):
        half = n >> (step + 1)
        copies = []
        for p in range(parts):
            mine, other = partner_of(orders[p][step])
            send = pltpu.make_async_remote_copy(
                src_ref=work.at[p, pl.ds((1 - mine) * half, half)], dst_ref=recvs[step].at[p],
                send_sem=send_sems.at[p, step], recv_sem=recv_sems.at[p, step],
                device_id=device_of(other, sizes), device_id_type=MESH,
            )
            send.start()
            copies.append((mine, send))
        if step == 1:
            def product(t, carry):
                rows = pl.ds(pl.multiple_of(t * tile, tile), tile)
                grad_out[rows, :] = (
                    jnp.dot(dq_ref[rows, :], w_ref[...], preferred_element_type=jnp.float32) + res_ref[rows, :]
                )
                return carry

            lax.fori_loop(0, grad_out.shape[0] // tile, product, 0)
        for p in range(parts):
            mine, send = copies[p]
            send.wait_recv()
            send.wait_send()

            def accumulate(i, carry, p=p, mine=mine, half=half, step=step):
                total = work[p, mine * half + i].astype(jnp.float32) + recvs[step][p, i].astype(jnp.float32)
                work[p, i] = total.astype(work.dtype)
                return carry

            lax.fori_loop(0, half, accumulate, 0)
    for p in range(parts):
        out_ref[p] = work[p, 0]

    def vec_finish(k, carry):
        vec_copy(k).wait_send()
        src = lax.rem(me + n - k, n)
        pltpu.make_async_remote_copy(
            src_ref=vec_ref.at[src], dst_ref=vec_out.at[src], send_sem=vec_send.at[k], recv_sem=vec_recv.at[src],
            device_id=device_of(src, sizes), device_id_type=MESH,
        ).wait_recv()
        return carry

    lax.fori_loop(1, n, vec_finish, 0)


def halving_scatter(grouped, vec, grad_b, weight_t, residual, sizes, parts, cid):
    n = math.prod(sizes)
    groups = tuple(len(g) for g in grouped)
    grads = [s for g in grouped for s in g]
    width = grads[0].shape[-1]
    rows = sum(math.prod(g.shape[:-1]) for g in grads) // n
    cols = width // parts
    orders = halving_orders(n, parts)
    steps = len(orders[0])
    dtype = grads[0].dtype
    tile = 128
    dma = pltpu.SemaphoreType.DMA
    vmem = pl.BlockSpec(memory_space=pltpu.VMEM)
    scratch = [pltpu.VMEM((parts, n // 2, rows, cols), dtype)]
    scratch += [pltpu.VMEM((parts, n >> (k + 1), rows, cols), dtype) for k in range(steps)]
    scratch += [dma((parts,)), dma((parts, steps)), dma((parts, steps)), dma((n,)), dma((n,))]
    return pl.pallas_call(
        functools.partial(halving_kernel, n, sizes, orders, cols, tile, groups),
        out_shape=(
            jax.ShapeDtypeStruct((parts, rows, cols), dtype),
            jax.ShapeDtypeStruct(vec.shape, vec.dtype),
            jax.ShapeDtypeStruct(residual.shape, jnp.float32),
        ),
        in_specs=[pl.BlockSpec(memory_space=pl.ANY)] * len(grads) + [vmem, vmem, vmem, vmem],
        out_specs=(vmem, vmem, vmem),
        scratch_shapes=scratch,
        compiler_params=pltpu.CompilerParams(
            collective_id=cid, has_side_effects=True, vmem_limit_bytes=60 * 1024 * 1024
        ),
    )(*grads, vec, grad_b, weight_t, residual)


def contrastive(embed_b, gathered, partner_all, me):
    own_texts = embed_b.shape[0]
    all_texts = gathered.shape[0]
    chunk = min(all_texts, 1024)
    on_rows = (((1,), (1,)), ((), ()))

    def chunk_stats(c):
        rows_b = lax.dynamic_slice_in_dim(gathered, c * chunk, chunk)
        sim = lax.dot_general(rows_b, gathered, on_rows, preferred_element_type=jnp.float32) / logit_divisor
        column_ids = lax.broadcasted_iota(jnp.int32, sim.shape, 1)
        row_ids = lax.broadcasted_iota(jnp.int32, sim.shape, 0) + c * chunk
        masked = jnp.where(column_ids == row_ids, masked_value, sim)
        row_max = jnp.max(masked, -1, keepdims=True)
        log_sum = row_max + jnp.log(jnp.sum(jnp.exp(masked - row_max), -1, keepdims=True))
        wanted = lax.dynamic_slice_in_dim(partner_all, c * chunk, chunk)
        positive = jnp.sum(jnp.where(column_ids == wanted[:, None], sim, 0.0), -1)
        return log_sum[:, 0], positive

    if all_texts == chunk:
        log_sum_all, positive_all = chunk_stats(0)
    else:
        log_sum_all, positive_all = lax.map(chunk_stats, jnp.arange(all_texts // chunk))
        log_sum_all = log_sum_all.reshape(-1)
        positive_all = positive_all.reshape(-1)
    mean_loss = jnp.sum(log_sum_all - positive_all) / all_texts

    own_start = me * own_texts
    own_ids = lax.broadcasted_iota(jnp.int32, (own_texts,), 0) + own_start
    own_partner = lax.dynamic_slice_in_dim(partner_all, own_start, own_texts)
    own_log_sum = lax.dynamic_slice_in_dim(log_sum_all, own_start, own_texts)

    sim_rows = lax.dot_general(embed_b, gathered, on_rows, preferred_element_type=jnp.float32) / logit_divisor
    column_ids = lax.broadcasted_iota(jnp.int32, sim_rows.shape, 1)
    masked_rows = jnp.where(column_ids == own_ids[:, None], masked_value, sim_rows)
    grad_rows = (
        jnp.exp(masked_rows - own_log_sum[:, None]) - (column_ids == own_partner[:, None]).astype(jnp.float32)
    ).astype(jnp.bfloat16)

    sim_cols = lax.dot_general(gathered, embed_b, on_rows, preferred_element_type=jnp.float32) / logit_divisor
    row_ids = lax.broadcasted_iota(jnp.int32, sim_cols.shape, 0)
    masked_cols = jnp.where(row_ids == own_ids[None, :], masked_value, sim_cols)
    grad_cols = (
        jnp.exp(masked_cols - log_sum_all[:, None]) - (partner_all[:, None] == own_ids[None, :]).astype(jnp.float32)
    ).astype(jnp.bfloat16)

    on_tokens = (((0,), (0,)), ((), ()))
    embedding_gradient = (
        jnp.dot(grad_rows, gathered, preferred_element_type=jnp.float32)
        + lax.dot_general(grad_cols, gathered, on_tokens, preferred_element_type=jnp.float32)
    ) / logit_divisor
    return mean_loss, embedding_gradient


def shards(
    hidden_in,
    segments,
    partner,
    attn_weights,
    ffn_weights,
    vectors,
    attn_momentum,
    ffn_momentum,
    vector_momentum,
    attn_averaged,
    ffn_averaged,
    vector_averaged,
):
    sizes = tuple(lax.axis_size(name) for name in AXES)
    n_dev = math.prod(sizes)
    me = flat_index(sizes)
    vec_len = vectors.shape[0]
    small = jnp.concatenate([vectors, partner.astype(jnp.float32)])[None, :]
    small_all = small_gather(small, sizes, 0)[:, 0, :]
    vector_f = bf16_round(small_all[:, :vec_len].reshape(-1))
    partner_all = small_all[:, vec_len:].reshape(-1).astype(jnp.int32)
    attn_full, ffn_full = (
        lax.all_gather(attn_weights.astype(jnp.bfloat16), AXES, axis=1, tiled=True),
        lax.all_gather(ffn_weights.astype(jnp.bfloat16), AXES, axis=1, tiled=True),
    )
    width = attn_full.shape[0]
    hidden = ffn_full.shape[1] // 2
    query_bias = vector_f[0:width]
    value_bias = vector_f[width : 2 * width]
    output_bias = vector_f[2 * width : 3 * width]
    gain_first = vector_f[3 * width : 4 * width]
    shift_first = vector_f[4 * width : 5 * width]
    upper_bias = vector_f[5 * width : 5 * width + hidden]
    lower_bias = vector_f[5 * width + hidden : 6 * width + hidden]
    gain_second = vector_f[6 * width + hidden : 7 * width + hidden]
    shift_second = vector_f[7 * width + hidden : 8 * width + hidden]
    w_qkv = attn_full[:, : 3 * width]
    w_output = attn_full[:, 3 * width :]
    w_upper = ffn_full[:, :hidden]
    w_lower = ffn_full[:, hidden:]
    rows_dev, seq_len = segments.shape
    tokens_n = rows_dev * seq_len
    on_rows = (((1,), (1,)), ((), ()))
    on_tokens = (((0,), (0,)), ((), ()))
    qkv_bias = jnp.concatenate([query_bias, jnp.zeros_like(query_bias), value_bias])
    qkv_rows = (jnp.dot(hidden_in, w_qkv, preferred_element_type=jnp.float32) + qkv_bias).astype(
        jnp.bfloat16
    )
    heads = qkv_rows.reshape(rows_dev, seq_len, 3, HEADS, HD)
    query_rows = heads[:, :, 0]
    key_rows = heads[:, :, 1]
    value_rows = heads[:, :, 2]
    mixed, log_norm = attend_rows(query_rows, key_rows, value_rows, segments)
    mixed_flat = mixed.reshape(tokens_n, width)
    first_sum = (
        hidden_in.astype(jnp.float32)
        + jnp.dot(mixed_flat, w_output, preferred_element_type=jnp.float32)
        + output_bias
    )
    normed, normal_one, inverse_one = layer_norm_parts(first_sum, gain_first, shift_first)
    normed_r = bf16_round(normed)
    normed_b = normed_r.astype(jnp.bfloat16)
    upper = lax.optimization_barrier(
        jnp.dot(normed_b, w_upper, preferred_element_type=jnp.float32) + upper_bias
    )
    active_b = jax.nn.gelu(upper, approximate=False).astype(jnp.bfloat16)
    second_sum = (
        normed_r
        + lax.dot_general(active_b, w_lower, on_rows, preferred_element_type=jnp.float32)
        + lower_bias
    )
    result, normal_two, inverse_two = layer_norm_parts(second_sum, gain_second, shift_second)
    text_ids = jnp.arange(SEGS, dtype=jnp.int32)
    one_hot = (segments[:, None, :] == text_ids[None, :, None]).astype(jnp.float32)
    counts = jnp.sum(one_hot, -1, keepdims=True)
    pooled = (
        jnp.einsum(
            "rts,rsd->rtd",
            one_hot,
            result.reshape(rows_dev, seq_len, width),
            precision=lax.Precision.HIGHEST,
        )
        / counts
    ).reshape(-1, width)
    inv_norm = lax.rsqrt(jnp.sum(pooled * pooled, -1, keepdims=True) + pool_epsilon)
    embed_b = (pooled * inv_norm).astype(jnp.bfloat16)
    gathered_embeddings = pair_gather(embed_b, sizes, 2).reshape(-1, width)
    mean_loss, embedding_gradient = contrastive(embed_b, gathered_embeddings, partner_all, me)
    grad_pooled = inv_norm * embedding_gradient - pooled * (
        inv_norm * inv_norm * inv_norm
    ) * jnp.sum(embedding_gradient * pooled, -1, keepdims=True)
    derivative_output = jnp.einsum(
        "rts,rtd->rsd",
        one_hot,
        grad_pooled.reshape(rows_dev, SEGS, width) / counts,
        precision=lax.Precision.HIGHEST,
    ).reshape(tokens_n, width)
    grad_second, gain_two_grad, shift_two_grad = layer_norm_back(
        derivative_output, normal_two, inverse_two, gain_second
    )
    lower_bias_grad = jnp.sum(grad_second, 0)
    lower_grad_b = grad_second.astype(jnp.bfloat16)
    lower_w_grad_t = lax.dot_general(
        active_b, lower_grad_b, on_tokens, preferred_element_type=jnp.float32
    )
    grad_active = jnp.dot(lower_grad_b, w_lower, preferred_element_type=jnp.float32)
    cumulative = 0.5 * (1.0 + lax.erf(upper / math.sqrt(2.0)))
    density = jnp.exp(-0.5 * upper * upper) / math.sqrt(2.0 * math.pi)
    grad_upper = grad_active * (cumulative + upper * density)
    upper_bias_grad = jnp.sum(grad_upper, 0)
    upper_grad_b = grad_upper.astype(jnp.bfloat16)
    upper_w_grad_t = lax.dot_general(
        upper_grad_b, normed_b, on_tokens, preferred_element_type=jnp.float32
    )
    grad_normed = (
        lax.dot_general(upper_grad_b, w_upper, on_rows, preferred_element_type=jnp.float32)
        + grad_second
    )
    grad_first, gain_one_grad, shift_one_grad = layer_norm_back(
        grad_normed, normal_one, inverse_one, gain_first
    )
    output_bias_grad = jnp.sum(grad_first, 0)
    first_grad_b = grad_first.astype(jnp.bfloat16)
    output_w_grad_t = lax.dot_general(
        first_grad_b, mixed_flat, on_tokens, preferred_element_type=jnp.float32
    )
    grad_mixed = lax.dot_general(
        first_grad_b, w_output, on_rows, preferred_element_type=jnp.float32
    ).astype(jnp.bfloat16)
    grad_mixed = grad_mixed.reshape(rows_dev, seq_len, HEADS, HD)
    norm_tokens = jnp.swapaxes(log_norm, 1, 2).reshape(tokens_n, HEADS)
    qkv_grad = jnp.concatenate(
        attention_back(qkv_rows, grad_mixed.reshape(tokens_n, width), norm_tokens, segments, HEADS, HD), 1
    ).astype(jnp.float32)
    qkv_grad_f = bf16_round(qkv_grad)
    qkv_grad_b = qkv_grad_f.astype(jnp.bfloat16)
    query_bias_grad = jnp.sum(qkv_grad_f[:, :width], 0)
    value_bias_grad = jnp.sum(qkv_grad_f[:, 2 * width :], 0)
    qkv_w_grad_t = lax.dot_general(
        qkv_grad_b, hidden_in, on_tokens, preferred_element_type=jnp.float32
    )
    vector_grad = jnp.concatenate(
        [
            query_bias_grad,
            value_bias_grad,
            output_bias_grad,
            gain_one_grad,
            shift_one_grad,
            upper_bias_grad,
            lower_bias_grad,
            gain_two_grad,
            shift_two_grad,
        ]
    )
    attn_cols = (qkv_w_grad_t.shape[0] + output_w_grad_t.shape[0]) // n_dev
    ffn_cols = (upper_w_grad_t.shape[0] + lower_w_grad_t.shape[0]) // n_dev
    if attn_cols % 16 == 0 and ffn_cols % 16 == 0:
        grads = (
            (qkv_w_grad_t.astype(GRAD_SEND), output_w_grad_t.astype(GRAD_SEND)),
            (upper_w_grad_t.astype(GRAD_SEND), lower_w_grad_t.astype(GRAD_SEND)),
        )
    else:
        attn_blocks = jnp.concatenate(
            [qkv_w_grad_t.reshape(-1, attn_cols, width), output_w_grad_t.reshape(-1, attn_cols, width)], 0
        )
        ffn_blocks = jnp.concatenate(
            [upper_w_grad_t.reshape(-1, ffn_cols, width), lower_w_grad_t.reshape(-1, ffn_cols, width)], 0
        )
        grads = ((jnp.concatenate([attn_blocks, ffn_blocks], 1).astype(GRAD_SEND),),)
    parts = 3
    mine_parts, vector_slots, input_grad = halving_scatter(
        grads, vector_grad.reshape(n_dev, 1, -1), qkv_grad_b, w_qkv.T, grad_first, sizes, parts, 3
    )
    vector_reduced = jnp.sum(vector_slots[:, 0, :], 0)
    joined_reduced = jnp.transpose(mine_parts, (1, 0, 2)).reshape(-1, width).astype(jnp.float32)
    attn_reduced = joined_reduced[:attn_cols].T
    ffn_reduced = joined_reduced[attn_cols:].T
    attn_new, attn_moment, attn_average = apply_update(
        attn_weights, attn_reduced, attn_momentum, attn_averaged, decay_rate
    )
    ffn_new, ffn_moment, ffn_average = apply_update(
        ffn_weights, ffn_reduced, ffn_momentum, ffn_averaged, decay_rate
    )
    vector_new, vector_moment, vector_average = apply_update(
        vectors, vector_reduced, vector_momentum, vector_averaged, 0.0
    )
    return (
        mean_loss,
        input_grad,
        attn_reduced,
        ffn_reduced,
        vector_reduced,
        attn_new,
        ffn_new,
        vector_new,
        attn_moment,
        ffn_moment,
        vector_moment,
        attn_average,
        ffn_average,
        vector_average,
    )


def solution(mesh):
    in_specs = (
        P(("dp", "rep"), None),
        P(("dp", "rep"), None),
        P(("dp", "rep")),
        P(None, ("dp", "rep")),
        P(None, ("dp", "rep")),
        P(("dp", "rep")),
        P(None, ("dp", "rep")),
        P(None, ("dp", "rep")),
        P(("dp", "rep")),
        P(None, ("dp", "rep")),
        P(None, ("dp", "rep")),
        P(("dp", "rep")),
    )
    out_specs = (
        P(),
        P(("dp", "rep"), None),
        P(None, ("dp", "rep")),
        P(None, ("dp", "rep")),
        P(("dp", "rep")),
        P(None, ("dp", "rep")),
        P(None, ("dp", "rep")),
        P(("dp", "rep")),
        P(None, ("dp", "rep")),
        P(None, ("dp", "rep")),
        P(("dp", "rep")),
        P(None, ("dp", "rep")),
        P(None, ("dp", "rep")),
        P(("dp", "rep")),
    )
    return jax.shard_map(shards, mesh=mesh, in_specs=in_specs, out_specs=out_specs, check_vma=False)
```

```python
import functools
import math

import jax
import jax.numpy as jnp
from jax import lax
from jax.experimental import pallas as pl
from jax.experimental.pallas import tpu as pltpu
from jax.sharding import PartitionSpec as P

MESH = pl.DeviceIdType.MESH
GRAD_SEND = jnp.bfloat16
AXES = ("dp", "rep")

HEADS = 12
HD = 64
SEGS = 16


ln_epsilon = 1e-12
pool_epsilon = 1e-06
logit_divisor = 0.025
learn_rate = 0.01
momentum_rate = 0.9
decay_rate = 0.01
average_rate = 0.75
masked_value = -1e30


def layer_norm_parts(values, gain, shift):
    per_line_average = jnp.mean(values, -1, keepdims=True)
    centred = values - per_line_average
    inverse = lax.rsqrt(jnp.mean(centred * centred, -1, keepdims=True) + ln_epsilon)
    normal_part = centred * inverse
    return (normal_part * gain + shift, normal_part, inverse)


def layer_norm_back(grad_out, normal_part, inverse, gain):
    scaled = grad_out * gain
    grad_in = inverse * (
        scaled
        - jnp.mean(scaled, -1, keepdims=True)
        - normal_part * jnp.mean(scaled * normal_part, -1, keepdims=True)
    )
    return (grad_in, jnp.sum(grad_out * normal_part, 0), jnp.sum(grad_out, 0))


def row_scores(query_one, key_one, segment_one, scale):
    scores = (
        jnp.einsum("qhd,khd->hqk", query_one, key_one, preferred_element_type=jnp.float32) * scale
    )
    same_text = segment_one[:, None] == segment_one[None, :]
    return jnp.where(same_text[None], scores, masked_value)


def attend_rows(query_rows, key_rows, value_rows, row_segments):
    scale = 1.0 / math.sqrt(query_rows.shape[-1])

    def one_row(row_args):
        query_one, key_one, value_one, segment_one = row_args
        scores = row_scores(query_one, key_one, segment_one, scale)
        row_max = jnp.max(scores, -1, keepdims=True)
        exp_scores = jnp.exp(scores - row_max)
        sums = jnp.sum(exp_scores, -1, keepdims=True)
        attn_probs = exp_scores / sums
        mixed = jnp.einsum(
            "hqk,khd->qhd",
            attn_probs.astype(jnp.bfloat16),
            value_one,
            preferred_element_type=jnp.float32,
        )
        return (mixed.astype(jnp.bfloat16), (row_max + jnp.log(sums))[..., 0])

    return lax.map(one_row, (query_rows, key_rows, value_rows, row_segments))


def attend_back(query_rows, key_rows, value_rows, row_segments, log_norm, grad_mixed):
    scale = 1.0 / math.sqrt(query_rows.shape[-1])

    def one_row(row_args):
        query_one, key_one, value_one, segment_one, norm_one, grad_one = row_args
        scores = row_scores(query_one, key_one, segment_one, scale)
        attn_probs = jnp.exp(scores - norm_one[..., None])
        grad_value = jnp.einsum(
            "hqk,qhd->khd",
            attn_probs.astype(jnp.bfloat16),
            grad_one,
            preferred_element_type=jnp.float32,
        )
        grad_probs = jnp.einsum(
            "qhd,khd->hqk", grad_one, value_one, preferred_element_type=jnp.float32
        )
        inner = jnp.sum(attn_probs * grad_probs, -1, keepdims=True)
        grad_scores = (attn_probs * (grad_probs - inner)).astype(jnp.bfloat16)
        grad_query = (
            jnp.einsum("hqk,khd->qhd", grad_scores, key_one, preferred_element_type=jnp.float32)
            * scale
        )
        grad_key = (
            jnp.einsum("hqk,qhd->khd", grad_scores, query_one, preferred_element_type=jnp.float32)
            * scale
        )
        return jnp.concatenate([grad_query, grad_key, grad_value], axis=1)

    return lax.map(one_row, (query_rows, key_rows, value_rows, row_segments, log_norm, grad_mixed))


def attention_back_kernel(scale, q_ref, k_ref, v_ref, g_ref, norm_ref, seg_col_ref, seg_row_ref, dq_ref, dk_ref, dv_ref):
    pair = pl.program_id(1)
    width = q_ref.shape[1]
    half = width // 2
    lane = lax.broadcasted_iota(jnp.int32, (1, width), 1)
    same = seg_col_ref[...] == seg_row_ref[0]
    norms = norm_ref[...]
    norm_lane = lax.broadcasted_iota(jnp.int32, norms.shape, 1)
    q = q_ref[...]
    k = k_ref[...]
    v = v_ref[...]
    g = g_ref[...]
    zero_b = jnp.zeros_like(q)
    on_last = (((1,), (1,)), ((), ()))
    on_first = (((0,), (0,)), ((), ()))
    dq = jnp.zeros(q.shape, jnp.float32)
    dk = jnp.zeros(q.shape, jnp.float32)
    dv = jnp.zeros(q.shape, jnp.float32)
    for head in range(2):
        mine = (lane >= head * half) & (lane < (head + 1) * half)
        q_h = jnp.where(mine, q, zero_b)
        g_h = jnp.where(mine, g, zero_b)
        norm_h = jnp.sum(jnp.where(norm_lane == 2 * pair + head, norms, 0.0), 1, keepdims=True)
        scores = lax.dot_general(q_h, k, on_last, preferred_element_type=jnp.float32) * scale
        scores = jnp.where(same, scores, masked_value)
        probs = jnp.exp(scores - norm_h)
        grad_v = lax.dot_general(probs.astype(jnp.bfloat16), g, on_first, preferred_element_type=jnp.float32)
        grad_p = lax.dot_general(g_h, v, on_last, preferred_element_type=jnp.float32)
        inner = jnp.sum(probs * grad_p, -1, keepdims=True)
        grad_s = (probs * (grad_p - inner)).astype(jnp.bfloat16)
        grad_q = jnp.dot(grad_s, k, preferred_element_type=jnp.float32) * scale
        grad_k = lax.dot_general(grad_s, q, on_first, preferred_element_type=jnp.float32) * scale
        dq = jnp.where(mine, grad_q, dq)
        dk = jnp.where(mine, grad_k, dk)
        dv = jnp.where(mine, grad_v, dv)
    dq_ref[...] = dq.astype(dq_ref.dtype)
    dk_ref[...] = dk.astype(dk_ref.dtype)
    dv_ref[...] = dv.astype(dv_ref.dtype)


def attention_back(qkv_rows, grad_mixed_flat, norm_tokens, segments, heads, head_dim):
    tokens, three_width = qkv_rows.shape
    width = three_width // 3
    rows, seq_len = segments.shape
    pair_width = 2 * head_dim
    pairs = heads // 2
    seg_col = segments.reshape(tokens, 1)
    seg_row = segments.reshape(rows, 1, seq_len)
    scale = 1.0 / math.sqrt(head_dim)
    out = jax.ShapeDtypeStruct((tokens, width), jnp.bfloat16)
    return pl.pallas_call(
        functools.partial(attention_back_kernel, scale),
        grid=(rows, pairs),
        in_specs=[
            pl.BlockSpec((seq_len, pair_width), lambda r, p: (r, p)),
            pl.BlockSpec((seq_len, pair_width), lambda r, p: (r, pairs + p)),
            pl.BlockSpec((seq_len, pair_width), lambda r, p: (r, 2 * pairs + p)),
            pl.BlockSpec((seq_len, pair_width), lambda r, p: (r, p)),
            pl.BlockSpec((seq_len, heads), lambda r, p: (r, 0)),
            pl.BlockSpec((seq_len, 1), lambda r, p: (r, 0)),
            pl.BlockSpec((1, 1, seq_len), lambda r, p: (r, 0, 0)),
        ],
        out_specs=[pl.BlockSpec((seq_len, pair_width), lambda r, p: (r, p))] * 3,
        out_shape=[out, out, out],
        compiler_params=pltpu.CompilerParams(vmem_limit_bytes=48 * 1024 * 1024),
        cost_estimate=pl.CostEstimate(
            flops=10 * rows * heads * seq_len * seq_len * pair_width,
            transcendentals=rows * heads * seq_len * seq_len,
            bytes_accessed=tokens * (three_width + 4 * width) * 2,
        ),
    )(qkv_rows, qkv_rows, qkv_rows, grad_mixed_flat, norm_tokens, seg_col, seg_row)


def apply_update(weight, grad, moment, average, decay):
    step_grad = grad + decay * weight
    new_moment = momentum_rate * moment + step_grad
    new_weight = weight - learn_rate * (step_grad + momentum_rate * new_moment)
    fresh_running_mean = average_rate * average + (1.0 - average_rate) * new_weight
    return (new_weight, new_moment, fresh_running_mean)


def bf16_round(values):
    return lax.reduce_precision(values, exponent_bits=8, mantissa_bits=7)


def flat_index(sizes):
    idx = 0
    for name, size in zip(AXES, sizes):
        idx = idx * size + lax.axis_index(name)
    return idx


def device_of(flat, sizes):
    coords = []
    for size in reversed(sizes):
        coords.append(lax.rem(flat, size))
        flat = flat // size
    return tuple(reversed(coords))


def enter_all(n, sizes, me):
    barrier = pltpu.get_barrier_semaphore()

    def greet(k, carry):
        peer = lax.rem(me + k, n)
        pl.semaphore_signal(barrier, inc=1, device_id=device_of(peer, sizes), device_id_type=MESH)
        return carry

    lax.fori_loop(1, n, greet, 0)
    pl.semaphore_wait(barrier, n - 1)


def gather_kernel(n, sizes, x_ref, out_ref, send_sem, recv_sem):
    me = flat_index(sizes)
    enter_all(n, sizes, me)

    def send(k, carry):
        peer = lax.rem(me + k, n)
        pltpu.make_async_remote_copy(
            src_ref=x_ref, dst_ref=out_ref.at[me], send_sem=send_sem.at[k], recv_sem=recv_sem.at[me],
            device_id=device_of(peer, sizes), device_id_type=MESH,
        ).start()
        return carry

    lax.fori_loop(1, n, send, 0)
    out_ref[me] = x_ref[...]

    def finish(k, carry):
        peer = lax.rem(me + k, n)
        src = lax.rem(me + n - k, n)
        pltpu.make_async_remote_copy(
            src_ref=x_ref, dst_ref=out_ref.at[me], send_sem=send_sem.at[k], recv_sem=recv_sem.at[me],
            device_id=device_of(peer, sizes), device_id_type=MESH,
        ).wait_send()
        pltpu.make_async_remote_copy(
            src_ref=x_ref, dst_ref=out_ref.at[src], send_sem=send_sem.at[k], recv_sem=recv_sem.at[src],
            device_id=device_of(src, sizes), device_id_type=MESH,
        ).wait_recv()
        return carry

    lax.fori_loop(1, n, finish, 0)


def small_gather(x, sizes, cid):
    n = math.prod(sizes)
    return pl.pallas_call(
        functools.partial(gather_kernel, n, sizes),
        out_shape=jax.ShapeDtypeStruct((n,) + x.shape, x.dtype),
        in_specs=[pl.BlockSpec(memory_space=pltpu.VMEM)],
        out_specs=pl.BlockSpec(memory_space=pltpu.VMEM),
        scratch_shapes=[pltpu.SemaphoreType.DMA((n,)), pltpu.SemaphoreType.DMA((n,))],
        compiler_params=pltpu.CompilerParams(collective_id=cid, has_side_effects=True),
    )(x)


def scatter_kernel(n, sizes, x_ref, out_ref, send_sem, recv_sem):
    me = flat_index(sizes)
    enter_all(n, sizes, me)

    def send(k, carry):
        peer = lax.rem(me + k, n)
        pltpu.make_async_remote_copy(
            src_ref=x_ref.at[peer], dst_ref=out_ref.at[me], send_sem=send_sem.at[k], recv_sem=recv_sem.at[me],
            device_id=device_of(peer, sizes), device_id_type=MESH,
        ).start()
        return carry

    lax.fori_loop(1, n, send, 0)
    out_ref[me] = x_ref[me]

    def finish(k, carry):
        peer = lax.rem(me + k, n)
        src = lax.rem(me + n - k, n)
        pltpu.make_async_remote_copy(
            src_ref=x_ref.at[peer], dst_ref=out_ref.at[me], send_sem=send_sem.at[k], recv_sem=recv_sem.at[me],
            device_id=device_of(peer, sizes), device_id_type=MESH,
        ).wait_send()
        pltpu.make_async_remote_copy(
            src_ref=x_ref.at[src], dst_ref=out_ref.at[src], send_sem=send_sem.at[k], recv_sem=recv_sem.at[src],
            device_id=device_of(src, sizes), device_id_type=MESH,
        ).wait_recv()
        return carry

    lax.fori_loop(1, n, finish, 0)


def small_scatter(x, sizes, cid):
    n = math.prod(sizes)
    return pl.pallas_call(
        functools.partial(scatter_kernel, n, sizes),
        out_shape=jax.ShapeDtypeStruct(x.shape, x.dtype),
        in_specs=[pl.BlockSpec(memory_space=pltpu.VMEM)],
        out_specs=pl.BlockSpec(memory_space=pltpu.VMEM),
        scratch_shapes=[pltpu.SemaphoreType.DMA((n,)), pltpu.SemaphoreType.DMA((n,))],
        compiler_params=pltpu.CompilerParams(collective_id=cid, has_side_effects=True),
    )(x)


def pair_gather_kernel(n, sizes, x_ref, out_ref, local_sem, send1, recv1, send2, recv2, send3, recv3):
    me = flat_index(sizes)
    chips = n // 2
    chip = me // 2
    core = lax.rem(me, 2)
    partner = me + 1 - 2 * core
    enter_all(n, sizes, me)

    local = pltpu.make_async_copy(x_ref, out_ref.at[me], local_sem)
    local.start()
    first = pltpu.make_async_remote_copy(
        src_ref=x_ref, dst_ref=out_ref.at[me], send_sem=send1, recv_sem=recv1,
        device_id=device_of(partner, sizes), device_id_type=MESH,
    )
    first.start()
    local.wait()
    first.wait_send()
    pltpu.make_async_remote_copy(
        src_ref=x_ref, dst_ref=out_ref.at[partner], send_sem=send1, recv_sem=recv1,
        device_id=device_of(partner, sizes), device_id_type=MESH,
    ).wait_recv()

    def pair(c):
        return out_ref.at[pl.ds(2 * c, 2)]

    def target(k):
        return lax.rem(chip + 2 * k - 1 + core, chips)

    def source(k):
        return lax.rem(chip + chips - (2 * k - 1 + core), chips)

    count = (chips - core) // 2

    def send_out(k, carry):
        other = target(k)
        pltpu.make_async_remote_copy(
            src_ref=pair(chip), dst_ref=pair(chip), send_sem=send2.at[other], recv_sem=recv2.at[chip],
            device_id=device_of(2 * other + core, sizes), device_id_type=MESH,
        ).start()
        return carry

    lax.fori_loop(1, count + 1, send_out, 0)

    def take_in(k, carry):
        other = source(k)
        pltpu.make_async_remote_copy(
            src_ref=pair(other), dst_ref=pair(other), send_sem=send2.at[other], recv_sem=recv2.at[other],
            device_id=device_of(2 * other + core, sizes), device_id_type=MESH,
        ).wait_recv()
        pltpu.make_async_remote_copy(
            src_ref=pair(other), dst_ref=pair(other), send_sem=send3.at[other], recv_sem=recv3.at[other],
            device_id=device_of(partner, sizes), device_id_type=MESH,
        ).start()
        return carry

    lax.fori_loop(1, count + 1, take_in, 0)

    def sent_out(k, carry):
        other = target(k)
        pltpu.make_async_remote_copy(
            src_ref=pair(chip), dst_ref=pair(chip), send_sem=send2.at[other], recv_sem=recv2.at[chip],
            device_id=device_of(2 * other + core, sizes), device_id_type=MESH,
        ).wait_send()
        return carry

    lax.fori_loop(1, count + 1, sent_out, 0)

    def forwarded(k, carry):
        other = source(k)
        pltpu.make_async_remote_copy(
            src_ref=pair(other), dst_ref=pair(other), send_sem=send3.at[other], recv_sem=recv3.at[other],
            device_id=device_of(partner, sizes), device_id_type=MESH,
        ).wait_send()
        return carry

    lax.fori_loop(1, count + 1, forwarded, 0)

    other_count = (chips - (1 - core)) // 2

    def partner_source(k):
        return lax.rem(chip + chips - (2 * k - 1 + (1 - core)), chips)

    def from_partner(k, carry):
        other = partner_source(k)
        pltpu.make_async_remote_copy(
            src_ref=pair(other), dst_ref=pair(other), send_sem=send3.at[other], recv_sem=recv3.at[other],
            device_id=device_of(partner, sizes), device_id_type=MESH,
        ).wait_recv()
        return carry

    lax.fori_loop(1, other_count + 1, from_partner, 0)


def pair_gather(x, sizes, cid):
    n = math.prod(sizes)
    chips = n // 2
    dma = pltpu.SemaphoreType.DMA
    return pl.pallas_call(
        functools.partial(pair_gather_kernel, n, sizes),
        out_shape=jax.ShapeDtypeStruct((n,) + x.shape, x.dtype),
        in_specs=[pl.BlockSpec(memory_space=pltpu.VMEM)],
        out_specs=pl.BlockSpec(memory_space=pltpu.VMEM),
        scratch_shapes=[dma(()), dma(()), dma(()), dma((chips,)), dma((chips,)), dma((chips,)), dma((chips,))],
        compiler_params=pltpu.CompilerParams(collective_id=cid, has_side_effects=True),
    )(x)


def halving_orders(n, parts):
    bits = n.bit_length() - 1
    middle = list(range(1, bits - 1))
    orders = []
    for p in range(parts):
        shift = p % len(middle) if middle else 0
        orders.append(tuple([0] + middle[shift:] + middle[:shift] + [bits - 1]))
    return tuple(orders)


def halving_kernel(n, sizes, orders, cols, tile, groups, *refs):
    count = sum(groups)
    sources = refs[:count]
    vec_ref, dq_ref, w_ref, res_ref, out_ref, vec_out, grad_out, work = refs[count : count + 8]
    rest = refs[count + 8 :]
    grouped = []
    at = 0
    for g in groups:
        grouped.append(sources[at : at + g])
        at += g
    steps = len(orders[0])
    parts = len(orders)
    layout = []
    head = 0
    for group in grouped:
        size = sum(math.prod(s.shape[:-1]) for s in group) // n
        layout.append((group, size, head))
        head += size
    recvs = rest[:steps]
    local_sem, send_sems, recv_sems, vec_send, vec_recv = rest[steps:]
    me = flat_index(sizes)

    def partner_of(bit):
        mine = lax.rem(me // (2**bit), 2)
        return mine, me + (1 - 2 * mine) * (2**bit)

    enter_all(n, sizes, me)

    def vec_copy(k):
        peer = lax.rem(me + k, n)
        return pltpu.make_async_remote_copy(
            src_ref=vec_ref.at[peer], dst_ref=vec_out.at[me], send_sem=vec_send.at[k], recv_sem=vec_recv.at[me],
            device_id=device_of(peer, sizes), device_id_type=MESH,
        )

    def vec_start(k, carry):
        vec_copy(k).start()
        return carry

    lax.fori_loop(1, n, vec_start, 0)
    vec_out[me] = vec_ref[me]

    half = n // 2
    first = []
    for p in range(parts):
        order = orders[p]
        mine, other = partner_of(order[0])
        column = pl.ds(p * cols, cols)

        def owner(j, side, order=order):
            o = side * (2 ** order[0])
            for m, bit in enumerate(order[1:]):
                o = o + lax.rem(j // (2 ** (steps - 2 - m)), 2) * (2**bit)
            return o

        def issue(j, carry, p=p, owner=owner, mine=mine, other=other, column=column):
            for o, dst, remote in ((owner(j, 1 - mine), recvs[0].at[p, j], True), (owner(j, mine), work.at[p, j], False)):
                for group, size, head in layout:
                    offset = 0
                    for chosen in group:
                        split = math.prod(chosen.shape[:-1]) // size

                        def move(chosen=chosen, offset=offset, o=o, dst=dst, remote=remote, size=size, head=head):
                            if len(chosen.shape) == 3:
                                src_ref = chosen.at[o - offset, :, column]
                            else:
                                src_ref = chosen.at[pl.ds((o - offset) * size, size), column]
                            dst_ref = dst.at[pl.ds(head, size)]
                            if remote:
                                pltpu.make_async_remote_copy(
                                    src_ref=src_ref, dst_ref=dst_ref,
                                    send_sem=send_sems.at[p, 0], recv_sem=recv_sems.at[p, 0],
                                    device_id=device_of(other, sizes), device_id_type=MESH,
                                ).start()
                            else:
                                pltpu.make_async_copy(src_ref, dst_ref, local_sem.at[p]).start()

                        if len(group) == 1:
                            move()
                        else:
                            pl.when((o >= offset) & (o < offset + split))(move)
                        offset += split

            return carry

        lax.fori_loop(0, half, issue, 0)
        first.append(other)
    for p in range(parts):
        whole = pltpu.make_async_remote_copy(
            src_ref=work.at[p, pl.ds(0, half)], dst_ref=recvs[0].at[p],
            send_sem=send_sems.at[p, 0], recv_sem=recv_sems.at[p, 0],
            device_id=device_of(first[p], sizes), device_id_type=MESH,
        )
        pltpu.make_async_copy(work.at[p, pl.ds(0, half)], work.at[p, pl.ds(0, half)], local_sem.at[p]).wait()
        whole.wait_recv()
        whole.wait_send()

        def accumulate0(i, carry, p=p):
            total = work[p, i].astype(jnp.float32) + recvs[0][p, i].astype(jnp.float32)
            work[p, i] = total.astype(work.dtype)
            return carry

        lax.fori_loop(0, half, accumulate0, 0)

    for step in range(1, steps):
        half = n >> (step + 1)
        copies = []
        for p in range(parts):
            mine, other = partner_of(orders[p][step])
            send = pltpu.make_async_remote_copy(
                src_ref=work.at[p, pl.ds((1 - mine) * half, half)], dst_ref=recvs[step].at[p],
                send_sem=send_sems.at[p, step], recv_sem=recv_sems.at[p, step],
                device_id=device_of(other, sizes), device_id_type=MESH,
            )
            send.start()
            copies.append((mine, send))
        if step == 1:
            def product(t, carry):
                rows = pl.ds(pl.multiple_of(t * tile, tile), tile)
                grad_out[rows, :] = (
                    jnp.dot(dq_ref[rows, :], w_ref[...], preferred_element_type=jnp.float32) + res_ref[rows, :]
                )
                return carry

            lax.fori_loop(0, grad_out.shape[0] // tile, product, 0)
        for p in range(parts):
            mine, send = copies[p]
            send.wait_recv()
            send.wait_send()

            def accumulate(i, carry, p=p, mine=mine, half=half, step=step):
                total = work[p, mine * half + i].astype(jnp.float32) + recvs[step][p, i].astype(jnp.float32)
                work[p, i] = total.astype(work.dtype)
                return carry

            lax.fori_loop(0, half, accumulate, 0)
    for p in range(parts):
        out_ref[p] = work[p, 0]

    def vec_finish(k, carry):
        vec_copy(k).wait_send()
        src = lax.rem(me + n - k, n)
        pltpu.make_async_remote_copy(
            src_ref=vec_ref.at[src], dst_ref=vec_out.at[src], send_sem=vec_send.at[k], recv_sem=vec_recv.at[src],
            device_id=device_of(src, sizes), device_id_type=MESH,
        ).wait_recv()
        return carry

    lax.fori_loop(1, n, vec_finish, 0)


def halving_scatter(grouped, vec, grad_b, weight_t, residual, sizes, parts, cid):
    n = math.prod(sizes)
    groups = tuple(len(g) for g in grouped)
    grads = [s for g in grouped for s in g]
    width = grads[0].shape[-1]
    rows = sum(math.prod(g.shape[:-1]) for g in grads) // n
    cols = width // parts
    orders = halving_orders(n, parts)
    steps = len(orders[0])
    dtype = grads[0].dtype
    tile = 128
    dma = pltpu.SemaphoreType.DMA
    vmem = pl.BlockSpec(memory_space=pltpu.VMEM)
    scratch = [pltpu.VMEM((parts, n // 2, rows, cols), dtype)]
    scratch += [pltpu.VMEM((parts, n >> (k + 1), rows, cols), dtype) for k in range(steps)]
    scratch += [dma((parts,)), dma((parts, steps)), dma((parts, steps)), dma((n,)), dma((n,))]
    return pl.pallas_call(
        functools.partial(halving_kernel, n, sizes, orders, cols, tile, groups),
        out_shape=(
            jax.ShapeDtypeStruct((parts, rows, cols), dtype),
            jax.ShapeDtypeStruct(vec.shape, vec.dtype),
            jax.ShapeDtypeStruct(residual.shape, jnp.float32),
        ),
        in_specs=[pl.BlockSpec(memory_space=pl.ANY)] * len(grads) + [vmem, vmem, vmem, vmem],
        out_specs=(vmem, vmem, vmem),
        scratch_shapes=scratch,
        compiler_params=pltpu.CompilerParams(
            collective_id=cid, has_side_effects=True, vmem_limit_bytes=60 * 1024 * 1024
        ),
    )(*grads, vec, grad_b, weight_t, residual)


def contrastive(embed_b, gathered, partner_all, me):
    own_texts = embed_b.shape[0]
    all_texts = gathered.shape[0]
    chunk = min(all_texts, 1024)
    on_rows = (((1,), (1,)), ((), ()))

    def chunk_stats(c):
        rows_b = lax.dynamic_slice_in_dim(gathered, c * chunk, chunk)
        sim = lax.dot_general(rows_b, gathered, on_rows, preferred_element_type=jnp.float32) / logit_divisor
        column_ids = lax.broadcasted_iota(jnp.int32, sim.shape, 1)
        row_ids = lax.broadcasted_iota(jnp.int32, sim.shape, 0) + c * chunk
        masked = jnp.where(column_ids == row_ids, masked_value, sim)
        row_max = jnp.max(masked, -1, keepdims=True)
        log_sum = row_max + jnp.log(jnp.sum(jnp.exp(masked - row_max), -1, keepdims=True))
        wanted = lax.dynamic_slice_in_dim(partner_all, c * chunk, chunk)
        positive = jnp.sum(jnp.where(column_ids == wanted[:, None], sim, 0.0), -1)
        return log_sum[:, 0], positive

    if all_texts == chunk:
        log_sum_all, positive_all = chunk_stats(0)
    else:
        log_sum_all, positive_all = lax.map(chunk_stats, jnp.arange(all_texts // chunk))
        log_sum_all = log_sum_all.reshape(-1)
        positive_all = positive_all.reshape(-1)
    mean_loss = jnp.sum(log_sum_all - positive_all) / all_texts

    own_start = me * own_texts
    own_ids = lax.broadcasted_iota(jnp.int32, (own_texts,), 0) + own_start
    own_partner = lax.dynamic_slice_in_dim(partner_all, own_start, own_texts)
    own_log_sum = lax.dynamic_slice_in_dim(log_sum_all, own_start, own_texts)

    sim_rows = lax.dot_general(embed_b, gathered, on_rows, preferred_element_type=jnp.float32) / logit_divisor
    column_ids = lax.broadcasted_iota(jnp.int32, sim_rows.shape, 1)
    masked_rows = jnp.where(column_ids == own_ids[:, None], masked_value, sim_rows)
    grad_rows = (
        jnp.exp(masked_rows - own_log_sum[:, None]) - (column_ids == own_partner[:, None]).astype(jnp.float32)
    ).astype(jnp.bfloat16)

    sim_cols = lax.dot_general(gathered, embed_b, on_rows, preferred_element_type=jnp.float32) / logit_divisor
    row_ids = lax.broadcasted_iota(jnp.int32, sim_cols.shape, 0)
    masked_cols = jnp.where(row_ids == own_ids[None, :], masked_value, sim_cols)
    grad_cols = (
        jnp.exp(masked_cols - log_sum_all[:, None]) - (partner_all[:, None] == own_ids[None, :]).astype(jnp.float32)
    ).astype(jnp.bfloat16)

    on_tokens = (((0,), (0,)), ((), ()))
    embedding_gradient = (
        jnp.dot(grad_rows, gathered, preferred_element_type=jnp.float32)
        + lax.dot_general(grad_cols, gathered, on_tokens, preferred_element_type=jnp.float32)
    ) / logit_divisor
    return mean_loss, embedding_gradient


def shards(
    hidden_in,
    segments,
    partner,
    attn_weights,
    ffn_weights,
    vectors,
    attn_momentum,
    ffn_momentum,
    vector_momentum,
    attn_averaged,
    ffn_averaged,
    vector_averaged,
):
    sizes = tuple(lax.axis_size(name) for name in AXES)
    n_dev = math.prod(sizes)
    me = flat_index(sizes)
    vec_len = vectors.shape[0]
    small = jnp.concatenate([vectors, partner.astype(jnp.float32)])[None, :]
    small_all = small_gather(small, sizes, 0)[:, 0, :]
    vector_f = bf16_round(small_all[:, :vec_len].reshape(-1))
    partner_all = small_all[:, vec_len:].reshape(-1).astype(jnp.int32)
    attn_full, ffn_full = (
        lax.all_gather(attn_weights.astype(jnp.bfloat16), AXES, axis=1, tiled=True),
        lax.all_gather(ffn_weights.astype(jnp.bfloat16), AXES, axis=1, tiled=True),
    )
    width = attn_full.shape[0]
    hidden = ffn_full.shape[1] // 2
    query_bias = vector_f[0:width]
    value_bias = vector_f[width : 2 * width]
    output_bias = vector_f[2 * width : 3 * width]
    gain_first = vector_f[3 * width : 4 * width]
    shift_first = vector_f[4 * width : 5 * width]
    upper_bias = vector_f[5 * width : 5 * width + hidden]
    lower_bias = vector_f[5 * width + hidden : 6 * width + hidden]
    gain_second = vector_f[6 * width + hidden : 7 * width + hidden]
    shift_second = vector_f[7 * width + hidden : 8 * width + hidden]
    w_qkv = attn_full[:, : 3 * width]
    w_output = attn_full[:, 3 * width :]
    w_upper = ffn_full[:, :hidden]
    w_lower = ffn_full[:, hidden:]
    rows_dev, seq_len = segments.shape
    tokens_n = rows_dev * seq_len
    on_rows = (((1,), (1,)), ((), ()))
    on_tokens = (((0,), (0,)), ((), ()))
    qkv_bias = jnp.concatenate([query_bias, jnp.zeros_like(query_bias), value_bias])
    qkv_rows = (jnp.dot(hidden_in, w_qkv, preferred_element_type=jnp.float32) + qkv_bias).astype(
        jnp.bfloat16
    )
    heads = qkv_rows.reshape(rows_dev, seq_len, 3, HEADS, HD)
    query_rows = heads[:, :, 0]
    key_rows = heads[:, :, 1]
    value_rows = heads[:, :, 2]
    mixed, log_norm = attend_rows(query_rows, key_rows, value_rows, segments)
    mixed_flat = mixed.reshape(tokens_n, width)
    first_sum = (
        hidden_in.astype(jnp.float32)
        + jnp.dot(mixed_flat, w_output, preferred_element_type=jnp.float32)
        + output_bias
    )
    normed, normal_one, inverse_one = layer_norm_parts(first_sum, gain_first, shift_first)
    normed_r = bf16_round(normed)
    normed_b = normed_r.astype(jnp.bfloat16)
    upper = jnp.dot(normed_b, w_upper, preferred_element_type=jnp.float32) + upper_bias
    active_b = (0.5 * upper * (1.0 + lax.erf(upper / math.sqrt(2.0)))).astype(jnp.bfloat16)
    second_sum = (
        normed_r
        + lax.dot_general(active_b, w_lower, on_rows, preferred_element_type=jnp.float32)
        + lower_bias
    )
    result, normal_two, inverse_two = layer_norm_parts(second_sum, gain_second, shift_second)
    text_ids = jnp.arange(SEGS, dtype=jnp.int32)
    one_hot = (segments[:, None, :] == text_ids[None, :, None]).astype(jnp.float32)
    counts = jnp.sum(one_hot, -1, keepdims=True)
    pooled = (
        jnp.einsum(
            "rts,rsd->rtd",
            one_hot,
            result.reshape(rows_dev, seq_len, width),
            precision=lax.Precision.HIGHEST,
        )
        / counts
    ).reshape(-1, width)
    inv_norm = lax.rsqrt(jnp.sum(pooled * pooled, -1, keepdims=True) + pool_epsilon)
    embed_b = (pooled * inv_norm).astype(jnp.bfloat16)
    gathered_embeddings = pair_gather(embed_b, sizes, 2).reshape(-1, width)
    mean_loss, embedding_gradient = contrastive(embed_b, gathered_embeddings, partner_all, me)
    grad_pooled = inv_norm * embedding_gradient - pooled * (
        inv_norm * inv_norm * inv_norm
    ) * jnp.sum(embedding_gradient * pooled, -1, keepdims=True)
    derivative_output = jnp.einsum(
        "rts,rtd->rsd",
        one_hot,
        grad_pooled.reshape(rows_dev, SEGS, width) / counts,
        precision=lax.Precision.HIGHEST,
    ).reshape(tokens_n, width)
    grad_second, gain_two_grad, shift_two_grad = layer_norm_back(
        derivative_output, normal_two, inverse_two, gain_second
    )
    lower_bias_grad = jnp.sum(grad_second, 0)
    lower_grad_b = grad_second.astype(jnp.bfloat16)
    lower_w_grad_t = lax.dot_general(
        active_b, lower_grad_b, on_tokens, preferred_element_type=jnp.float32
    )
    grad_active = jnp.dot(lower_grad_b, w_lower, preferred_element_type=jnp.float32)
    cumulative = 0.5 * (1.0 + lax.erf(upper / math.sqrt(2.0)))
    density = jnp.exp(-0.5 * upper * upper) / math.sqrt(2.0 * math.pi)
    grad_upper = grad_active * (cumulative + upper * density)
    upper_bias_grad = jnp.sum(grad_upper, 0)
    upper_grad_b = grad_upper.astype(jnp.bfloat16)
    upper_w_grad_t = lax.dot_general(
        upper_grad_b, normed_b, on_tokens, preferred_element_type=jnp.float32
    )
    grad_normed = (
        lax.dot_general(upper_grad_b, w_upper, on_rows, preferred_element_type=jnp.float32)
        + grad_second
    )
    grad_first, gain_one_grad, shift_one_grad = layer_norm_back(
        grad_normed, normal_one, inverse_one, gain_first
    )
    output_bias_grad = jnp.sum(grad_first, 0)
    first_grad_b = grad_first.astype(jnp.bfloat16)
    output_w_grad_t = lax.dot_general(
        first_grad_b, mixed_flat, on_tokens, preferred_element_type=jnp.float32
    )
    grad_mixed = lax.dot_general(
        first_grad_b, w_output, on_rows, preferred_element_type=jnp.float32
    ).astype(jnp.bfloat16)
    grad_mixed = grad_mixed.reshape(rows_dev, seq_len, HEADS, HD)
    norm_tokens = jnp.swapaxes(log_norm, 1, 2).reshape(tokens_n, HEADS)
    qkv_grad = jnp.concatenate(
        attention_back(qkv_rows, grad_mixed.reshape(tokens_n, width), norm_tokens, segments, HEADS, HD), 1
    ).astype(jnp.float32)
    qkv_grad_f = bf16_round(qkv_grad)
    qkv_grad_b = qkv_grad_f.astype(jnp.bfloat16)
    query_bias_grad = jnp.sum(qkv_grad_f[:, :width], 0)
    value_bias_grad = jnp.sum(qkv_grad_f[:, 2 * width :], 0)
    qkv_w_grad_t = lax.dot_general(
        qkv_grad_b, hidden_in, on_tokens, preferred_element_type=jnp.float32
    )
    vector_grad = jnp.concatenate(
        [
            query_bias_grad,
            value_bias_grad,
            output_bias_grad,
            gain_one_grad,
            shift_one_grad,
            upper_bias_grad,
            lower_bias_grad,
            gain_two_grad,
            shift_two_grad,
        ]
    )
    attn_cols = (qkv_w_grad_t.shape[0] + output_w_grad_t.shape[0]) // n_dev
    ffn_cols = (upper_w_grad_t.shape[0] + lower_w_grad_t.shape[0]) // n_dev
    if attn_cols % 16 == 0 and ffn_cols % 16 == 0:
        grads = (
            (qkv_w_grad_t.astype(GRAD_SEND), output_w_grad_t.astype(GRAD_SEND)),
            (upper_w_grad_t.astype(GRAD_SEND), lower_w_grad_t.astype(GRAD_SEND)),
        )
    else:
        attn_blocks = jnp.concatenate(
            [qkv_w_grad_t.reshape(-1, attn_cols, width), output_w_grad_t.reshape(-1, attn_cols, width)], 0
        )
        ffn_blocks = jnp.concatenate(
            [upper_w_grad_t.reshape(-1, ffn_cols, width), lower_w_grad_t.reshape(-1, ffn_cols, width)], 0
        )
        grads = ((jnp.concatenate([attn_blocks, ffn_blocks], 1).astype(GRAD_SEND),),)
    parts = 3
    mine_parts, vector_slots, input_grad = halving_scatter(
        grads, vector_grad.reshape(n_dev, 1, -1), qkv_grad_b, w_qkv.T, grad_first, sizes, parts, 3
    )
    vector_reduced = jnp.sum(vector_slots[:, 0, :], 0)
    joined_reduced = jnp.transpose(mine_parts, (1, 0, 2)).reshape(-1, width).astype(jnp.float32)
    attn_reduced = joined_reduced[:attn_cols].T
    ffn_reduced = joined_reduced[attn_cols:].T
    attn_new, attn_moment, attn_average = apply_update(
        attn_weights, attn_reduced, attn_momentum, attn_averaged, decay_rate
    )
    ffn_new, ffn_moment, ffn_average = apply_update(
        ffn_weights, ffn_reduced, ffn_momentum, ffn_averaged, decay_rate
    )
    vector_new, vector_moment, vector_average = apply_update(
        vectors, vector_reduced, vector_momentum, vector_averaged, 0.0
    )
    return (
        mean_loss,
        input_grad,
        attn_reduced,
        ffn_reduced,
        vector_reduced,
        attn_new,
        ffn_new,
        vector_new,
        attn_moment,
        ffn_moment,
        vector_moment,
        attn_average,
        ffn_average,
        vector_average,
    )


def solution(mesh):
    in_specs = (
        P(("dp", "rep"), None),
        P(("dp", "rep"), None),
        P(("dp", "rep")),
        P(None, ("dp", "rep")),
        P(None, ("dp", "rep")),
        P(("dp", "rep")),
        P(None, ("dp", "rep")),
        P(None, ("dp", "rep")),
        P(("dp", "rep")),
        P(None, ("dp", "rep")),
        P(None, ("dp", "rep")),
        P(("dp", "rep")),
    )
    out_specs = (
        P(),
        P(("dp", "rep"), None),
        P(None, ("dp", "rep")),
        P(None, ("dp", "rep")),
        P(("dp", "rep")),
        P(None, ("dp", "rep")),
        P(None, ("dp", "rep")),
        P(("dp", "rep")),
        P(None, ("dp", "rep")),
        P(None, ("dp", "rep")),
        P(("dp", "rep")),
        P(None, ("dp", "rep")),
        P(None, ("dp", "rep")),
        P(("dp", "rep")),
    )
    return jax.shard_map(shards, mesh=mesh, in_specs=in_specs, out_specs=out_specs, check_vma=False)
```

```python
import functools
import math

import jax
import jax.numpy as jnp
from jax import lax
from jax.experimental import pallas as pl
from jax.experimental.pallas import tpu as pltpu
from jax.sharding import PartitionSpec as P

MESH = pl.DeviceIdType.MESH
GRAD_SEND = jnp.bfloat16
AXES = ("dp", "rep")

HEADS = 12
HD = 64
SEGS = 16


ln_epsilon = 1e-12
pool_epsilon = 1e-06
logit_divisor = 0.025
learn_rate = 0.01
momentum_rate = 0.9
decay_rate = 0.01
average_rate = 0.75
masked_value = -1e30


def layer_norm_parts(values, gain, shift):
    per_line_average = jnp.mean(values, -1, keepdims=True)
    centred = values - per_line_average
    inverse = lax.rsqrt(jnp.mean(centred * centred, -1, keepdims=True) + ln_epsilon)
    normal_part = centred * inverse
    return (normal_part * gain + shift, normal_part, inverse)


def layer_norm_back(grad_out, normal_part, inverse, gain):
    scaled = grad_out * gain
    grad_in = inverse * (
        scaled
        - jnp.mean(scaled, -1, keepdims=True)
        - normal_part * jnp.mean(scaled * normal_part, -1, keepdims=True)
    )
    return (grad_in, jnp.sum(grad_out * normal_part, 0), jnp.sum(grad_out, 0))


def row_scores(query_one, key_one, segment_one, scale):
    scores = (
        jnp.einsum("qhd,khd->hqk", query_one, key_one, preferred_element_type=jnp.float32) * scale
    )
    same_text = segment_one[:, None] == segment_one[None, :]
    return jnp.where(same_text[None], scores, masked_value)


def attend_rows(query_rows, key_rows, value_rows, row_segments):
    scale = 1.0 / math.sqrt(query_rows.shape[-1])

    def one_row(row_args):
        query_one, key_one, value_one, segment_one = row_args
        scores = row_scores(query_one, key_one, segment_one, scale)
        row_max = jnp.max(scores, -1, keepdims=True)
        exp_scores = jnp.exp(scores - row_max)
        sums = jnp.sum(exp_scores, -1, keepdims=True)
        attn_probs = exp_scores / sums
        mixed = jnp.einsum(
            "hqk,khd->qhd",
            attn_probs.astype(jnp.bfloat16),
            value_one,
            preferred_element_type=jnp.float32,
        )
        return (mixed.astype(jnp.bfloat16), (row_max + jnp.log(sums))[..., 0])

    return lax.map(one_row, (query_rows, key_rows, value_rows, row_segments))


def attend_back(query_rows, key_rows, value_rows, row_segments, log_norm, grad_mixed):
    scale = 1.0 / math.sqrt(query_rows.shape[-1])

    def one_row(row_args):
        query_one, key_one, value_one, segment_one, norm_one, grad_one = row_args
        scores = row_scores(query_one, key_one, segment_one, scale)
        attn_probs = jnp.exp(scores - norm_one[..., None])
        grad_value = jnp.einsum(
            "hqk,qhd->khd",
            attn_probs.astype(jnp.bfloat16),
            grad_one,
            preferred_element_type=jnp.float32,
        )
        grad_probs = jnp.einsum(
            "qhd,khd->hqk", grad_one, value_one, preferred_element_type=jnp.float32
        )
        inner = jnp.sum(attn_probs * grad_probs, -1, keepdims=True)
        grad_scores = (attn_probs * (grad_probs - inner)).astype(jnp.bfloat16)
        grad_query = (
            jnp.einsum("hqk,khd->qhd", grad_scores, key_one, preferred_element_type=jnp.float32)
            * scale
        )
        grad_key = (
            jnp.einsum("hqk,qhd->khd", grad_scores, query_one, preferred_element_type=jnp.float32)
            * scale
        )
        return jnp.concatenate([grad_query, grad_key, grad_value], axis=1)

    return lax.map(one_row, (query_rows, key_rows, value_rows, row_segments, log_norm, grad_mixed))


def attention_back_kernel(scale, q_ref, k_ref, v_ref, g_ref, norm_ref, seg_col_ref, seg_row_ref, dq_ref, dk_ref, dv_ref,
                          dk_acc, dv_acc):
    pair = pl.program_id(1)
    seq_len, width = q_ref.shape
    half = width // 2
    block = 128
    window = 3 * block
    lane = lax.broadcasted_iota(jnp.int32, (1, width), 1)
    norms = norm_ref[...]
    norm_lane = lax.broadcasted_iota(jnp.int32, norms.shape, 1)
    on_last = (((1,), (1,)), ((), ()))
    on_first = (((0,), (0,)), ((), ()))
    dk_acc[...] = jnp.zeros_like(dk_acc)
    dv_acc[...] = jnp.zeros_like(dv_acc)
    for qb in range(seq_len // block):
        start = min(max(qb - 1, 0), seq_len // block - 3) * block
        rows = slice(qb * block, (qb + 1) * block)
        keys = slice(start, start + window)
        q = q_ref[rows, :]
        g = g_ref[rows, :]
        k = k_ref[keys, :]
        v = v_ref[keys, :]
        same = seg_col_ref[rows, :] == seg_row_ref[0][:, keys]
        zero_b = jnp.zeros_like(q)
        dq = jnp.zeros(q.shape, jnp.float32)
        for head in range(2):
            mine = (lane >= head * half) & (lane < (head + 1) * half)
            q_h = jnp.where(mine, q, zero_b)
            g_h = jnp.where(mine, g, zero_b)
            norm_h = jnp.sum(jnp.where(norm_lane[rows] == 2 * pair + head, norms[rows], 0.0), 1, keepdims=True)
            scores = lax.dot_general(q_h, k, on_last, preferred_element_type=jnp.float32) * scale
            scores = jnp.where(same, scores, masked_value)
            probs = jnp.exp(scores - norm_h)
            grad_v = lax.dot_general(probs.astype(jnp.bfloat16), g, on_first, preferred_element_type=jnp.float32)
            grad_p = lax.dot_general(g_h, v, on_last, preferred_element_type=jnp.float32)
            inner = jnp.sum(probs * grad_p, -1, keepdims=True)
            grad_s = (probs * (grad_p - inner)).astype(jnp.bfloat16)
            grad_q = jnp.dot(grad_s, k, preferred_element_type=jnp.float32) * scale
            grad_k = lax.dot_general(grad_s, q, on_first, preferred_element_type=jnp.float32) * scale
            dq = jnp.where(mine, grad_q, dq)
            dk_acc[keys, :] += jnp.where(mine, grad_k, 0.0)
            dv_acc[keys, :] += jnp.where(mine, grad_v, 0.0)
        dq_ref[rows, :] = dq.astype(dq_ref.dtype)
    dk_ref[...] = dk_acc[...].astype(dk_ref.dtype)
    dv_ref[...] = dv_acc[...].astype(dv_ref.dtype)


def attention_back(qkv_rows, grad_mixed_flat, norm_tokens, segments, heads, head_dim):
    tokens, three_width = qkv_rows.shape
    width = three_width // 3
    rows, seq_len = segments.shape
    pair_width = 2 * head_dim
    pairs = heads // 2
    seg_col = segments.reshape(tokens, 1)
    seg_row = segments.reshape(rows, 1, seq_len)
    scale = 1.0 / math.sqrt(head_dim)
    out = jax.ShapeDtypeStruct((tokens, width), jnp.bfloat16)
    return pl.pallas_call(
        functools.partial(attention_back_kernel, scale),
        grid=(rows, pairs),
        in_specs=[
            pl.BlockSpec((seq_len, pair_width), lambda r, p: (r, p)),
            pl.BlockSpec((seq_len, pair_width), lambda r, p: (r, pairs + p)),
            pl.BlockSpec((seq_len, pair_width), lambda r, p: (r, 2 * pairs + p)),
            pl.BlockSpec((seq_len, pair_width), lambda r, p: (r, p)),
            pl.BlockSpec((seq_len, heads), lambda r, p: (r, 0)),
            pl.BlockSpec((seq_len, 1), lambda r, p: (r, 0)),
            pl.BlockSpec((1, 1, seq_len), lambda r, p: (r, 0, 0)),
        ],
        out_specs=[pl.BlockSpec((seq_len, pair_width), lambda r, p: (r, p))] * 3,
        out_shape=[out, out, out],
        scratch_shapes=[pltpu.VMEM((seq_len, pair_width), jnp.float32)] * 2,
        compiler_params=pltpu.CompilerParams(vmem_limit_bytes=48 * 1024 * 1024),
        cost_estimate=pl.CostEstimate(
            flops=10 * rows * heads * seq_len * seq_len * pair_width,
            transcendentals=rows * heads * seq_len * seq_len,
            bytes_accessed=tokens * (three_width + 4 * width) * 2,
        ),
    )(qkv_rows, qkv_rows, qkv_rows, grad_mixed_flat, norm_tokens, seg_col, seg_row)


def apply_update(weight, grad, moment, average, decay):
    step_grad = grad + decay * weight
    new_moment = momentum_rate * moment + step_grad
    new_weight = weight - learn_rate * (step_grad + momentum_rate * new_moment)
    fresh_running_mean = average_rate * average + (1.0 - average_rate) * new_weight
    return (new_weight, new_moment, fresh_running_mean)


def bf16_round(values):
    return lax.reduce_precision(values, exponent_bits=8, mantissa_bits=7)


def flat_index(sizes):
    idx = 0
    for name, size in zip(AXES, sizes):
        idx = idx * size + lax.axis_index(name)
    return idx


def device_of(flat, sizes):
    coords = []
    for size in reversed(sizes):
        coords.append(lax.rem(flat, size))
        flat = flat // size
    return tuple(reversed(coords))


def enter_all(n, sizes, me):
    barrier = pltpu.get_barrier_semaphore()

    def greet(k, carry):
        peer = lax.rem(me + k, n)
        pl.semaphore_signal(barrier, inc=1, device_id=device_of(peer, sizes), device_id_type=MESH)
        return carry

    lax.fori_loop(1, n, greet, 0)
    pl.semaphore_wait(barrier, n - 1)


def gather_kernel(n, sizes, x_ref, out_ref, send_sem, recv_sem):
    me = flat_index(sizes)
    enter_all(n, sizes, me)

    def send(k, carry):
        peer = lax.rem(me + k, n)
        pltpu.make_async_remote_copy(
            src_ref=x_ref, dst_ref=out_ref.at[me], send_sem=send_sem.at[k], recv_sem=recv_sem.at[me],
            device_id=device_of(peer, sizes), device_id_type=MESH,
        ).start()
        return carry

    lax.fori_loop(1, n, send, 0)
    out_ref[me] = x_ref[...]

    def finish(k, carry):
        peer = lax.rem(me + k, n)
        src = lax.rem(me + n - k, n)
        pltpu.make_async_remote_copy(
            src_ref=x_ref, dst_ref=out_ref.at[me], send_sem=send_sem.at[k], recv_sem=recv_sem.at[me],
            device_id=device_of(peer, sizes), device_id_type=MESH,
        ).wait_send()
        pltpu.make_async_remote_copy(
            src_ref=x_ref, dst_ref=out_ref.at[src], send_sem=send_sem.at[k], recv_sem=recv_sem.at[src],
            device_id=device_of(src, sizes), device_id_type=MESH,
        ).wait_recv()
        return carry

    lax.fori_loop(1, n, finish, 0)


def small_gather(x, sizes, cid):
    n = math.prod(sizes)
    return pl.pallas_call(
        functools.partial(gather_kernel, n, sizes),
        out_shape=jax.ShapeDtypeStruct((n,) + x.shape, x.dtype),
        in_specs=[pl.BlockSpec(memory_space=pltpu.VMEM)],
        out_specs=pl.BlockSpec(memory_space=pltpu.VMEM),
        scratch_shapes=[pltpu.SemaphoreType.DMA((n,)), pltpu.SemaphoreType.DMA((n,))],
        compiler_params=pltpu.CompilerParams(collective_id=cid, has_side_effects=True),
    )(x)


def scatter_kernel(n, sizes, x_ref, out_ref, send_sem, recv_sem):
    me = flat_index(sizes)
    enter_all(n, sizes, me)

    def send(k, carry):
        peer = lax.rem(me + k, n)
        pltpu.make_async_remote_copy(
            src_ref=x_ref.at[peer], dst_ref=out_ref.at[me], send_sem=send_sem.at[k], recv_sem=recv_sem.at[me],
            device_id=device_of(peer, sizes), device_id_type=MESH,
        ).start()
        return carry

    lax.fori_loop(1, n, send, 0)
    out_ref[me] = x_ref[me]

    def finish(k, carry):
        peer = lax.rem(me + k, n)
        src = lax.rem(me + n - k, n)
        pltpu.make_async_remote_copy(
            src_ref=x_ref.at[peer], dst_ref=out_ref.at[me], send_sem=send_sem.at[k], recv_sem=recv_sem.at[me],
            device_id=device_of(peer, sizes), device_id_type=MESH,
        ).wait_send()
        pltpu.make_async_remote_copy(
            src_ref=x_ref.at[src], dst_ref=out_ref.at[src], send_sem=send_sem.at[k], recv_sem=recv_sem.at[src],
            device_id=device_of(src, sizes), device_id_type=MESH,
        ).wait_recv()
        return carry

    lax.fori_loop(1, n, finish, 0)


def small_scatter(x, sizes, cid):
    n = math.prod(sizes)
    return pl.pallas_call(
        functools.partial(scatter_kernel, n, sizes),
        out_shape=jax.ShapeDtypeStruct(x.shape, x.dtype),
        in_specs=[pl.BlockSpec(memory_space=pltpu.VMEM)],
        out_specs=pl.BlockSpec(memory_space=pltpu.VMEM),
        scratch_shapes=[pltpu.SemaphoreType.DMA((n,)), pltpu.SemaphoreType.DMA((n,))],
        compiler_params=pltpu.CompilerParams(collective_id=cid, has_side_effects=True),
    )(x)


def pair_gather_kernel(n, sizes, x_ref, out_ref, local_sem, send1, recv1, send2, recv2, send3, recv3):
    me = flat_index(sizes)
    chips = n // 2
    chip = me // 2
    core = lax.rem(me, 2)
    partner = me + 1 - 2 * core
    enter_all(n, sizes, me)

    local = pltpu.make_async_copy(x_ref, out_ref.at[me], local_sem)
    local.start()
    first = pltpu.make_async_remote_copy(
        src_ref=x_ref, dst_ref=out_ref.at[me], send_sem=send1, recv_sem=recv1,
        device_id=device_of(partner, sizes), device_id_type=MESH,
    )
    first.start()
    local.wait()
    first.wait_send()
    pltpu.make_async_remote_copy(
        src_ref=x_ref, dst_ref=out_ref.at[partner], send_sem=send1, recv_sem=recv1,
        device_id=device_of(partner, sizes), device_id_type=MESH,
    ).wait_recv()

    def pair(c):
        return out_ref.at[pl.ds(2 * c, 2)]

    def target(k):
        return lax.rem(chip + 2 * k - 1 + core, chips)

    def source(k):
        return lax.rem(chip + chips - (2 * k - 1 + core), chips)

    count = (chips - core) // 2

    def send_out(k, carry):
        other = target(k)
        pltpu.make_async_remote_copy(
            src_ref=pair(chip), dst_ref=pair(chip), send_sem=send2.at[other], recv_sem=recv2.at[chip],
            device_id=device_of(2 * other + core, sizes), device_id_type=MESH,
        ).start()
        return carry

    lax.fori_loop(1, count + 1, send_out, 0)

    def take_in(k, carry):
        other = source(k)
        pltpu.make_async_remote_copy(
            src_ref=pair(other), dst_ref=pair(other), send_sem=send2.at[other], recv_sem=recv2.at[other],
            device_id=device_of(2 * other + core, sizes), device_id_type=MESH,
        ).wait_recv()
        pltpu.make_async_remote_copy(
            src_ref=pair(other), dst_ref=pair(other), send_sem=send3.at[other], recv_sem=recv3.at[other],
            device_id=device_of(partner, sizes), device_id_type=MESH,
        ).start()
        return carry

    lax.fori_loop(1, count + 1, take_in, 0)

    def sent_out(k, carry):
        other = target(k)
        pltpu.make_async_remote_copy(
            src_ref=pair(chip), dst_ref=pair(chip), send_sem=send2.at[other], recv_sem=recv2.at[chip],
            device_id=device_of(2 * other + core, sizes), device_id_type=MESH,
        ).wait_send()
        return carry

    lax.fori_loop(1, count + 1, sent_out, 0)

    def forwarded(k, carry):
        other = source(k)
        pltpu.make_async_remote_copy(
            src_ref=pair(other), dst_ref=pair(other), send_sem=send3.at[other], recv_sem=recv3.at[other],
            device_id=device_of(partner, sizes), device_id_type=MESH,
        ).wait_send()
        return carry

    lax.fori_loop(1, count + 1, forwarded, 0)

    other_count = (chips - (1 - core)) // 2

    def partner_source(k):
        return lax.rem(chip + chips - (2 * k - 1 + (1 - core)), chips)

    def from_partner(k, carry):
        other = partner_source(k)
        pltpu.make_async_remote_copy(
            src_ref=pair(other), dst_ref=pair(other), send_sem=send3.at[other], recv_sem=recv3.at[other],
            device_id=device_of(partner, sizes), device_id_type=MESH,
        ).wait_recv()
        return carry

    lax.fori_loop(1, other_count + 1, from_partner, 0)


def pair_gather(x, sizes, cid):
    n = math.prod(sizes)
    chips = n // 2
    dma = pltpu.SemaphoreType.DMA
    return pl.pallas_call(
        functools.partial(pair_gather_kernel, n, sizes),
        out_shape=jax.ShapeDtypeStruct((n,) + x.shape, x.dtype),
        in_specs=[pl.BlockSpec(memory_space=pltpu.VMEM)],
        out_specs=pl.BlockSpec(memory_space=pltpu.VMEM),
        scratch_shapes=[dma(()), dma(()), dma(()), dma((chips,)), dma((chips,)), dma((chips,)), dma((chips,))],
        compiler_params=pltpu.CompilerParams(collective_id=cid, has_side_effects=True),
    )(x)


def halving_orders(n, parts):
    bits = n.bit_length() - 1
    middle = list(range(1, bits - 1))
    orders = []
    for p in range(parts):
        shift = p % len(middle) if middle else 0
        orders.append(tuple([0] + middle[shift:] + middle[:shift] + [bits - 1]))
    return tuple(orders)


def halving_kernel(n, sizes, orders, cols, tile, groups, *refs):
    count = sum(groups)
    sources = refs[:count]
    vec_ref, dq_ref, w_ref, res_ref, out_ref, vec_out, grad_out, work = refs[count : count + 8]
    rest = refs[count + 8 :]
    grouped = []
    at = 0
    for g in groups:
        grouped.append(sources[at : at + g])
        at += g
    steps = len(orders[0])
    parts = len(orders)
    layout = []
    head = 0
    for group in grouped:
        size = sum(math.prod(s.shape[:-1]) for s in group) // n
        layout.append((group, size, head))
        head += size
    recvs = rest[:steps]
    local_sem, send_sems, recv_sems, vec_send, vec_recv = rest[steps:]
    me = flat_index(sizes)

    def partner_of(bit):
        mine = lax.rem(me // (2**bit), 2)
        return mine, me + (1 - 2 * mine) * (2**bit)

    enter_all(n, sizes, me)

    def vec_copy(k):
        peer = lax.rem(me + k, n)
        return pltpu.make_async_remote_copy(
            src_ref=vec_ref.at[peer], dst_ref=vec_out.at[me], send_sem=vec_send.at[k], recv_sem=vec_recv.at[me],
            device_id=device_of(peer, sizes), device_id_type=MESH,
        )

    def vec_start(k, carry):
        vec_copy(k).start()
        return carry

    lax.fori_loop(1, n, vec_start, 0)
    vec_out[me] = vec_ref[me]

    half = n // 2
    first = []
    for p in range(parts):
        order = orders[p]
        mine, other = partner_of(order[0])
        column = pl.ds(p * cols, cols)

        def owner(j, side, order=order):
            o = side * (2 ** order[0])
            for m, bit in enumerate(order[1:]):
                o = o + lax.rem(j // (2 ** (steps - 2 - m)), 2) * (2**bit)
            return o

        def issue(j, carry, p=p, owner=owner, mine=mine, other=other, column=column):
            for o, dst, remote in ((owner(j, 1 - mine), recvs[0].at[p, j], True), (owner(j, mine), work.at[p, j], False)):
                for group, size, head in layout:
                    offset = 0
                    for chosen in group:
                        split = math.prod(chosen.shape[:-1]) // size

                        def move(chosen=chosen, offset=offset, o=o, dst=dst, remote=remote, size=size, head=head):
                            if len(chosen.shape) == 3:
                                src_ref = chosen.at[o - offset, :, column]
                            else:
                                src_ref = chosen.at[pl.ds((o - offset) * size, size), column]
                            dst_ref = dst.at[pl.ds(head, size)]
                            if remote:
                                pltpu.make_async_remote_copy(
                                    src_ref=src_ref, dst_ref=dst_ref,
                                    send_sem=send_sems.at[p, 0], recv_sem=recv_sems.at[p, 0],
                                    device_id=device_of(other, sizes), device_id_type=MESH,
                                ).start()
                            else:
                                pltpu.make_async_copy(src_ref, dst_ref, local_sem.at[p]).start()

                        if len(group) == 1:
                            move()
                        else:
                            pl.when((o >= offset) & (o < offset + split))(move)
                        offset += split

            return carry

        lax.fori_loop(0, half, issue, 0)
        first.append(other)
    for p in range(parts):
        whole = pltpu.make_async_remote_copy(
            src_ref=work.at[p, pl.ds(0, half)], dst_ref=recvs[0].at[p],
            send_sem=send_sems.at[p, 0], recv_sem=recv_sems.at[p, 0],
            device_id=device_of(first[p], sizes), device_id_type=MESH,
        )
        pltpu.make_async_copy(work.at[p, pl.ds(0, half)], work.at[p, pl.ds(0, half)], local_sem.at[p]).wait()
        whole.wait_recv()
        whole.wait_send()

        def accumulate0(i, carry, p=p):
            total = work[p, i].astype(jnp.float32) + recvs[0][p, i].astype(jnp.float32)
            work[p, i] = total.astype(work.dtype)
            return carry

        lax.fori_loop(0, half, accumulate0, 0)

    for step in range(1, steps):
        half = n >> (step + 1)
        copies = []
        for p in range(parts):
            mine, other = partner_of(orders[p][step])
            send = pltpu.make_async_remote_copy(
                src_ref=work.at[p, pl.ds((1 - mine) * half, half)], dst_ref=recvs[step].at[p],
                send_sem=send_sems.at[p, step], recv_sem=recv_sems.at[p, step],
                device_id=device_of(other, sizes), device_id_type=MESH,
            )
            send.start()
            copies.append((mine, send))
        if step == 1:
            def product(t, carry):
                rows = pl.ds(pl.multiple_of(t * tile, tile), tile)
                grad_out[rows, :] = (
                    jnp.dot(dq_ref[rows, :], w_ref[...], preferred_element_type=jnp.float32) + res_ref[rows, :]
                )
                return carry

            lax.fori_loop(0, grad_out.shape[0] // tile, product, 0)
        for p in range(parts):
            mine, send = copies[p]
            send.wait_recv()
            send.wait_send()

            def accumulate(i, carry, p=p, mine=mine, half=half, step=step):
                total = work[p, mine * half + i].astype(jnp.float32) + recvs[step][p, i].astype(jnp.float32)
                work[p, i] = total.astype(work.dtype)
                return carry

            lax.fori_loop(0, half, accumulate, 0)
    for p in range(parts):
        out_ref[p] = work[p, 0]

    def vec_finish(k, carry):
        vec_copy(k).wait_send()
        src = lax.rem(me + n - k, n)
        pltpu.make_async_remote_copy(
            src_ref=vec_ref.at[src], dst_ref=vec_out.at[src], send_sem=vec_send.at[k], recv_sem=vec_recv.at[src],
            device_id=device_of(src, sizes), device_id_type=MESH,
        ).wait_recv()
        return carry

    lax.fori_loop(1, n, vec_finish, 0)


def halving_scatter(grouped, vec, grad_b, weight_t, residual, sizes, parts, cid):
    n = math.prod(sizes)
    groups = tuple(len(g) for g in grouped)
    grads = [s for g in grouped for s in g]
    width = grads[0].shape[-1]
    rows = sum(math.prod(g.shape[:-1]) for g in grads) // n
    cols = width // parts
    orders = halving_orders(n, parts)
    steps = len(orders[0])
    dtype = grads[0].dtype
    tile = 128
    dma = pltpu.SemaphoreType.DMA
    vmem = pl.BlockSpec(memory_space=pltpu.VMEM)
    scratch = [pltpu.VMEM((parts, n // 2, rows, cols), dtype)]
    scratch += [pltpu.VMEM((parts, n >> (k + 1), rows, cols), dtype) for k in range(steps)]
    scratch += [dma((parts,)), dma((parts, steps)), dma((parts, steps)), dma((n,)), dma((n,))]
    return pl.pallas_call(
        functools.partial(halving_kernel, n, sizes, orders, cols, tile, groups),
        out_shape=(
            jax.ShapeDtypeStruct((parts, rows, cols), dtype),
            jax.ShapeDtypeStruct(vec.shape, vec.dtype),
            jax.ShapeDtypeStruct(residual.shape, jnp.float32),
        ),
        in_specs=[pl.BlockSpec(memory_space=pl.ANY)] * len(grads) + [vmem, vmem, vmem, vmem],
        out_specs=(vmem, vmem, vmem),
        scratch_shapes=scratch,
        compiler_params=pltpu.CompilerParams(
            collective_id=cid, has_side_effects=True, vmem_limit_bytes=60 * 1024 * 1024
        ),
    )(*grads, vec, grad_b, weight_t, residual)


def contrastive(embed_b, gathered, partner_all, me):
    own_texts = embed_b.shape[0]
    all_texts = gathered.shape[0]
    chunk = min(all_texts, 1024)
    on_rows = (((1,), (1,)), ((), ()))

    def chunk_stats(c):
        rows_b = lax.dynamic_slice_in_dim(gathered, c * chunk, chunk)
        sim = lax.dot_general(rows_b, gathered, on_rows, preferred_element_type=jnp.float32) / logit_divisor
        column_ids = lax.broadcasted_iota(jnp.int32, sim.shape, 1)
        row_ids = lax.broadcasted_iota(jnp.int32, sim.shape, 0) + c * chunk
        masked = jnp.where(column_ids == row_ids, masked_value, sim)
        row_max = jnp.max(masked, -1, keepdims=True)
        log_sum = row_max + jnp.log(jnp.sum(jnp.exp(masked - row_max), -1, keepdims=True))
        wanted = lax.dynamic_slice_in_dim(partner_all, c * chunk, chunk)
        positive = jnp.sum(jnp.where(column_ids == wanted[:, None], sim, 0.0), -1)
        return log_sum[:, 0], positive

    if all_texts == chunk:
        log_sum_all, positive_all = chunk_stats(0)
    else:
        log_sum_all, positive_all = lax.map(chunk_stats, jnp.arange(all_texts // chunk))
        log_sum_all = log_sum_all.reshape(-1)
        positive_all = positive_all.reshape(-1)
    mean_loss = jnp.sum(log_sum_all - positive_all) / all_texts

    own_start = me * own_texts
    own_ids = lax.broadcasted_iota(jnp.int32, (own_texts,), 0) + own_start
    own_partner = lax.dynamic_slice_in_dim(partner_all, own_start, own_texts)
    own_log_sum = lax.dynamic_slice_in_dim(log_sum_all, own_start, own_texts)

    sim_rows = lax.dot_general(embed_b, gathered, on_rows, preferred_element_type=jnp.float32) / logit_divisor
    column_ids = lax.broadcasted_iota(jnp.int32, sim_rows.shape, 1)
    masked_rows = jnp.where(column_ids == own_ids[:, None], masked_value, sim_rows)
    grad_rows = (
        jnp.exp(masked_rows - own_log_sum[:, None]) - (column_ids == own_partner[:, None]).astype(jnp.float32)
    ).astype(jnp.bfloat16)

    sim_cols = lax.dot_general(gathered, embed_b, on_rows, preferred_element_type=jnp.float32) / logit_divisor
    row_ids = lax.broadcasted_iota(jnp.int32, sim_cols.shape, 0)
    masked_cols = jnp.where(row_ids == own_ids[None, :], masked_value, sim_cols)
    grad_cols = (
        jnp.exp(masked_cols - log_sum_all[:, None]) - (partner_all[:, None] == own_ids[None, :]).astype(jnp.float32)
    ).astype(jnp.bfloat16)

    on_tokens = (((0,), (0,)), ((), ()))
    embedding_gradient = (
        jnp.dot(grad_rows, gathered, preferred_element_type=jnp.float32)
        + lax.dot_general(grad_cols, gathered, on_tokens, preferred_element_type=jnp.float32)
    ) / logit_divisor
    return mean_loss, embedding_gradient


def shards(
    hidden_in,
    segments,
    partner,
    attn_weights,
    ffn_weights,
    vectors,
    attn_momentum,
    ffn_momentum,
    vector_momentum,
    attn_averaged,
    ffn_averaged,
    vector_averaged,
):
    sizes = tuple(lax.axis_size(name) for name in AXES)
    n_dev = math.prod(sizes)
    me = flat_index(sizes)
    vec_len = vectors.shape[0]
    small = jnp.concatenate([vectors, partner.astype(jnp.float32)])[None, :]
    small_all = small_gather(small, sizes, 0)[:, 0, :]
    vector_f = bf16_round(small_all[:, :vec_len].reshape(-1))
    partner_all = small_all[:, vec_len:].reshape(-1).astype(jnp.int32)
    attn_full, ffn_full = (
        lax.all_gather(attn_weights.astype(jnp.bfloat16), AXES, axis=1, tiled=True),
        lax.all_gather(ffn_weights.astype(jnp.bfloat16), AXES, axis=1, tiled=True),
    )
    width = attn_full.shape[0]
    hidden = ffn_full.shape[1] // 2
    query_bias = vector_f[0:width]
    value_bias = vector_f[width : 2 * width]
    output_bias = vector_f[2 * width : 3 * width]
    gain_first = vector_f[3 * width : 4 * width]
    shift_first = vector_f[4 * width : 5 * width]
    upper_bias = vector_f[5 * width : 5 * width + hidden]
    lower_bias = vector_f[5 * width + hidden : 6 * width + hidden]
    gain_second = vector_f[6 * width + hidden : 7 * width + hidden]
    shift_second = vector_f[7 * width + hidden : 8 * width + hidden]
    w_qkv = attn_full[:, : 3 * width]
    w_output = attn_full[:, 3 * width :]
    w_upper = ffn_full[:, :hidden]
    w_lower = ffn_full[:, hidden:]
    rows_dev, seq_len = segments.shape
    tokens_n = rows_dev * seq_len
    on_rows = (((1,), (1,)), ((), ()))
    on_tokens = (((0,), (0,)), ((), ()))
    qkv_bias = jnp.concatenate([query_bias, jnp.zeros_like(query_bias), value_bias])
    qkv_rows = (jnp.dot(hidden_in, w_qkv, preferred_element_type=jnp.float32) + qkv_bias).astype(
        jnp.bfloat16
    )
    heads = qkv_rows.reshape(rows_dev, seq_len, 3, HEADS, HD)
    query_rows = heads[:, :, 0]
    key_rows = heads[:, :, 1]
    value_rows = heads[:, :, 2]
    mixed, log_norm = attend_rows(query_rows, key_rows, value_rows, segments)
    mixed_flat = mixed.reshape(tokens_n, width)
    first_sum = (
        hidden_in.astype(jnp.float32)
        + jnp.dot(mixed_flat, w_output, preferred_element_type=jnp.float32)
        + output_bias
    )
    normed, normal_one, inverse_one = layer_norm_parts(first_sum, gain_first, shift_first)
    normed_r = bf16_round(normed)
    normed_b = normed_r.astype(jnp.bfloat16)
    upper = jnp.dot(normed_b, w_upper, preferred_element_type=jnp.float32) + upper_bias
    active_b = (0.5 * upper * (1.0 + lax.erf(upper / math.sqrt(2.0)))).astype(jnp.bfloat16)
    second_sum = (
        normed_r
        + lax.dot_general(active_b, w_lower, on_rows, preferred_element_type=jnp.float32)
        + lower_bias
    )
    result, normal_two, inverse_two = layer_norm_parts(second_sum, gain_second, shift_second)
    text_ids = jnp.arange(SEGS, dtype=jnp.int32)
    one_hot = (segments[:, None, :] == text_ids[None, :, None]).astype(jnp.float32)
    counts = jnp.sum(one_hot, -1, keepdims=True)
    pooled = (
        jnp.einsum(
            "rts,rsd->rtd",
            one_hot,
            result.reshape(rows_dev, seq_len, width),
            precision=lax.Precision.HIGHEST,
        )
        / counts
    ).reshape(-1, width)
    inv_norm = lax.rsqrt(jnp.sum(pooled * pooled, -1, keepdims=True) + pool_epsilon)
    embed_b = (pooled * inv_norm).astype(jnp.bfloat16)
    gathered_embeddings = pair_gather(embed_b, sizes, 2).reshape(-1, width)
    mean_loss, embedding_gradient = contrastive(embed_b, gathered_embeddings, partner_all, me)
    grad_pooled = inv_norm * embedding_gradient - pooled * (
        inv_norm * inv_norm * inv_norm
    ) * jnp.sum(embedding_gradient * pooled, -1, keepdims=True)
    derivative_output = jnp.einsum(
        "rts,rtd->rsd",
        one_hot,
        grad_pooled.reshape(rows_dev, SEGS, width) / counts,
        precision=lax.Precision.HIGHEST,
    ).reshape(tokens_n, width)
    grad_second, gain_two_grad, shift_two_grad = layer_norm_back(
        derivative_output, normal_two, inverse_two, gain_second
    )
    lower_bias_grad = jnp.sum(grad_second, 0)
    lower_grad_b = grad_second.astype(jnp.bfloat16)
    lower_w_grad_t = lax.dot_general(
        active_b, lower_grad_b, on_tokens, preferred_element_type=jnp.float32
    )
    grad_active = jnp.dot(lower_grad_b, w_lower, preferred_element_type=jnp.float32)
    cumulative = 0.5 * (1.0 + lax.erf(upper / math.sqrt(2.0)))
    density = jnp.exp(-0.5 * upper * upper) / math.sqrt(2.0 * math.pi)
    grad_upper = grad_active * (cumulative + upper * density)
    upper_bias_grad = jnp.sum(grad_upper, 0)
    upper_grad_b = grad_upper.astype(jnp.bfloat16)
    upper_w_grad_t = lax.dot_general(
        upper_grad_b, normed_b, on_tokens, preferred_element_type=jnp.float32
    )
    grad_normed = (
        lax.dot_general(upper_grad_b, w_upper, on_rows, preferred_element_type=jnp.float32)
        + grad_second
    )
    grad_first, gain_one_grad, shift_one_grad = layer_norm_back(
        grad_normed, normal_one, inverse_one, gain_first
    )
    output_bias_grad = jnp.sum(grad_first, 0)
    first_grad_b = grad_first.astype(jnp.bfloat16)
    output_w_grad_t = lax.dot_general(
        first_grad_b, mixed_flat, on_tokens, preferred_element_type=jnp.float32
    )
    grad_mixed = lax.dot_general(
        first_grad_b, w_output, on_rows, preferred_element_type=jnp.float32
    ).astype(jnp.bfloat16)
    grad_mixed = grad_mixed.reshape(rows_dev, seq_len, HEADS, HD)
    norm_tokens = jnp.swapaxes(log_norm, 1, 2).reshape(tokens_n, HEADS)
    qkv_grad = jnp.concatenate(
        attention_back(qkv_rows, grad_mixed.reshape(tokens_n, width), norm_tokens, segments, HEADS, HD), 1
    ).astype(jnp.float32)
    qkv_grad_f = bf16_round(qkv_grad)
    qkv_grad_b = qkv_grad_f.astype(jnp.bfloat16)
    query_bias_grad = jnp.sum(qkv_grad_f[:, :width], 0)
    value_bias_grad = jnp.sum(qkv_grad_f[:, 2 * width :], 0)
    qkv_w_grad_t = lax.dot_general(
        qkv_grad_b, hidden_in, on_tokens, preferred_element_type=jnp.float32
    )
    vector_grad = jnp.concatenate(
        [
            query_bias_grad,
            value_bias_grad,
            output_bias_grad,
            gain_one_grad,
            shift_one_grad,
            upper_bias_grad,
            lower_bias_grad,
            gain_two_grad,
            shift_two_grad,
        ]
    )
    attn_cols = (qkv_w_grad_t.shape[0] + output_w_grad_t.shape[0]) // n_dev
    ffn_cols = (upper_w_grad_t.shape[0] + lower_w_grad_t.shape[0]) // n_dev
    if attn_cols % 16 == 0 and ffn_cols % 16 == 0:
        grads = (
            (qkv_w_grad_t.astype(GRAD_SEND), output_w_grad_t.astype(GRAD_SEND)),
            (upper_w_grad_t.astype(GRAD_SEND), lower_w_grad_t.astype(GRAD_SEND)),
        )
    else:
        attn_blocks = jnp.concatenate(
            [qkv_w_grad_t.reshape(-1, attn_cols, width), output_w_grad_t.reshape(-1, attn_cols, width)], 0
        )
        ffn_blocks = jnp.concatenate(
            [upper_w_grad_t.reshape(-1, ffn_cols, width), lower_w_grad_t.reshape(-1, ffn_cols, width)], 0
        )
        grads = ((jnp.concatenate([attn_blocks, ffn_blocks], 1).astype(GRAD_SEND),),)
    parts = 3
    mine_parts, vector_slots, input_grad = halving_scatter(
        grads, vector_grad.reshape(n_dev, 1, -1), qkv_grad_b, w_qkv.T, grad_first, sizes, parts, 3
    )
    vector_reduced = jnp.sum(vector_slots[:, 0, :], 0)
    joined_reduced = jnp.transpose(mine_parts, (1, 0, 2)).reshape(-1, width).astype(jnp.float32)
    attn_reduced = joined_reduced[:attn_cols].T
    ffn_reduced = joined_reduced[attn_cols:].T
    attn_new, attn_moment, attn_average = apply_update(
        attn_weights, attn_reduced, attn_momentum, attn_averaged, decay_rate
    )
    ffn_new, ffn_moment, ffn_average = apply_update(
        ffn_weights, ffn_reduced, ffn_momentum, ffn_averaged, decay_rate
    )
    vector_new, vector_moment, vector_average = apply_update(
        vectors, vector_reduced, vector_momentum, vector_averaged, 0.0
    )
    return (
        mean_loss,
        input_grad,
        attn_reduced,
        ffn_reduced,
        vector_reduced,
        attn_new,
        ffn_new,
        vector_new,
        attn_moment,
        ffn_moment,
        vector_moment,
        attn_average,
        ffn_average,
        vector_average,
    )


def solution(mesh):
    in_specs = (
        P(("dp", "rep"), None),
        P(("dp", "rep"), None),
        P(("dp", "rep")),
        P(None, ("dp", "rep")),
        P(None, ("dp", "rep")),
        P(("dp", "rep")),
        P(None, ("dp", "rep")),
        P(None, ("dp", "rep")),
        P(("dp", "rep")),
        P(None, ("dp", "rep")),
        P(None, ("dp", "rep")),
        P(("dp", "rep")),
    )
    out_specs = (
        P(),
        P(("dp", "rep"), None),
        P(None, ("dp", "rep")),
        P(None, ("dp", "rep")),
        P(("dp", "rep")),
        P(None, ("dp", "rep")),
        P(None, ("dp", "rep")),
        P(("dp", "rep")),
        P(None, ("dp", "rep")),
        P(None, ("dp", "rep")),
        P(("dp", "rep")),
        P(None, ("dp", "rep")),
        P(None, ("dp", "rep")),
        P(("dp", "rep")),
    )
    return jax.shard_map(shards, mesh=mesh, in_specs=in_specs, out_specs=out_specs, check_vma=False)
```

```python
import functools
import math

import jax
import jax.numpy as jnp
from jax import lax
from jax.experimental import pallas as pl
from jax.experimental.pallas import tpu as pltpu
from jax.sharding import PartitionSpec as P

MESH = pl.DeviceIdType.MESH
GRAD_SEND = jnp.bfloat16
AXES = ("dp", "rep")

HEADS = 12
HD = 64
SEGS = 16


ln_epsilon = 1e-12
pool_epsilon = 1e-06
logit_divisor = 0.025
learn_rate = 0.01
momentum_rate = 0.9
decay_rate = 0.01
average_rate = 0.75
masked_value = -1e30


def layer_norm_parts(values, gain, shift):
    per_line_average = jnp.mean(values, -1, keepdims=True)
    centred = values - per_line_average
    inverse = lax.rsqrt(jnp.mean(centred * centred, -1, keepdims=True) + ln_epsilon)
    normal_part = centred * inverse
    return (normal_part * gain + shift, normal_part, inverse)


def layer_norm_back(grad_out, normal_part, inverse, gain):
    scaled = grad_out * gain
    grad_in = inverse * (
        scaled
        - jnp.mean(scaled, -1, keepdims=True)
        - normal_part * jnp.mean(scaled * normal_part, -1, keepdims=True)
    )
    return (grad_in, jnp.sum(grad_out * normal_part, 0), jnp.sum(grad_out, 0))


def row_scores(query_one, key_one, segment_one, scale):
    scores = (
        jnp.einsum("qhd,khd->hqk", query_one, key_one, preferred_element_type=jnp.float32) * scale
    )
    same_text = segment_one[:, None] == segment_one[None, :]
    return jnp.where(same_text[None], scores, masked_value)


def attend_rows(query_rows, key_rows, value_rows, row_segments):
    scale = 1.0 / math.sqrt(query_rows.shape[-1])

    def one_row(row_args):
        query_one, key_one, value_one, segment_one = row_args
        scores = row_scores(query_one, key_one, segment_one, scale)
        row_max = jnp.max(scores, -1, keepdims=True)
        exp_scores = jnp.exp(scores - row_max)
        sums = jnp.sum(exp_scores, -1, keepdims=True)
        attn_probs = exp_scores / sums
        mixed = jnp.einsum(
            "hqk,khd->qhd",
            attn_probs.astype(jnp.bfloat16),
            value_one,
            preferred_element_type=jnp.float32,
        )
        return (mixed.astype(jnp.bfloat16), (row_max + jnp.log(sums))[..., 0])

    return lax.map(one_row, (query_rows, key_rows, value_rows, row_segments))


def attend_back(query_rows, key_rows, value_rows, row_segments, log_norm, grad_mixed):
    scale = 1.0 / math.sqrt(query_rows.shape[-1])

    def one_row(row_args):
        query_one, key_one, value_one, segment_one, norm_one, grad_one = row_args
        scores = row_scores(query_one, key_one, segment_one, scale)
        attn_probs = jnp.exp(scores - norm_one[..., None])
        grad_value = jnp.einsum(
            "hqk,qhd->khd",
            attn_probs.astype(jnp.bfloat16),
            grad_one,
            preferred_element_type=jnp.float32,
        )
        grad_probs = jnp.einsum(
            "qhd,khd->hqk", grad_one, value_one, preferred_element_type=jnp.float32
        )
        inner = jnp.sum(attn_probs * grad_probs, -1, keepdims=True)
        grad_scores = (attn_probs * (grad_probs - inner)).astype(jnp.bfloat16)
        grad_query = (
            jnp.einsum("hqk,khd->qhd", grad_scores, key_one, preferred_element_type=jnp.float32)
            * scale
        )
        grad_key = (
            jnp.einsum("hqk,qhd->khd", grad_scores, query_one, preferred_element_type=jnp.float32)
            * scale
        )
        return jnp.concatenate([grad_query, grad_key, grad_value], axis=1)

    return lax.map(one_row, (query_rows, key_rows, value_rows, row_segments, log_norm, grad_mixed))


def attention_back_kernel(scale, q_ref, k_ref, v_ref, g_ref, norm_ref, seg_col_ref, seg_row_ref, dq_ref, dk_ref, dv_ref):
    pair = pl.program_id(1)
    width = q_ref.shape[1]
    half = width // 2
    lane = lax.broadcasted_iota(jnp.int32, (1, width), 1)
    same = seg_col_ref[...] == seg_row_ref[0]
    norms = norm_ref[...]
    norm_lane = lax.broadcasted_iota(jnp.int32, norms.shape, 1)
    q = q_ref[...]
    k = k_ref[...]
    v = v_ref[...]
    g = g_ref[...]
    zero_b = jnp.zeros_like(q)
    on_last = (((1,), (1,)), ((), ()))
    on_first = (((0,), (0,)), ((), ()))
    dq = jnp.zeros(q.shape, jnp.float32)
    dk = jnp.zeros(q.shape, jnp.float32)
    dv = jnp.zeros(q.shape, jnp.float32)
    for head in range(2):
        mine = (lane >= head * half) & (lane < (head + 1) * half)
        q_h = jnp.where(mine, q, zero_b)
        g_h = jnp.where(mine, g, zero_b)
        norm_h = jnp.sum(jnp.where(norm_lane == 2 * pair + head, norms, 0.0), 1, keepdims=True)
        scores = lax.dot_general(q_h, k, on_last, preferred_element_type=jnp.float32) * scale
        scores = jnp.where(same, scores, masked_value)
        probs = jnp.exp(scores - norm_h)
        grad_v = lax.dot_general(probs.astype(jnp.bfloat16), g, on_first, preferred_element_type=jnp.float32)
        grad_p = lax.dot_general(g_h, v, on_last, preferred_element_type=jnp.float32)
        inner = jnp.sum(probs * grad_p, -1, keepdims=True)
        grad_s = (probs * (grad_p - inner)).astype(jnp.bfloat16)
        grad_q = jnp.dot(grad_s, k, preferred_element_type=jnp.float32) * scale
        grad_k = lax.dot_general(grad_s, q, on_first, preferred_element_type=jnp.float32) * scale
        dq = jnp.where(mine, grad_q, dq)
        dk = jnp.where(mine, grad_k, dk)
        dv = jnp.where(mine, grad_v, dv)
    dq_ref[...] = dq.astype(dq_ref.dtype)
    dk_ref[...] = dk.astype(dk_ref.dtype)
    dv_ref[...] = dv.astype(dv_ref.dtype)


def attention_back(qkv_rows, grad_mixed_flat, norm_tokens, segments, heads, head_dim):
    tokens, three_width = qkv_rows.shape
    width = three_width // 3
    rows, seq_len = segments.shape
    pair_width = 2 * head_dim
    pairs = heads // 2
    seg_col = segments.reshape(tokens, 1)
    seg_row = segments.reshape(rows, 1, seq_len)
    scale = 1.0 / math.sqrt(head_dim)
    out = jax.ShapeDtypeStruct((tokens, width), jnp.bfloat16)
    return pl.pallas_call(
        functools.partial(attention_back_kernel, scale),
        grid=(rows, pairs),
        in_specs=[
            pl.BlockSpec((seq_len, pair_width), lambda r, p: (r, p)),
            pl.BlockSpec((seq_len, pair_width), lambda r, p: (r, pairs + p)),
            pl.BlockSpec((seq_len, pair_width), lambda r, p: (r, 2 * pairs + p)),
            pl.BlockSpec((seq_len, pair_width), lambda r, p: (r, p)),
            pl.BlockSpec((seq_len, heads), lambda r, p: (r, 0)),
            pl.BlockSpec((seq_len, 1), lambda r, p: (r, 0)),
            pl.BlockSpec((1, 1, seq_len), lambda r, p: (r, 0, 0)),
        ],
        out_specs=[pl.BlockSpec((seq_len, pair_width), lambda r, p: (r, p))] * 3,
        out_shape=[out, out, out],
        compiler_params=pltpu.CompilerParams(vmem_limit_bytes=48 * 1024 * 1024),
        cost_estimate=pl.CostEstimate(
            flops=10 * rows * heads * seq_len * seq_len * pair_width,
            transcendentals=rows * heads * seq_len * seq_len,
            bytes_accessed=tokens * (three_width + 4 * width) * 2,
        ),
    )(qkv_rows, qkv_rows, qkv_rows, grad_mixed_flat, norm_tokens, seg_col, seg_row)


def apply_update(weight, grad, moment, average, decay):
    step_grad = grad + decay * weight
    new_moment = momentum_rate * moment + step_grad
    new_weight = weight - learn_rate * (step_grad + momentum_rate * new_moment)
    fresh_running_mean = average_rate * average + (1.0 - average_rate) * new_weight
    return (new_weight, new_moment, fresh_running_mean)


def bf16_round(values):
    return lax.reduce_precision(values, exponent_bits=8, mantissa_bits=7)


def flat_index(sizes):
    idx = 0
    for name, size in zip(AXES, sizes):
        idx = idx * size + lax.axis_index(name)
    return idx


def device_of(flat, sizes):
    coords = []
    for size in reversed(sizes):
        coords.append(lax.rem(flat, size))
        flat = flat // size
    return tuple(reversed(coords))


def enter_all(n, sizes, me):
    barrier = pltpu.get_barrier_semaphore()

    def greet(k, carry):
        peer = lax.rem(me + k, n)
        pl.semaphore_signal(barrier, inc=1, device_id=device_of(peer, sizes), device_id_type=MESH)
        return carry

    lax.fori_loop(1, n, greet, 0)
    pl.semaphore_wait(barrier, n - 1)


def gather_kernel(n, sizes, x_ref, out_ref, send_sem, recv_sem):
    me = flat_index(sizes)
    enter_all(n, sizes, me)

    def send(k, carry):
        peer = lax.rem(me + k, n)
        pltpu.make_async_remote_copy(
            src_ref=x_ref, dst_ref=out_ref.at[me], send_sem=send_sem.at[k], recv_sem=recv_sem.at[me],
            device_id=device_of(peer, sizes), device_id_type=MESH,
        ).start()
        return carry

    lax.fori_loop(1, n, send, 0)
    out_ref[me] = x_ref[...]

    def finish(k, carry):
        peer = lax.rem(me + k, n)
        src = lax.rem(me + n - k, n)
        pltpu.make_async_remote_copy(
            src_ref=x_ref, dst_ref=out_ref.at[me], send_sem=send_sem.at[k], recv_sem=recv_sem.at[me],
            device_id=device_of(peer, sizes), device_id_type=MESH,
        ).wait_send()
        pltpu.make_async_remote_copy(
            src_ref=x_ref, dst_ref=out_ref.at[src], send_sem=send_sem.at[k], recv_sem=recv_sem.at[src],
            device_id=device_of(src, sizes), device_id_type=MESH,
        ).wait_recv()
        return carry

    lax.fori_loop(1, n, finish, 0)


def small_gather(x, sizes, cid):
    n = math.prod(sizes)
    return pl.pallas_call(
        functools.partial(gather_kernel, n, sizes),
        out_shape=jax.ShapeDtypeStruct((n,) + x.shape, x.dtype),
        in_specs=[pl.BlockSpec(memory_space=pltpu.VMEM)],
        out_specs=pl.BlockSpec(memory_space=pltpu.VMEM),
        scratch_shapes=[pltpu.SemaphoreType.DMA((n,)), pltpu.SemaphoreType.DMA((n,))],
        compiler_params=pltpu.CompilerParams(collective_id=cid, has_side_effects=True),
    )(x)


def scatter_kernel(n, sizes, x_ref, out_ref, send_sem, recv_sem):
    me = flat_index(sizes)
    enter_all(n, sizes, me)

    def send(k, carry):
        peer = lax.rem(me + k, n)
        pltpu.make_async_remote_copy(
            src_ref=x_ref.at[peer], dst_ref=out_ref.at[me], send_sem=send_sem.at[k], recv_sem=recv_sem.at[me],
            device_id=device_of(peer, sizes), device_id_type=MESH,
        ).start()
        return carry

    lax.fori_loop(1, n, send, 0)
    out_ref[me] = x_ref[me]

    def finish(k, carry):
        peer = lax.rem(me + k, n)
        src = lax.rem(me + n - k, n)
        pltpu.make_async_remote_copy(
            src_ref=x_ref.at[peer], dst_ref=out_ref.at[me], send_sem=send_sem.at[k], recv_sem=recv_sem.at[me],
            device_id=device_of(peer, sizes), device_id_type=MESH,
        ).wait_send()
        pltpu.make_async_remote_copy(
            src_ref=x_ref.at[src], dst_ref=out_ref.at[src], send_sem=send_sem.at[k], recv_sem=recv_sem.at[src],
            device_id=device_of(src, sizes), device_id_type=MESH,
        ).wait_recv()
        return carry

    lax.fori_loop(1, n, finish, 0)


def small_scatter(x, sizes, cid):
    n = math.prod(sizes)
    return pl.pallas_call(
        functools.partial(scatter_kernel, n, sizes),
        out_shape=jax.ShapeDtypeStruct(x.shape, x.dtype),
        in_specs=[pl.BlockSpec(memory_space=pltpu.VMEM)],
        out_specs=pl.BlockSpec(memory_space=pltpu.VMEM),
        scratch_shapes=[pltpu.SemaphoreType.DMA((n,)), pltpu.SemaphoreType.DMA((n,))],
        compiler_params=pltpu.CompilerParams(collective_id=cid, has_side_effects=True),
    )(x)


def pair_gather_kernel(n, sizes, x_ref, out_ref, local_sem, send1, recv1, send2, recv2, send3, recv3):
    me = flat_index(sizes)
    chips = n // 2
    chip = me // 2
    core = lax.rem(me, 2)
    partner = me + 1 - 2 * core
    enter_all(n, sizes, me)

    local = pltpu.make_async_copy(x_ref, out_ref.at[me], local_sem)
    local.start()
    first = pltpu.make_async_remote_copy(
        src_ref=x_ref, dst_ref=out_ref.at[me], send_sem=send1, recv_sem=recv1,
        device_id=device_of(partner, sizes), device_id_type=MESH,
    )
    first.start()
    local.wait()
    first.wait_send()
    pltpu.make_async_remote_copy(
        src_ref=x_ref, dst_ref=out_ref.at[partner], send_sem=send1, recv_sem=recv1,
        device_id=device_of(partner, sizes), device_id_type=MESH,
    ).wait_recv()

    def pair(c):
        return out_ref.at[pl.ds(2 * c, 2)]

    def target(k):
        return lax.rem(chip + 2 * k - 1 + core, chips)

    def source(k):
        return lax.rem(chip + chips - (2 * k - 1 + core), chips)

    count = (chips - core) // 2

    def send_out(k, carry):
        other = target(k)
        pltpu.make_async_remote_copy(
            src_ref=pair(chip), dst_ref=pair(chip), send_sem=send2.at[other], recv_sem=recv2.at[chip],
            device_id=device_of(2 * other + core, sizes), device_id_type=MESH,
        ).start()
        return carry

    lax.fori_loop(1, count + 1, send_out, 0)

    def take_in(k, carry):
        other = source(k)
        pltpu.make_async_remote_copy(
            src_ref=pair(other), dst_ref=pair(other), send_sem=send2.at[other], recv_sem=recv2.at[other],
            device_id=device_of(2 * other + core, sizes), device_id_type=MESH,
        ).wait_recv()
        pltpu.make_async_remote_copy(
            src_ref=pair(other), dst_ref=pair(other), send_sem=send3.at[other], recv_sem=recv3.at[other],
            device_id=device_of(partner, sizes), device_id_type=MESH,
        ).start()
        return carry

    lax.fori_loop(1, count + 1, take_in, 0)

    def sent_out(k, carry):
        other = target(k)
        pltpu.make_async_remote_copy(
            src_ref=pair(chip), dst_ref=pair(chip), send_sem=send2.at[other], recv_sem=recv2.at[chip],
            device_id=device_of(2 * other + core, sizes), device_id_type=MESH,
        ).wait_send()
        return carry

    lax.fori_loop(1, count + 1, sent_out, 0)

    def forwarded(k, carry):
        other = source(k)
        pltpu.make_async_remote_copy(
            src_ref=pair(other), dst_ref=pair(other), send_sem=send3.at[other], recv_sem=recv3.at[other],
            device_id=device_of(partner, sizes), device_id_type=MESH,
        ).wait_send()
        return carry

    lax.fori_loop(1, count + 1, forwarded, 0)

    other_count = (chips - (1 - core)) // 2

    def partner_source(k):
        return lax.rem(chip + chips - (2 * k - 1 + (1 - core)), chips)

    def from_partner(k, carry):
        other = partner_source(k)
        pltpu.make_async_remote_copy(
            src_ref=pair(other), dst_ref=pair(other), send_sem=send3.at[other], recv_sem=recv3.at[other],
            device_id=device_of(partner, sizes), device_id_type=MESH,
        ).wait_recv()
        return carry

    lax.fori_loop(1, other_count + 1, from_partner, 0)


def pair_gather(x, sizes, cid):
    n = math.prod(sizes)
    chips = n // 2
    dma = pltpu.SemaphoreType.DMA
    return pl.pallas_call(
        functools.partial(pair_gather_kernel, n, sizes),
        out_shape=jax.ShapeDtypeStruct((n,) + x.shape, x.dtype),
        in_specs=[pl.BlockSpec(memory_space=pltpu.VMEM)],
        out_specs=pl.BlockSpec(memory_space=pltpu.VMEM),
        scratch_shapes=[dma(()), dma(()), dma(()), dma((chips,)), dma((chips,)), dma((chips,)), dma((chips,))],
        compiler_params=pltpu.CompilerParams(collective_id=cid, has_side_effects=True),
    )(x)


def halving_orders(n, parts):
    bits = n.bit_length() - 1
    middle = list(range(1, bits - 1))
    orders = []
    for p in range(parts):
        shift = p % len(middle) if middle else 0
        orders.append(tuple([0] + middle[shift:] + middle[:shift] + [bits - 1]))
    return tuple(orders)


def halving_kernel(n, sizes, orders, cols, tile, groups, *refs):
    count = sum(groups)
    sources = refs[:count]
    vec_ref, dq_ref, w_ref, res_ref, out_ref, vec_out, grad_out, work = refs[count : count + 8]
    rest = refs[count + 8 :]
    grouped = []
    at = 0
    for g in groups:
        grouped.append(sources[at : at + g])
        at += g
    steps = len(orders[0])
    parts = len(orders)
    layout = []
    head = 0
    for group in grouped:
        size = sum(math.prod(s.shape[:-1]) for s in group) // n
        layout.append((group, size, head))
        head += size
    recvs = rest[:steps]
    local_sem, send_sems, recv_sems, vec_send, vec_recv = rest[steps:]
    me = flat_index(sizes)

    def partner_of(bit):
        mine = lax.rem(me // (2**bit), 2)
        return mine, me + (1 - 2 * mine) * (2**bit)

    enter_all(n, sizes, me)

    def vec_copy(k):
        peer = lax.rem(me + k, n)
        return pltpu.make_async_remote_copy(
            src_ref=vec_ref.at[peer], dst_ref=vec_out.at[me], send_sem=vec_send.at[k], recv_sem=vec_recv.at[me],
            device_id=device_of(peer, sizes), device_id_type=MESH,
        )

    def vec_start(k, carry):
        vec_copy(k).start()
        return carry

    lax.fori_loop(1, n, vec_start, 0)
    vec_out[me] = vec_ref[me]

    half = n // 2
    first = []
    for p in range(parts):
        order = orders[p]
        mine, other = partner_of(order[0])
        column = pl.ds(p * cols, cols)

        def owner(j, side, order=order):
            o = side * (2 ** order[0])
            for m, bit in enumerate(order[1:]):
                o = o + lax.rem(j // (2 ** (steps - 2 - m)), 2) * (2**bit)
            return o

        def issue(j, carry, p=p, owner=owner, mine=mine, other=other, column=column):
            for o, dst, remote in ((owner(j, 1 - mine), recvs[0].at[p, j], True), (owner(j, mine), work.at[p, j], False)):
                for group, size, head in layout:
                    offset = 0
                    for chosen in group:
                        split = math.prod(chosen.shape[:-1]) // size

                        def move(chosen=chosen, offset=offset, o=o, dst=dst, remote=remote, size=size, head=head):
                            if len(chosen.shape) == 3:
                                src_ref = chosen.at[o - offset, :, column]
                            else:
                                src_ref = chosen.at[pl.ds((o - offset) * size, size), column]
                            dst_ref = dst.at[pl.ds(head, size)]
                            if remote:
                                pltpu.make_async_remote_copy(
                                    src_ref=src_ref, dst_ref=dst_ref,
                                    send_sem=send_sems.at[p, 0], recv_sem=recv_sems.at[p, 0],
                                    device_id=device_of(other, sizes), device_id_type=MESH,
                                ).start()
                            else:
                                pltpu.make_async_copy(src_ref, dst_ref, local_sem.at[p]).start()

                        if len(group) == 1:
                            move()
                        else:
                            pl.when((o >= offset) & (o < offset + split))(move)
                        offset += split

            return carry

        lax.fori_loop(0, half, issue, 0)
        first.append(other)
    for p in range(parts):
        whole = pltpu.make_async_remote_copy(
            src_ref=work.at[p, pl.ds(0, half)], dst_ref=recvs[0].at[p],
            send_sem=send_sems.at[p, 0], recv_sem=recv_sems.at[p, 0],
            device_id=device_of(first[p], sizes), device_id_type=MESH,
        )
        pltpu.make_async_copy(work.at[p, pl.ds(0, half)], work.at[p, pl.ds(0, half)], local_sem.at[p]).wait()
        whole.wait_recv()
        whole.wait_send()

        def accumulate0(i, carry, p=p):
            total = work[p, i].astype(jnp.float32) + recvs[0][p, i].astype(jnp.float32)
            work[p, i] = total.astype(work.dtype)
            return carry

        lax.fori_loop(0, half, accumulate0, 0)

    for step in range(1, steps):
        half = n >> (step + 1)
        copies = []
        for p in range(parts):
            mine, other = partner_of(orders[p][step])
            send = pltpu.make_async_remote_copy(
                src_ref=work.at[p, pl.ds((1 - mine) * half, half)], dst_ref=recvs[step].at[p],
                send_sem=send_sems.at[p, step], recv_sem=recv_sems.at[p, step],
                device_id=device_of(other, sizes), device_id_type=MESH,
            )
            send.start()
            copies.append((mine, send))
        if step == 1:
            def product(t, carry):
                rows = pl.ds(pl.multiple_of(t * tile, tile), tile)
                grad_out[rows, :] = (
                    jnp.dot(dq_ref[rows, :], w_ref[...], preferred_element_type=jnp.float32) + res_ref[rows, :]
                )
                return carry

            lax.fori_loop(0, grad_out.shape[0] // tile, product, 0)
        for p in range(parts):
            mine, send = copies[p]
            send.wait_recv()
            send.wait_send()

            def accumulate(i, carry, p=p, mine=mine, half=half, step=step):
                total = work[p, mine * half + i].astype(jnp.float32) + recvs[step][p, i].astype(jnp.float32)
                work[p, i] = total.astype(work.dtype)
                return carry

            lax.fori_loop(0, half, accumulate, 0)
    for p in range(parts):
        out_ref[p] = work[p, 0]

    def vec_finish(k, carry):
        vec_copy(k).wait_send()
        src = lax.rem(me + n - k, n)
        pltpu.make_async_remote_copy(
            src_ref=vec_ref.at[src], dst_ref=vec_out.at[src], send_sem=vec_send.at[k], recv_sem=vec_recv.at[src],
            device_id=device_of(src, sizes), device_id_type=MESH,
        ).wait_recv()
        return carry

    lax.fori_loop(1, n, vec_finish, 0)


def halving_scatter(grouped, vec, grad_b, weight_t, residual, sizes, parts, cid):
    n = math.prod(sizes)
    groups = tuple(len(g) for g in grouped)
    grads = [s for g in grouped for s in g]
    width = grads[0].shape[-1]
    rows = sum(math.prod(g.shape[:-1]) for g in grads) // n
    cols = width // parts
    orders = halving_orders(n, parts)
    steps = len(orders[0])
    dtype = grads[0].dtype
    tile = 128
    dma = pltpu.SemaphoreType.DMA
    vmem = pl.BlockSpec(memory_space=pltpu.VMEM)
    scratch = [pltpu.VMEM((parts, n // 2, rows, cols), dtype)]
    scratch += [pltpu.VMEM((parts, n >> (k + 1), rows, cols), dtype) for k in range(steps)]
    scratch += [dma((parts,)), dma((parts, steps)), dma((parts, steps)), dma((n,)), dma((n,))]
    return pl.pallas_call(
        functools.partial(halving_kernel, n, sizes, orders, cols, tile, groups),
        out_shape=(
            jax.ShapeDtypeStruct((parts, rows, cols), dtype),
            jax.ShapeDtypeStruct(vec.shape, vec.dtype),
            jax.ShapeDtypeStruct(residual.shape, jnp.float32),
        ),
        in_specs=[pl.BlockSpec(memory_space=pl.ANY)] * len(grads) + [vmem, vmem, vmem, vmem],
        out_specs=(vmem, vmem, vmem),
        scratch_shapes=scratch,
        compiler_params=pltpu.CompilerParams(
            collective_id=cid, has_side_effects=True, vmem_limit_bytes=60 * 1024 * 1024
        ),
    )(*grads, vec, grad_b, weight_t, residual)


def contrastive(embed_b, gathered, partner_all, me):
    own_texts = embed_b.shape[0]
    all_texts = gathered.shape[0]
    chunk = min(all_texts, 1024)
    on_rows = (((1,), (1,)), ((), ()))

    def chunk_stats(c):
        rows_b = lax.dynamic_slice_in_dim(gathered, c * chunk, chunk)
        sim = lax.dot_general(rows_b, gathered, on_rows, preferred_element_type=jnp.float32) / logit_divisor
        column_ids = lax.broadcasted_iota(jnp.int32, sim.shape, 1)
        row_ids = lax.broadcasted_iota(jnp.int32, sim.shape, 0) + c * chunk
        masked = jnp.where(column_ids == row_ids, masked_value, sim)
        row_max = jnp.max(masked, -1, keepdims=True)
        log_sum = row_max + jnp.log(jnp.sum(jnp.exp(masked - row_max), -1, keepdims=True))
        wanted = lax.dynamic_slice_in_dim(partner_all, c * chunk, chunk)
        positive = jnp.sum(jnp.where(column_ids == wanted[:, None], sim, 0.0), -1)
        return log_sum[:, 0], positive

    if all_texts == chunk:
        log_sum_all, positive_all = chunk_stats(0)
    else:
        log_sum_all, positive_all = lax.map(chunk_stats, jnp.arange(all_texts // chunk))
        log_sum_all = log_sum_all.reshape(-1)
        positive_all = positive_all.reshape(-1)
    mean_loss = jnp.sum(log_sum_all - positive_all) / all_texts

    own_start = me * own_texts
    own_ids = lax.broadcasted_iota(jnp.int32, (own_texts,), 0) + own_start
    own_partner = lax.dynamic_slice_in_dim(partner_all, own_start, own_texts)
    own_log_sum = lax.dynamic_slice_in_dim(log_sum_all, own_start, own_texts)

    sim_rows = lax.dot_general(embed_b, gathered, on_rows, preferred_element_type=jnp.float32) / logit_divisor
    column_ids = lax.broadcasted_iota(jnp.int32, sim_rows.shape, 1)
    masked_rows = jnp.where(column_ids == own_ids[:, None], masked_value, sim_rows)
    grad_rows = (
        jnp.exp(masked_rows - own_log_sum[:, None]) - (column_ids == own_partner[:, None]).astype(jnp.float32)
    ).astype(jnp.bfloat16)

    sim_cols = lax.dot_general(gathered, embed_b, on_rows, preferred_element_type=jnp.float32) / logit_divisor
    row_ids = lax.broadcasted_iota(jnp.int32, sim_cols.shape, 0)
    masked_cols = jnp.where(row_ids == own_ids[None, :], masked_value, sim_cols)
    grad_cols = (
        jnp.exp(masked_cols - log_sum_all[:, None]) - (partner_all[:, None] == own_ids[None, :]).astype(jnp.float32)
    ).astype(jnp.bfloat16)

    on_tokens = (((0,), (0,)), ((), ()))
    embedding_gradient = (
        jnp.dot(grad_rows, gathered, preferred_element_type=jnp.float32)
        + lax.dot_general(grad_cols, gathered, on_tokens, preferred_element_type=jnp.float32)
    ) / logit_divisor
    return mean_loss, embedding_gradient


def shards(
    hidden_in,
    segments,
    partner,
    attn_weights,
    ffn_weights,
    vectors,
    attn_momentum,
    ffn_momentum,
    vector_momentum,
    attn_averaged,
    ffn_averaged,
    vector_averaged,
):
    sizes = tuple(lax.axis_size(name) for name in AXES)
    n_dev = math.prod(sizes)
    me = flat_index(sizes)
    vec_len = vectors.shape[0]
    own_texts_n = partner.shape[0]
    width = attn_weights.shape[0]
    attn_local_t = attn_weights.T.astype(jnp.bfloat16)
    digit = 64
    extra = jnp.concatenate(
        [
            vectors.astype(jnp.bfloat16),
            (partner // digit).astype(jnp.bfloat16),
            (partner % digit).astype(jnp.bfloat16),
        ]
    )
    extra = jnp.pad(extra, (0, width - extra.shape[0]))[None, :]
    attn_block = jnp.concatenate([attn_local_t, extra], 0)
    attn_gathered = pair_gather(attn_block, sizes, 0)
    local_cols = attn_local_t.shape[0]
    attn_full_t = attn_gathered[:, :local_cols, :].reshape(-1, width)
    extra_all = attn_gathered[:, local_cols, :]
    vector_f = extra_all[:, :vec_len].reshape(-1).astype(jnp.float32)
    partner_all = (
        extra_all[:, vec_len : vec_len + own_texts_n].astype(jnp.int32) * digit
        + extra_all[:, vec_len + own_texts_n : vec_len + 2 * own_texts_n].astype(jnp.int32)
    ).reshape(-1)
    ffn_local, attn_gathered = lax.optimization_barrier((ffn_weights.astype(jnp.bfloat16), attn_gathered))
    ffn_full = lax.all_gather(ffn_local, AXES, axis=1, tiled=True)
    hidden = ffn_full.shape[1] // 2
    query_bias = vector_f[0:width]
    value_bias = vector_f[width : 2 * width]
    output_bias = vector_f[2 * width : 3 * width]
    gain_first = vector_f[3 * width : 4 * width]
    shift_first = vector_f[4 * width : 5 * width]
    upper_bias = vector_f[5 * width : 5 * width + hidden]
    lower_bias = vector_f[5 * width + hidden : 6 * width + hidden]
    gain_second = vector_f[6 * width + hidden : 7 * width + hidden]
    shift_second = vector_f[7 * width + hidden : 8 * width + hidden]
    w_qkv_t = attn_full_t[: 3 * width]
    w_output_t = attn_full_t[3 * width :]
    w_upper = ffn_full[:, :hidden]
    w_lower = ffn_full[:, hidden:]
    rows_dev, seq_len = segments.shape
    tokens_n = rows_dev * seq_len
    on_rows = (((1,), (1,)), ((), ()))
    on_tokens = (((0,), (0,)), ((), ()))
    qkv_bias = jnp.concatenate([query_bias, jnp.zeros_like(query_bias), value_bias])
    qkv_rows = (lax.dot_general(hidden_in, w_qkv_t, (((1,), (1,)), ((), ())), preferred_element_type=jnp.float32) + qkv_bias).astype(
        jnp.bfloat16
    )
    heads = qkv_rows.reshape(rows_dev, seq_len, 3, HEADS, HD)
    query_rows = heads[:, :, 0]
    key_rows = heads[:, :, 1]
    value_rows = heads[:, :, 2]
    mixed, log_norm = attend_rows(query_rows, key_rows, value_rows, segments)
    mixed_flat = mixed.reshape(tokens_n, width)
    first_sum = (
        hidden_in.astype(jnp.float32)
        + lax.dot_general(mixed_flat, w_output_t, (((1,), (1,)), ((), ())), preferred_element_type=jnp.float32)
        + output_bias
    )
    normed, normal_one, inverse_one = layer_norm_parts(first_sum, gain_first, shift_first)
    normed_r = bf16_round(normed)
    normed_b = normed_r.astype(jnp.bfloat16)
    upper = jnp.dot(normed_b, w_upper, preferred_element_type=jnp.float32) + upper_bias
    active_b = (0.5 * upper * (1.0 + lax.erf(upper / math.sqrt(2.0)))).astype(jnp.bfloat16)
    second_sum = (
        normed_r
        + lax.dot_general(active_b, w_lower, on_rows, preferred_element_type=jnp.float32)
        + lower_bias
    )
    result, normal_two, inverse_two = layer_norm_parts(second_sum, gain_second, shift_second)
    text_ids = jnp.arange(SEGS, dtype=jnp.int32)
    one_hot = (segments[:, None, :] == text_ids[None, :, None]).astype(jnp.float32)
    counts = jnp.sum(one_hot, -1, keepdims=True)
    pooled = (
        jnp.einsum(
            "rts,rsd->rtd",
            one_hot,
            result.reshape(rows_dev, seq_len, width),
            precision=lax.Precision.HIGHEST,
        )
        / counts
    ).reshape(-1, width)
    inv_norm = lax.rsqrt(jnp.sum(pooled * pooled, -1, keepdims=True) + pool_epsilon)
    embed_b = (pooled * inv_norm).astype(jnp.bfloat16)
    gathered_embeddings = pair_gather(embed_b, sizes, 2).reshape(-1, width)
    mean_loss, embedding_gradient = contrastive(embed_b, gathered_embeddings, partner_all, me)
    grad_pooled = inv_norm * embedding_gradient - pooled * (
        inv_norm * inv_norm * inv_norm
    ) * jnp.sum(embedding_gradient * pooled, -1, keepdims=True)
    derivative_output = jnp.einsum(
        "rts,rtd->rsd",
        one_hot,
        grad_pooled.reshape(rows_dev, SEGS, width) / counts,
        precision=lax.Precision.HIGHEST,
    ).reshape(tokens_n, width)
    grad_second, gain_two_grad, shift_two_grad = layer_norm_back(
        derivative_output, normal_two, inverse_two, gain_second
    )
    lower_bias_grad = jnp.sum(grad_second, 0)
    lower_grad_b = grad_second.astype(jnp.bfloat16)
    lower_w_grad_t = lax.dot_general(
        active_b, lower_grad_b, on_tokens, preferred_element_type=jnp.float32
    )
    grad_active = jnp.dot(lower_grad_b, w_lower, preferred_element_type=jnp.float32)
    cumulative = 0.5 * (1.0 + lax.erf(upper / math.sqrt(2.0)))
    density = jnp.exp(-0.5 * upper * upper) / math.sqrt(2.0 * math.pi)
    grad_upper = grad_active * (cumulative + upper * density)
    upper_bias_grad = jnp.sum(grad_upper, 0)
    upper_grad_b = grad_upper.astype(jnp.bfloat16)
    upper_w_grad_t = lax.dot_general(
        upper_grad_b, normed_b, on_tokens, preferred_element_type=jnp.float32
    )
    grad_normed = (
        lax.dot_general(upper_grad_b, w_upper, on_rows, preferred_element_type=jnp.float32)
        + grad_second
    )
    grad_first, gain_one_grad, shift_one_grad = layer_norm_back(
        grad_normed, normal_one, inverse_one, gain_first
    )
    output_bias_grad = jnp.sum(grad_first, 0)
    first_grad_b = grad_first.astype(jnp.bfloat16)
    output_w_grad_t = lax.dot_general(
        first_grad_b, mixed_flat, on_tokens, preferred_element_type=jnp.float32
    )
    grad_mixed = jnp.dot(
        first_grad_b, w_output_t, preferred_element_type=jnp.float32
    ).astype(jnp.bfloat16)
    grad_mixed = grad_mixed.reshape(rows_dev, seq_len, HEADS, HD)
    norm_tokens = jnp.swapaxes(log_norm, 1, 2).reshape(tokens_n, HEADS)
    qkv_grad = jnp.concatenate(
        attention_back(qkv_rows, grad_mixed.reshape(tokens_n, width), norm_tokens, segments, HEADS, HD), 1
    ).astype(jnp.float32)
    qkv_grad_f = bf16_round(qkv_grad)
    qkv_grad_b = qkv_grad_f.astype(jnp.bfloat16)
    query_bias_grad = jnp.sum(qkv_grad_f[:, :width], 0)
    value_bias_grad = jnp.sum(qkv_grad_f[:, 2 * width :], 0)
    qkv_w_grad_t = lax.dot_general(
        qkv_grad_b, hidden_in, on_tokens, preferred_element_type=jnp.float32
    )
    vector_grad = jnp.concatenate(
        [
            query_bias_grad,
            value_bias_grad,
            output_bias_grad,
            gain_one_grad,
            shift_one_grad,
            upper_bias_grad,
            lower_bias_grad,
            gain_two_grad,
            shift_two_grad,
        ]
    )
    attn_cols = (qkv_w_grad_t.shape[0] + output_w_grad_t.shape[0]) // n_dev
    ffn_cols = (upper_w_grad_t.shape[0] + lower_w_grad_t.shape[0]) // n_dev
    if attn_cols % 16 == 0 and ffn_cols % 16 == 0:
        grads = (
            (qkv_w_grad_t.astype(GRAD_SEND), output_w_grad_t.astype(GRAD_SEND)),
            (upper_w_grad_t.astype(GRAD_SEND), lower_w_grad_t.astype(GRAD_SEND)),
        )
    else:
        attn_blocks = jnp.concatenate(
            [qkv_w_grad_t.reshape(-1, attn_cols, width), output_w_grad_t.reshape(-1, attn_cols, width)], 0
        )
        ffn_blocks = jnp.concatenate(
            [upper_w_grad_t.reshape(-1, ffn_cols, width), lower_w_grad_t.reshape(-1, ffn_cols, width)], 0
        )
        grads = ((jnp.concatenate([attn_blocks, ffn_blocks], 1).astype(GRAD_SEND),),)
    parts = 3
    mine_parts, vector_slots, input_grad = halving_scatter(
        grads, vector_grad.reshape(n_dev, 1, -1), qkv_grad_b, w_qkv_t, grad_first, sizes, parts, 3
    )
    vector_reduced = jnp.sum(vector_slots[:, 0, :], 0)
    joined_reduced = jnp.transpose(mine_parts, (1, 0, 2)).reshape(-1, width).astype(jnp.float32)
    attn_reduced = joined_reduced[:attn_cols].T
    ffn_reduced = joined_reduced[attn_cols:].T
    attn_new, attn_moment, attn_average = apply_update(
        attn_weights, attn_reduced, attn_momentum, attn_averaged, decay_rate
    )
    ffn_new, ffn_moment, ffn_average = apply_update(
        ffn_weights, ffn_reduced, ffn_momentum, ffn_averaged, decay_rate
    )
    vector_new, vector_moment, vector_average = apply_update(
        vectors, vector_reduced, vector_momentum, vector_averaged, 0.0
    )
    return (
        mean_loss,
        input_grad,
        attn_reduced,
        ffn_reduced,
        vector_reduced,
        attn_new,
        ffn_new,
        vector_new,
        attn_moment,
        ffn_moment,
        vector_moment,
        attn_average,
        ffn_average,
        vector_average,
    )


def solution(mesh):
    in_specs = (
        P(("dp", "rep"), None),
        P(("dp", "rep"), None),
        P(("dp", "rep")),
        P(None, ("dp", "rep")),
        P(None, ("dp", "rep")),
        P(("dp", "rep")),
        P(None, ("dp", "rep")),
        P(None, ("dp", "rep")),
        P(("dp", "rep")),
        P(None, ("dp", "rep")),
        P(None, ("dp", "rep")),
        P(("dp", "rep")),
    )
    out_specs = (
        P(),
        P(("dp", "rep"), None),
        P(None, ("dp", "rep")),
        P(None, ("dp", "rep")),
        P(("dp", "rep")),
        P(None, ("dp", "rep")),
        P(None, ("dp", "rep")),
        P(("dp", "rep")),
        P(None, ("dp", "rep")),
        P(None, ("dp", "rep")),
        P(("dp", "rep")),
        P(None, ("dp", "rep")),
        P(None, ("dp", "rep")),
        P(("dp", "rep")),
    )
    return jax.shard_map(shards, mesh=mesh, in_specs=in_specs, out_specs=out_specs, check_vma=False)
```

```python
import functools
import math

import jax
import jax.numpy as jnp
from jax import lax
from jax.experimental import pallas as pl
from jax.experimental.pallas import tpu as pltpu
from jax.sharding import PartitionSpec as P

MESH = pl.DeviceIdType.MESH
GRAD_SEND = jnp.bfloat16
AXES = ("dp", "rep")

HEADS = 12
HD = 64
SEGS = 16


ln_epsilon = 1e-12
pool_epsilon = 1e-06
logit_divisor = 0.025
learn_rate = 0.01
momentum_rate = 0.9
decay_rate = 0.01
average_rate = 0.75
masked_value = -1e30


def layer_norm_parts(values, gain, shift):
    per_line_average = jnp.mean(values, -1, keepdims=True)
    centred = values - per_line_average
    inverse = lax.rsqrt(jnp.mean(centred * centred, -1, keepdims=True) + ln_epsilon)
    normal_part = centred * inverse
    return (normal_part * gain + shift, normal_part, inverse)


def layer_norm_back(grad_out, normal_part, inverse, gain):
    scaled = grad_out * gain
    grad_in = inverse * (
        scaled
        - jnp.mean(scaled, -1, keepdims=True)
        - normal_part * jnp.mean(scaled * normal_part, -1, keepdims=True)
    )
    return (grad_in, jnp.sum(grad_out * normal_part, 0), jnp.sum(grad_out, 0))


def row_scores(query_one, key_one, segment_one, scale):
    scores = (
        jnp.einsum("qhd,khd->hqk", query_one, key_one, preferred_element_type=jnp.float32) * scale
    )
    same_text = segment_one[:, None] == segment_one[None, :]
    return jnp.where(same_text[None], scores, masked_value)


def attend_rows(query_rows, key_rows, value_rows, row_segments):
    scale = 1.0 / math.sqrt(query_rows.shape[-1])

    def one_row(row_args):
        query_one, key_one, value_one, segment_one = row_args
        scores = row_scores(query_one, key_one, segment_one, scale)
        row_max = jnp.max(scores, -1, keepdims=True)
        exp_scores = jnp.exp(scores - row_max)
        sums = jnp.sum(exp_scores, -1, keepdims=True)
        attn_probs = exp_scores / sums
        mixed = jnp.einsum(
            "hqk,khd->qhd",
            attn_probs.astype(jnp.bfloat16),
            value_one,
            preferred_element_type=jnp.float32,
        )
        return (mixed.astype(jnp.bfloat16), (row_max + jnp.log(sums))[..., 0])

    return lax.map(one_row, (query_rows, key_rows, value_rows, row_segments))


def attend_back(query_rows, key_rows, value_rows, row_segments, log_norm, grad_mixed):
    scale = 1.0 / math.sqrt(query_rows.shape[-1])

    def one_row(row_args):
        query_one, key_one, value_one, segment_one, norm_one, grad_one = row_args
        scores = row_scores(query_one, key_one, segment_one, scale)
        attn_probs = jnp.exp(scores - norm_one[..., None])
        grad_value = jnp.einsum(
            "hqk,qhd->khd",
            attn_probs.astype(jnp.bfloat16),
            grad_one,
            preferred_element_type=jnp.float32,
        )
        grad_probs = jnp.einsum(
            "qhd,khd->hqk", grad_one, value_one, preferred_element_type=jnp.float32
        )
        inner = jnp.sum(attn_probs * grad_probs, -1, keepdims=True)
        grad_scores = (attn_probs * (grad_probs - inner)).astype(jnp.bfloat16)
        grad_query = (
            jnp.einsum("hqk,khd->qhd", grad_scores, key_one, preferred_element_type=jnp.float32)
            * scale
        )
        grad_key = (
            jnp.einsum("hqk,qhd->khd", grad_scores, query_one, preferred_element_type=jnp.float32)
            * scale
        )
        return jnp.concatenate([grad_query, grad_key, grad_value], axis=1)

    return lax.map(one_row, (query_rows, key_rows, value_rows, row_segments, log_norm, grad_mixed))


def attention_back_kernel(scale, q_ref, k_ref, v_ref, g_ref, norm_ref, seg_col_ref, seg_row_ref, dq_ref, dk_ref, dv_ref):
    pair = pl.program_id(1)
    width = q_ref.shape[1]
    half = width // 2
    lane = lax.broadcasted_iota(jnp.int32, (1, width), 1)
    same = seg_col_ref[...] == seg_row_ref[0]
    norms = norm_ref[...]
    norm_lane = lax.broadcasted_iota(jnp.int32, norms.shape, 1)
    q = q_ref[...]
    k = k_ref[...]
    v = v_ref[...]
    g = g_ref[...]
    zero_b = jnp.zeros_like(q)
    on_last = (((1,), (1,)), ((), ()))
    on_first = (((0,), (0,)), ((), ()))
    dq = jnp.zeros(q.shape, jnp.float32)
    dk = jnp.zeros(q.shape, jnp.float32)
    dv = jnp.zeros(q.shape, jnp.float32)
    for head in range(2):
        mine = (lane >= head * half) & (lane < (head + 1) * half)
        q_h = jnp.where(mine, q, zero_b)
        g_h = jnp.where(mine, g, zero_b)
        norm_h = jnp.sum(jnp.where(norm_lane == 2 * pair + head, norms, 0.0), 1, keepdims=True)
        scores = lax.dot_general(q_h, k, on_last, preferred_element_type=jnp.float32) * scale
        scores = jnp.where(same, scores, masked_value)
        probs = jnp.exp(scores - norm_h)
        grad_v = lax.dot_general(probs.astype(jnp.bfloat16), g, on_first, preferred_element_type=jnp.float32)
        grad_p = lax.dot_general(g_h, v, on_last, preferred_element_type=jnp.float32)
        inner = jnp.sum(probs * grad_p, -1, keepdims=True)
        grad_s = (probs * (grad_p - inner)).astype(jnp.bfloat16)
        grad_q = jnp.dot(grad_s, k, preferred_element_type=jnp.float32) * scale
        grad_k = lax.dot_general(grad_s, q, on_first, preferred_element_type=jnp.float32) * scale
        dq = jnp.where(mine, grad_q, dq)
        dk = jnp.where(mine, grad_k, dk)
        dv = jnp.where(mine, grad_v, dv)
    dq_ref[...] = dq.astype(dq_ref.dtype)
    dk_ref[...] = dk.astype(dk_ref.dtype)
    dv_ref[...] = dv.astype(dv_ref.dtype)


def attention_back(qkv_rows, grad_mixed_flat, norm_tokens, segments, heads, head_dim):
    tokens, three_width = qkv_rows.shape
    width = three_width // 3
    rows, seq_len = segments.shape
    pair_width = 2 * head_dim
    pairs = heads // 2
    seg_col = segments.reshape(tokens, 1)
    seg_row = segments.reshape(rows, 1, seq_len)
    scale = 1.0 / math.sqrt(head_dim)
    out = jax.ShapeDtypeStruct((tokens, width), jnp.bfloat16)
    return pl.pallas_call(
        functools.partial(attention_back_kernel, scale),
        grid=(rows, pairs),
        in_specs=[
            pl.BlockSpec((seq_len, pair_width), lambda r, p: (r, p)),
            pl.BlockSpec((seq_len, pair_width), lambda r, p: (r, pairs + p)),
            pl.BlockSpec((seq_len, pair_width), lambda r, p: (r, 2 * pairs + p)),
            pl.BlockSpec((seq_len, pair_width), lambda r, p: (r, p)),
            pl.BlockSpec((seq_len, heads), lambda r, p: (r, 0)),
            pl.BlockSpec((seq_len, 1), lambda r, p: (r, 0)),
            pl.BlockSpec((1, 1, seq_len), lambda r, p: (r, 0, 0)),
        ],
        out_specs=[pl.BlockSpec((seq_len, pair_width), lambda r, p: (r, p))] * 3,
        out_shape=[out, out, out],
        compiler_params=pltpu.CompilerParams(vmem_limit_bytes=48 * 1024 * 1024),
        cost_estimate=pl.CostEstimate(
            flops=10 * rows * heads * seq_len * seq_len * pair_width,
            transcendentals=rows * heads * seq_len * seq_len,
            bytes_accessed=tokens * (three_width + 4 * width) * 2,
        ),
    )(qkv_rows, qkv_rows, qkv_rows, grad_mixed_flat, norm_tokens, seg_col, seg_row)


def apply_update(weight, grad, moment, average, decay):
    step_grad = grad + decay * weight
    new_moment = momentum_rate * moment + step_grad
    new_weight = weight - learn_rate * (step_grad + momentum_rate * new_moment)
    fresh_running_mean = average_rate * average + (1.0 - average_rate) * new_weight
    return (new_weight, new_moment, fresh_running_mean)


def bf16_round(values):
    return lax.reduce_precision(values, exponent_bits=8, mantissa_bits=7)


def flat_index(sizes):
    idx = 0
    for name, size in zip(AXES, sizes):
        idx = idx * size + lax.axis_index(name)
    return idx


def device_of(flat, sizes):
    coords = []
    for size in reversed(sizes):
        coords.append(lax.rem(flat, size))
        flat = flat // size
    return tuple(reversed(coords))


def enter_all(n, sizes, me):
    barrier = pltpu.get_barrier_semaphore()

    def greet(k, carry):
        peer = lax.rem(me + k, n)
        pl.semaphore_signal(barrier, inc=1, device_id=device_of(peer, sizes), device_id_type=MESH)
        return carry

    lax.fori_loop(1, n, greet, 0)
    pl.semaphore_wait(barrier, n - 1)


def gather_kernel(n, sizes, x_ref, out_ref, send_sem, recv_sem):
    me = flat_index(sizes)
    enter_all(n, sizes, me)

    def send(k, carry):
        peer = lax.rem(me + k, n)
        pltpu.make_async_remote_copy(
            src_ref=x_ref, dst_ref=out_ref.at[me], send_sem=send_sem.at[k], recv_sem=recv_sem.at[me],
            device_id=device_of(peer, sizes), device_id_type=MESH,
        ).start()
        return carry

    lax.fori_loop(1, n, send, 0)
    out_ref[me] = x_ref[...]

    def finish(k, carry):
        peer = lax.rem(me + k, n)
        src = lax.rem(me + n - k, n)
        pltpu.make_async_remote_copy(
            src_ref=x_ref, dst_ref=out_ref.at[me], send_sem=send_sem.at[k], recv_sem=recv_sem.at[me],
            device_id=device_of(peer, sizes), device_id_type=MESH,
        ).wait_send()
        pltpu.make_async_remote_copy(
            src_ref=x_ref, dst_ref=out_ref.at[src], send_sem=send_sem.at[k], recv_sem=recv_sem.at[src],
            device_id=device_of(src, sizes), device_id_type=MESH,
        ).wait_recv()
        return carry

    lax.fori_loop(1, n, finish, 0)


def small_gather(x, sizes, cid):
    n = math.prod(sizes)
    return pl.pallas_call(
        functools.partial(gather_kernel, n, sizes),
        out_shape=jax.ShapeDtypeStruct((n,) + x.shape, x.dtype),
        in_specs=[pl.BlockSpec(memory_space=pltpu.VMEM)],
        out_specs=pl.BlockSpec(memory_space=pltpu.VMEM),
        scratch_shapes=[pltpu.SemaphoreType.DMA((n,)), pltpu.SemaphoreType.DMA((n,))],
        compiler_params=pltpu.CompilerParams(collective_id=cid, has_side_effects=True),
    )(x)


def scatter_kernel(n, sizes, x_ref, out_ref, send_sem, recv_sem):
    me = flat_index(sizes)
    enter_all(n, sizes, me)

    def send(k, carry):
        peer = lax.rem(me + k, n)
        pltpu.make_async_remote_copy(
            src_ref=x_ref.at[peer], dst_ref=out_ref.at[me], send_sem=send_sem.at[k], recv_sem=recv_sem.at[me],
            device_id=device_of(peer, sizes), device_id_type=MESH,
        ).start()
        return carry

    lax.fori_loop(1, n, send, 0)
    out_ref[me] = x_ref[me]

    def finish(k, carry):
        peer = lax.rem(me + k, n)
        src = lax.rem(me + n - k, n)
        pltpu.make_async_remote_copy(
            src_ref=x_ref.at[peer], dst_ref=out_ref.at[me], send_sem=send_sem.at[k], recv_sem=recv_sem.at[me],
            device_id=device_of(peer, sizes), device_id_type=MESH,
        ).wait_send()
        pltpu.make_async_remote_copy(
            src_ref=x_ref.at[src], dst_ref=out_ref.at[src], send_sem=send_sem.at[k], recv_sem=recv_sem.at[src],
            device_id=device_of(src, sizes), device_id_type=MESH,
        ).wait_recv()
        return carry

    lax.fori_loop(1, n, finish, 0)


def small_scatter(x, sizes, cid):
    n = math.prod(sizes)
    return pl.pallas_call(
        functools.partial(scatter_kernel, n, sizes),
        out_shape=jax.ShapeDtypeStruct(x.shape, x.dtype),
        in_specs=[pl.BlockSpec(memory_space=pltpu.VMEM)],
        out_specs=pl.BlockSpec(memory_space=pltpu.VMEM),
        scratch_shapes=[pltpu.SemaphoreType.DMA((n,)), pltpu.SemaphoreType.DMA((n,))],
        compiler_params=pltpu.CompilerParams(collective_id=cid, has_side_effects=True),
    )(x)


def pair_gather_kernel(n, sizes, x_ref, out_ref, local_sem, send1, recv1, send2, recv2, send3, recv3):
    me = flat_index(sizes)
    chips = n // 2
    chip = me // 2
    core = lax.rem(me, 2)
    partner = me + 1 - 2 * core
    enter_all(n, sizes, me)

    local = pltpu.make_async_copy(x_ref, out_ref.at[me], local_sem)
    local.start()
    first = pltpu.make_async_remote_copy(
        src_ref=x_ref, dst_ref=out_ref.at[me], send_sem=send1, recv_sem=recv1,
        device_id=device_of(partner, sizes), device_id_type=MESH,
    )
    first.start()
    local.wait()
    first.wait_send()
    pltpu.make_async_remote_copy(
        src_ref=x_ref, dst_ref=out_ref.at[partner], send_sem=send1, recv_sem=recv1,
        device_id=device_of(partner, sizes), device_id_type=MESH,
    ).wait_recv()

    def pair(c):
        return out_ref.at[pl.ds(2 * c, 2)]

    def target(k):
        return lax.rem(chip + 2 * k - 1 + core, chips)

    def source(k):
        return lax.rem(chip + chips - (2 * k - 1 + core), chips)

    count = (chips - core) // 2

    def send_out(k, carry):
        other = target(k)
        pltpu.make_async_remote_copy(
            src_ref=pair(chip), dst_ref=pair(chip), send_sem=send2.at[other], recv_sem=recv2.at[chip],
            device_id=device_of(2 * other + core, sizes), device_id_type=MESH,
        ).start()
        return carry

    lax.fori_loop(1, count + 1, send_out, 0)

    def take_in(k, carry):
        other = source(k)
        pltpu.make_async_remote_copy(
            src_ref=pair(other), dst_ref=pair(other), send_sem=send2.at[other], recv_sem=recv2.at[other],
            device_id=device_of(2 * other + core, sizes), device_id_type=MESH,
        ).wait_recv()
        pltpu.make_async_remote_copy(
            src_ref=pair(other), dst_ref=pair(other), send_sem=send3.at[other], recv_sem=recv3.at[other],
            device_id=device_of(partner, sizes), device_id_type=MESH,
        ).start()
        return carry

    lax.fori_loop(1, count + 1, take_in, 0)

    def sent_out(k, carry):
        other = target(k)
        pltpu.make_async_remote_copy(
            src_ref=pair(chip), dst_ref=pair(chip), send_sem=send2.at[other], recv_sem=recv2.at[chip],
            device_id=device_of(2 * other + core, sizes), device_id_type=MESH,
        ).wait_send()
        return carry

    lax.fori_loop(1, count + 1, sent_out, 0)

    def forwarded(k, carry):
        other = source(k)
        pltpu.make_async_remote_copy(
            src_ref=pair(other), dst_ref=pair(other), send_sem=send3.at[other], recv_sem=recv3.at[other],
            device_id=device_of(partner, sizes), device_id_type=MESH,
        ).wait_send()
        return carry

    lax.fori_loop(1, count + 1, forwarded, 0)

    other_count = (chips - (1 - core)) // 2

    def partner_source(k):
        return lax.rem(chip + chips - (2 * k - 1 + (1 - core)), chips)

    def from_partner(k, carry):
        other = partner_source(k)
        pltpu.make_async_remote_copy(
            src_ref=pair(other), dst_ref=pair(other), send_sem=send3.at[other], recv_sem=recv3.at[other],
            device_id=device_of(partner, sizes), device_id_type=MESH,
        ).wait_recv()
        return carry

    lax.fori_loop(1, other_count + 1, from_partner, 0)


def pair_gather(x, sizes, cid):
    n = math.prod(sizes)
    chips = n // 2
    dma = pltpu.SemaphoreType.DMA
    return pl.pallas_call(
        functools.partial(pair_gather_kernel, n, sizes),
        out_shape=jax.ShapeDtypeStruct((n,) + x.shape, x.dtype),
        in_specs=[pl.BlockSpec(memory_space=pltpu.VMEM)],
        out_specs=pl.BlockSpec(memory_space=pltpu.VMEM),
        scratch_shapes=[dma(()), dma(()), dma(()), dma((chips,)), dma((chips,)), dma((chips,)), dma((chips,))],
        compiler_params=pltpu.CompilerParams(collective_id=cid, has_side_effects=True),
    )(x)


def halving_orders(n, parts):
    bits = n.bit_length() - 1
    middle = list(range(1, bits - 1))
    orders = []
    for p in range(parts):
        shift = p % len(middle) if middle else 0
        orders.append(tuple([0] + middle[shift:] + middle[:shift] + [bits - 1]))
    return tuple(orders)


def halving_kernel(n, sizes, orders, cols, tile, groups, computed, *refs):
    count = sum(groups) - int(computed)
    sources = list(refs[:count])
    vec_ref, dq_ref, w_ref, res_ref = refs[count : count + 4]
    at = count + 4
    if computed:
        x_ref = refs[at]
        at += 1
    out_ref, vec_out, grad_out, work = refs[at : at + 4]
    at += 4
    if computed:
        made = refs[at]
        at += 1
        sources.insert(0, made)
    rest = refs[at:]
    grouped = []
    at = 0
    for g in groups:
        grouped.append(sources[at : at + g])
        at += g
    steps = len(orders[0])
    parts = len(orders)
    layout = []
    head = 0
    for group in grouped:
        size = sum(math.prod(s.shape[:-1]) for s in group) // n
        layout.append((group, size, head))
        head += size
    recvs = rest[:steps]
    local_sem, send_sems, recv_sems, vec_send, vec_recv = rest[steps:]
    me = flat_index(sizes)

    def partner_of(bit):
        mine = lax.rem(me // (2**bit), 2)
        return mine, me + (1 - 2 * mine) * (2**bit)

    enter_all(n, sizes, me)

    def vec_copy(k):
        peer = lax.rem(me + k, n)
        return pltpu.make_async_remote_copy(
            src_ref=vec_ref.at[peer], dst_ref=vec_out.at[me], send_sem=vec_send.at[k], recv_sem=vec_recv.at[me],
            device_id=device_of(peer, sizes), device_id_type=MESH,
        )

    def vec_start(k, carry):
        vec_copy(k).start()
        return carry

    lax.fori_loop(1, n, vec_start, 0)
    vec_out[me] = vec_ref[me]

    half = n // 2
    first = []
    issuers = []
    for p in range(parts):
        order = orders[p]
        mine, other = partner_of(order[0])
        column = pl.ds(p * cols, cols)

        def owner(j, side, order=order):
            o = side * (2 ** order[0])
            for m, bit in enumerate(order[1:]):
                o = o + lax.rem(j // (2 ** (steps - 2 - m)), 2) * (2**bit)
            return o

        def issue(j, carry, p=p, owner=owner, mine=mine, other=other, column=column, which=None):
            for o, dst, remote in ((owner(j, 1 - mine), recvs[0].at[p, j], True), (owner(j, mine), work.at[p, j], False)):
                for group, size, head in [layout[w] for w in which]:
                    offset = 0
                    for chosen in group:
                        split = math.prod(chosen.shape[:-1]) // size

                        def move(chosen=chosen, offset=offset, o=o, dst=dst, remote=remote, size=size, head=head):
                            if len(chosen.shape) == 3:
                                src_ref = chosen.at[o - offset, :, column]
                            else:
                                src_ref = chosen.at[pl.ds((o - offset) * size, size), column]
                            dst_ref = dst.at[pl.ds(head, size)]
                            if remote:
                                pltpu.make_async_remote_copy(
                                    src_ref=src_ref, dst_ref=dst_ref,
                                    send_sem=send_sems.at[p, 0], recv_sem=recv_sems.at[p, 0],
                                    device_id=device_of(other, sizes), device_id_type=MESH,
                                ).start()
                            else:
                                pltpu.make_async_copy(src_ref, dst_ref, local_sem.at[p]).start()

                        if len(group) == 1:
                            move()
                        else:
                            pl.when((o >= offset) & (o < offset + split))(move)
                        offset += split

            return carry

        issuers.append(issue)
        first.append(other)
    later = [0] if computed else []
    sooner = [w for w in range(len(layout)) if w not in later]
    for issue in issuers:
        lax.fori_loop(0, half, functools.partial(issue, which=sooner), 0)
    if computed:
        on_first = (((0,), (0,)), ((), ()))

        def product_t(t, carry):
            rows = pl.ds(pl.multiple_of(t * tile, tile), tile)
            made[rows, :] = lax.dot_general(
                dq_ref[:, rows], x_ref[...], on_first, preferred_element_type=jnp.float32
            ).astype(made.dtype)
            return carry

        lax.fori_loop(0, made.shape[0] // tile, product_t, 0)
        for issue in issuers:
            lax.fori_loop(0, half, functools.partial(issue, which=later), 0)
    for p in range(parts):
        whole = pltpu.make_async_remote_copy(
            src_ref=work.at[p, pl.ds(0, half)], dst_ref=recvs[0].at[p],
            send_sem=send_sems.at[p, 0], recv_sem=recv_sems.at[p, 0],
            device_id=device_of(first[p], sizes), device_id_type=MESH,
        )
        pltpu.make_async_copy(work.at[p, pl.ds(0, half)], work.at[p, pl.ds(0, half)], local_sem.at[p]).wait()
        whole.wait_recv()
        whole.wait_send()

        def accumulate0(i, carry, p=p):
            total = work[p, i].astype(jnp.float32) + recvs[0][p, i].astype(jnp.float32)
            work[p, i] = total.astype(work.dtype)
            return carry

        lax.fori_loop(0, half, accumulate0, 0)

    for step in range(1, steps):
        half = n >> (step + 1)
        copies = []
        for p in range(parts):
            mine, other = partner_of(orders[p][step])
            send = pltpu.make_async_remote_copy(
                src_ref=work.at[p, pl.ds((1 - mine) * half, half)], dst_ref=recvs[step].at[p],
                send_sem=send_sems.at[p, step], recv_sem=recv_sems.at[p, step],
                device_id=device_of(other, sizes), device_id_type=MESH,
            )
            send.start()
            copies.append((mine, send))
        if step == 1:
            def product(t, carry):
                rows = pl.ds(pl.multiple_of(t * tile, tile), tile)
                grad_out[rows, :] = (
                    jnp.dot(dq_ref[rows, :], w_ref[...], preferred_element_type=jnp.float32) + res_ref[rows, :]
                )
                return carry

            lax.fori_loop(0, grad_out.shape[0] // tile, product, 0)
        for p in range(parts):
            mine, send = copies[p]
            send.wait_recv()
            send.wait_send()

            def accumulate(i, carry, p=p, mine=mine, half=half, step=step):
                total = work[p, mine * half + i].astype(jnp.float32) + recvs[step][p, i].astype(jnp.float32)
                work[p, i] = total.astype(work.dtype)
                return carry

            lax.fori_loop(0, half, accumulate, 0)
    for p in range(parts):
        out_ref[p] = work[p, 0]

    def vec_finish(k, carry):
        vec_copy(k).wait_send()
        src = lax.rem(me + n - k, n)
        pltpu.make_async_remote_copy(
            src_ref=vec_ref.at[src], dst_ref=vec_out.at[src], send_sem=vec_send.at[k], recv_sem=vec_recv.at[src],
            device_id=device_of(src, sizes), device_id_type=MESH,
        ).wait_recv()
        return carry

    lax.fori_loop(1, n, vec_finish, 0)


def halving_scatter(grouped, vec, grad_b, weight_t, residual, sizes, parts, cid, tokens=None):
    n = math.prod(sizes)
    computed = tokens is not None
    groups = tuple(len(g) for g in grouped)
    given = [s for g in grouped for s in g if s is not None]
    made_shape = (grad_b.shape[1], tokens.shape[1]) if computed else None
    assert not computed or made_shape[0] % 128 == 0
    shapes = [made_shape if s is None else s.shape for g in grouped for s in g]
    dtype = given[0].dtype
    width = shapes[0][-1]
    rows = sum(math.prod(s[:-1]) for s in shapes) // n
    cols = width // parts
    orders = halving_orders(n, parts)
    steps = len(orders[0])
    tile = 128
    dma = pltpu.SemaphoreType.DMA
    vmem = pl.BlockSpec(memory_space=pltpu.VMEM)
    scratch = [pltpu.VMEM((parts, n // 2, rows, cols), dtype)]
    if computed:
        scratch.append(pltpu.VMEM(made_shape, dtype))
    scratch += [pltpu.VMEM((parts, n >> (k + 1), rows, cols), dtype) for k in range(steps)]
    scratch += [dma((parts,)), dma((parts, steps)), dma((parts, steps)), dma((n,)), dma((n,))]
    return pl.pallas_call(
        functools.partial(halving_kernel, n, sizes, orders, cols, tile, groups, computed),
        out_shape=(
            jax.ShapeDtypeStruct((parts, rows, cols), dtype),
            jax.ShapeDtypeStruct(vec.shape, vec.dtype),
            jax.ShapeDtypeStruct(residual.shape, jnp.float32),
        ),
        in_specs=[pl.BlockSpec(memory_space=pl.ANY)] * len(given) + [vmem] * (4 + int(computed)),
        out_specs=(vmem, vmem, vmem),
        scratch_shapes=scratch,
        compiler_params=pltpu.CompilerParams(
            collective_id=cid, has_side_effects=True, vmem_limit_bytes=60 * 1024 * 1024
        ),
    )(*given, vec, grad_b, weight_t, residual, *([tokens] if computed else []))


def contrastive(embed_b, gathered, partner_all, me):
    own_texts = embed_b.shape[0]
    all_texts = gathered.shape[0]
    chunk = min(all_texts, 1024)
    on_rows = (((1,), (1,)), ((), ()))

    def chunk_stats(c):
        rows_b = lax.dynamic_slice_in_dim(gathered, c * chunk, chunk)
        sim = lax.dot_general(rows_b, gathered, on_rows, preferred_element_type=jnp.float32) / logit_divisor
        column_ids = lax.broadcasted_iota(jnp.int32, sim.shape, 1)
        row_ids = lax.broadcasted_iota(jnp.int32, sim.shape, 0) + c * chunk
        masked = jnp.where(column_ids == row_ids, masked_value, sim)
        row_max = jnp.max(masked, -1, keepdims=True)
        log_sum = row_max + jnp.log(jnp.sum(jnp.exp(masked - row_max), -1, keepdims=True))
        wanted = lax.dynamic_slice_in_dim(partner_all, c * chunk, chunk)
        positive = jnp.sum(jnp.where(column_ids == wanted[:, None], sim, 0.0), -1)
        return log_sum[:, 0], positive

    if all_texts == chunk:
        log_sum_all, positive_all = chunk_stats(0)
    else:
        log_sum_all, positive_all = lax.map(chunk_stats, jnp.arange(all_texts // chunk))
        log_sum_all = log_sum_all.reshape(-1)
        positive_all = positive_all.reshape(-1)
    mean_loss = jnp.sum(log_sum_all - positive_all) / all_texts

    own_start = me * own_texts
    own_ids = lax.broadcasted_iota(jnp.int32, (own_texts,), 0) + own_start
    own_partner = lax.dynamic_slice_in_dim(partner_all, own_start, own_texts)
    own_log_sum = lax.dynamic_slice_in_dim(log_sum_all, own_start, own_texts)

    sim_rows = lax.dot_general(embed_b, gathered, on_rows, preferred_element_type=jnp.float32) / logit_divisor
    column_ids = lax.broadcasted_iota(jnp.int32, sim_rows.shape, 1)
    masked_rows = jnp.where(column_ids == own_ids[:, None], masked_value, sim_rows)
    grad_rows = (
        jnp.exp(masked_rows - own_log_sum[:, None]) - (column_ids == own_partner[:, None]).astype(jnp.float32)
    ).astype(jnp.bfloat16)

    sim_cols = lax.dot_general(gathered, embed_b, on_rows, preferred_element_type=jnp.float32) / logit_divisor
    row_ids = lax.broadcasted_iota(jnp.int32, sim_cols.shape, 0)
    masked_cols = jnp.where(row_ids == own_ids[None, :], masked_value, sim_cols)
    grad_cols = (
        jnp.exp(masked_cols - log_sum_all[:, None]) - (partner_all[:, None] == own_ids[None, :]).astype(jnp.float32)
    ).astype(jnp.bfloat16)

    on_tokens = (((0,), (0,)), ((), ()))
    embedding_gradient = (
        jnp.dot(grad_rows, gathered, preferred_element_type=jnp.float32)
        + lax.dot_general(grad_cols, gathered, on_tokens, preferred_element_type=jnp.float32)
    ) / logit_divisor
    return mean_loss, embedding_gradient


def shards(
    hidden_in,
    segments,
    partner,
    attn_weights,
    ffn_weights,
    vectors,
    attn_momentum,
    ffn_momentum,
    vector_momentum,
    attn_averaged,
    ffn_averaged,
    vector_averaged,
):
    sizes = tuple(lax.axis_size(name) for name in AXES)
    n_dev = math.prod(sizes)
    me = flat_index(sizes)
    vec_len = vectors.shape[0]
    small = jnp.concatenate([vectors, partner.astype(jnp.float32)])[None, :]
    small_all = small_gather(small, sizes, 0)[:, 0, :]
    vector_f = bf16_round(small_all[:, :vec_len].reshape(-1))
    partner_all = small_all[:, vec_len:].reshape(-1).astype(jnp.int32)
    attn_full, ffn_full = (
        lax.all_gather(attn_weights.astype(jnp.bfloat16), AXES, axis=1, tiled=True),
        lax.all_gather(ffn_weights.astype(jnp.bfloat16), AXES, axis=1, tiled=True),
    )
    width = attn_full.shape[0]
    hidden = ffn_full.shape[1] // 2
    query_bias = vector_f[0:width]
    value_bias = vector_f[width : 2 * width]
    output_bias = vector_f[2 * width : 3 * width]
    gain_first = vector_f[3 * width : 4 * width]
    shift_first = vector_f[4 * width : 5 * width]
    upper_bias = vector_f[5 * width : 5 * width + hidden]
    lower_bias = vector_f[5 * width + hidden : 6 * width + hidden]
    gain_second = vector_f[6 * width + hidden : 7 * width + hidden]
    shift_second = vector_f[7 * width + hidden : 8 * width + hidden]
    w_qkv = attn_full[:, : 3 * width]
    w_output = attn_full[:, 3 * width :]
    w_upper = ffn_full[:, :hidden]
    w_lower = ffn_full[:, hidden:]
    rows_dev, seq_len = segments.shape
    tokens_n = rows_dev * seq_len
    on_rows = (((1,), (1,)), ((), ()))
    on_tokens = (((0,), (0,)), ((), ()))
    qkv_bias = jnp.concatenate([query_bias, jnp.zeros_like(query_bias), value_bias])
    qkv_rows = (jnp.dot(hidden_in, w_qkv, preferred_element_type=jnp.float32) + qkv_bias).astype(
        jnp.bfloat16
    )
    heads = qkv_rows.reshape(rows_dev, seq_len, 3, HEADS, HD)
    query_rows = heads[:, :, 0]
    key_rows = heads[:, :, 1]
    value_rows = heads[:, :, 2]
    mixed, log_norm = attend_rows(query_rows, key_rows, value_rows, segments)
    mixed_flat = mixed.reshape(tokens_n, width)
    first_sum = (
        hidden_in.astype(jnp.float32)
        + jnp.dot(mixed_flat, w_output, preferred_element_type=jnp.float32)
        + output_bias
    )
    normed, normal_one, inverse_one = layer_norm_parts(first_sum, gain_first, shift_first)
    normed_r = bf16_round(normed)
    normed_b = normed_r.astype(jnp.bfloat16)
    upper = jnp.dot(normed_b, w_upper, preferred_element_type=jnp.float32) + upper_bias
    active_b = (0.5 * upper * (1.0 + lax.erf(upper / math.sqrt(2.0)))).astype(jnp.bfloat16)
    second_sum = (
        normed_r
        + lax.dot_general(active_b, w_lower, on_rows, preferred_element_type=jnp.float32)
        + lower_bias
    )
    result, normal_two, inverse_two = layer_norm_parts(second_sum, gain_second, shift_second)
    text_ids = jnp.arange(SEGS, dtype=jnp.int32)
    one_hot = (segments[:, None, :] == text_ids[None, :, None]).astype(jnp.float32)
    counts = jnp.sum(one_hot, -1, keepdims=True)
    pooled = (
        jnp.einsum(
            "rts,rsd->rtd",
            one_hot,
            result.reshape(rows_dev, seq_len, width),
            precision=lax.Precision.HIGHEST,
        )
        / counts
    ).reshape(-1, width)
    inv_norm = lax.rsqrt(jnp.sum(pooled * pooled, -1, keepdims=True) + pool_epsilon)
    embed_b = (pooled * inv_norm).astype(jnp.bfloat16)
    gathered_embeddings = pair_gather(embed_b, sizes, 2).reshape(-1, width)
    mean_loss, embedding_gradient = contrastive(embed_b, gathered_embeddings, partner_all, me)
    grad_pooled = inv_norm * embedding_gradient - pooled * (
        inv_norm * inv_norm * inv_norm
    ) * jnp.sum(embedding_gradient * pooled, -1, keepdims=True)
    derivative_output = jnp.einsum(
        "rts,rtd->rsd",
        one_hot,
        grad_pooled.reshape(rows_dev, SEGS, width) / counts,
        precision=lax.Precision.HIGHEST,
    ).reshape(tokens_n, width)
    grad_second, gain_two_grad, shift_two_grad = layer_norm_back(
        derivative_output, normal_two, inverse_two, gain_second
    )
    lower_bias_grad = jnp.sum(grad_second, 0)
    lower_grad_b = grad_second.astype(jnp.bfloat16)
    lower_w_grad_t = lax.dot_general(
        active_b, lower_grad_b, on_tokens, preferred_element_type=jnp.float32
    )
    grad_active = jnp.dot(lower_grad_b, w_lower, preferred_element_type=jnp.float32)
    cumulative = 0.5 * (1.0 + lax.erf(upper / math.sqrt(2.0)))
    density = jnp.exp(-0.5 * upper * upper) / math.sqrt(2.0 * math.pi)
    grad_upper = grad_active * (cumulative + upper * density)
    upper_bias_grad = jnp.sum(grad_upper, 0)
    upper_grad_b = grad_upper.astype(jnp.bfloat16)
    upper_w_grad_t = lax.dot_general(
        upper_grad_b, normed_b, on_tokens, preferred_element_type=jnp.float32
    )
    grad_normed = (
        lax.dot_general(upper_grad_b, w_upper, on_rows, preferred_element_type=jnp.float32)
        + grad_second
    )
    grad_first, gain_one_grad, shift_one_grad = layer_norm_back(
        grad_normed, normal_one, inverse_one, gain_first
    )
    output_bias_grad = jnp.sum(grad_first, 0)
    first_grad_b = grad_first.astype(jnp.bfloat16)
    output_w_grad_t = lax.dot_general(
        first_grad_b, mixed_flat, on_tokens, preferred_element_type=jnp.float32
    )
    grad_mixed = lax.dot_general(
        first_grad_b, w_output, on_rows, preferred_element_type=jnp.float32
    ).astype(jnp.bfloat16)
    grad_mixed = grad_mixed.reshape(rows_dev, seq_len, HEADS, HD)
    norm_tokens = jnp.swapaxes(log_norm, 1, 2).reshape(tokens_n, HEADS)
    qkv_grad = jnp.concatenate(
        attention_back(qkv_rows, grad_mixed.reshape(tokens_n, width), norm_tokens, segments, HEADS, HD), 1
    ).astype(jnp.float32)
    qkv_grad_f = bf16_round(qkv_grad)
    qkv_grad_b = qkv_grad_f.astype(jnp.bfloat16)
    query_bias_grad = jnp.sum(qkv_grad_f[:, :width], 0)
    value_bias_grad = jnp.sum(qkv_grad_f[:, 2 * width :], 0)
    qkv_w_grad_t = lax.dot_general(
        qkv_grad_b, hidden_in, on_tokens, preferred_element_type=jnp.float32
    )
    vector_grad = jnp.concatenate(
        [
            query_bias_grad,
            value_bias_grad,
            output_bias_grad,
            gain_one_grad,
            shift_one_grad,
            upper_bias_grad,
            lower_bias_grad,
            gain_two_grad,
            shift_two_grad,
        ]
    )
    attn_cols = (qkv_w_grad_t.shape[0] + output_w_grad_t.shape[0]) // n_dev
    ffn_cols = (upper_w_grad_t.shape[0] + lower_w_grad_t.shape[0]) // n_dev
    if attn_cols % 16 == 0 and ffn_cols % 16 == 0:
        grads = (
            (None, output_w_grad_t.astype(GRAD_SEND)),
            (upper_w_grad_t.astype(GRAD_SEND), lower_w_grad_t.astype(GRAD_SEND)),
        )
        made_from = hidden_in
    else:
        attn_blocks = jnp.concatenate(
            [qkv_w_grad_t.reshape(-1, attn_cols, width), output_w_grad_t.reshape(-1, attn_cols, width)], 0
        )
        ffn_blocks = jnp.concatenate(
            [upper_w_grad_t.reshape(-1, ffn_cols, width), lower_w_grad_t.reshape(-1, ffn_cols, width)], 0
        )
        grads = ((jnp.concatenate([attn_blocks, ffn_blocks], 1).astype(GRAD_SEND),),)
        made_from = None
    parts = 3
    mine_parts, vector_slots, input_grad = halving_scatter(
        grads, vector_grad.reshape(n_dev, 1, -1), qkv_grad_b, w_qkv.T, grad_first, sizes, parts, 3, made_from
    )
    vector_reduced = jnp.sum(vector_slots[:, 0, :], 0)
    joined_reduced = jnp.transpose(mine_parts, (1, 0, 2)).reshape(-1, width).astype(jnp.float32)
    attn_reduced = joined_reduced[:attn_cols].T
    ffn_reduced = joined_reduced[attn_cols:].T
    attn_new, attn_moment, attn_average = apply_update(
        attn_weights, attn_reduced, attn_momentum, attn_averaged, decay_rate
    )
    ffn_new, ffn_moment, ffn_average = apply_update(
        ffn_weights, ffn_reduced, ffn_momentum, ffn_averaged, decay_rate
    )
    vector_new, vector_moment, vector_average = apply_update(
        vectors, vector_reduced, vector_momentum, vector_averaged, 0.0
    )
    return (
        mean_loss,
        input_grad,
        attn_reduced,
        ffn_reduced,
        vector_reduced,
        attn_new,
        ffn_new,
        vector_new,
        attn_moment,
        ffn_moment,
        vector_moment,
        attn_average,
        ffn_average,
        vector_average,
    )


def solution(mesh):
    in_specs = (
        P(("dp", "rep"), None),
        P(("dp", "rep"), None),
        P(("dp", "rep")),
        P(None, ("dp", "rep")),
        P(None, ("dp", "rep")),
        P(("dp", "rep")),
        P(None, ("dp", "rep")),
        P(None, ("dp", "rep")),
        P(("dp", "rep")),
        P(None, ("dp", "rep")),
        P(None, ("dp", "rep")),
        P(("dp", "rep")),
    )
    out_specs = (
        P(),
        P(("dp", "rep"), None),
        P(None, ("dp", "rep")),
        P(None, ("dp", "rep")),
        P(("dp", "rep")),
        P(None, ("dp", "rep")),
        P(None, ("dp", "rep")),
        P(("dp", "rep")),
        P(None, ("dp", "rep")),
        P(None, ("dp", "rep")),
        P(("dp", "rep")),
        P(None, ("dp", "rep")),
        P(None, ("dp", "rep")),
        P(("dp", "rep")),
    )
    return jax.shard_map(shards, mesh=mesh, in_specs=in_specs, out_specs=out_specs, check_vma=False)
```

```python
import functools
import math

import jax
import jax.numpy as jnp
from jax import lax
from jax.experimental import pallas as pl
from jax.experimental.pallas import tpu as pltpu
from jax.sharding import PartitionSpec as P

MESH = pl.DeviceIdType.MESH
GRAD_SEND = jnp.bfloat16
AXES = ("dp", "rep")

HEADS = 12
HD = 64
SEGS = 16


ln_epsilon = 1e-12
pool_epsilon = 1e-06
logit_divisor = 0.025
learn_rate = 0.01
momentum_rate = 0.9
decay_rate = 0.01
average_rate = 0.75
masked_value = -1e30


def layer_norm_parts(values, gain, shift):
    per_line_average = jnp.mean(values, -1, keepdims=True)
    centred = values - per_line_average
    inverse = lax.rsqrt(jnp.mean(centred * centred, -1, keepdims=True) + ln_epsilon)
    normal_part = centred * inverse
    return (normal_part * gain + shift, normal_part, inverse)


def layer_norm_back(grad_out, normal_part, inverse, gain):
    scaled = grad_out * gain
    grad_in = inverse * (
        scaled
        - jnp.mean(scaled, -1, keepdims=True)
        - normal_part * jnp.mean(scaled * normal_part, -1, keepdims=True)
    )
    return (grad_in, jnp.sum(grad_out * normal_part, 0), jnp.sum(grad_out, 0))


def row_scores(query_one, key_one, segment_one, scale):
    scores = (
        jnp.einsum("qhd,khd->hqk", query_one, key_one, preferred_element_type=jnp.float32) * scale
    )
    same_text = segment_one[:, None] == segment_one[None, :]
    return jnp.where(same_text[None], scores, masked_value)


def attend_rows(query_rows, key_rows, value_rows, row_segments):
    scale = 1.0 / math.sqrt(query_rows.shape[-1])

    def one_row(row_args):
        query_one, key_one, value_one, segment_one = row_args
        scores = row_scores(query_one, key_one, segment_one, scale)
        row_max = jnp.max(scores, -1, keepdims=True)
        exp_scores = jnp.exp(scores - row_max)
        sums = jnp.sum(exp_scores, -1, keepdims=True)
        attn_probs = exp_scores / sums
        mixed = jnp.einsum(
            "hqk,khd->qhd",
            attn_probs.astype(jnp.bfloat16),
            value_one,
            preferred_element_type=jnp.float32,
        )
        return (mixed.astype(jnp.bfloat16), (row_max + jnp.log(sums))[..., 0])

    return lax.map(one_row, (query_rows, key_rows, value_rows, row_segments))


def attend_back(query_rows, key_rows, value_rows, row_segments, log_norm, grad_mixed):
    scale = 1.0 / math.sqrt(query_rows.shape[-1])

    def one_row(row_args):
        query_one, key_one, value_one, segment_one, norm_one, grad_one = row_args
        scores = row_scores(query_one, key_one, segment_one, scale)
        attn_probs = jnp.exp(scores - norm_one[..., None])
        grad_value = jnp.einsum(
            "hqk,qhd->khd",
            attn_probs.astype(jnp.bfloat16),
            grad_one,
            preferred_element_type=jnp.float32,
        )
        grad_probs = jnp.einsum(
            "qhd,khd->hqk", grad_one, value_one, preferred_element_type=jnp.float32
        )
        inner = jnp.sum(attn_probs * grad_probs, -1, keepdims=True)
        grad_scores = (attn_probs * (grad_probs - inner)).astype(jnp.bfloat16)
        grad_query = (
            jnp.einsum("hqk,khd->qhd", grad_scores, key_one, preferred_element_type=jnp.float32)
            * scale
        )
        grad_key = (
            jnp.einsum("hqk,qhd->khd", grad_scores, query_one, preferred_element_type=jnp.float32)
            * scale
        )
        return jnp.concatenate([grad_query, grad_key, grad_value], axis=1)

    return lax.map(one_row, (query_rows, key_rows, value_rows, row_segments, log_norm, grad_mixed))


def attention_back_kernel(scale, q_ref, k_ref, v_ref, g_ref, norm_ref, seg_col_ref, seg_row_ref, dq_ref, dk_ref, dv_ref):
    pair = pl.program_id(1)
    width = q_ref.shape[1]
    half = width // 2
    lane = lax.broadcasted_iota(jnp.int32, (1, width), 1)
    same = seg_col_ref[...] == seg_row_ref[0]
    norms = norm_ref[...]
    norm_lane = lax.broadcasted_iota(jnp.int32, norms.shape, 1)
    q = q_ref[...]
    k = k_ref[...]
    v = v_ref[...]
    g = g_ref[...]
    zero_b = jnp.zeros_like(q)
    on_last = (((1,), (1,)), ((), ()))
    on_first = (((0,), (0,)), ((), ()))
    dq = jnp.zeros(q.shape, jnp.float32)
    dk = jnp.zeros(q.shape, jnp.float32)
    dv = jnp.zeros(q.shape, jnp.float32)
    for head in range(2):
        mine = (lane >= head * half) & (lane < (head + 1) * half)
        q_h = jnp.where(mine, q, zero_b)
        g_h = jnp.where(mine, g, zero_b)
        norm_h = jnp.sum(jnp.where(norm_lane == 2 * pair + head, norms, 0.0), 1, keepdims=True)
        scores = lax.dot_general(q_h, k, on_last, preferred_element_type=jnp.float32) * scale
        scores = jnp.where(same, scores, masked_value)
        probs = jnp.exp(scores - norm_h)
        grad_v = lax.dot_general(probs.astype(jnp.bfloat16), g, on_first, preferred_element_type=jnp.float32)
        grad_p = lax.dot_general(g_h, v, on_last, preferred_element_type=jnp.float32)
        inner = jnp.sum(probs * grad_p, -1, keepdims=True)
        grad_s = (probs * (grad_p - inner)).astype(jnp.bfloat16)
        grad_q = jnp.dot(grad_s, k, preferred_element_type=jnp.float32) * scale
        grad_k = lax.dot_general(grad_s, q, on_first, preferred_element_type=jnp.float32) * scale
        dq = jnp.where(mine, grad_q, dq)
        dk = jnp.where(mine, grad_k, dk)
        dv = jnp.where(mine, grad_v, dv)
    dq_ref[...] = dq.astype(dq_ref.dtype)
    dk_ref[...] = dk.astype(dk_ref.dtype)
    dv_ref[...] = dv.astype(dv_ref.dtype)


def attention_back(qkv_rows, grad_mixed_flat, norm_tokens, segments, heads, head_dim):
    tokens, three_width = qkv_rows.shape
    width = three_width // 3
    rows, seq_len = segments.shape
    pair_width = 2 * head_dim
    pairs = heads // 2
    seg_col = segments.reshape(tokens, 1)
    seg_row = segments.reshape(rows, 1, seq_len)
    scale = 1.0 / math.sqrt(head_dim)
    out = jax.ShapeDtypeStruct((tokens, width), jnp.bfloat16)
    return pl.pallas_call(
        functools.partial(attention_back_kernel, scale),
        grid=(rows, pairs),
        in_specs=[
            pl.BlockSpec((seq_len, pair_width), lambda r, p: (r, p)),
            pl.BlockSpec((seq_len, pair_width), lambda r, p: (r, pairs + p)),
            pl.BlockSpec((seq_len, pair_width), lambda r, p: (r, 2 * pairs + p)),
            pl.BlockSpec((seq_len, pair_width), lambda r, p: (r, p)),
            pl.BlockSpec((seq_len, heads), lambda r, p: (r, 0)),
            pl.BlockSpec((seq_len, 1), lambda r, p: (r, 0)),
            pl.BlockSpec((1, 1, seq_len), lambda r, p: (r, 0, 0)),
        ],
        out_specs=[pl.BlockSpec((seq_len, pair_width), lambda r, p: (r, p))] * 3,
        out_shape=[out, out, out],
        compiler_params=pltpu.CompilerParams(vmem_limit_bytes=48 * 1024 * 1024),
        cost_estimate=pl.CostEstimate(
            flops=10 * rows * heads * seq_len * seq_len * pair_width,
            transcendentals=rows * heads * seq_len * seq_len,
            bytes_accessed=tokens * (three_width + 4 * width) * 2,
        ),
    )(qkv_rows, qkv_rows, qkv_rows, grad_mixed_flat, norm_tokens, seg_col, seg_row)


def apply_update(weight, grad, moment, average, decay):
    step_grad = grad + decay * weight
    new_moment = momentum_rate * moment + step_grad
    new_weight = weight - learn_rate * (step_grad + momentum_rate * new_moment)
    fresh_running_mean = average_rate * average + (1.0 - average_rate) * new_weight
    return (new_weight, new_moment, fresh_running_mean)


def bf16_round(values):
    return lax.reduce_precision(values, exponent_bits=8, mantissa_bits=7)


def flat_index(sizes):
    idx = 0
    for name, size in zip(AXES, sizes):
        idx = idx * size + lax.axis_index(name)
    return idx


def device_of(flat, sizes):
    coords = []
    for size in reversed(sizes):
        coords.append(lax.rem(flat, size))
        flat = flat // size
    return tuple(reversed(coords))


def enter_all(n, sizes, me):
    barrier = pltpu.get_barrier_semaphore()

    def greet(k, carry):
        peer = lax.rem(me + k, n)
        pl.semaphore_signal(barrier, inc=1, device_id=device_of(peer, sizes), device_id_type=MESH)
        return carry

    lax.fori_loop(1, n, greet, 0)
    pl.semaphore_wait(barrier, n - 1)


def gather_kernel(n, sizes, x_ref, out_ref, send_sem, recv_sem):
    me = flat_index(sizes)
    enter_all(n, sizes, me)

    def send(k, carry):
        peer = lax.rem(me + k, n)
        pltpu.make_async_remote_copy(
            src_ref=x_ref, dst_ref=out_ref.at[me], send_sem=send_sem.at[k], recv_sem=recv_sem.at[me],
            device_id=device_of(peer, sizes), device_id_type=MESH,
        ).start()
        return carry

    lax.fori_loop(1, n, send, 0)
    out_ref[me] = x_ref[...]

    def finish(k, carry):
        peer = lax.rem(me + k, n)
        src = lax.rem(me + n - k, n)
        pltpu.make_async_remote_copy(
            src_ref=x_ref, dst_ref=out_ref.at[me], send_sem=send_sem.at[k], recv_sem=recv_sem.at[me],
            device_id=device_of(peer, sizes), device_id_type=MESH,
        ).wait_send()
        pltpu.make_async_remote_copy(
            src_ref=x_ref, dst_ref=out_ref.at[src], send_sem=send_sem.at[k], recv_sem=recv_sem.at[src],
            device_id=device_of(src, sizes), device_id_type=MESH,
        ).wait_recv()
        return carry

    lax.fori_loop(1, n, finish, 0)


def small_gather(x, sizes, cid):
    n = math.prod(sizes)
    return pl.pallas_call(
        functools.partial(gather_kernel, n, sizes),
        out_shape=jax.ShapeDtypeStruct((n,) + x.shape, x.dtype),
        in_specs=[pl.BlockSpec(memory_space=pltpu.VMEM)],
        out_specs=pl.BlockSpec(memory_space=pltpu.VMEM),
        scratch_shapes=[pltpu.SemaphoreType.DMA((n,)), pltpu.SemaphoreType.DMA((n,))],
        compiler_params=pltpu.CompilerParams(collective_id=cid, has_side_effects=True),
    )(x)


def scatter_kernel(n, sizes, x_ref, out_ref, send_sem, recv_sem):
    me = flat_index(sizes)
    enter_all(n, sizes, me)

    def send(k, carry):
        peer = lax.rem(me + k, n)
        pltpu.make_async_remote_copy(
            src_ref=x_ref.at[peer], dst_ref=out_ref.at[me], send_sem=send_sem.at[k], recv_sem=recv_sem.at[me],
            device_id=device_of(peer, sizes), device_id_type=MESH,
        ).start()
        return carry

    lax.fori_loop(1, n, send, 0)
    out_ref[me] = x_ref[me]

    def finish(k, carry):
        peer = lax.rem(me + k, n)
        src = lax.rem(me + n - k, n)
        pltpu.make_async_remote_copy(
            src_ref=x_ref.at[peer], dst_ref=out_ref.at[me], send_sem=send_sem.at[k], recv_sem=recv_sem.at[me],
            device_id=device_of(peer, sizes), device_id_type=MESH,
        ).wait_send()
        pltpu.make_async_remote_copy(
            src_ref=x_ref.at[src], dst_ref=out_ref.at[src], send_sem=send_sem.at[k], recv_sem=recv_sem.at[src],
            device_id=device_of(src, sizes), device_id_type=MESH,
        ).wait_recv()
        return carry

    lax.fori_loop(1, n, finish, 0)


def small_scatter(x, sizes, cid):
    n = math.prod(sizes)
    return pl.pallas_call(
        functools.partial(scatter_kernel, n, sizes),
        out_shape=jax.ShapeDtypeStruct(x.shape, x.dtype),
        in_specs=[pl.BlockSpec(memory_space=pltpu.VMEM)],
        out_specs=pl.BlockSpec(memory_space=pltpu.VMEM),
        scratch_shapes=[pltpu.SemaphoreType.DMA((n,)), pltpu.SemaphoreType.DMA((n,))],
        compiler_params=pltpu.CompilerParams(collective_id=cid, has_side_effects=True),
    )(x)


def pair_gather_kernel(n, sizes, x_ref, out_ref, local_sem, send1, recv1, send2, recv2, send3, recv3):
    me = flat_index(sizes)
    chips = n // 2
    chip = me // 2
    core = lax.rem(me, 2)
    partner = me + 1 - 2 * core
    enter_all(n, sizes, me)

    local = pltpu.make_async_copy(x_ref, out_ref.at[me], local_sem)
    local.start()
    first = pltpu.make_async_remote_copy(
        src_ref=x_ref, dst_ref=out_ref.at[me], send_sem=send1, recv_sem=recv1,
        device_id=device_of(partner, sizes), device_id_type=MESH,
    )
    first.start()
    local.wait()
    first.wait_send()
    pltpu.make_async_remote_copy(
        src_ref=x_ref, dst_ref=out_ref.at[partner], send_sem=send1, recv_sem=recv1,
        device_id=device_of(partner, sizes), device_id_type=MESH,
    ).wait_recv()

    def pair(c):
        return out_ref.at[pl.ds(2 * c, 2)]

    def target(k):
        return lax.rem(chip + 2 * k - 1 + core, chips)

    def source(k):
        return lax.rem(chip + chips - (2 * k - 1 + core), chips)

    count = (chips - core) // 2

    def send_out(k, carry):
        other = target(k)
        pltpu.make_async_remote_copy(
            src_ref=pair(chip), dst_ref=pair(chip), send_sem=send2.at[other], recv_sem=recv2.at[chip],
            device_id=device_of(2 * other + core, sizes), device_id_type=MESH,
        ).start()
        return carry

    lax.fori_loop(1, count + 1, send_out, 0)

    def take_in(k, carry):
        other = source(k)
        pltpu.make_async_remote_copy(
            src_ref=pair(other), dst_ref=pair(other), send_sem=send2.at[other], recv_sem=recv2.at[other],
            device_id=device_of(2 * other + core, sizes), device_id_type=MESH,
        ).wait_recv()
        pltpu.make_async_remote_copy(
            src_ref=pair(other), dst_ref=pair(other), send_sem=send3.at[other], recv_sem=recv3.at[other],
            device_id=device_of(partner, sizes), device_id_type=MESH,
        ).start()
        return carry

    lax.fori_loop(1, count + 1, take_in, 0)

    def sent_out(k, carry):
        other = target(k)
        pltpu.make_async_remote_copy(
            src_ref=pair(chip), dst_ref=pair(chip), send_sem=send2.at[other], recv_sem=recv2.at[chip],
            device_id=device_of(2 * other + core, sizes), device_id_type=MESH,
        ).wait_send()
        return carry

    lax.fori_loop(1, count + 1, sent_out, 0)

    def forwarded(k, carry):
        other = source(k)
        pltpu.make_async_remote_copy(
            src_ref=pair(other), dst_ref=pair(other), send_sem=send3.at[other], recv_sem=recv3.at[other],
            device_id=device_of(partner, sizes), device_id_type=MESH,
        ).wait_send()
        return carry

    lax.fori_loop(1, count + 1, forwarded, 0)

    other_count = (chips - (1 - core)) // 2

    def partner_source(k):
        return lax.rem(chip + chips - (2 * k - 1 + (1 - core)), chips)

    def from_partner(k, carry):
        other = partner_source(k)
        pltpu.make_async_remote_copy(
            src_ref=pair(other), dst_ref=pair(other), send_sem=send3.at[other], recv_sem=recv3.at[other],
            device_id=device_of(partner, sizes), device_id_type=MESH,
        ).wait_recv()
        return carry

    lax.fori_loop(1, other_count + 1, from_partner, 0)


def pair_gather(x, sizes, cid):
    n = math.prod(sizes)
    chips = n // 2
    dma = pltpu.SemaphoreType.DMA
    return pl.pallas_call(
        functools.partial(pair_gather_kernel, n, sizes),
        out_shape=jax.ShapeDtypeStruct((n,) + x.shape, x.dtype),
        in_specs=[pl.BlockSpec(memory_space=pltpu.VMEM)],
        out_specs=pl.BlockSpec(memory_space=pltpu.VMEM),
        scratch_shapes=[dma(()), dma(()), dma(()), dma((chips,)), dma((chips,)), dma((chips,)), dma((chips,))],
        compiler_params=pltpu.CompilerParams(collective_id=cid, has_side_effects=True),
    )(x)


def halving_orders(n, parts):
    bits = n.bit_length() - 1
    middle = list(range(1, bits - 1))
    orders = []
    for p in range(parts):
        shift = p % len(middle) if middle else 0
        orders.append(tuple([0] + middle[shift:] + middle[:shift] + [bits - 1]))
    return tuple(orders)


def halving_kernel(n, sizes, orders, cols, tile, groups, computed, *refs):
    count = sum(groups) - 2 * int(computed)
    sources = list(refs[:count])
    vec_ref, dq_ref, w_ref, res_ref = refs[count : count + 4]
    at = count + 4
    if computed:
        x_ref, l2_ref, r2_ref = refs[at : at + 3]
        at += 3
    out_ref, vec_out, grad_out, work = refs[at : at + 4]
    at += 4
    if computed:
        made, made2 = refs[at : at + 2]
        at += 2
        sources = [made, made2] + sources
    rest = refs[at:]
    grouped = []
    at = 0
    for g in groups:
        grouped.append(sources[at : at + g])
        at += g
    steps = len(orders[0])
    parts = len(orders)
    layout = []
    head = 0
    for group in grouped:
        size = sum(math.prod(s.shape[:-1]) for s in group) // n
        layout.append((group, size, head))
        head += size
    recvs = rest[:steps]
    local_sem, send_sems, recv_sems, vec_send, vec_recv = rest[steps:]
    me = flat_index(sizes)

    def partner_of(bit):
        mine = lax.rem(me // (2**bit), 2)
        return mine, me + (1 - 2 * mine) * (2**bit)

    enter_all(n, sizes, me)

    def vec_copy(k):
        peer = lax.rem(me + k, n)
        return pltpu.make_async_remote_copy(
            src_ref=vec_ref.at[peer], dst_ref=vec_out.at[me], send_sem=vec_send.at[k], recv_sem=vec_recv.at[me],
            device_id=device_of(peer, sizes), device_id_type=MESH,
        )

    def vec_start(k, carry):
        vec_copy(k).start()
        return carry

    lax.fori_loop(1, n, vec_start, 0)
    vec_out[me] = vec_ref[me]

    half = n // 2
    first = []
    issuers = []
    for p in range(parts):
        order = orders[p]
        mine, other = partner_of(order[0])
        column = pl.ds(p * cols, cols)

        def owner(j, side, order=order):
            o = side * (2 ** order[0])
            for m, bit in enumerate(order[1:]):
                o = o + lax.rem(j // (2 ** (steps - 2 - m)), 2) * (2**bit)
            return o

        def issue(j, carry, p=p, owner=owner, mine=mine, other=other, column=column, which=None):
            for o, dst, remote in ((owner(j, 1 - mine), recvs[0].at[p, j], True), (owner(j, mine), work.at[p, j], False)):
                for group, size, head in [layout[w] for w in which]:
                    offset = 0
                    for chosen in group:
                        split = math.prod(chosen.shape[:-1]) // size

                        def move(chosen=chosen, offset=offset, o=o, dst=dst, remote=remote, size=size, head=head):
                            if len(chosen.shape) == 3:
                                src_ref = chosen.at[o - offset, :, column]
                            else:
                                src_ref = chosen.at[pl.ds((o - offset) * size, size), column]
                            dst_ref = dst.at[pl.ds(head, size)]
                            if remote:
                                pltpu.make_async_remote_copy(
                                    src_ref=src_ref, dst_ref=dst_ref,
                                    send_sem=send_sems.at[p, 0], recv_sem=recv_sems.at[p, 0],
                                    device_id=device_of(other, sizes), device_id_type=MESH,
                                ).start()
                            else:
                                pltpu.make_async_copy(src_ref, dst_ref, local_sem.at[p]).start()

                        if len(group) == 1:
                            move()
                        else:
                            pl.when((o >= offset) & (o < offset + split))(move)
                        offset += split

            return carry

        issuers.append(issue)
        first.append(other)
    later = [0] if computed else []
    sooner = [w for w in range(len(layout)) if w not in later]
    for issue in issuers:
        lax.fori_loop(0, half, functools.partial(issue, which=sooner), 0)
    if computed:
        on_first = (((0,), (0,)), ((), ()))

        def product_t(t, carry):
            rows = pl.ds(pl.multiple_of(t * tile, tile), tile)
            made[rows, :] = lax.dot_general(
                dq_ref[:, rows], x_ref[...], on_first, preferred_element_type=jnp.float32
            ).astype(made.dtype)
            return carry

        lax.fori_loop(0, made.shape[0] // tile, product_t, 0)

        def product_t2(t, carry):
            rows = pl.ds(pl.multiple_of(t * tile, tile), tile)
            made2[rows, :] = lax.dot_general(
                l2_ref[:, rows], r2_ref[...], on_first, preferred_element_type=jnp.float32
            ).astype(made2.dtype)
            return carry

        lax.fori_loop(0, made2.shape[0] // tile, product_t2, 0)
        for issue in issuers:
            lax.fori_loop(0, half, functools.partial(issue, which=later), 0)
    for p in range(parts):
        whole = pltpu.make_async_remote_copy(
            src_ref=work.at[p, pl.ds(0, half)], dst_ref=recvs[0].at[p],
            send_sem=send_sems.at[p, 0], recv_sem=recv_sems.at[p, 0],
            device_id=device_of(first[p], sizes), device_id_type=MESH,
        )
        pltpu.make_async_copy(work.at[p, pl.ds(0, half)], work.at[p, pl.ds(0, half)], local_sem.at[p]).wait()
        whole.wait_recv()
        whole.wait_send()

        def accumulate0(i, carry, p=p):
            total = work[p, i].astype(jnp.float32) + recvs[0][p, i].astype(jnp.float32)
            work[p, i] = total.astype(work.dtype)
            return carry

        lax.fori_loop(0, half, accumulate0, 0)

    for step in range(1, steps):
        half = n >> (step + 1)
        copies = []
        for p in range(parts):
            mine, other = partner_of(orders[p][step])
            send = pltpu.make_async_remote_copy(
                src_ref=work.at[p, pl.ds((1 - mine) * half, half)], dst_ref=recvs[step].at[p],
                send_sem=send_sems.at[p, step], recv_sem=recv_sems.at[p, step],
                device_id=device_of(other, sizes), device_id_type=MESH,
            )
            send.start()
            copies.append((mine, send))
        if step == 1:
            def product(t, carry):
                rows = pl.ds(pl.multiple_of(t * tile, tile), tile)
                grad_out[rows, :] = (
                    jnp.dot(dq_ref[rows, :], w_ref[...], preferred_element_type=jnp.float32) + res_ref[rows, :]
                )
                return carry

            lax.fori_loop(0, grad_out.shape[0] // tile, product, 0)
        for p in range(parts):
            mine, send = copies[p]
            send.wait_recv()
            send.wait_send()

            def accumulate(i, carry, p=p, mine=mine, half=half, step=step):
                total = work[p, mine * half + i].astype(jnp.float32) + recvs[step][p, i].astype(jnp.float32)
                work[p, i] = total.astype(work.dtype)
                return carry

            lax.fori_loop(0, half, accumulate, 0)
    for p in range(parts):
        out_ref[p] = work[p, 0]

    def vec_finish(k, carry):
        vec_copy(k).wait_send()
        src = lax.rem(me + n - k, n)
        pltpu.make_async_remote_copy(
            src_ref=vec_ref.at[src], dst_ref=vec_out.at[src], send_sem=vec_send.at[k], recv_sem=vec_recv.at[src],
            device_id=device_of(src, sizes), device_id_type=MESH,
        ).wait_recv()
        return carry

    lax.fori_loop(1, n, vec_finish, 0)


def halving_scatter(grouped, vec, grad_b, weight_t, residual, sizes, parts, cid, tokens=None, second=None):
    n = math.prod(sizes)
    computed = tokens is not None
    groups = tuple(len(g) for g in grouped)
    given = [s for g in grouped for s in g if s is not None]
    made_shape = (grad_b.shape[1], tokens.shape[1]) if computed else None
    made2_shape = (second[0].shape[1], second[1].shape[1]) if computed else None
    assert not computed or (made_shape[0] % 128 == 0 and made2_shape[0] % 128 == 0)
    shapes = [s.shape for s in given]
    if computed:
        shapes = [made_shape, made2_shape] + shapes
    dtype = given[0].dtype
    width = shapes[0][-1]
    rows = sum(math.prod(s[:-1]) for s in shapes) // n
    cols = width // parts
    orders = halving_orders(n, parts)
    steps = len(orders[0])
    tile = 128
    dma = pltpu.SemaphoreType.DMA
    vmem = pl.BlockSpec(memory_space=pltpu.VMEM)
    scratch = [pltpu.VMEM((parts, n // 2, rows, cols), dtype)]
    if computed:
        scratch += [pltpu.VMEM(made_shape, dtype), pltpu.VMEM(made2_shape, dtype)]
    scratch += [pltpu.VMEM((parts, n >> (k + 1), rows, cols), dtype) for k in range(steps)]
    scratch += [dma((parts,)), dma((parts, steps)), dma((parts, steps)), dma((n,)), dma((n,))]
    return pl.pallas_call(
        functools.partial(halving_kernel, n, sizes, orders, cols, tile, groups, computed),
        out_shape=(
            jax.ShapeDtypeStruct((parts, rows, cols), dtype),
            jax.ShapeDtypeStruct(vec.shape, vec.dtype),
            jax.ShapeDtypeStruct(residual.shape, jnp.float32),
        ),
        in_specs=[pl.BlockSpec(memory_space=pl.ANY)] * len(given) + [vmem] * (4 + 3 * int(computed)),
        out_specs=(vmem, vmem, vmem),
        scratch_shapes=scratch,
        compiler_params=pltpu.CompilerParams(
            collective_id=cid, has_side_effects=True, vmem_limit_bytes=60 * 1024 * 1024
        ),
    )(*given, vec, grad_b, weight_t, residual, *([tokens, *second] if computed else []))


def contrastive(embed_b, gathered, partner_all, me):
    own_texts = embed_b.shape[0]
    all_texts = gathered.shape[0]
    chunk = min(all_texts, 1024)
    on_rows = (((1,), (1,)), ((), ()))

    def chunk_stats(c):
        rows_b = lax.dynamic_slice_in_dim(gathered, c * chunk, chunk)
        sim = lax.dot_general(rows_b, gathered, on_rows, preferred_element_type=jnp.float32) / logit_divisor
        column_ids = lax.broadcasted_iota(jnp.int32, sim.shape, 1)
        row_ids = lax.broadcasted_iota(jnp.int32, sim.shape, 0) + c * chunk
        masked = jnp.where(column_ids == row_ids, masked_value, sim)
        row_max = jnp.max(masked, -1, keepdims=True)
        log_sum = row_max + jnp.log(jnp.sum(jnp.exp(masked - row_max), -1, keepdims=True))
        wanted = lax.dynamic_slice_in_dim(partner_all, c * chunk, chunk)
        positive = jnp.sum(jnp.where(column_ids == wanted[:, None], sim, 0.0), -1)
        return log_sum[:, 0], positive

    if all_texts == chunk:
        log_sum_all, positive_all = chunk_stats(0)
    else:
        log_sum_all, positive_all = lax.map(chunk_stats, jnp.arange(all_texts // chunk))
        log_sum_all = log_sum_all.reshape(-1)
        positive_all = positive_all.reshape(-1)
    mean_loss = jnp.sum(log_sum_all - positive_all) / all_texts

    own_start = me * own_texts
    own_ids = lax.broadcasted_iota(jnp.int32, (own_texts,), 0) + own_start
    own_partner = lax.dynamic_slice_in_dim(partner_all, own_start, own_texts)
    own_log_sum = lax.dynamic_slice_in_dim(log_sum_all, own_start, own_texts)

    sim_rows = lax.dot_general(embed_b, gathered, on_rows, preferred_element_type=jnp.float32) / logit_divisor
    column_ids = lax.broadcasted_iota(jnp.int32, sim_rows.shape, 1)
    masked_rows = jnp.where(column_ids == own_ids[:, None], masked_value, sim_rows)
    grad_rows = (
        jnp.exp(masked_rows - own_log_sum[:, None]) - (column_ids == own_partner[:, None]).astype(jnp.float32)
    ).astype(jnp.bfloat16)

    sim_cols = lax.dot_general(gathered, embed_b, on_rows, preferred_element_type=jnp.float32) / logit_divisor
    row_ids = lax.broadcasted_iota(jnp.int32, sim_cols.shape, 0)
    masked_cols = jnp.where(row_ids == own_ids[None, :], masked_value, sim_cols)
    grad_cols = (
        jnp.exp(masked_cols - log_sum_all[:, None]) - (partner_all[:, None] == own_ids[None, :]).astype(jnp.float32)
    ).astype(jnp.bfloat16)

    on_tokens = (((0,), (0,)), ((), ()))
    embedding_gradient = (
        jnp.dot(grad_rows, gathered, preferred_element_type=jnp.float32)
        + lax.dot_general(grad_cols, gathered, on_tokens, preferred_element_type=jnp.float32)
    ) / logit_divisor
    return mean_loss, embedding_gradient


def shards(
    hidden_in,
    segments,
    partner,
    attn_weights,
    ffn_weights,
    vectors,
    attn_momentum,
    ffn_momentum,
    vector_momentum,
    attn_averaged,
    ffn_averaged,
    vector_averaged,
):
    sizes = tuple(lax.axis_size(name) for name in AXES)
    n_dev = math.prod(sizes)
    me = flat_index(sizes)
    vec_len = vectors.shape[0]
    small = jnp.concatenate([vectors, partner.astype(jnp.float32)])[None, :]
    small_all = small_gather(small, sizes, 0)[:, 0, :]
    vector_f = bf16_round(small_all[:, :vec_len].reshape(-1))
    partner_all = small_all[:, vec_len:].reshape(-1).astype(jnp.int32)
    attn_full, ffn_full = (
        lax.all_gather(attn_weights.astype(jnp.bfloat16), AXES, axis=1, tiled=True),
        lax.all_gather(ffn_weights.astype(jnp.bfloat16), AXES, axis=1, tiled=True),
    )
    width = attn_full.shape[0]
    hidden = ffn_full.shape[1] // 2
    query_bias = vector_f[0:width]
    value_bias = vector_f[width : 2 * width]
    output_bias = vector_f[2 * width : 3 * width]
    gain_first = vector_f[3 * width : 4 * width]
    shift_first = vector_f[4 * width : 5 * width]
    upper_bias = vector_f[5 * width : 5 * width + hidden]
    lower_bias = vector_f[5 * width + hidden : 6 * width + hidden]
    gain_second = vector_f[6 * width + hidden : 7 * width + hidden]
    shift_second = vector_f[7 * width + hidden : 8 * width + hidden]
    w_qkv = attn_full[:, : 3 * width]
    w_output = attn_full[:, 3 * width :]
    w_upper = ffn_full[:, :hidden]
    w_lower = ffn_full[:, hidden:]
    rows_dev, seq_len = segments.shape
    tokens_n = rows_dev * seq_len
    on_rows = (((1,), (1,)), ((), ()))
    on_tokens = (((0,), (0,)), ((), ()))
    qkv_bias = jnp.concatenate([query_bias, jnp.zeros_like(query_bias), value_bias])
    qkv_rows = (jnp.dot(hidden_in, w_qkv, preferred_element_type=jnp.float32) + qkv_bias).astype(
        jnp.bfloat16
    )
    heads = qkv_rows.reshape(rows_dev, seq_len, 3, HEADS, HD)
    query_rows = heads[:, :, 0]
    key_rows = heads[:, :, 1]
    value_rows = heads[:, :, 2]
    mixed, log_norm = attend_rows(query_rows, key_rows, value_rows, segments)
    mixed_flat = mixed.reshape(tokens_n, width)
    first_sum = (
        hidden_in.astype(jnp.float32)
        + jnp.dot(mixed_flat, w_output, preferred_element_type=jnp.float32)
        + output_bias
    )
    normed, normal_one, inverse_one = layer_norm_parts(first_sum, gain_first, shift_first)
    normed_r = bf16_round(normed)
    normed_b = normed_r.astype(jnp.bfloat16)
    upper = jnp.dot(normed_b, w_upper, preferred_element_type=jnp.float32) + upper_bias
    active_b = (0.5 * upper * (1.0 + lax.erf(upper / math.sqrt(2.0)))).astype(jnp.bfloat16)
    second_sum = (
        normed_r
        + lax.dot_general(active_b, w_lower, on_rows, preferred_element_type=jnp.float32)
        + lower_bias
    )
    result, normal_two, inverse_two = layer_norm_parts(second_sum, gain_second, shift_second)
    text_ids = jnp.arange(SEGS, dtype=jnp.int32)
    one_hot = (segments[:, None, :] == text_ids[None, :, None]).astype(jnp.float32)
    counts = jnp.sum(one_hot, -1, keepdims=True)
    pooled = (
        jnp.einsum(
            "rts,rsd->rtd",
            one_hot,
            result.reshape(rows_dev, seq_len, width),
            precision=lax.Precision.HIGHEST,
        )
        / counts
    ).reshape(-1, width)
    inv_norm = lax.rsqrt(jnp.sum(pooled * pooled, -1, keepdims=True) + pool_epsilon)
    embed_b = (pooled * inv_norm).astype(jnp.bfloat16)
    gathered_embeddings = pair_gather(embed_b, sizes, 2).reshape(-1, width)
    mean_loss, embedding_gradient = contrastive(embed_b, gathered_embeddings, partner_all, me)
    grad_pooled = inv_norm * embedding_gradient - pooled * (
        inv_norm * inv_norm * inv_norm
    ) * jnp.sum(embedding_gradient * pooled, -1, keepdims=True)
    derivative_output = jnp.einsum(
        "rts,rtd->rsd",
        one_hot,
        grad_pooled.reshape(rows_dev, SEGS, width) / counts,
        precision=lax.Precision.HIGHEST,
    ).reshape(tokens_n, width)
    grad_second, gain_two_grad, shift_two_grad = layer_norm_back(
        derivative_output, normal_two, inverse_two, gain_second
    )
    lower_bias_grad = jnp.sum(grad_second, 0)
    lower_grad_b = grad_second.astype(jnp.bfloat16)
    lower_w_grad_t = lax.dot_general(
        active_b, lower_grad_b, on_tokens, preferred_element_type=jnp.float32
    )
    grad_active = jnp.dot(lower_grad_b, w_lower, preferred_element_type=jnp.float32)
    cumulative = 0.5 * (1.0 + lax.erf(upper / math.sqrt(2.0)))
    density = jnp.exp(-0.5 * upper * upper) / math.sqrt(2.0 * math.pi)
    grad_upper = grad_active * (cumulative + upper * density)
    upper_bias_grad = jnp.sum(grad_upper, 0)
    upper_grad_b = grad_upper.astype(jnp.bfloat16)
    upper_w_grad_t = lax.dot_general(
        upper_grad_b, normed_b, on_tokens, preferred_element_type=jnp.float32
    )
    grad_normed = (
        lax.dot_general(upper_grad_b, w_upper, on_rows, preferred_element_type=jnp.float32)
        + grad_second
    )
    grad_first, gain_one_grad, shift_one_grad = layer_norm_back(
        grad_normed, normal_one, inverse_one, gain_first
    )
    output_bias_grad = jnp.sum(grad_first, 0)
    first_grad_b = grad_first.astype(jnp.bfloat16)
    output_w_grad_t = lax.dot_general(
        first_grad_b, mixed_flat, on_tokens, preferred_element_type=jnp.float32
    )
    grad_mixed = lax.dot_general(
        first_grad_b, w_output, on_rows, preferred_element_type=jnp.float32
    ).astype(jnp.bfloat16)
    grad_mixed = grad_mixed.reshape(rows_dev, seq_len, HEADS, HD)
    norm_tokens = jnp.swapaxes(log_norm, 1, 2).reshape(tokens_n, HEADS)
    qkv_grad = jnp.concatenate(
        attention_back(qkv_rows, grad_mixed.reshape(tokens_n, width), norm_tokens, segments, HEADS, HD), 1
    ).astype(jnp.float32)
    qkv_grad_f = bf16_round(qkv_grad)
    qkv_grad_b = qkv_grad_f.astype(jnp.bfloat16)
    query_bias_grad = jnp.sum(qkv_grad_f[:, :width], 0)
    value_bias_grad = jnp.sum(qkv_grad_f[:, 2 * width :], 0)
    qkv_w_grad_t = lax.dot_general(
        qkv_grad_b, hidden_in, on_tokens, preferred_element_type=jnp.float32
    )
    vector_grad = jnp.concatenate(
        [
            query_bias_grad,
            value_bias_grad,
            output_bias_grad,
            gain_one_grad,
            shift_one_grad,
            upper_bias_grad,
            lower_bias_grad,
            gain_two_grad,
            shift_two_grad,
        ]
    )
    attn_cols = (qkv_w_grad_t.shape[0] + output_w_grad_t.shape[0]) // n_dev
    ffn_cols = (upper_w_grad_t.shape[0] + lower_w_grad_t.shape[0]) // n_dev
    if attn_cols % 16 == 0 and ffn_cols % 16 == 0:
        grads = (
            (None, None),
            (upper_w_grad_t.astype(GRAD_SEND), lower_w_grad_t.astype(GRAD_SEND)),
        )
        made_from = hidden_in
        second_from = (first_grad_b, mixed_flat)
    else:
        attn_blocks = jnp.concatenate(
            [qkv_w_grad_t.reshape(-1, attn_cols, width), output_w_grad_t.reshape(-1, attn_cols, width)], 0
        )
        ffn_blocks = jnp.concatenate(
            [upper_w_grad_t.reshape(-1, ffn_cols, width), lower_w_grad_t.reshape(-1, ffn_cols, width)], 0
        )
        grads = ((jnp.concatenate([attn_blocks, ffn_blocks], 1).astype(GRAD_SEND),),)
        made_from = None
        second_from = None
    parts = 3
    mine_parts, vector_slots, input_grad = halving_scatter(
        grads, vector_grad.reshape(n_dev, 1, -1), qkv_grad_b, w_qkv.T, grad_first, sizes, parts, 3, made_from, second_from
    )
    vector_reduced = jnp.sum(vector_slots[:, 0, :], 0)
    joined_reduced = jnp.transpose(mine_parts, (1, 0, 2)).reshape(-1, width).astype(jnp.float32)
    attn_reduced = joined_reduced[:attn_cols].T
    ffn_reduced = joined_reduced[attn_cols:].T
    attn_new, attn_moment, attn_average = apply_update(
        attn_weights, attn_reduced, attn_momentum, attn_averaged, decay_rate
    )
    ffn_new, ffn_moment, ffn_average = apply_update(
        ffn_weights, ffn_reduced, ffn_momentum, ffn_averaged, decay_rate
    )
    vector_new, vector_moment, vector_average = apply_update(
        vectors, vector_reduced, vector_momentum, vector_averaged, 0.0
    )
    return (
        mean_loss,
        input_grad,
        attn_reduced,
        ffn_reduced,
        vector_reduced,
        attn_new,
        ffn_new,
        vector_new,
        attn_moment,
        ffn_moment,
        vector_moment,
        attn_average,
        ffn_average,
        vector_average,
    )


def solution(mesh):
    in_specs = (
        P(("dp", "rep"), None),
        P(("dp", "rep"), None),
        P(("dp", "rep")),
        P(None, ("dp", "rep")),
        P(None, ("dp", "rep")),
        P(("dp", "rep")),
        P(None, ("dp", "rep")),
        P(None, ("dp", "rep")),
        P(("dp", "rep")),
        P(None, ("dp", "rep")),
        P(None, ("dp", "rep")),
        P(("dp", "rep")),
    )
    out_specs = (
        P(),
        P(("dp", "rep"), None),
        P(None, ("dp", "rep")),
        P(None, ("dp", "rep")),
        P(("dp", "rep")),
        P(None, ("dp", "rep")),
        P(None, ("dp", "rep")),
        P(("dp", "rep")),
        P(None, ("dp", "rep")),
        P(None, ("dp", "rep")),
        P(("dp", "rep")),
        P(None, ("dp", "rep")),
        P(None, ("dp", "rep")),
        P(("dp", "rep")),
    )
    return jax.shard_map(shards, mesh=mesh, in_specs=in_specs, out_specs=out_specs, check_vma=False)
```

```python
import functools
import math

import jax
import jax.numpy as jnp
from jax import lax
from jax.experimental import pallas as pl
from jax.experimental.pallas import tpu as pltpu
from jax.sharding import PartitionSpec as P

MESH = pl.DeviceIdType.MESH
GRAD_SEND = jnp.bfloat16
AXES = ("dp", "rep")

HEADS = 12
HD = 64
SEGS = 16


ln_epsilon = 1e-12
pool_epsilon = 1e-06
logit_divisor = 0.025
learn_rate = 0.01
momentum_rate = 0.9
decay_rate = 0.01
average_rate = 0.75
masked_value = -1e30


def layer_norm_parts(values, gain, shift):
    per_line_average = jnp.mean(values, -1, keepdims=True)
    centred = values - per_line_average
    inverse = lax.rsqrt(jnp.mean(centred * centred, -1, keepdims=True) + ln_epsilon)
    normal_part = centred * inverse
    return (normal_part * gain + shift, normal_part, inverse)


def layer_norm_back(grad_out, normal_part, inverse, gain):
    scaled = grad_out * gain
    grad_in = inverse * (
        scaled
        - jnp.mean(scaled, -1, keepdims=True)
        - normal_part * jnp.mean(scaled * normal_part, -1, keepdims=True)
    )
    return (grad_in, jnp.sum(grad_out * normal_part, 0), jnp.sum(grad_out, 0))


def row_scores(query_one, key_one, segment_one, scale):
    scores = (
        jnp.einsum("qhd,khd->hqk", query_one, key_one, preferred_element_type=jnp.float32) * scale
    )
    same_text = segment_one[:, None] == segment_one[None, :]
    return jnp.where(same_text[None], scores, masked_value)


def attend_rows(query_rows, key_rows, value_rows, row_segments):
    scale = 1.0 / math.sqrt(query_rows.shape[-1])

    def one_row(row_args):
        query_one, key_one, value_one, segment_one = row_args
        scores = row_scores(query_one, key_one, segment_one, scale)
        row_max = jnp.max(scores, -1, keepdims=True)
        exp_scores = jnp.exp(scores - row_max)
        sums = jnp.sum(exp_scores, -1, keepdims=True)
        attn_probs = exp_scores / sums
        mixed = jnp.einsum(
            "hqk,khd->qhd",
            attn_probs.astype(jnp.bfloat16),
            value_one,
            preferred_element_type=jnp.float32,
        )
        return (mixed.astype(jnp.bfloat16), (row_max + jnp.log(sums))[..., 0])

    return lax.map(one_row, (query_rows, key_rows, value_rows, row_segments))


def attend_back(query_rows, key_rows, value_rows, row_segments, log_norm, grad_mixed):
    scale = 1.0 / math.sqrt(query_rows.shape[-1])

    def one_row(row_args):
        query_one, key_one, value_one, segment_one, norm_one, grad_one = row_args
        scores = row_scores(query_one, key_one, segment_one, scale)
        attn_probs = jnp.exp(scores - norm_one[..., None])
        grad_value = jnp.einsum(
            "hqk,qhd->khd",
            attn_probs.astype(jnp.bfloat16),
            grad_one,
            preferred_element_type=jnp.float32,
        )
        grad_probs = jnp.einsum(
            "qhd,khd->hqk", grad_one, value_one, preferred_element_type=jnp.float32
        )
        inner = jnp.sum(attn_probs * grad_probs, -1, keepdims=True)
        grad_scores = (attn_probs * (grad_probs - inner)).astype(jnp.bfloat16)
        grad_query = (
            jnp.einsum("hqk,khd->qhd", grad_scores, key_one, preferred_element_type=jnp.float32)
            * scale
        )
        grad_key = (
            jnp.einsum("hqk,qhd->khd", grad_scores, query_one, preferred_element_type=jnp.float32)
            * scale
        )
        return jnp.concatenate([grad_query, grad_key, grad_value], axis=1)

    return lax.map(one_row, (query_rows, key_rows, value_rows, row_segments, log_norm, grad_mixed))


def attention_back_kernel(scale, q_ref, k_ref, v_ref, g_ref, norm_ref, seg_col_ref, seg_row_ref, dq_ref, dk_ref, dv_ref):
    pair = pl.program_id(1)
    width = q_ref.shape[1]
    half = width // 2
    lane = lax.broadcasted_iota(jnp.int32, (1, width), 1)
    same = seg_col_ref[...] == seg_row_ref[0]
    norms = norm_ref[...]
    norm_lane = lax.broadcasted_iota(jnp.int32, norms.shape, 1)
    q = q_ref[...]
    k = k_ref[...]
    v = v_ref[...]
    g = g_ref[...]
    zero_b = jnp.zeros_like(q)
    on_last = (((1,), (1,)), ((), ()))
    on_first = (((0,), (0,)), ((), ()))
    dq = jnp.zeros(q.shape, jnp.float32)
    dk = jnp.zeros(q.shape, jnp.float32)
    dv = jnp.zeros(q.shape, jnp.float32)
    for head in range(2):
        mine = (lane >= head * half) & (lane < (head + 1) * half)
        q_h = jnp.where(mine, q, zero_b)
        g_h = jnp.where(mine, g, zero_b)
        norm_h = jnp.sum(jnp.where(norm_lane == 2 * pair + head, norms, 0.0), 1, keepdims=True)
        scores = lax.dot_general(q_h, k, on_last, preferred_element_type=jnp.float32) * scale
        scores = jnp.where(same, scores, masked_value)
        probs = jnp.exp(scores - norm_h)
        grad_v = lax.dot_general(probs.astype(jnp.bfloat16), g, on_first, preferred_element_type=jnp.float32)
        grad_p = lax.dot_general(g_h, v, on_last, preferred_element_type=jnp.float32)
        inner = jnp.sum(probs * grad_p, -1, keepdims=True)
        grad_s = (probs * (grad_p - inner)).astype(jnp.bfloat16)
        grad_q = jnp.dot(grad_s, k, preferred_element_type=jnp.float32) * scale
        grad_k = lax.dot_general(grad_s, q, on_first, preferred_element_type=jnp.float32) * scale
        dq = jnp.where(mine, grad_q, dq)
        dk = jnp.where(mine, grad_k, dk)
        dv = jnp.where(mine, grad_v, dv)
    dq_ref[...] = dq.astype(dq_ref.dtype)
    dk_ref[...] = dk.astype(dk_ref.dtype)
    dv_ref[...] = dv.astype(dv_ref.dtype)


def attention_back(qkv_rows, grad_mixed_flat, norm_tokens, segments, heads, head_dim):
    tokens, three_width = qkv_rows.shape
    width = three_width // 3
    rows, seq_len = segments.shape
    pair_width = 2 * head_dim
    pairs = heads // 2
    seg_col = segments.reshape(tokens, 1)
    seg_row = segments.reshape(rows, 1, seq_len)
    scale = 1.0 / math.sqrt(head_dim)
    out = jax.ShapeDtypeStruct((tokens, width), jnp.bfloat16)
    return pl.pallas_call(
        functools.partial(attention_back_kernel, scale),
        grid=(rows, pairs),
        in_specs=[
            pl.BlockSpec((seq_len, pair_width), lambda r, p: (r, p)),
            pl.BlockSpec((seq_len, pair_width), lambda r, p: (r, pairs + p)),
            pl.BlockSpec((seq_len, pair_width), lambda r, p: (r, 2 * pairs + p)),
            pl.BlockSpec((seq_len, pair_width), lambda r, p: (r, p)),
            pl.BlockSpec((seq_len, heads), lambda r, p: (r, 0)),
            pl.BlockSpec((seq_len, 1), lambda r, p: (r, 0)),
            pl.BlockSpec((1, 1, seq_len), lambda r, p: (r, 0, 0)),
        ],
        out_specs=[pl.BlockSpec((seq_len, pair_width), lambda r, p: (r, p))] * 3,
        out_shape=[out, out, out],
        compiler_params=pltpu.CompilerParams(vmem_limit_bytes=48 * 1024 * 1024),
        cost_estimate=pl.CostEstimate(
            flops=10 * rows * heads * seq_len * seq_len * pair_width,
            transcendentals=rows * heads * seq_len * seq_len,
            bytes_accessed=tokens * (three_width + 4 * width) * 2,
        ),
    )(qkv_rows, qkv_rows, qkv_rows, grad_mixed_flat, norm_tokens, seg_col, seg_row)


def apply_update(weight, grad, moment, average, decay):
    step_grad = grad + decay * weight
    new_moment = momentum_rate * moment + step_grad
    new_weight = weight - learn_rate * (step_grad + momentum_rate * new_moment)
    fresh_running_mean = average_rate * average + (1.0 - average_rate) * new_weight
    return (new_weight, new_moment, fresh_running_mean)


def bf16_round(values):
    return lax.reduce_precision(values, exponent_bits=8, mantissa_bits=7)


def flat_index(sizes):
    idx = 0
    for name, size in zip(AXES, sizes):
        idx = idx * size + lax.axis_index(name)
    return idx


def device_of(flat, sizes):
    coords = []
    for size in reversed(sizes):
        coords.append(lax.rem(flat, size))
        flat = flat // size
    return tuple(reversed(coords))


def enter_all(n, sizes, me):
    barrier = pltpu.get_barrier_semaphore()

    def greet(k, carry):
        peer = lax.rem(me + k, n)
        pl.semaphore_signal(barrier, inc=1, device_id=device_of(peer, sizes), device_id_type=MESH)
        return carry

    lax.fori_loop(1, n, greet, 0)
    pl.semaphore_wait(barrier, n - 1)


def gather_kernel(n, sizes, x_ref, out_ref, send_sem, recv_sem):
    me = flat_index(sizes)
    enter_all(n, sizes, me)

    def send(k, carry):
        peer = lax.rem(me + k, n)
        pltpu.make_async_remote_copy(
            src_ref=x_ref, dst_ref=out_ref.at[me], send_sem=send_sem.at[k], recv_sem=recv_sem.at[me],
            device_id=device_of(peer, sizes), device_id_type=MESH,
        ).start()
        return carry

    lax.fori_loop(1, n, send, 0)
    out_ref[me] = x_ref[...]

    def finish(k, carry):
        peer = lax.rem(me + k, n)
        src = lax.rem(me + n - k, n)
        pltpu.make_async_remote_copy(
            src_ref=x_ref, dst_ref=out_ref.at[me], send_sem=send_sem.at[k], recv_sem=recv_sem.at[me],
            device_id=device_of(peer, sizes), device_id_type=MESH,
        ).wait_send()
        pltpu.make_async_remote_copy(
            src_ref=x_ref, dst_ref=out_ref.at[src], send_sem=send_sem.at[k], recv_sem=recv_sem.at[src],
            device_id=device_of(src, sizes), device_id_type=MESH,
        ).wait_recv()
        return carry

    lax.fori_loop(1, n, finish, 0)


def small_gather(x, sizes, cid):
    n = math.prod(sizes)
    return pl.pallas_call(
        functools.partial(gather_kernel, n, sizes),
        out_shape=jax.ShapeDtypeStruct((n,) + x.shape, x.dtype),
        in_specs=[pl.BlockSpec(memory_space=pltpu.VMEM)],
        out_specs=pl.BlockSpec(memory_space=pltpu.VMEM),
        scratch_shapes=[pltpu.SemaphoreType.DMA((n,)), pltpu.SemaphoreType.DMA((n,))],
        compiler_params=pltpu.CompilerParams(collective_id=cid, has_side_effects=True),
    )(x)


def scatter_kernel(n, sizes, x_ref, out_ref, send_sem, recv_sem):
    me = flat_index(sizes)
    enter_all(n, sizes, me)

    def send(k, carry):
        peer = lax.rem(me + k, n)
        pltpu.make_async_remote_copy(
            src_ref=x_ref.at[peer], dst_ref=out_ref.at[me], send_sem=send_sem.at[k], recv_sem=recv_sem.at[me],
            device_id=device_of(peer, sizes), device_id_type=MESH,
        ).start()
        return carry

    lax.fori_loop(1, n, send, 0)
    out_ref[me] = x_ref[me]

    def finish(k, carry):
        peer = lax.rem(me + k, n)
        src = lax.rem(me + n - k, n)
        pltpu.make_async_remote_copy(
            src_ref=x_ref.at[peer], dst_ref=out_ref.at[me], send_sem=send_sem.at[k], recv_sem=recv_sem.at[me],
            device_id=device_of(peer, sizes), device_id_type=MESH,
        ).wait_send()
        pltpu.make_async_remote_copy(
            src_ref=x_ref.at[src], dst_ref=out_ref.at[src], send_sem=send_sem.at[k], recv_sem=recv_sem.at[src],
            device_id=device_of(src, sizes), device_id_type=MESH,
        ).wait_recv()
        return carry

    lax.fori_loop(1, n, finish, 0)


def small_scatter(x, sizes, cid):
    n = math.prod(sizes)
    return pl.pallas_call(
        functools.partial(scatter_kernel, n, sizes),
        out_shape=jax.ShapeDtypeStruct(x.shape, x.dtype),
        in_specs=[pl.BlockSpec(memory_space=pltpu.VMEM)],
        out_specs=pl.BlockSpec(memory_space=pltpu.VMEM),
        scratch_shapes=[pltpu.SemaphoreType.DMA((n,)), pltpu.SemaphoreType.DMA((n,))],
        compiler_params=pltpu.CompilerParams(collective_id=cid, has_side_effects=True),
    )(x)


def pair_gather_kernel(n, sizes, x_ref, out_ref, local_sem, send1, recv1, send2, recv2, send3, recv3):
    me = flat_index(sizes)
    chips = n // 2
    chip = me // 2
    core = lax.rem(me, 2)
    partner = me + 1 - 2 * core
    enter_all(n, sizes, me)

    local = pltpu.make_async_copy(x_ref, out_ref.at[me], local_sem)
    local.start()
    first = pltpu.make_async_remote_copy(
        src_ref=x_ref, dst_ref=out_ref.at[me], send_sem=send1, recv_sem=recv1,
        device_id=device_of(partner, sizes), device_id_type=MESH,
    )
    first.start()
    local.wait()
    first.wait_send()
    pltpu.make_async_remote_copy(
        src_ref=x_ref, dst_ref=out_ref.at[partner], send_sem=send1, recv_sem=recv1,
        device_id=device_of(partner, sizes), device_id_type=MESH,
    ).wait_recv()

    def pair(c):
        return out_ref.at[pl.ds(2 * c, 2)]

    def target(k):
        return lax.rem(chip + 2 * k - 1 + core, chips)

    def source(k):
        return lax.rem(chip + chips - (2 * k - 1 + core), chips)

    count = (chips - core) // 2

    def send_out(k, carry):
        other = target(k)
        pltpu.make_async_remote_copy(
            src_ref=pair(chip), dst_ref=pair(chip), send_sem=send2.at[other], recv_sem=recv2.at[chip],
            device_id=device_of(2 * other + core, sizes), device_id_type=MESH,
        ).start()
        return carry

    lax.fori_loop(1, count + 1, send_out, 0)

    def take_in(k, carry):
        other = source(k)
        pltpu.make_async_remote_copy(
            src_ref=pair(other), dst_ref=pair(other), send_sem=send2.at[other], recv_sem=recv2.at[other],
            device_id=device_of(2 * other + core, sizes), device_id_type=MESH,
        ).wait_recv()
        pltpu.make_async_remote_copy(
            src_ref=pair(other), dst_ref=pair(other), send_sem=send3.at[other], recv_sem=recv3.at[other],
            device_id=device_of(partner, sizes), device_id_type=MESH,
        ).start()
        return carry

    lax.fori_loop(1, count + 1, take_in, 0)

    def sent_out(k, carry):
        other = target(k)
        pltpu.make_async_remote_copy(
            src_ref=pair(chip), dst_ref=pair(chip), send_sem=send2.at[other], recv_sem=recv2.at[chip],
            device_id=device_of(2 * other + core, sizes), device_id_type=MESH,
        ).wait_send()
        return carry

    lax.fori_loop(1, count + 1, sent_out, 0)

    def forwarded(k, carry):
        other = source(k)
        pltpu.make_async_remote_copy(
            src_ref=pair(other), dst_ref=pair(other), send_sem=send3.at[other], recv_sem=recv3.at[other],
            device_id=device_of(partner, sizes), device_id_type=MESH,
        ).wait_send()
        return carry

    lax.fori_loop(1, count + 1, forwarded, 0)

    other_count = (chips - (1 - core)) // 2

    def partner_source(k):
        return lax.rem(chip + chips - (2 * k - 1 + (1 - core)), chips)

    def from_partner(k, carry):
        other = partner_source(k)
        pltpu.make_async_remote_copy(
            src_ref=pair(other), dst_ref=pair(other), send_sem=send3.at[other], recv_sem=recv3.at[other],
            device_id=device_of(partner, sizes), device_id_type=MESH,
        ).wait_recv()
        return carry

    lax.fori_loop(1, other_count + 1, from_partner, 0)


def pair_gather(x, sizes, cid):
    n = math.prod(sizes)
    chips = n // 2
    dma = pltpu.SemaphoreType.DMA
    return pl.pallas_call(
        functools.partial(pair_gather_kernel, n, sizes),
        out_shape=jax.ShapeDtypeStruct((n,) + x.shape, x.dtype),
        in_specs=[pl.BlockSpec(memory_space=pltpu.VMEM)],
        out_specs=pl.BlockSpec(memory_space=pltpu.VMEM),
        scratch_shapes=[dma(()), dma(()), dma(()), dma((chips,)), dma((chips,)), dma((chips,)), dma((chips,))],
        compiler_params=pltpu.CompilerParams(collective_id=cid, has_side_effects=True),
    )(x)


def halving_orders(n, parts):
    bits = n.bit_length() - 1
    middle = list(range(1, bits - 1))
    orders = []
    for p in range(parts):
        shift = p % len(middle) if middle else 0
        orders.append(tuple([0] + middle[shift:] + middle[:shift] + [bits - 1]))
    return tuple(orders)


def halving_kernel(n, sizes, orders, cols, tile, groups, computed, *refs):
    count = sum(groups) - int(computed)
    sources = list(refs[:count])
    vec_ref, dq_ref, w_ref, res_ref = refs[count : count + 4]
    at = count + 4
    if computed:
        x_ref = refs[at]
        at += 1
    out_ref, vec_out, grad_out, work = refs[at : at + 4]
    at += 4
    if computed:
        made = refs[at]
        at += 1
        sources.insert(0, made)
    rest = refs[at:]
    grouped = []
    at = 0
    for g in groups:
        grouped.append(sources[at : at + g])
        at += g
    steps = len(orders[0])
    parts = len(orders)
    layout = []
    head = 0
    for group in grouped:
        size = sum(math.prod(s.shape[:-1]) for s in group) // n
        layout.append((group, size, head))
        head += size
    recvs = rest[:steps]
    local_sem, send_sems, recv_sems, vec_send, vec_recv = rest[steps:]
    me = flat_index(sizes)

    def partner_of(bit):
        mine = lax.rem(me // (2**bit), 2)
        return mine, me + (1 - 2 * mine) * (2**bit)

    enter_all(n, sizes, me)

    def vec_copy(k):
        peer = lax.rem(me + k, n)
        return pltpu.make_async_remote_copy(
            src_ref=vec_ref.at[peer], dst_ref=vec_out.at[me], send_sem=vec_send.at[k], recv_sem=vec_recv.at[me],
            device_id=device_of(peer, sizes), device_id_type=MESH,
        )

    def vec_start(k, carry):
        vec_copy(k).start()
        return carry

    lax.fori_loop(1, n, vec_start, 0)
    vec_out[me] = vec_ref[me]

    half = n // 2
    first = []
    issuers = []
    for p in range(parts):
        order = orders[p]
        mine, other = partner_of(order[0])
        column = pl.ds(p * cols, cols)

        def owner(j, side, order=order):
            o = side * (2 ** order[0])
            for m, bit in enumerate(order[1:]):
                o = o + lax.rem(j // (2 ** (steps - 2 - m)), 2) * (2**bit)
            return o

        def issue(j, carry, p=p, owner=owner, mine=mine, other=other, column=column, which=None):
            for o, dst, remote in ((owner(j, 1 - mine), recvs[0].at[p, j], True), (owner(j, mine), work.at[p, j], False)):
                for group, size, head in [layout[w] for w in which]:
                    offset = 0
                    for chosen in group:
                        split = math.prod(chosen.shape[:-1]) // size

                        def move(chosen=chosen, offset=offset, o=o, dst=dst, remote=remote, size=size, head=head):
                            if len(chosen.shape) == 3:
                                src_ref = chosen.at[o - offset, :, column]
                            else:
                                src_ref = chosen.at[pl.ds((o - offset) * size, size), column]
                            dst_ref = dst.at[pl.ds(head, size)]
                            if remote:
                                pltpu.make_async_remote_copy(
                                    src_ref=src_ref, dst_ref=dst_ref,
                                    send_sem=send_sems.at[p, 0], recv_sem=recv_sems.at[p, 0],
                                    device_id=device_of(other, sizes), device_id_type=MESH,
                                ).start()
                            else:
                                pltpu.make_async_copy(src_ref, dst_ref, local_sem.at[p]).start()

                        if len(group) == 1:
                            move()
                        else:
                            pl.when((o >= offset) & (o < offset + split))(move)
                        offset += split

            return carry

        issuers.append(issue)
        first.append(other)
    later = [0] if computed else []
    sooner = [w for w in range(len(layout)) if w not in later]
    for issue in issuers:
        lax.fori_loop(0, half, functools.partial(issue, which=sooner), 0)
    if computed:
        on_first = (((0,), (0,)), ((), ()))

        def product_t(t, carry):
            rows = pl.ds(pl.multiple_of(t * tile, tile), tile)
            made[rows, :] = lax.dot_general(
                dq_ref[:, rows], x_ref[...], on_first, preferred_element_type=jnp.float32
            ).astype(made.dtype)
            return carry

        lax.fori_loop(0, made.shape[0] // tile, product_t, 0)
        for issue in issuers:
            lax.fori_loop(0, half, functools.partial(issue, which=later), 0)
    for p in range(parts):
        whole = pltpu.make_async_remote_copy(
            src_ref=work.at[p, pl.ds(0, half)], dst_ref=recvs[0].at[p],
            send_sem=send_sems.at[p, 0], recv_sem=recv_sems.at[p, 0],
            device_id=device_of(first[p], sizes), device_id_type=MESH,
        )
        pltpu.make_async_copy(work.at[p, pl.ds(0, half)], work.at[p, pl.ds(0, half)], local_sem.at[p]).wait()
        whole.wait_recv()
        whole.wait_send()

        def accumulate0(i, carry, p=p):
            total = work[p, i].astype(jnp.float32) + recvs[0][p, i].astype(jnp.float32)
            work[p, i] = total.astype(work.dtype)
            return carry

        lax.fori_loop(0, half, accumulate0, 0)

    for step in range(1, steps):
        half = n >> (step + 1)
        copies = []
        for p in range(parts):
            mine, other = partner_of(orders[p][step])
            send = pltpu.make_async_remote_copy(
                src_ref=work.at[p, pl.ds((1 - mine) * half, half)], dst_ref=recvs[step].at[p],
                send_sem=send_sems.at[p, step], recv_sem=recv_sems.at[p, step],
                device_id=device_of(other, sizes), device_id_type=MESH,
            )
            send.start()
            copies.append((mine, send))
        if step == 1:
            def product(t, carry):
                rows = pl.ds(pl.multiple_of(t * tile, tile), tile)
                grad_out[rows, :] = (
                    jnp.dot(dq_ref[rows, :], w_ref[...], preferred_element_type=jnp.float32) + res_ref[rows, :]
                )
                return carry

            lax.fori_loop(0, grad_out.shape[0] // tile, product, 0)
        for p in range(parts):
            mine, send = copies[p]
            send.wait_recv()
            send.wait_send()

            def accumulate(i, carry, p=p, mine=mine, half=half, step=step):
                total = work[p, mine * half + i].astype(jnp.float32) + recvs[step][p, i].astype(jnp.float32)
                work[p, i] = total.astype(work.dtype)
                return carry

            lax.fori_loop(0, half, accumulate, 0)
    for p in range(parts):
        out_ref[:, p * cols : (p + 1) * cols] = work[p, 0].astype(out_ref.dtype)

    def vec_finish(k, carry):
        vec_copy(k).wait_send()
        src = lax.rem(me + n - k, n)
        pltpu.make_async_remote_copy(
            src_ref=vec_ref.at[src], dst_ref=vec_out.at[src], send_sem=vec_send.at[k], recv_sem=vec_recv.at[src],
            device_id=device_of(src, sizes), device_id_type=MESH,
        ).wait_recv()
        return carry

    lax.fori_loop(1, n, vec_finish, 0)


def halving_scatter(grouped, vec, grad_b, weight_t, residual, sizes, parts, cid, tokens=None):
    n = math.prod(sizes)
    computed = tokens is not None
    groups = tuple(len(g) for g in grouped)
    given = [s for g in grouped for s in g if s is not None]
    made_shape = (grad_b.shape[1], tokens.shape[1]) if computed else None
    assert not computed or made_shape[0] % 128 == 0
    shapes = [made_shape if s is None else s.shape for g in grouped for s in g]
    dtype = given[0].dtype
    width = shapes[0][-1]
    rows = sum(math.prod(s[:-1]) for s in shapes) // n
    cols = width // parts
    orders = halving_orders(n, parts)
    steps = len(orders[0])
    tile = 128
    dma = pltpu.SemaphoreType.DMA
    vmem = pl.BlockSpec(memory_space=pltpu.VMEM)
    scratch = [pltpu.VMEM((parts, n // 2, rows, cols), dtype)]
    if computed:
        scratch.append(pltpu.VMEM(made_shape, dtype))
    scratch += [pltpu.VMEM((parts, n >> (k + 1), rows, cols), dtype) for k in range(steps)]
    scratch += [dma((parts,)), dma((parts, steps)), dma((parts, steps)), dma((n,)), dma((n,))]
    return pl.pallas_call(
        functools.partial(halving_kernel, n, sizes, orders, cols, tile, groups, computed),
        out_shape=(
            jax.ShapeDtypeStruct((rows, parts * cols), jnp.float32),
            jax.ShapeDtypeStruct(vec.shape, vec.dtype),
            jax.ShapeDtypeStruct(residual.shape, jnp.float32),
        ),
        in_specs=[pl.BlockSpec(memory_space=pl.ANY)] * len(given) + [vmem] * (4 + int(computed)),
        out_specs=(vmem, vmem, vmem),
        scratch_shapes=scratch,
        compiler_params=pltpu.CompilerParams(
            collective_id=cid, has_side_effects=True, vmem_limit_bytes=60 * 1024 * 1024
        ),
    )(*given, vec, grad_b, weight_t, residual, *([tokens] if computed else []))


def contrastive(embed_b, gathered, partner_all, me):
    own_texts = embed_b.shape[0]
    all_texts = gathered.shape[0]
    chunk = min(all_texts, 1024)
    on_rows = (((1,), (1,)), ((), ()))

    def chunk_stats(c):
        rows_b = lax.dynamic_slice_in_dim(gathered, c * chunk, chunk)
        sim = lax.dot_general(rows_b, gathered, on_rows, preferred_element_type=jnp.float32) / logit_divisor
        column_ids = lax.broadcasted_iota(jnp.int32, sim.shape, 1)
        row_ids = lax.broadcasted_iota(jnp.int32, sim.shape, 0) + c * chunk
        masked = jnp.where(column_ids == row_ids, masked_value, sim)
        row_max = jnp.max(masked, -1, keepdims=True)
        log_sum = row_max + jnp.log(jnp.sum(jnp.exp(masked - row_max), -1, keepdims=True))
        wanted = lax.dynamic_slice_in_dim(partner_all, c * chunk, chunk)
        positive = jnp.sum(jnp.where(column_ids == wanted[:, None], sim, 0.0), -1)
        return log_sum[:, 0], positive

    if all_texts == chunk:
        log_sum_all, positive_all = chunk_stats(0)
    else:
        log_sum_all, positive_all = lax.map(chunk_stats, jnp.arange(all_texts // chunk))
        log_sum_all = log_sum_all.reshape(-1)
        positive_all = positive_all.reshape(-1)
    mean_loss = jnp.sum(log_sum_all - positive_all) / all_texts

    own_start = me * own_texts
    own_ids = lax.broadcasted_iota(jnp.int32, (own_texts,), 0) + own_start
    own_partner = lax.dynamic_slice_in_dim(partner_all, own_start, own_texts)
    own_log_sum = lax.dynamic_slice_in_dim(log_sum_all, own_start, own_texts)

    sim_rows = lax.dot_general(embed_b, gathered, on_rows, preferred_element_type=jnp.float32) / logit_divisor
    column_ids = lax.broadcasted_iota(jnp.int32, sim_rows.shape, 1)
    masked_rows = jnp.where(column_ids == own_ids[:, None], masked_value, sim_rows)
    grad_rows = (
        jnp.exp(masked_rows - own_log_sum[:, None]) - (column_ids == own_partner[:, None]).astype(jnp.float32)
    ).astype(jnp.bfloat16)

    sim_cols = lax.dot_general(gathered, embed_b, on_rows, preferred_element_type=jnp.float32) / logit_divisor
    row_ids = lax.broadcasted_iota(jnp.int32, sim_cols.shape, 0)
    masked_cols = jnp.where(row_ids == own_ids[None, :], masked_value, sim_cols)
    grad_cols = (
        jnp.exp(masked_cols - log_sum_all[:, None]) - (partner_all[:, None] == own_ids[None, :]).astype(jnp.float32)
    ).astype(jnp.bfloat16)

    on_tokens = (((0,), (0,)), ((), ()))
    embedding_gradient = (
        jnp.dot(grad_rows, gathered, preferred_element_type=jnp.float32)
        + lax.dot_general(grad_cols, gathered, on_tokens, preferred_element_type=jnp.float32)
    ) / logit_divisor
    return mean_loss, embedding_gradient


def shards(
    hidden_in,
    segments,
    partner,
    attn_weights,
    ffn_weights,
    vectors,
    attn_momentum,
    ffn_momentum,
    vector_momentum,
    attn_averaged,
    ffn_averaged,
    vector_averaged,
):
    sizes = tuple(lax.axis_size(name) for name in AXES)
    n_dev = math.prod(sizes)
    me = flat_index(sizes)
    vec_len = vectors.shape[0]
    small = jnp.concatenate([vectors, partner.astype(jnp.float32)])[None, :]
    small_all = small_gather(small, sizes, 0)[:, 0, :]
    vector_f = bf16_round(small_all[:, :vec_len].reshape(-1))
    partner_all = small_all[:, vec_len:].reshape(-1).astype(jnp.int32)
    attn_full, ffn_full = (
        lax.all_gather(attn_weights.astype(jnp.bfloat16), AXES, axis=1, tiled=True),
        lax.all_gather(ffn_weights.astype(jnp.bfloat16), AXES, axis=1, tiled=True),
    )
    width = attn_full.shape[0]
    hidden = ffn_full.shape[1] // 2
    query_bias = vector_f[0:width]
    value_bias = vector_f[width : 2 * width]
    output_bias = vector_f[2 * width : 3 * width]
    gain_first = vector_f[3 * width : 4 * width]
    shift_first = vector_f[4 * width : 5 * width]
    upper_bias = vector_f[5 * width : 5 * width + hidden]
    lower_bias = vector_f[5 * width + hidden : 6 * width + hidden]
    gain_second = vector_f[6 * width + hidden : 7 * width + hidden]
    shift_second = vector_f[7 * width + hidden : 8 * width + hidden]
    w_qkv = attn_full[:, : 3 * width]
    w_output = attn_full[:, 3 * width :]
    w_upper = ffn_full[:, :hidden]
    w_lower = ffn_full[:, hidden:]
    rows_dev, seq_len = segments.shape
    tokens_n = rows_dev * seq_len
    on_rows = (((1,), (1,)), ((), ()))
    on_tokens = (((0,), (0,)), ((), ()))
    qkv_bias = jnp.concatenate([query_bias, jnp.zeros_like(query_bias), value_bias])
    qkv_rows = (jnp.dot(hidden_in, w_qkv, preferred_element_type=jnp.float32) + qkv_bias).astype(
        jnp.bfloat16
    )
    heads = qkv_rows.reshape(rows_dev, seq_len, 3, HEADS, HD)
    query_rows = heads[:, :, 0]
    key_rows = heads[:, :, 1]
    value_rows = heads[:, :, 2]
    mixed, log_norm = attend_rows(query_rows, key_rows, value_rows, segments)
    mixed_flat = mixed.reshape(tokens_n, width)
    first_sum = (
        hidden_in.astype(jnp.float32)
        + jnp.dot(mixed_flat, w_output, preferred_element_type=jnp.float32)
        + output_bias
    )
    normed, normal_one, inverse_one = layer_norm_parts(first_sum, gain_first, shift_first)
    normed_r = bf16_round(normed)
    normed_b = normed_r.astype(jnp.bfloat16)
    upper = jnp.dot(normed_b, w_upper, preferred_element_type=jnp.float32) + upper_bias
    active_b = (0.5 * upper * (1.0 + lax.erf(upper / math.sqrt(2.0)))).astype(jnp.bfloat16)
    second_sum = (
        normed_r
        + lax.dot_general(active_b, w_lower, on_rows, preferred_element_type=jnp.float32)
        + lower_bias
    )
    result, normal_two, inverse_two = layer_norm_parts(second_sum, gain_second, shift_second)
    text_ids = jnp.arange(SEGS, dtype=jnp.int32)
    one_hot = (segments[:, None, :] == text_ids[None, :, None]).astype(jnp.float32)
    counts = jnp.sum(one_hot, -1, keepdims=True)
    pooled = (
        jnp.einsum(
            "rts,rsd->rtd",
            one_hot,
            result.reshape(rows_dev, seq_len, width),
            precision=lax.Precision.HIGHEST,
        )
        / counts
    ).reshape(-1, width)
    inv_norm = lax.rsqrt(jnp.sum(pooled * pooled, -1, keepdims=True) + pool_epsilon)
    embed_b = (pooled * inv_norm).astype(jnp.bfloat16)
    gathered_embeddings = pair_gather(embed_b, sizes, 2).reshape(-1, width)
    mean_loss, embedding_gradient = contrastive(embed_b, gathered_embeddings, partner_all, me)
    grad_pooled = inv_norm * embedding_gradient - pooled * (
        inv_norm * inv_norm * inv_norm
    ) * jnp.sum(embedding_gradient * pooled, -1, keepdims=True)
    derivative_output = jnp.einsum(
        "rts,rtd->rsd",
        one_hot,
        grad_pooled.reshape(rows_dev, SEGS, width) / counts,
        precision=lax.Precision.HIGHEST,
    ).reshape(tokens_n, width)
    grad_second, gain_two_grad, shift_two_grad = layer_norm_back(
        derivative_output, normal_two, inverse_two, gain_second
    )
    lower_bias_grad = jnp.sum(grad_second, 0)
    lower_grad_b = grad_second.astype(jnp.bfloat16)
    lower_w_grad_t = lax.dot_general(
        active_b, lower_grad_b, on_tokens, preferred_element_type=jnp.float32
    )
    grad_active = jnp.dot(lower_grad_b, w_lower, preferred_element_type=jnp.float32)
    cumulative = 0.5 * (1.0 + lax.erf(upper / math.sqrt(2.0)))
    density = jnp.exp(-0.5 * upper * upper) / math.sqrt(2.0 * math.pi)
    grad_upper = grad_active * (cumulative + upper * density)
    upper_bias_grad = jnp.sum(grad_upper, 0)
    upper_grad_b = grad_upper.astype(jnp.bfloat16)
    upper_w_grad_t = lax.dot_general(
        upper_grad_b, normed_b, on_tokens, preferred_element_type=jnp.float32
    )
    grad_normed = (
        lax.dot_general(upper_grad_b, w_upper, on_rows, preferred_element_type=jnp.float32)
        + grad_second
    )
    grad_first, gain_one_grad, shift_one_grad = layer_norm_back(
        grad_normed, normal_one, inverse_one, gain_first
    )
    output_bias_grad = jnp.sum(grad_first, 0)
    first_grad_b = grad_first.astype(jnp.bfloat16)
    output_w_grad_t = lax.dot_general(
        first_grad_b, mixed_flat, on_tokens, preferred_element_type=jnp.float32
    )
    grad_mixed = lax.dot_general(
        first_grad_b, w_output, on_rows, preferred_element_type=jnp.float32
    ).astype(jnp.bfloat16)
    grad_mixed = grad_mixed.reshape(rows_dev, seq_len, HEADS, HD)
    norm_tokens = jnp.swapaxes(log_norm, 1, 2).reshape(tokens_n, HEADS)
    qkv_grad = jnp.concatenate(
        attention_back(qkv_rows, grad_mixed.reshape(tokens_n, width), norm_tokens, segments, HEADS, HD), 1
    ).astype(jnp.float32)
    qkv_grad_f = bf16_round(qkv_grad)
    qkv_grad_b = qkv_grad_f.astype(jnp.bfloat16)
    query_bias_grad = jnp.sum(qkv_grad_f[:, :width], 0)
    value_bias_grad = jnp.sum(qkv_grad_f[:, 2 * width :], 0)
    qkv_w_grad_t = lax.dot_general(
        qkv_grad_b, hidden_in, on_tokens, preferred_element_type=jnp.float32
    )
    vector_grad = jnp.concatenate(
        [
            query_bias_grad,
            value_bias_grad,
            output_bias_grad,
            gain_one_grad,
            shift_one_grad,
            upper_bias_grad,
            lower_bias_grad,
            gain_two_grad,
            shift_two_grad,
        ]
    )
    attn_cols = (qkv_w_grad_t.shape[0] + output_w_grad_t.shape[0]) // n_dev
    ffn_cols = (upper_w_grad_t.shape[0] + lower_w_grad_t.shape[0]) // n_dev
    if attn_cols % 16 == 0 and ffn_cols % 16 == 0:
        grads = (
            (None, output_w_grad_t.astype(GRAD_SEND)),
            (upper_w_grad_t.astype(GRAD_SEND), lower_w_grad_t.astype(GRAD_SEND)),
        )
        made_from = hidden_in
    else:
        attn_blocks = jnp.concatenate(
            [qkv_w_grad_t.reshape(-1, attn_cols, width), output_w_grad_t.reshape(-1, attn_cols, width)], 0
        )
        ffn_blocks = jnp.concatenate(
            [upper_w_grad_t.reshape(-1, ffn_cols, width), lower_w_grad_t.reshape(-1, ffn_cols, width)], 0
        )
        grads = ((jnp.concatenate([attn_blocks, ffn_blocks], 1).astype(GRAD_SEND),),)
        made_from = None
    parts = 3
    mine_parts, vector_slots, input_grad = halving_scatter(
        grads, vector_grad.reshape(n_dev, 1, -1), qkv_grad_b, w_qkv.T, grad_first, sizes, parts, 3, made_from
    )
    vector_reduced = jnp.sum(vector_slots[:, 0, :], 0)
    joined_reduced = mine_parts
    attn_reduced = joined_reduced[:attn_cols].T
    ffn_reduced = joined_reduced[attn_cols:].T
    attn_new, attn_moment, attn_average = apply_update(
        attn_weights, attn_reduced, attn_momentum, attn_averaged, decay_rate
    )
    ffn_new, ffn_moment, ffn_average = apply_update(
        ffn_weights, ffn_reduced, ffn_momentum, ffn_averaged, decay_rate
    )
    vector_new, vector_moment, vector_average = apply_update(
        vectors, vector_reduced, vector_momentum, vector_averaged, 0.0
    )
    return (
        mean_loss,
        input_grad,
        attn_reduced,
        ffn_reduced,
        vector_reduced,
        attn_new,
        ffn_new,
        vector_new,
        attn_moment,
        ffn_moment,
        vector_moment,
        attn_average,
        ffn_average,
        vector_average,
    )


def solution(mesh):
    in_specs = (
        P(("dp", "rep"), None),
        P(("dp", "rep"), None),
        P(("dp", "rep")),
        P(None, ("dp", "rep")),
        P(None, ("dp", "rep")),
        P(("dp", "rep")),
        P(None, ("dp", "rep")),
        P(None, ("dp", "rep")),
        P(("dp", "rep")),
        P(None, ("dp", "rep")),
        P(None, ("dp", "rep")),
        P(("dp", "rep")),
    )
    out_specs = (
        P(),
        P(("dp", "rep"), None),
        P(None, ("dp", "rep")),
        P(None, ("dp", "rep")),
        P(("dp", "rep")),
        P(None, ("dp", "rep")),
        P(None, ("dp", "rep")),
        P(("dp", "rep")),
        P(None, ("dp", "rep")),
        P(None, ("dp", "rep")),
        P(("dp", "rep")),
        P(None, ("dp", "rep")),
        P(None, ("dp", "rep")),
        P(("dp", "rep")),
    )
    return jax.shard_map(shards, mesh=mesh, in_specs=in_specs, out_specs=out_specs, check_vma=False)
```

```python
import functools
import math

import jax
import jax.numpy as jnp
from jax import lax
from jax.experimental import pallas as pl
from jax.experimental.pallas import tpu as pltpu
from jax.sharding import PartitionSpec as P

MESH = pl.DeviceIdType.MESH
GRAD_SEND = jnp.bfloat16
AXES = ("dp", "rep")

HEADS = 12
HD = 64
SEGS = 16


ln_epsilon = 1e-12
pool_epsilon = 1e-06
logit_divisor = 0.025
learn_rate = 0.01
momentum_rate = 0.9
decay_rate = 0.01
average_rate = 0.75
masked_value = -1e30


def layer_norm_parts(values, gain, shift):
    per_line_average = jnp.mean(values, -1, keepdims=True)
    centred = values - per_line_average
    inverse = lax.rsqrt(jnp.mean(centred * centred, -1, keepdims=True) + ln_epsilon)
    normal_part = centred * inverse
    return (normal_part * gain + shift, normal_part, inverse)


def layer_norm_back(grad_out, normal_part, inverse, gain):
    scaled = grad_out * gain
    grad_in = inverse * (
        scaled
        - jnp.mean(scaled, -1, keepdims=True)
        - normal_part * jnp.mean(scaled * normal_part, -1, keepdims=True)
    )
    return (grad_in, jnp.sum(grad_out * normal_part, 0), jnp.sum(grad_out, 0))


def row_scores(query_one, key_one, segment_one, scale):
    scores = (
        jnp.einsum("qhd,khd->hqk", query_one, key_one, preferred_element_type=jnp.float32) * scale
    )
    same_text = segment_one[:, None] == segment_one[None, :]
    return jnp.where(same_text[None], scores, masked_value)


def attend_rows(query_rows, key_rows, value_rows, row_segments):
    scale = 1.0 / math.sqrt(query_rows.shape[-1])

    def one_row(row_args):
        query_one, key_one, value_one, segment_one = row_args
        scores = row_scores(query_one, key_one, segment_one, scale)
        row_max = jnp.max(scores, -1, keepdims=True)
        exp_scores = jnp.exp(scores - row_max)
        sums = jnp.sum(exp_scores, -1, keepdims=True)
        attn_probs = exp_scores / sums
        mixed = jnp.einsum(
            "hqk,khd->qhd",
            attn_probs.astype(jnp.bfloat16),
            value_one,
            preferred_element_type=jnp.float32,
        )
        return (mixed.astype(jnp.bfloat16), (row_max + jnp.log(sums))[..., 0])

    return lax.map(one_row, (query_rows, key_rows, value_rows, row_segments))


def attend_back(query_rows, key_rows, value_rows, row_segments, log_norm, grad_mixed):
    scale = 1.0 / math.sqrt(query_rows.shape[-1])

    def one_row(row_args):
        query_one, key_one, value_one, segment_one, norm_one, grad_one = row_args
        scores = row_scores(query_one, key_one, segment_one, scale)
        attn_probs = jnp.exp(scores - norm_one[..., None])
        grad_value = jnp.einsum(
            "hqk,qhd->khd",
            attn_probs.astype(jnp.bfloat16),
            grad_one,
            preferred_element_type=jnp.float32,
        )
        grad_probs = jnp.einsum(
            "qhd,khd->hqk", grad_one, value_one, preferred_element_type=jnp.float32
        )
        inner = jnp.sum(attn_probs * grad_probs, -1, keepdims=True)
        grad_scores = (attn_probs * (grad_probs - inner)).astype(jnp.bfloat16)
        grad_query = (
            jnp.einsum("hqk,khd->qhd", grad_scores, key_one, preferred_element_type=jnp.float32)
            * scale
        )
        grad_key = (
            jnp.einsum("hqk,qhd->khd", grad_scores, query_one, preferred_element_type=jnp.float32)
            * scale
        )
        return jnp.concatenate([grad_query, grad_key, grad_value], axis=1)

    return lax.map(one_row, (query_rows, key_rows, value_rows, row_segments, log_norm, grad_mixed))


def attention_back_kernel(scale, q_ref, k_ref, v_ref, g_ref, norm_ref, seg_col_ref, seg_row_ref, dq_ref, dk_ref, dv_ref):
    pair = pl.program_id(1)
    width = q_ref.shape[1]
    half = width // 2
    lane = lax.broadcasted_iota(jnp.int32, (1, width), 1)
    same = seg_col_ref[...] == seg_row_ref[0]
    norms = norm_ref[...]
    norm_lane = lax.broadcasted_iota(jnp.int32, norms.shape, 1)
    q = q_ref[...]
    k = k_ref[...]
    v = v_ref[...]
    g = g_ref[...]
    zero_b = jnp.zeros_like(q)
    on_last = (((1,), (1,)), ((), ()))
    on_first = (((0,), (0,)), ((), ()))
    dq = jnp.zeros(q.shape, jnp.float32)
    dk = jnp.zeros(q.shape, jnp.float32)
    dv = jnp.zeros(q.shape, jnp.float32)
    for head in range(2):
        mine = (lane >= head * half) & (lane < (head + 1) * half)
        q_h = jnp.where(mine, q, zero_b)
        g_h = jnp.where(mine, g, zero_b)
        norm_h = jnp.sum(jnp.where(norm_lane == 2 * pair + head, norms, 0.0), 1, keepdims=True)
        scores = lax.dot_general(q_h, k, on_last, preferred_element_type=jnp.float32) * scale
        scores = jnp.where(same, scores, masked_value)
        probs = jnp.exp(scores - norm_h)
        grad_v = lax.dot_general(probs.astype(jnp.bfloat16), g, on_first, preferred_element_type=jnp.float32)
        grad_p = lax.dot_general(g_h, v, on_last, preferred_element_type=jnp.float32)
        inner = jnp.sum(probs * grad_p, -1, keepdims=True)
        grad_s = (probs * (grad_p - inner)).astype(jnp.bfloat16)
        grad_q = jnp.dot(grad_s, k, preferred_element_type=jnp.float32) * scale
        grad_k = lax.dot_general(grad_s, q, on_first, preferred_element_type=jnp.float32) * scale
        dq = jnp.where(mine, grad_q, dq)
        dk = jnp.where(mine, grad_k, dk)
        dv = jnp.where(mine, grad_v, dv)
    dq_ref[...] = dq.astype(dq_ref.dtype)
    dk_ref[...] = dk.astype(dk_ref.dtype)
    dv_ref[...] = dv.astype(dv_ref.dtype)


def attention_back(qkv_rows, grad_mixed_flat, norm_tokens, segments, heads, head_dim):
    tokens, three_width = qkv_rows.shape
    width = three_width // 3
    rows, seq_len = segments.shape
    pair_width = 2 * head_dim
    pairs = heads // 2
    seg_col = segments.reshape(tokens, 1)
    seg_row = segments.reshape(rows, 1, seq_len)
    scale = 1.0 / math.sqrt(head_dim)
    out = jax.ShapeDtypeStruct((tokens, width), jnp.bfloat16)
    return pl.pallas_call(
        functools.partial(attention_back_kernel, scale),
        grid=(rows, pairs),
        in_specs=[
            pl.BlockSpec((seq_len, pair_width), lambda r, p: (r, p)),
            pl.BlockSpec((seq_len, pair_width), lambda r, p: (r, pairs + p)),
            pl.BlockSpec((seq_len, pair_width), lambda r, p: (r, 2 * pairs + p)),
            pl.BlockSpec((seq_len, pair_width), lambda r, p: (r, p)),
            pl.BlockSpec((seq_len, heads), lambda r, p: (r, 0)),
            pl.BlockSpec((seq_len, 1), lambda r, p: (r, 0)),
            pl.BlockSpec((1, 1, seq_len), lambda r, p: (r, 0, 0)),
        ],
        out_specs=[pl.BlockSpec((seq_len, pair_width), lambda r, p: (r, p))] * 3,
        out_shape=[out, out, out],
        compiler_params=pltpu.CompilerParams(vmem_limit_bytes=48 * 1024 * 1024),
        cost_estimate=pl.CostEstimate(
            flops=10 * rows * heads * seq_len * seq_len * pair_width,
            transcendentals=rows * heads * seq_len * seq_len,
            bytes_accessed=tokens * (three_width + 4 * width) * 2,
        ),
    )(qkv_rows, qkv_rows, qkv_rows, grad_mixed_flat, norm_tokens, seg_col, seg_row)


def apply_update(weight, grad, moment, average, decay):
    step_grad = grad + decay * weight
    new_moment = momentum_rate * moment + step_grad
    new_weight = weight - learn_rate * (step_grad + momentum_rate * new_moment)
    fresh_running_mean = average_rate * average + (1.0 - average_rate) * new_weight
    return (new_weight, new_moment, fresh_running_mean)


def bf16_round(values):
    return lax.reduce_precision(values, exponent_bits=8, mantissa_bits=7)


def flat_index(sizes):
    idx = 0
    for name, size in zip(AXES, sizes):
        idx = idx * size + lax.axis_index(name)
    return idx


def device_of(flat, sizes):
    coords = []
    for size in reversed(sizes):
        coords.append(lax.rem(flat, size))
        flat = flat // size
    return tuple(reversed(coords))


def enter_all(n, sizes, me):
    barrier = pltpu.get_barrier_semaphore()

    def greet(k, carry):
        peer = lax.rem(me + k, n)
        pl.semaphore_signal(barrier, inc=1, device_id=device_of(peer, sizes), device_id_type=MESH)
        return carry

    lax.fori_loop(1, n, greet, 0)
    pl.semaphore_wait(barrier, n - 1)


def gather_kernel(n, sizes, x_ref, out_ref, send_sem, recv_sem):
    me = flat_index(sizes)
    enter_all(n, sizes, me)

    def send(k, carry):
        peer = lax.rem(me + k, n)
        pltpu.make_async_remote_copy(
            src_ref=x_ref, dst_ref=out_ref.at[me], send_sem=send_sem.at[k], recv_sem=recv_sem.at[me],
            device_id=device_of(peer, sizes), device_id_type=MESH,
        ).start()
        return carry

    lax.fori_loop(1, n, send, 0)
    out_ref[me] = x_ref[...]

    def finish(k, carry):
        peer = lax.rem(me + k, n)
        src = lax.rem(me + n - k, n)
        pltpu.make_async_remote_copy(
            src_ref=x_ref, dst_ref=out_ref.at[me], send_sem=send_sem.at[k], recv_sem=recv_sem.at[me],
            device_id=device_of(peer, sizes), device_id_type=MESH,
        ).wait_send()
        pltpu.make_async_remote_copy(
            src_ref=x_ref, dst_ref=out_ref.at[src], send_sem=send_sem.at[k], recv_sem=recv_sem.at[src],
            device_id=device_of(src, sizes), device_id_type=MESH,
        ).wait_recv()
        return carry

    lax.fori_loop(1, n, finish, 0)


def small_gather(x, sizes, cid):
    n = math.prod(sizes)
    return pl.pallas_call(
        functools.partial(gather_kernel, n, sizes),
        out_shape=jax.ShapeDtypeStruct((n,) + x.shape, x.dtype),
        in_specs=[pl.BlockSpec(memory_space=pltpu.VMEM)],
        out_specs=pl.BlockSpec(memory_space=pltpu.VMEM),
        scratch_shapes=[pltpu.SemaphoreType.DMA((n,)), pltpu.SemaphoreType.DMA((n,))],
        compiler_params=pltpu.CompilerParams(collective_id=cid, has_side_effects=True),
    )(x)


def scatter_kernel(n, sizes, x_ref, out_ref, send_sem, recv_sem):
    me = flat_index(sizes)
    enter_all(n, sizes, me)

    def send(k, carry):
        peer = lax.rem(me + k, n)
        pltpu.make_async_remote_copy(
            src_ref=x_ref.at[peer], dst_ref=out_ref.at[me], send_sem=send_sem.at[k], recv_sem=recv_sem.at[me],
            device_id=device_of(peer, sizes), device_id_type=MESH,
        ).start()
        return carry

    lax.fori_loop(1, n, send, 0)
    out_ref[me] = x_ref[me]

    def finish(k, carry):
        peer = lax.rem(me + k, n)
        src = lax.rem(me + n - k, n)
        pltpu.make_async_remote_copy(
            src_ref=x_ref.at[peer], dst_ref=out_ref.at[me], send_sem=send_sem.at[k], recv_sem=recv_sem.at[me],
            device_id=device_of(peer, sizes), device_id_type=MESH,
        ).wait_send()
        pltpu.make_async_remote_copy(
            src_ref=x_ref.at[src], dst_ref=out_ref.at[src], send_sem=send_sem.at[k], recv_sem=recv_sem.at[src],
            device_id=device_of(src, sizes), device_id_type=MESH,
        ).wait_recv()
        return carry

    lax.fori_loop(1, n, finish, 0)


def small_scatter(x, sizes, cid):
    n = math.prod(sizes)
    return pl.pallas_call(
        functools.partial(scatter_kernel, n, sizes),
        out_shape=jax.ShapeDtypeStruct(x.shape, x.dtype),
        in_specs=[pl.BlockSpec(memory_space=pltpu.VMEM)],
        out_specs=pl.BlockSpec(memory_space=pltpu.VMEM),
        scratch_shapes=[pltpu.SemaphoreType.DMA((n,)), pltpu.SemaphoreType.DMA((n,))],
        compiler_params=pltpu.CompilerParams(collective_id=cid, has_side_effects=True),
    )(x)


def pair_gather_kernel(n, sizes, x_ref, out_ref, local_sem, send1, recv1, send2, recv2, send3, recv3):
    me = flat_index(sizes)
    chips = n // 2
    chip = me // 2
    core = lax.rem(me, 2)
    partner = me + 1 - 2 * core
    enter_all(n, sizes, me)

    local = pltpu.make_async_copy(x_ref, out_ref.at[me], local_sem)
    local.start()
    first = pltpu.make_async_remote_copy(
        src_ref=x_ref, dst_ref=out_ref.at[me], send_sem=send1, recv_sem=recv1,
        device_id=device_of(partner, sizes), device_id_type=MESH,
    )
    first.start()
    local.wait()
    first.wait_send()
    pltpu.make_async_remote_copy(
        src_ref=x_ref, dst_ref=out_ref.at[partner], send_sem=send1, recv_sem=recv1,
        device_id=device_of(partner, sizes), device_id_type=MESH,
    ).wait_recv()

    def pair(c):
        return out_ref.at[pl.ds(2 * c, 2)]

    def target(k):
        return lax.rem(chip + 2 * k - 1 + core, chips)

    def source(k):
        return lax.rem(chip + chips - (2 * k - 1 + core), chips)

    count = (chips - core) // 2

    def send_out(k, carry):
        other = target(k)
        pltpu.make_async_remote_copy(
            src_ref=pair(chip), dst_ref=pair(chip), send_sem=send2.at[other], recv_sem=recv2.at[chip],
            device_id=device_of(2 * other + core, sizes), device_id_type=MESH,
        ).start()
        return carry

    lax.fori_loop(1, count + 1, send_out, 0)

    def take_in(k, carry):
        other = source(k)
        pltpu.make_async_remote_copy(
            src_ref=pair(other), dst_ref=pair(other), send_sem=send2.at[other], recv_sem=recv2.at[other],
            device_id=device_of(2 * other + core, sizes), device_id_type=MESH,
        ).wait_recv()
        pltpu.make_async_remote_copy(
            src_ref=pair(other), dst_ref=pair(other), send_sem=send3.at[other], recv_sem=recv3.at[other],
            device_id=device_of(partner, sizes), device_id_type=MESH,
        ).start()
        return carry

    lax.fori_loop(1, count + 1, take_in, 0)

    def sent_out(k, carry):
        other = target(k)
        pltpu.make_async_remote_copy(
            src_ref=pair(chip), dst_ref=pair(chip), send_sem=send2.at[other], recv_sem=recv2.at[chip],
            device_id=device_of(2 * other + core, sizes), device_id_type=MESH,
        ).wait_send()
        return carry

    lax.fori_loop(1, count + 1, sent_out, 0)

    def forwarded(k, carry):
        other = source(k)
        pltpu.make_async_remote_copy(
            src_ref=pair(other), dst_ref=pair(other), send_sem=send3.at[other], recv_sem=recv3.at[other],
            device_id=device_of(partner, sizes), device_id_type=MESH,
        ).wait_send()
        return carry

    lax.fori_loop(1, count + 1, forwarded, 0)

    other_count = (chips - (1 - core)) // 2

    def partner_source(k):
        return lax.rem(chip + chips - (2 * k - 1 + (1 - core)), chips)

    def from_partner(k, carry):
        other = partner_source(k)
        pltpu.make_async_remote_copy(
            src_ref=pair(other), dst_ref=pair(other), send_sem=send3.at[other], recv_sem=recv3.at[other],
            device_id=device_of(partner, sizes), device_id_type=MESH,
        ).wait_recv()
        return carry

    lax.fori_loop(1, other_count + 1, from_partner, 0)


def pair_gather(x, sizes, cid):
    n = math.prod(sizes)
    chips = n // 2
    dma = pltpu.SemaphoreType.DMA
    return pl.pallas_call(
        functools.partial(pair_gather_kernel, n, sizes),
        out_shape=jax.ShapeDtypeStruct((n,) + x.shape, x.dtype),
        in_specs=[pl.BlockSpec(memory_space=pltpu.VMEM)],
        out_specs=pl.BlockSpec(memory_space=pltpu.VMEM),
        scratch_shapes=[dma(()), dma(()), dma(()), dma((chips,)), dma((chips,)), dma((chips,)), dma((chips,))],
        compiler_params=pltpu.CompilerParams(collective_id=cid, has_side_effects=True),
    )(x)


def halving_orders(n, parts):
    bits = n.bit_length() - 1
    middle = list(range(1, bits - 1))
    orders = []
    for p in range(parts):
        shift = p % len(middle) if middle else 0
        orders.append(tuple([0] + middle[shift:] + middle[:shift] + [bits - 1]))
    return tuple(orders)


def halving_kernel(n, sizes, orders, cols, tile, groups, computed, *refs):
    count = sum(groups) - int(computed)
    sources = list(refs[:count])
    vec_ref, dq_ref, w_ref, res_ref = refs[count : count + 4]
    at = count + 4
    if computed:
        x_ref = refs[at]
        at += 1
    out_ref, vec_out, grad_out, work = refs[at : at + 4]
    at += 4
    if computed:
        made = refs[at]
        at += 1
        sources.insert(0, made)
    rest = refs[at:]
    grouped = []
    at = 0
    for g in groups:
        grouped.append(sources[at : at + g])
        at += g
    steps = len(orders[0])
    parts = len(orders)
    layout = []
    head = 0
    for group in grouped:
        size = sum(math.prod(s.shape[:-1]) for s in group) // n
        layout.append((group, size, head))
        head += size
    recvs = rest[:steps]
    local_sem, send_sems, recv_sems, vec_send, vec_recv = rest[steps:]
    me = flat_index(sizes)

    def partner_of(bit):
        mine = lax.rem(me // (2**bit), 2)
        return mine, me + (1 - 2 * mine) * (2**bit)

    enter_all(n, sizes, me)

    def vec_copy(k):
        peer = lax.rem(me + k, n)
        return pltpu.make_async_remote_copy(
            src_ref=vec_ref.at[peer], dst_ref=vec_out.at[me], send_sem=vec_send.at[k], recv_sem=vec_recv.at[me],
            device_id=device_of(peer, sizes), device_id_type=MESH,
        )

    def vec_start(k, carry):
        vec_copy(k).start()
        return carry

    lax.fori_loop(1, n, vec_start, 0)
    vec_out[me] = vec_ref[me]

    half = n // 2
    first = []
    issuers = []
    for p in range(parts):
        order = orders[p]
        mine, other = partner_of(order[0])
        column = pl.ds(p * cols, cols)

        def owner(j, side, order=order):
            o = side * (2 ** order[0])
            for m, bit in enumerate(order[1:]):
                o = o + lax.rem(j // (2 ** (steps - 2 - m)), 2) * (2**bit)
            return o

        def issue(j, carry, p=p, owner=owner, mine=mine, other=other, column=column, which=None):
            for o, dst, remote in ((owner(j, 1 - mine), recvs[0].at[p, j], True), (owner(j, mine), work.at[p, j], False)):
                for group, size, head in [layout[w] for w in which]:
                    offset = 0
                    for chosen in group:
                        split = math.prod(chosen.shape[:-1]) // size

                        def move(chosen=chosen, offset=offset, o=o, dst=dst, remote=remote, size=size, head=head):
                            if len(chosen.shape) == 3:
                                src_ref = chosen.at[o - offset, :, column]
                            else:
                                src_ref = chosen.at[pl.ds((o - offset) * size, size), column]
                            dst_ref = dst.at[pl.ds(head, size)]
                            if remote:
                                pltpu.make_async_remote_copy(
                                    src_ref=src_ref, dst_ref=dst_ref,
                                    send_sem=send_sems.at[p, 0], recv_sem=recv_sems.at[p, 0],
                                    device_id=device_of(other, sizes), device_id_type=MESH,
                                ).start()
                            else:
                                pltpu.make_async_copy(src_ref, dst_ref, local_sem.at[p]).start()

                        if len(group) == 1:
                            move()
                        else:
                            pl.when((o >= offset) & (o < offset + split))(move)
                        offset += split

            return carry

        issuers.append(issue)
        first.append(other)
    later = [0] if computed else []
    sooner = [w for w in range(len(layout)) if w not in later]
    for issue in issuers:
        lax.fori_loop(0, half, functools.partial(issue, which=sooner), 0)
    if computed:
        on_first = (((0,), (0,)), ((), ()))

        def product_t(t, carry):
            rows = pl.ds(pl.multiple_of(t * tile, tile), tile)
            made[rows, :] = lax.dot_general(
                dq_ref[:, rows], x_ref[...], on_first, preferred_element_type=jnp.float32
            ).astype(made.dtype)
            return carry

        lax.fori_loop(0, made.shape[0] // tile, product_t, 0)
        for issue in issuers:
            lax.fori_loop(0, half, functools.partial(issue, which=later), 0)
    for p in range(parts):
        whole = pltpu.make_async_remote_copy(
            src_ref=work.at[p, pl.ds(0, half)], dst_ref=recvs[0].at[p],
            send_sem=send_sems.at[p, 0], recv_sem=recv_sems.at[p, 0],
            device_id=device_of(first[p], sizes), device_id_type=MESH,
        )
        pltpu.make_async_copy(work.at[p, pl.ds(0, half)], work.at[p, pl.ds(0, half)], local_sem.at[p]).wait()
        whole.wait_recv()
        whole.wait_send()

        def accumulate0(i, carry, p=p):
            total = work[p, i].astype(jnp.float32) + recvs[0][p, i].astype(jnp.float32)
            work[p, i] = total.astype(work.dtype)
            return carry

        lax.fori_loop(0, half, accumulate0, 0)

    for step in range(1, steps):
        half = n >> (step + 1)
        copies = []
        for p in range(parts):
            mine, other = partner_of(orders[p][step])
            send = pltpu.make_async_remote_copy(
                src_ref=work.at[p, pl.ds((1 - mine) * half, half)], dst_ref=recvs[step].at[p],
                send_sem=send_sems.at[p, step], recv_sem=recv_sems.at[p, step],
                device_id=device_of(other, sizes), device_id_type=MESH,
            )
            send.start()
            copies.append((mine, send))
        if step == 1:
            def product(t, carry):
                rows = pl.ds(pl.multiple_of(t * tile, tile), tile)
                grad_out[rows, :] = (
                    jnp.dot(dq_ref[rows, :], w_ref[...], preferred_element_type=jnp.float32) + res_ref[rows, :]
                )
                return carry

            lax.fori_loop(0, grad_out.shape[0] // tile, product, 0)
        for p in range(parts):
            mine, send = copies[p]
            send.wait_recv()
            send.wait_send()

            def accumulate(i, carry, p=p, mine=mine, half=half, step=step):
                total = work[p, mine * half + i].astype(jnp.float32) + recvs[step][p, i].astype(jnp.float32)
                work[p, i] = total.astype(work.dtype)
                return carry

            lax.fori_loop(0, half, accumulate, 0)
    for p in range(parts):
        out_ref[:, p * cols : (p + 1) * cols] = work[p, 0].astype(out_ref.dtype)

    def vec_finish(k, carry):
        vec_copy(k).wait_send()
        src = lax.rem(me + n - k, n)
        pltpu.make_async_remote_copy(
            src_ref=vec_ref.at[src], dst_ref=vec_out.at[src], send_sem=vec_send.at[k], recv_sem=vec_recv.at[src],
            device_id=device_of(src, sizes), device_id_type=MESH,
        ).wait_recv()
        return carry

    lax.fori_loop(1, n, vec_finish, 0)


def halving_scatter(grouped, vec, grad_b, weight_t, residual, sizes, parts, cid, tokens=None):
    n = math.prod(sizes)
    computed = tokens is not None
    groups = tuple(len(g) for g in grouped)
    given = [s for g in grouped for s in g if s is not None]
    made_shape = (grad_b.shape[1], tokens.shape[1]) if computed else None
    assert not computed or made_shape[0] % 128 == 0
    shapes = [made_shape if s is None else s.shape for g in grouped for s in g]
    dtype = given[0].dtype
    width = shapes[0][-1]
    rows = sum(math.prod(s[:-1]) for s in shapes) // n
    cols = width // parts
    orders = halving_orders(n, parts)
    steps = len(orders[0])
    tile = 128
    dma = pltpu.SemaphoreType.DMA
    vmem = pl.BlockSpec(memory_space=pltpu.VMEM)
    scratch = [pltpu.VMEM((parts, n // 2, rows, cols), dtype)]
    if computed:
        scratch.append(pltpu.VMEM(made_shape, dtype))
    scratch += [pltpu.VMEM((parts, n >> (k + 1), rows, cols), dtype) for k in range(steps)]
    scratch += [dma((parts,)), dma((parts, steps)), dma((parts, steps)), dma((n,)), dma((n,))]
    return pl.pallas_call(
        functools.partial(halving_kernel, n, sizes, orders, cols, tile, groups, computed),
        out_shape=(
            jax.ShapeDtypeStruct((rows, parts * cols), jnp.float32),
            jax.ShapeDtypeStruct(vec.shape, vec.dtype),
            jax.ShapeDtypeStruct(residual.shape, jnp.float32),
        ),
        in_specs=[pl.BlockSpec(memory_space=pl.ANY)] * len(given) + [vmem] * (4 + int(computed)),
        out_specs=(vmem, vmem, vmem),
        scratch_shapes=scratch,
        compiler_params=pltpu.CompilerParams(
            collective_id=cid, has_side_effects=True, vmem_limit_bytes=60 * 1024 * 1024
        ),
    )(*given, vec, grad_b, weight_t, residual, *([tokens] if computed else []))


def contrastive(embed_b, gathered, partner_all, me):
    own_texts = embed_b.shape[0]
    all_texts = gathered.shape[0]
    chunk = min(all_texts, 1024)
    on_rows = (((1,), (1,)), ((), ()))

    def chunk_stats(c):
        rows_b = lax.dynamic_slice_in_dim(gathered, c * chunk, chunk)
        sim = lax.dot_general(rows_b, gathered, on_rows, preferred_element_type=jnp.float32) / logit_divisor
        column_ids = lax.broadcasted_iota(jnp.int32, sim.shape, 1)
        row_ids = lax.broadcasted_iota(jnp.int32, sim.shape, 0) + c * chunk
        masked = jnp.where(column_ids == row_ids, masked_value, sim)
        row_max = jnp.max(masked, -1, keepdims=True)
        log_sum = row_max + jnp.log(jnp.sum(jnp.exp(masked - row_max), -1, keepdims=True))
        wanted = lax.dynamic_slice_in_dim(partner_all, c * chunk, chunk)
        positive = jnp.sum(jnp.where(column_ids == wanted[:, None], sim, 0.0), -1)
        return log_sum[:, 0], positive

    if all_texts == chunk:
        log_sum_all, positive_all = chunk_stats(0)
    else:
        log_sum_all, positive_all = lax.map(chunk_stats, jnp.arange(all_texts // chunk))
        log_sum_all = log_sum_all.reshape(-1)
        positive_all = positive_all.reshape(-1)
    mean_loss = jnp.sum(log_sum_all - positive_all) / all_texts

    own_start = me * own_texts
    own_ids = lax.broadcasted_iota(jnp.int32, (own_texts,), 0) + own_start
    own_partner = lax.dynamic_slice_in_dim(partner_all, own_start, own_texts)
    own_log_sum = lax.dynamic_slice_in_dim(log_sum_all, own_start, own_texts)

    sim_rows = lax.dot_general(embed_b, gathered, on_rows, preferred_element_type=jnp.float32) / logit_divisor
    column_ids = lax.broadcasted_iota(jnp.int32, sim_rows.shape, 1)
    masked_rows = jnp.where(column_ids == own_ids[:, None], masked_value, sim_rows)
    grad_rows = (
        jnp.exp(masked_rows - own_log_sum[:, None]) - (column_ids == own_partner[:, None]).astype(jnp.float32)
    ).astype(jnp.bfloat16)

    sim_cols = lax.dot_general(gathered, embed_b, on_rows, preferred_element_type=jnp.float32) / logit_divisor
    row_ids = lax.broadcasted_iota(jnp.int32, sim_cols.shape, 0)
    masked_cols = jnp.where(row_ids == own_ids[None, :], masked_value, sim_cols)
    grad_cols = (
        jnp.exp(masked_cols - log_sum_all[:, None]) - (partner_all[:, None] == own_ids[None, :]).astype(jnp.float32)
    ).astype(jnp.bfloat16)

    on_tokens = (((0,), (0,)), ((), ()))
    embedding_gradient = (
        jnp.dot(grad_rows, gathered, preferred_element_type=jnp.float32)
        + lax.dot_general(grad_cols, gathered, on_tokens, preferred_element_type=jnp.float32)
    ) / logit_divisor
    return mean_loss, embedding_gradient


def shards(
    hidden_in,
    segments,
    partner,
    attn_weights,
    ffn_weights,
    vectors,
    attn_momentum,
    ffn_momentum,
    vector_momentum,
    attn_averaged,
    ffn_averaged,
    vector_averaged,
):
    sizes = tuple(lax.axis_size(name) for name in AXES)
    n_dev = math.prod(sizes)
    me = flat_index(sizes)
    vec_len = vectors.shape[0]
    small = jnp.concatenate([vectors, partner.astype(jnp.float32)])[None, :]
    small_all = small_gather(small, sizes, 0)[:, 0, :]
    vector_f = bf16_round(small_all[:, :vec_len].reshape(-1))
    partner_all = small_all[:, vec_len:].reshape(-1).astype(jnp.int32)
    attn_full, ffn_full = (
        lax.all_gather(attn_weights.astype(jnp.bfloat16), AXES, axis=1, tiled=True),
        lax.all_gather(ffn_weights.astype(jnp.bfloat16), AXES, axis=1, tiled=True),
    )
    width = attn_full.shape[0]
    hidden = ffn_full.shape[1] // 2
    query_bias = vector_f[0:width]
    value_bias = vector_f[width : 2 * width]
    output_bias = vector_f[2 * width : 3 * width]
    gain_first = vector_f[3 * width : 4 * width]
    shift_first = vector_f[4 * width : 5 * width]
    upper_bias = vector_f[5 * width : 5 * width + hidden]
    lower_bias = vector_f[5 * width + hidden : 6 * width + hidden]
    gain_second = vector_f[6 * width + hidden : 7 * width + hidden]
    shift_second = vector_f[7 * width + hidden : 8 * width + hidden]
    w_qkv = attn_full[:, : 3 * width]
    w_output = attn_full[:, 3 * width :]
    w_upper = ffn_full[:, :hidden]
    w_lower = ffn_full[:, hidden:]
    rows_dev, seq_len = segments.shape
    tokens_n = rows_dev * seq_len
    on_rows = (((1,), (1,)), ((), ()))
    on_tokens = (((0,), (0,)), ((), ()))
    qkv_bias = jnp.concatenate([query_bias, jnp.zeros_like(query_bias), value_bias])
    qkv_rows = (jnp.dot(hidden_in, w_qkv, preferred_element_type=jnp.float32) + qkv_bias).astype(
        jnp.bfloat16
    )
    heads = qkv_rows.reshape(rows_dev, seq_len, 3, HEADS, HD)
    query_rows = heads[:, :, 0]
    key_rows = heads[:, :, 1]
    value_rows = heads[:, :, 2]
    mixed, log_norm = attend_rows(query_rows, key_rows, value_rows, segments)
    mixed_flat = mixed.reshape(tokens_n, width)
    first_sum = (
        hidden_in.astype(jnp.float32)
        + jnp.dot(mixed_flat, w_output, preferred_element_type=jnp.float32)
        + output_bias
    )
    normed, normal_one, inverse_one = layer_norm_parts(first_sum, gain_first, shift_first)
    normed_r = bf16_round(normed)
    normed_b = normed_r.astype(jnp.bfloat16)
    upper = jnp.dot(normed_b, w_upper, preferred_element_type=jnp.float32) + upper_bias
    active_b = (0.5 * upper * (1.0 + lax.erf(upper / math.sqrt(2.0)))).astype(jnp.bfloat16)
    second_sum = (
        normed_r
        + lax.dot_general(active_b, w_lower, on_rows, preferred_element_type=jnp.float32)
        + lower_bias
    )
    result, normal_two, inverse_two = layer_norm_parts(second_sum, gain_second, shift_second)
    text_ids = jnp.arange(SEGS, dtype=jnp.int32)
    one_hot = (segments[:, None, :] == text_ids[None, :, None]).astype(jnp.float32)
    counts = jnp.sum(one_hot, -1, keepdims=True)
    pooled = (
        jnp.einsum(
            "rts,rsd->rtd",
            one_hot,
            result.reshape(rows_dev, seq_len, width),
            precision=lax.Precision.HIGHEST,
        )
        / counts
    ).reshape(-1, width)
    inv_norm = lax.rsqrt(jnp.sum(pooled * pooled, -1, keepdims=True) + pool_epsilon)
    embed_b = (pooled * inv_norm).astype(jnp.bfloat16)
    gathered_embeddings = pair_gather(embed_b, sizes, 2).reshape(-1, width)
    mean_loss, embedding_gradient = contrastive(embed_b, gathered_embeddings, partner_all, me)
    grad_pooled = inv_norm * embedding_gradient - pooled * (
        inv_norm * inv_norm * inv_norm
    ) * jnp.sum(embedding_gradient * pooled, -1, keepdims=True)
    derivative_output = jnp.einsum(
        "rts,rtd->rsd",
        one_hot,
        grad_pooled.reshape(rows_dev, SEGS, width) / counts,
        precision=lax.Precision.HIGHEST,
    ).reshape(tokens_n, width)
    grad_second, gain_two_grad, shift_two_grad = layer_norm_back(
        derivative_output, normal_two, inverse_two, gain_second
    )
    lower_bias_grad = jnp.sum(grad_second, 0)
    lower_grad_b = grad_second.astype(jnp.bfloat16)
    lower_w_grad_t = lax.dot_general(
        active_b, lower_grad_b, on_tokens, preferred_element_type=jnp.float32
    )
    grad_active = jnp.dot(lower_grad_b, w_lower, preferred_element_type=jnp.float32)
    cumulative = 0.5 * (1.0 + lax.erf(upper / math.sqrt(2.0)))
    density = jnp.exp(-0.5 * upper * upper) / math.sqrt(2.0 * math.pi)
    grad_upper = grad_active * (cumulative + upper * density)
    upper_bias_grad = jnp.sum(grad_upper, 0)
    upper_grad_b = grad_upper.astype(jnp.bfloat16)
    upper_w_grad_t = lax.dot_general(
        upper_grad_b, normed_b, on_tokens, preferred_element_type=jnp.float32
    )
    grad_normed = (
        lax.dot_general(upper_grad_b, w_upper, on_rows, preferred_element_type=jnp.float32)
        + grad_second
    )
    grad_first, gain_one_grad, shift_one_grad = layer_norm_back(
        grad_normed, normal_one, inverse_one, gain_first
    )
    output_bias_grad = jnp.sum(grad_first, 0)
    first_grad_b = grad_first.astype(jnp.bfloat16)
    output_w_grad_t = lax.dot_general(
        first_grad_b, mixed_flat, on_tokens, preferred_element_type=jnp.float32
    )
    grad_mixed = lax.dot_general(
        first_grad_b, w_output, on_rows, preferred_element_type=jnp.float32
    ).astype(jnp.bfloat16)
    grad_mixed = grad_mixed.reshape(rows_dev, seq_len, HEADS, HD)
    norm_tokens = jnp.swapaxes(log_norm, 1, 2).reshape(tokens_n, HEADS)
    qkv_grad = jnp.concatenate(
        attention_back(qkv_rows, grad_mixed.reshape(tokens_n, width), norm_tokens, segments, HEADS, HD), 1
    ).astype(jnp.float32)
    qkv_grad_f = bf16_round(qkv_grad)
    qkv_grad_b = qkv_grad_f.astype(jnp.bfloat16)
    query_bias_grad = jnp.sum(qkv_grad_f[:, :width], 0)
    value_bias_grad = jnp.sum(qkv_grad_f[:, 2 * width :], 0)
    qkv_w_grad_t = lax.dot_general(
        qkv_grad_b, hidden_in, on_tokens, preferred_element_type=jnp.float32
    )
    vector_grad = jnp.concatenate(
        [
            query_bias_grad,
            value_bias_grad,
            output_bias_grad,
            gain_one_grad,
            shift_one_grad,
            upper_bias_grad,
            lower_bias_grad,
            gain_two_grad,
            shift_two_grad,
        ]
    )
    attn_cols = (qkv_w_grad_t.shape[0] + output_w_grad_t.shape[0]) // n_dev
    ffn_cols = (upper_w_grad_t.shape[0] + lower_w_grad_t.shape[0]) // n_dev
    if attn_cols % 16 == 0 and ffn_cols % 16 == 0:
        grads = (
            (None, output_w_grad_t.astype(GRAD_SEND)),
            (upper_w_grad_t.astype(GRAD_SEND), lower_w_grad_t.astype(GRAD_SEND)),
        )
        made_from = hidden_in
    else:
        attn_blocks = jnp.concatenate(
            [qkv_w_grad_t.reshape(-1, attn_cols, width), output_w_grad_t.reshape(-1, attn_cols, width)], 0
        )
        ffn_blocks = jnp.concatenate(
            [upper_w_grad_t.reshape(-1, ffn_cols, width), lower_w_grad_t.reshape(-1, ffn_cols, width)], 0
        )
        grads = ((jnp.concatenate([attn_blocks, ffn_blocks], 1).astype(GRAD_SEND),),)
        made_from = None
    parts = 6
    mine_parts, vector_slots, input_grad = halving_scatter(
        grads, vector_grad.reshape(n_dev, 1, -1), qkv_grad_b, w_qkv.T, grad_first, sizes, parts, 3, made_from
    )
    vector_reduced = jnp.sum(vector_slots[:, 0, :], 0)
    joined_reduced = mine_parts
    attn_reduced = joined_reduced[:attn_cols].T
    ffn_reduced = joined_reduced[attn_cols:].T
    attn_new, attn_moment, attn_average = apply_update(
        attn_weights, attn_reduced, attn_momentum, attn_averaged, decay_rate
    )
    ffn_new, ffn_moment, ffn_average = apply_update(
        ffn_weights, ffn_reduced, ffn_momentum, ffn_averaged, decay_rate
    )
    vector_new, vector_moment, vector_average = apply_update(
        vectors, vector_reduced, vector_momentum, vector_averaged, 0.0
    )
    return (
        mean_loss,
        input_grad,
        attn_reduced,
        ffn_reduced,
        vector_reduced,
        attn_new,
        ffn_new,
        vector_new,
        attn_moment,
        ffn_moment,
        vector_moment,
        attn_average,
        ffn_average,
        vector_average,
    )


def solution(mesh):
    in_specs = (
        P(("dp", "rep"), None),
        P(("dp", "rep"), None),
        P(("dp", "rep")),
        P(None, ("dp", "rep")),
        P(None, ("dp", "rep")),
        P(("dp", "rep")),
        P(None, ("dp", "rep")),
        P(None, ("dp", "rep")),
        P(("dp", "rep")),
        P(None, ("dp", "rep")),
        P(None, ("dp", "rep")),
        P(("dp", "rep")),
    )
    out_specs = (
        P(),
        P(("dp", "rep"), None),
        P(None, ("dp", "rep")),
        P(None, ("dp", "rep")),
        P(("dp", "rep")),
        P(None, ("dp", "rep")),
        P(None, ("dp", "rep")),
        P(("dp", "rep")),
        P(None, ("dp", "rep")),
        P(None, ("dp", "rep")),
        P(("dp", "rep")),
        P(None, ("dp", "rep")),
        P(None, ("dp", "rep")),
        P(("dp", "rep")),
    )
    return jax.shard_map(shards, mesh=mesh, in_specs=in_specs, out_specs=out_specs, check_vma=False)
```

```python
import functools
import math

import jax
import jax.numpy as jnp
from jax import lax
from jax.experimental import pallas as pl
from jax.experimental.pallas import tpu as pltpu
from jax.sharding import PartitionSpec as P

MESH = pl.DeviceIdType.MESH
GRAD_SEND = jnp.bfloat16
AXES = ("dp", "rep")

HEADS = 12
HD = 64
SEGS = 16


ln_epsilon = 1e-12
pool_epsilon = 1e-06
logit_divisor = 0.025
learn_rate = 0.01
momentum_rate = 0.9
decay_rate = 0.01
average_rate = 0.75
masked_value = -1e30


def layer_norm_parts(values, gain, shift):
    per_line_average = jnp.mean(values, -1, keepdims=True)
    centred = values - per_line_average
    inverse = lax.rsqrt(jnp.mean(centred * centred, -1, keepdims=True) + ln_epsilon)
    normal_part = centred * inverse
    return (normal_part * gain + shift, normal_part, inverse)


def layer_norm_back(grad_out, normal_part, inverse, gain):
    scaled = grad_out * gain
    grad_in = inverse * (
        scaled
        - jnp.mean(scaled, -1, keepdims=True)
        - normal_part * jnp.mean(scaled * normal_part, -1, keepdims=True)
    )
    return (grad_in, jnp.sum(grad_out * normal_part, 0), jnp.sum(grad_out, 0))


def row_scores(query_one, key_one, segment_one, scale):
    scores = (
        jnp.einsum("qhd,khd->hqk", query_one, key_one, preferred_element_type=jnp.float32) * scale
    )
    same_text = segment_one[:, None] == segment_one[None, :]
    return jnp.where(same_text[None], scores, masked_value)


def attend_rows(query_rows, key_rows, value_rows, row_segments):
    scale = 1.0 / math.sqrt(query_rows.shape[-1])

    def one_row(row_args):
        query_one, key_one, value_one, segment_one = row_args
        scores = row_scores(query_one, key_one, segment_one, scale)
        row_max = jnp.max(scores, -1, keepdims=True)
        exp_scores = jnp.exp(scores - row_max)
        sums = jnp.sum(exp_scores, -1, keepdims=True)
        attn_probs = exp_scores / sums
        mixed = jnp.einsum(
            "hqk,khd->qhd",
            attn_probs.astype(jnp.bfloat16),
            value_one,
            preferred_element_type=jnp.float32,
        )
        return (mixed.astype(jnp.bfloat16), (row_max + jnp.log(sums))[..., 0])

    return lax.map(one_row, (query_rows, key_rows, value_rows, row_segments))


def attend_back(query_rows, key_rows, value_rows, row_segments, log_norm, grad_mixed):
    scale = 1.0 / math.sqrt(query_rows.shape[-1])

    def one_row(row_args):
        query_one, key_one, value_one, segment_one, norm_one, grad_one = row_args
        scores = row_scores(query_one, key_one, segment_one, scale)
        attn_probs = jnp.exp(scores - norm_one[..., None])
        grad_value = jnp.einsum(
            "hqk,qhd->khd",
            attn_probs.astype(jnp.bfloat16),
            grad_one,
            preferred_element_type=jnp.float32,
        )
        grad_probs = jnp.einsum(
            "qhd,khd->hqk", grad_one, value_one, preferred_element_type=jnp.float32
        )
        inner = jnp.sum(attn_probs * grad_probs, -1, keepdims=True)
        grad_scores = (attn_probs * (grad_probs - inner)).astype(jnp.bfloat16)
        grad_query = (
            jnp.einsum("hqk,khd->qhd", grad_scores, key_one, preferred_element_type=jnp.float32)
            * scale
        )
        grad_key = (
            jnp.einsum("hqk,qhd->khd", grad_scores, query_one, preferred_element_type=jnp.float32)
            * scale
        )
        return jnp.concatenate([grad_query, grad_key, grad_value], axis=1)

    return lax.map(one_row, (query_rows, key_rows, value_rows, row_segments, log_norm, grad_mixed))


def attention_back_kernel(scale, q_ref, k_ref, v_ref, g_ref, norm_ref, seg_col_ref, seg_row_ref, dq_ref, dk_ref, dv_ref):
    pair = pl.program_id(1)
    width = q_ref.shape[1]
    half = width // 2
    lane = lax.broadcasted_iota(jnp.int32, (1, width), 1)
    same = seg_col_ref[...] == seg_row_ref[0]
    norms = norm_ref[...]
    norm_lane = lax.broadcasted_iota(jnp.int32, norms.shape, 1)
    q = q_ref[...]
    k = k_ref[...]
    v = v_ref[...]
    g = g_ref[...]
    zero_b = jnp.zeros_like(q)
    on_last = (((1,), (1,)), ((), ()))
    on_first = (((0,), (0,)), ((), ()))
    dq = jnp.zeros(q.shape, jnp.float32)
    dk = jnp.zeros(q.shape, jnp.float32)
    dv = jnp.zeros(q.shape, jnp.float32)
    for head in range(2):
        mine = (lane >= head * half) & (lane < (head + 1) * half)
        q_h = jnp.where(mine, q, zero_b)
        g_h = jnp.where(mine, g, zero_b)
        norm_h = jnp.sum(jnp.where(norm_lane == 2 * pair + head, norms, 0.0), 1, keepdims=True)
        scores = lax.dot_general(q_h, k, on_last, preferred_element_type=jnp.float32) * scale
        scores = jnp.where(same, scores, masked_value)
        probs = jnp.exp(scores - norm_h)
        grad_v = lax.dot_general(probs.astype(jnp.bfloat16), g, on_first, preferred_element_type=jnp.float32)
        grad_p = lax.dot_general(g_h, v, on_last, preferred_element_type=jnp.float32)
        inner = jnp.sum(probs * grad_p, -1, keepdims=True)
        grad_s = (probs * (grad_p - inner)).astype(jnp.bfloat16)
        grad_q = jnp.dot(grad_s, k, preferred_element_type=jnp.float32) * scale
        grad_k = lax.dot_general(grad_s, q, on_first, preferred_element_type=jnp.float32) * scale
        dq = jnp.where(mine, grad_q, dq)
        dk = jnp.where(mine, grad_k, dk)
        dv = jnp.where(mine, grad_v, dv)
    dq_ref[...] = dq.astype(dq_ref.dtype)
    dk_ref[...] = dk.astype(dk_ref.dtype)
    dv_ref[...] = dv.astype(dv_ref.dtype)


def attention_back(qkv_rows, grad_mixed_flat, norm_tokens, segments, heads, head_dim):
    tokens, three_width = qkv_rows.shape
    width = three_width // 3
    rows, seq_len = segments.shape
    pair_width = 2 * head_dim
    pairs = heads // 2
    seg_col = segments.reshape(tokens, 1)
    seg_row = segments.reshape(rows, 1, seq_len)
    scale = 1.0 / math.sqrt(head_dim)
    out = jax.ShapeDtypeStruct((tokens, width), jnp.bfloat16)
    return pl.pallas_call(
        functools.partial(attention_back_kernel, scale),
        grid=(rows, pairs),
        in_specs=[
            pl.BlockSpec((seq_len, pair_width), lambda r, p: (r, p)),
            pl.BlockSpec((seq_len, pair_width), lambda r, p: (r, pairs + p)),
            pl.BlockSpec((seq_len, pair_width), lambda r, p: (r, 2 * pairs + p)),
            pl.BlockSpec((seq_len, pair_width), lambda r, p: (r, p)),
            pl.BlockSpec((seq_len, heads), lambda r, p: (r, 0)),
            pl.BlockSpec((seq_len, 1), lambda r, p: (r, 0)),
            pl.BlockSpec((1, 1, seq_len), lambda r, p: (r, 0, 0)),
        ],
        out_specs=[pl.BlockSpec((seq_len, pair_width), lambda r, p: (r, p))] * 3,
        out_shape=[out, out, out],
        compiler_params=pltpu.CompilerParams(vmem_limit_bytes=48 * 1024 * 1024),
        cost_estimate=pl.CostEstimate(
            flops=10 * rows * heads * seq_len * seq_len * pair_width,
            transcendentals=rows * heads * seq_len * seq_len,
            bytes_accessed=tokens * (three_width + 4 * width) * 2,
        ),
    )(qkv_rows, qkv_rows, qkv_rows, grad_mixed_flat, norm_tokens, seg_col, seg_row)


def apply_update(weight, grad, moment, average, decay):
    step_grad = grad + decay * weight
    new_moment = momentum_rate * moment + step_grad
    new_weight = weight - learn_rate * (step_grad + momentum_rate * new_moment)
    fresh_running_mean = average_rate * average + (1.0 - average_rate) * new_weight
    return (new_weight, new_moment, fresh_running_mean)


def bf16_round(values):
    return lax.reduce_precision(values, exponent_bits=8, mantissa_bits=7)


def flat_index(sizes):
    idx = 0
    for name, size in zip(AXES, sizes):
        idx = idx * size + lax.axis_index(name)
    return idx


def device_of(flat, sizes):
    coords = []
    for size in reversed(sizes):
        coords.append(lax.rem(flat, size))
        flat = flat // size
    return tuple(reversed(coords))


def enter_all(n, sizes, me):
    barrier = pltpu.get_barrier_semaphore()

    def greet(k, carry):
        peer = lax.rem(me + k, n)
        pl.semaphore_signal(barrier, inc=1, device_id=device_of(peer, sizes), device_id_type=MESH)
        return carry

    lax.fori_loop(1, n, greet, 0)
    pl.semaphore_wait(barrier, n - 1)


def gather_kernel(n, sizes, x_ref, out_ref, send_sem, recv_sem):
    me = flat_index(sizes)
    enter_all(n, sizes, me)

    def send(k, carry):
        peer = lax.rem(me + k, n)
        pltpu.make_async_remote_copy(
            src_ref=x_ref, dst_ref=out_ref.at[me], send_sem=send_sem.at[k], recv_sem=recv_sem.at[me],
            device_id=device_of(peer, sizes), device_id_type=MESH,
        ).start()
        return carry

    lax.fori_loop(1, n, send, 0)
    out_ref[me] = x_ref[...]

    def finish(k, carry):
        peer = lax.rem(me + k, n)
        src = lax.rem(me + n - k, n)
        pltpu.make_async_remote_copy(
            src_ref=x_ref, dst_ref=out_ref.at[me], send_sem=send_sem.at[k], recv_sem=recv_sem.at[me],
            device_id=device_of(peer, sizes), device_id_type=MESH,
        ).wait_send()
        pltpu.make_async_remote_copy(
            src_ref=x_ref, dst_ref=out_ref.at[src], send_sem=send_sem.at[k], recv_sem=recv_sem.at[src],
            device_id=device_of(src, sizes), device_id_type=MESH,
        ).wait_recv()
        return carry

    lax.fori_loop(1, n, finish, 0)


def small_gather(x, sizes, cid):
    n = math.prod(sizes)
    return pl.pallas_call(
        functools.partial(gather_kernel, n, sizes),
        out_shape=jax.ShapeDtypeStruct((n,) + x.shape, x.dtype),
        in_specs=[pl.BlockSpec(memory_space=pltpu.VMEM)],
        out_specs=pl.BlockSpec(memory_space=pltpu.VMEM),
        scratch_shapes=[pltpu.SemaphoreType.DMA((n,)), pltpu.SemaphoreType.DMA((n,))],
        compiler_params=pltpu.CompilerParams(collective_id=cid, has_side_effects=True),
    )(x)


def scatter_kernel(n, sizes, x_ref, out_ref, send_sem, recv_sem):
    me = flat_index(sizes)
    enter_all(n, sizes, me)

    def send(k, carry):
        peer = lax.rem(me + k, n)
        pltpu.make_async_remote_copy(
            src_ref=x_ref.at[peer], dst_ref=out_ref.at[me], send_sem=send_sem.at[k], recv_sem=recv_sem.at[me],
            device_id=device_of(peer, sizes), device_id_type=MESH,
        ).start()
        return carry

    lax.fori_loop(1, n, send, 0)
    out_ref[me] = x_ref[me]

    def finish(k, carry):
        peer = lax.rem(me + k, n)
        src = lax.rem(me + n - k, n)
        pltpu.make_async_remote_copy(
            src_ref=x_ref.at[peer], dst_ref=out_ref.at[me], send_sem=send_sem.at[k], recv_sem=recv_sem.at[me],
            device_id=device_of(peer, sizes), device_id_type=MESH,
        ).wait_send()
        pltpu.make_async_remote_copy(
            src_ref=x_ref.at[src], dst_ref=out_ref.at[src], send_sem=send_sem.at[k], recv_sem=recv_sem.at[src],
            device_id=device_of(src, sizes), device_id_type=MESH,
        ).wait_recv()
        return carry

    lax.fori_loop(1, n, finish, 0)


def small_scatter(x, sizes, cid):
    n = math.prod(sizes)
    return pl.pallas_call(
        functools.partial(scatter_kernel, n, sizes),
        out_shape=jax.ShapeDtypeStruct(x.shape, x.dtype),
        in_specs=[pl.BlockSpec(memory_space=pltpu.VMEM)],
        out_specs=pl.BlockSpec(memory_space=pltpu.VMEM),
        scratch_shapes=[pltpu.SemaphoreType.DMA((n,)), pltpu.SemaphoreType.DMA((n,))],
        compiler_params=pltpu.CompilerParams(collective_id=cid, has_side_effects=True),
    )(x)


def pair_gather_kernel(n, sizes, x_ref, out_ref, local_sem, send1, recv1, send2, recv2, send3, recv3):
    me = flat_index(sizes)
    chips = n // 2
    chip = me // 2
    core = lax.rem(me, 2)
    partner = me + 1 - 2 * core
    enter_all(n, sizes, me)

    local = pltpu.make_async_copy(x_ref, out_ref.at[me], local_sem)
    local.start()
    first = pltpu.make_async_remote_copy(
        src_ref=x_ref, dst_ref=out_ref.at[me], send_sem=send1, recv_sem=recv1,
        device_id=device_of(partner, sizes), device_id_type=MESH,
    )
    first.start()
    local.wait()
    first.wait_send()
    pltpu.make_async_remote_copy(
        src_ref=x_ref, dst_ref=out_ref.at[partner], send_sem=send1, recv_sem=recv1,
        device_id=device_of(partner, sizes), device_id_type=MESH,
    ).wait_recv()

    def pair(c):
        return out_ref.at[pl.ds(2 * c, 2)]

    def target(k):
        return lax.rem(chip + 2 * k - 1 + core, chips)

    def source(k):
        return lax.rem(chip + chips - (2 * k - 1 + core), chips)

    count = (chips - core) // 2

    def send_out(k, carry):
        other = target(k)
        pltpu.make_async_remote_copy(
            src_ref=pair(chip), dst_ref=pair(chip), send_sem=send2.at[other], recv_sem=recv2.at[chip],
            device_id=device_of(2 * other + core, sizes), device_id_type=MESH,
        ).start()
        return carry

    lax.fori_loop(1, count + 1, send_out, 0)

    def take_in(k, carry):
        other = source(k)
        pltpu.make_async_remote_copy(
            src_ref=pair(other), dst_ref=pair(other), send_sem=send2.at[other], recv_sem=recv2.at[other],
            device_id=device_of(2 * other + core, sizes), device_id_type=MESH,
        ).wait_recv()
        pltpu.make_async_remote_copy(
            src_ref=pair(other), dst_ref=pair(other), send_sem=send3.at[other], recv_sem=recv3.at[other],
            device_id=device_of(partner, sizes), device_id_type=MESH,
        ).start()
        return carry

    lax.fori_loop(1, count + 1, take_in, 0)

    def sent_out(k, carry):
        other = target(k)
        pltpu.make_async_remote_copy(
            src_ref=pair(chip), dst_ref=pair(chip), send_sem=send2.at[other], recv_sem=recv2.at[chip],
            device_id=device_of(2 * other + core, sizes), device_id_type=MESH,
        ).wait_send()
        return carry

    lax.fori_loop(1, count + 1, sent_out, 0)

    def forwarded(k, carry):
        other = source(k)
        pltpu.make_async_remote_copy(
            src_ref=pair(other), dst_ref=pair(other), send_sem=send3.at[other], recv_sem=recv3.at[other],
            device_id=device_of(partner, sizes), device_id_type=MESH,
        ).wait_send()
        return carry

    lax.fori_loop(1, count + 1, forwarded, 0)

    other_count = (chips - (1 - core)) // 2

    def partner_source(k):
        return lax.rem(chip + chips - (2 * k - 1 + (1 - core)), chips)

    def from_partner(k, carry):
        other = partner_source(k)
        pltpu.make_async_remote_copy(
            src_ref=pair(other), dst_ref=pair(other), send_sem=send3.at[other], recv_sem=recv3.at[other],
            device_id=device_of(partner, sizes), device_id_type=MESH,
        ).wait_recv()
        return carry

    lax.fori_loop(1, other_count + 1, from_partner, 0)


def pair_gather(x, sizes, cid):
    n = math.prod(sizes)
    chips = n // 2
    dma = pltpu.SemaphoreType.DMA
    return pl.pallas_call(
        functools.partial(pair_gather_kernel, n, sizes),
        out_shape=jax.ShapeDtypeStruct((n,) + x.shape, x.dtype),
        in_specs=[pl.BlockSpec(memory_space=pltpu.VMEM)],
        out_specs=pl.BlockSpec(memory_space=pltpu.VMEM),
        scratch_shapes=[dma(()), dma(()), dma(()), dma((chips,)), dma((chips,)), dma((chips,)), dma((chips,))],
        compiler_params=pltpu.CompilerParams(collective_id=cid, has_side_effects=True),
    )(x)


def halving_orders(n, parts):
    bits = n.bit_length() - 1
    middle = list(range(1, bits - 1))
    orders = []
    for p in range(parts):
        shift = p % len(middle) if middle else 0
        orders.append(tuple([0] + middle[shift:] + middle[:shift] + [bits - 1]))
    return tuple(orders)


def halving_kernel(n, sizes, orders, cols, tile, groups, computed, *refs):
    count = sum(groups) - int(computed)
    sources = list(refs[:count])
    vec_ref, dq_ref, w_ref, res_ref = refs[count : count + 4]
    at = count + 4
    if computed:
        x_ref = refs[at]
        at += 1
    out_ref, vec_out, grad_out, work = refs[at : at + 4]
    at += 4
    if computed:
        made = refs[at]
        at += 1
        sources.insert(0, made)
    rest = refs[at:]
    grouped = []
    at = 0
    for g in groups:
        grouped.append(sources[at : at + g])
        at += g
    steps = len(orders[0])
    parts = len(orders)
    layout = []
    head = 0
    for group in grouped:
        size = sum(math.prod(s.shape[:-1]) for s in group) // n
        layout.append((group, size, head))
        head += size
    recvs = rest[:steps]
    local_sem, send_sems, recv_sems, vec_send, vec_recv = rest[steps:]
    me = flat_index(sizes)

    def partner_of(bit):
        mine = lax.rem(me // (2**bit), 2)
        return mine, me + (1 - 2 * mine) * (2**bit)

    enter_all(n, sizes, me)

    def vec_copy(k):
        peer = lax.rem(me + k, n)
        return pltpu.make_async_remote_copy(
            src_ref=vec_ref.at[peer], dst_ref=vec_out.at[me], send_sem=vec_send.at[k], recv_sem=vec_recv.at[me],
            device_id=device_of(peer, sizes), device_id_type=MESH,
        )

    def vec_start(k, carry):
        vec_copy(k).start()
        return carry

    lax.fori_loop(1, n, vec_start, 0)
    vec_out[me] = vec_ref[me]

    half = n // 2
    first = []
    issuers = []
    for p in range(parts):
        order = orders[p]
        mine, other = partner_of(order[0])
        column = pl.ds(p * cols, cols)

        def owner(j, side, order=order):
            o = side * (2 ** order[0])
            for m, bit in enumerate(order[1:]):
                o = o + lax.rem(j // (2 ** (steps - 2 - m)), 2) * (2**bit)
            return o

        def issue(j, carry, p=p, owner=owner, mine=mine, other=other, column=column, which=None):
            for o, dst, remote in ((owner(j, 1 - mine), recvs[0].at[p, j], True), (owner(j, mine), work.at[p, j], False)):
                for group, size, head in [layout[w] for w in which]:
                    offset = 0
                    for chosen in group:
                        split = math.prod(chosen.shape[:-1]) // size

                        def move(chosen=chosen, offset=offset, o=o, dst=dst, remote=remote, size=size, head=head):
                            if len(chosen.shape) == 3:
                                src_ref = chosen.at[o - offset, :, column]
                            else:
                                src_ref = chosen.at[pl.ds((o - offset) * size, size), column]
                            dst_ref = dst.at[pl.ds(head, size)]
                            if remote:
                                pltpu.make_async_remote_copy(
                                    src_ref=src_ref, dst_ref=dst_ref,
                                    send_sem=send_sems.at[p, 0], recv_sem=recv_sems.at[p, 0],
                                    device_id=device_of(other, sizes), device_id_type=MESH,
                                ).start()
                            else:
                                pltpu.make_async_copy(src_ref, dst_ref, local_sem.at[p]).start()

                        if len(group) == 1:
                            move()
                        else:
                            pl.when((o >= offset) & (o < offset + split))(move)
                        offset += split

            return carry

        issuers.append(issue)
        first.append(other)
    later = [0] if computed else []
    sooner = [w for w in range(len(layout)) if w not in later]
    for issue in issuers:
        lax.fori_loop(0, half, functools.partial(issue, which=sooner), 0)
    if computed:
        on_first = (((0,), (0,)), ((), ()))

        def product_t(t, carry):
            rows = pl.ds(pl.multiple_of(t * tile, tile), tile)
            made[rows, :] = lax.dot_general(
                dq_ref[:, rows], x_ref[...], on_first, preferred_element_type=jnp.float32
            ).astype(made.dtype)
            return carry

        lax.fori_loop(0, made.shape[0] // tile, product_t, 0)
        for issue in issuers:
            lax.fori_loop(0, half, functools.partial(issue, which=later), 0)
    for p in range(parts):
        whole = pltpu.make_async_remote_copy(
            src_ref=work.at[p, pl.ds(0, half)], dst_ref=recvs[0].at[p],
            send_sem=send_sems.at[p, 0], recv_sem=recv_sems.at[p, 0],
            device_id=device_of(first[p], sizes), device_id_type=MESH,
        )
        pltpu.make_async_copy(work.at[p, pl.ds(0, half)], work.at[p, pl.ds(0, half)], local_sem.at[p]).wait()
        whole.wait_recv()
        whole.wait_send()

        def accumulate0(i, carry, p=p):
            total = work[p, i].astype(jnp.float32) + recvs[0][p, i].astype(jnp.float32)
            work[p, i] = total.astype(work.dtype)
            return carry

        lax.fori_loop(0, half, accumulate0, 0)

    for step in range(1, steps):
        half = n >> (step + 1)
        copies = []
        for p in range(parts):
            mine, other = partner_of(orders[p][step])
            send = pltpu.make_async_remote_copy(
                src_ref=work.at[p, pl.ds((1 - mine) * half, half)], dst_ref=recvs[step].at[p],
                send_sem=send_sems.at[p, step], recv_sem=recv_sems.at[p, step],
                device_id=device_of(other, sizes), device_id_type=MESH,
            )
            send.start()
            copies.append((mine, send))
        if step == 1:
            def product(t, carry):
                rows = pl.ds(pl.multiple_of(t * tile, tile), tile)
                grad_out[rows, :] = (
                    jnp.dot(dq_ref[rows, :], w_ref[...], preferred_element_type=jnp.float32) + res_ref[rows, :]
                )
                return carry

            lax.fori_loop(0, grad_out.shape[0] // tile, product, 0)
        for p in range(parts):
            mine, send = copies[p]
            send.wait_recv()
            send.wait_send()

            def accumulate(i, carry, p=p, mine=mine, half=half, step=step):
                total = work[p, mine * half + i].astype(jnp.float32) + recvs[step][p, i].astype(jnp.float32)
                work[p, i] = total.astype(work.dtype)
                return carry

            lax.fori_loop(0, half, accumulate, 0)
    for p in range(parts):
        out_ref[:, p * cols : (p + 1) * cols] = work[p, 0].astype(out_ref.dtype)

    def vec_finish(k, carry):
        vec_copy(k).wait_send()
        src = lax.rem(me + n - k, n)
        pltpu.make_async_remote_copy(
            src_ref=vec_ref.at[src], dst_ref=vec_out.at[src], send_sem=vec_send.at[k], recv_sem=vec_recv.at[src],
            device_id=device_of(src, sizes), device_id_type=MESH,
        ).wait_recv()
        return carry

    lax.fori_loop(1, n, vec_finish, 0)


def halving_scatter(grouped, vec, grad_b, weight_t, residual, sizes, parts, cid, tokens=None):
    n = math.prod(sizes)
    computed = tokens is not None
    groups = tuple(len(g) for g in grouped)
    given = [s for g in grouped for s in g if s is not None]
    made_shape = (grad_b.shape[1], tokens.shape[1]) if computed else None
    assert not computed or made_shape[0] % 256 == 0
    shapes = [made_shape if s is None else s.shape for g in grouped for s in g]
    dtype = given[0].dtype
    width = shapes[0][-1]
    rows = sum(math.prod(s[:-1]) for s in shapes) // n
    cols = width // parts
    orders = halving_orders(n, parts)
    steps = len(orders[0])
    tile = 256
    dma = pltpu.SemaphoreType.DMA
    vmem = pl.BlockSpec(memory_space=pltpu.VMEM)
    scratch = [pltpu.VMEM((parts, n // 2, rows, cols), dtype)]
    if computed:
        scratch.append(pltpu.VMEM(made_shape, dtype))
    scratch += [pltpu.VMEM((parts, n >> (k + 1), rows, cols), dtype) for k in range(steps)]
    scratch += [dma((parts,)), dma((parts, steps)), dma((parts, steps)), dma((n,)), dma((n,))]
    return pl.pallas_call(
        functools.partial(halving_kernel, n, sizes, orders, cols, tile, groups, computed),
        out_shape=(
            jax.ShapeDtypeStruct((rows, parts * cols), jnp.float32),
            jax.ShapeDtypeStruct(vec.shape, vec.dtype),
            jax.ShapeDtypeStruct(residual.shape, jnp.float32),
        ),
        in_specs=[pl.BlockSpec(memory_space=pl.ANY)] * len(given) + [vmem] * (4 + int(computed)),
        out_specs=(vmem, vmem, vmem),
        scratch_shapes=scratch,
        compiler_params=pltpu.CompilerParams(
            collective_id=cid, has_side_effects=True, vmem_limit_bytes=60 * 1024 * 1024
        ),
    )(*given, vec, grad_b, weight_t, residual, *([tokens] if computed else []))


def contrastive(embed_b, gathered, partner_all, me):
    own_texts = embed_b.shape[0]
    all_texts = gathered.shape[0]
    chunk = min(all_texts, 1024)
    on_rows = (((1,), (1,)), ((), ()))

    def chunk_stats(c):
        rows_b = lax.dynamic_slice_in_dim(gathered, c * chunk, chunk)
        sim = lax.dot_general(rows_b, gathered, on_rows, preferred_element_type=jnp.float32) / logit_divisor
        column_ids = lax.broadcasted_iota(jnp.int32, sim.shape, 1)
        row_ids = lax.broadcasted_iota(jnp.int32, sim.shape, 0) + c * chunk
        masked = jnp.where(column_ids == row_ids, masked_value, sim)
        row_max = jnp.max(masked, -1, keepdims=True)
        log_sum = row_max + jnp.log(jnp.sum(jnp.exp(masked - row_max), -1, keepdims=True))
        wanted = lax.dynamic_slice_in_dim(partner_all, c * chunk, chunk)
        positive = jnp.sum(jnp.where(column_ids == wanted[:, None], sim, 0.0), -1)
        return log_sum[:, 0], positive

    if all_texts == chunk:
        log_sum_all, positive_all = chunk_stats(0)
    else:
        log_sum_all, positive_all = lax.map(chunk_stats, jnp.arange(all_texts // chunk))
        log_sum_all = log_sum_all.reshape(-1)
        positive_all = positive_all.reshape(-1)
    mean_loss = jnp.sum(log_sum_all - positive_all) / all_texts

    own_start = me * own_texts
    own_ids = lax.broadcasted_iota(jnp.int32, (own_texts,), 0) + own_start
    own_partner = lax.dynamic_slice_in_dim(partner_all, own_start, own_texts)
    own_log_sum = lax.dynamic_slice_in_dim(log_sum_all, own_start, own_texts)

    sim_rows = lax.dot_general(embed_b, gathered, on_rows, preferred_element_type=jnp.float32) / logit_divisor
    column_ids = lax.broadcasted_iota(jnp.int32, sim_rows.shape, 1)
    masked_rows = jnp.where(column_ids == own_ids[:, None], masked_value, sim_rows)
    grad_rows = (
        jnp.exp(masked_rows - own_log_sum[:, None]) - (column_ids == own_partner[:, None]).astype(jnp.float32)
    ).astype(jnp.bfloat16)

    sim_cols = lax.dot_general(gathered, embed_b, on_rows, preferred_element_type=jnp.float32) / logit_divisor
    row_ids = lax.broadcasted_iota(jnp.int32, sim_cols.shape, 0)
    masked_cols = jnp.where(row_ids == own_ids[None, :], masked_value, sim_cols)
    grad_cols = (
        jnp.exp(masked_cols - log_sum_all[:, None]) - (partner_all[:, None] == own_ids[None, :]).astype(jnp.float32)
    ).astype(jnp.bfloat16)

    on_tokens = (((0,), (0,)), ((), ()))
    embedding_gradient = (
        jnp.dot(grad_rows, gathered, preferred_element_type=jnp.float32)
        + lax.dot_general(grad_cols, gathered, on_tokens, preferred_element_type=jnp.float32)
    ) / logit_divisor
    return mean_loss, embedding_gradient


def shards(
    hidden_in,
    segments,
    partner,
    attn_weights,
    ffn_weights,
    vectors,
    attn_momentum,
    ffn_momentum,
    vector_momentum,
    attn_averaged,
    ffn_averaged,
    vector_averaged,
):
    sizes = tuple(lax.axis_size(name) for name in AXES)
    n_dev = math.prod(sizes)
    me = flat_index(sizes)
    vec_len = vectors.shape[0]
    small = jnp.concatenate([vectors, partner.astype(jnp.float32)])[None, :]
    small_all = small_gather(small, sizes, 0)[:, 0, :]
    vector_f = bf16_round(small_all[:, :vec_len].reshape(-1))
    partner_all = small_all[:, vec_len:].reshape(-1).astype(jnp.int32)
    attn_full, ffn_full = (
        lax.all_gather(attn_weights.astype(jnp.bfloat16), AXES, axis=1, tiled=True),
        lax.all_gather(ffn_weights.astype(jnp.bfloat16), AXES, axis=1, tiled=True),
    )
    width = attn_full.shape[0]
    hidden = ffn_full.shape[1] // 2
    query_bias = vector_f[0:width]
    value_bias = vector_f[width : 2 * width]
    output_bias = vector_f[2 * width : 3 * width]
    gain_first = vector_f[3 * width : 4 * width]
    shift_first = vector_f[4 * width : 5 * width]
    upper_bias = vector_f[5 * width : 5 * width + hidden]
    lower_bias = vector_f[5 * width + hidden : 6 * width + hidden]
    gain_second = vector_f[6 * width + hidden : 7 * width + hidden]
    shift_second = vector_f[7 * width + hidden : 8 * width + hidden]
    w_qkv = attn_full[:, : 3 * width]
    w_output = attn_full[:, 3 * width :]
    w_upper = ffn_full[:, :hidden]
    w_lower = ffn_full[:, hidden:]
    rows_dev, seq_len = segments.shape
    tokens_n = rows_dev * seq_len
    on_rows = (((1,), (1,)), ((), ()))
    on_tokens = (((0,), (0,)), ((), ()))
    qkv_bias = jnp.concatenate([query_bias, jnp.zeros_like(query_bias), value_bias])
    qkv_rows = (jnp.dot(hidden_in, w_qkv, preferred_element_type=jnp.float32) + qkv_bias).astype(
        jnp.bfloat16
    )
    heads = qkv_rows.reshape(rows_dev, seq_len, 3, HEADS, HD)
    query_rows = heads[:, :, 0]
    key_rows = heads[:, :, 1]
    value_rows = heads[:, :, 2]
    mixed, log_norm = attend_rows(query_rows, key_rows, value_rows, segments)
    mixed_flat = mixed.reshape(tokens_n, width)
    first_sum = (
        hidden_in.astype(jnp.float32)
        + jnp.dot(mixed_flat, w_output, preferred_element_type=jnp.float32)
        + output_bias
    )
    normed, normal_one, inverse_one = layer_norm_parts(first_sum, gain_first, shift_first)
    normed_r = bf16_round(normed)
    normed_b = normed_r.astype(jnp.bfloat16)
    upper = jnp.dot(normed_b, w_upper, preferred_element_type=jnp.float32) + upper_bias
    active_b = (0.5 * upper * (1.0 + lax.erf(upper / math.sqrt(2.0)))).astype(jnp.bfloat16)
    second_sum = (
        normed_r
        + lax.dot_general(active_b, w_lower, on_rows, preferred_element_type=jnp.float32)
        + lower_bias
    )
    result, normal_two, inverse_two = layer_norm_parts(second_sum, gain_second, shift_second)
    text_ids = jnp.arange(SEGS, dtype=jnp.int32)
    one_hot = (segments[:, None, :] == text_ids[None, :, None]).astype(jnp.float32)
    counts = jnp.sum(one_hot, -1, keepdims=True)
    pooled = (
        jnp.einsum(
            "rts,rsd->rtd",
            one_hot,
            result.reshape(rows_dev, seq_len, width),
            precision=lax.Precision.HIGHEST,
        )
        / counts
    ).reshape(-1, width)
    inv_norm = lax.rsqrt(jnp.sum(pooled * pooled, -1, keepdims=True) + pool_epsilon)
    embed_b = (pooled * inv_norm).astype(jnp.bfloat16)
    gathered_embeddings = pair_gather(embed_b, sizes, 2).reshape(-1, width)
    mean_loss, embedding_gradient = contrastive(embed_b, gathered_embeddings, partner_all, me)
    grad_pooled = inv_norm * embedding_gradient - pooled * (
        inv_norm * inv_norm * inv_norm
    ) * jnp.sum(embedding_gradient * pooled, -1, keepdims=True)
    derivative_output = jnp.einsum(
        "rts,rtd->rsd",
        one_hot,
        grad_pooled.reshape(rows_dev, SEGS, width) / counts,
        precision=lax.Precision.HIGHEST,
    ).reshape(tokens_n, width)
    grad_second, gain_two_grad, shift_two_grad = layer_norm_back(
        derivative_output, normal_two, inverse_two, gain_second
    )
    lower_bias_grad = jnp.sum(grad_second, 0)
    lower_grad_b = grad_second.astype(jnp.bfloat16)
    lower_w_grad_t = lax.dot_general(
        active_b, lower_grad_b, on_tokens, preferred_element_type=jnp.float32
    )
    grad_active = jnp.dot(lower_grad_b, w_lower, preferred_element_type=jnp.float32)
    cumulative = 0.5 * (1.0 + lax.erf(upper / math.sqrt(2.0)))
    density = jnp.exp(-0.5 * upper * upper) / math.sqrt(2.0 * math.pi)
    grad_upper = grad_active * (cumulative + upper * density)
    upper_bias_grad = jnp.sum(grad_upper, 0)
    upper_grad_b = grad_upper.astype(jnp.bfloat16)
    upper_w_grad_t = lax.dot_general(
        upper_grad_b, normed_b, on_tokens, preferred_element_type=jnp.float32
    )
    grad_normed = (
        lax.dot_general(upper_grad_b, w_upper, on_rows, preferred_element_type=jnp.float32)
        + grad_second
    )
    grad_first, gain_one_grad, shift_one_grad = layer_norm_back(
        grad_normed, normal_one, inverse_one, gain_first
    )
    output_bias_grad = jnp.sum(grad_first, 0)
    first_grad_b = grad_first.astype(jnp.bfloat16)
    output_w_grad_t = lax.dot_general(
        first_grad_b, mixed_flat, on_tokens, preferred_element_type=jnp.float32
    )
    grad_mixed = lax.dot_general(
        first_grad_b, w_output, on_rows, preferred_element_type=jnp.float32
    ).astype(jnp.bfloat16)
    grad_mixed = grad_mixed.reshape(rows_dev, seq_len, HEADS, HD)
    norm_tokens = jnp.swapaxes(log_norm, 1, 2).reshape(tokens_n, HEADS)
    qkv_grad = jnp.concatenate(
        attention_back(qkv_rows, grad_mixed.reshape(tokens_n, width), norm_tokens, segments, HEADS, HD), 1
    ).astype(jnp.float32)
    qkv_grad_f = bf16_round(qkv_grad)
    qkv_grad_b = qkv_grad_f.astype(jnp.bfloat16)
    query_bias_grad = jnp.sum(qkv_grad_f[:, :width], 0)
    value_bias_grad = jnp.sum(qkv_grad_f[:, 2 * width :], 0)
    qkv_w_grad_t = lax.dot_general(
        qkv_grad_b, hidden_in, on_tokens, preferred_element_type=jnp.float32
    )
    vector_grad = jnp.concatenate(
        [
            query_bias_grad,
            value_bias_grad,
            output_bias_grad,
            gain_one_grad,
            shift_one_grad,
            upper_bias_grad,
            lower_bias_grad,
            gain_two_grad,
            shift_two_grad,
        ]
    )
    attn_cols = (qkv_w_grad_t.shape[0] + output_w_grad_t.shape[0]) // n_dev
    ffn_cols = (upper_w_grad_t.shape[0] + lower_w_grad_t.shape[0]) // n_dev
    if attn_cols % 16 == 0 and ffn_cols % 16 == 0:
        grads = (
            (None, output_w_grad_t.astype(GRAD_SEND)),
            (upper_w_grad_t.astype(GRAD_SEND), lower_w_grad_t.astype(GRAD_SEND)),
        )
        made_from = hidden_in
    else:
        attn_blocks = jnp.concatenate(
            [qkv_w_grad_t.reshape(-1, attn_cols, width), output_w_grad_t.reshape(-1, attn_cols, width)], 0
        )
        ffn_blocks = jnp.concatenate(
            [upper_w_grad_t.reshape(-1, ffn_cols, width), lower_w_grad_t.reshape(-1, ffn_cols, width)], 0
        )
        grads = ((jnp.concatenate([attn_blocks, ffn_blocks], 1).astype(GRAD_SEND),),)
        made_from = None
    parts = 3
    mine_parts, vector_slots, input_grad = halving_scatter(
        grads, vector_grad.reshape(n_dev, 1, -1), qkv_grad_b, w_qkv.T, grad_first, sizes, parts, 3, made_from
    )
    vector_reduced = jnp.sum(vector_slots[:, 0, :], 0)
    joined_reduced = mine_parts
    attn_reduced = joined_reduced[:attn_cols].T
    ffn_reduced = joined_reduced[attn_cols:].T
    attn_new, attn_moment, attn_average = apply_update(
        attn_weights, attn_reduced, attn_momentum, attn_averaged, decay_rate
    )
    ffn_new, ffn_moment, ffn_average = apply_update(
        ffn_weights, ffn_reduced, ffn_momentum, ffn_averaged, decay_rate
    )
    vector_new, vector_moment, vector_average = apply_update(
        vectors, vector_reduced, vector_momentum, vector_averaged, 0.0
    )
    return (
        mean_loss,
        input_grad,
        attn_reduced,
        ffn_reduced,
        vector_reduced,
        attn_new,
        ffn_new,
        vector_new,
        attn_moment,
        ffn_moment,
        vector_moment,
        attn_average,
        ffn_average,
        vector_average,
    )


def solution(mesh):
    in_specs = (
        P(("dp", "rep"), None),
        P(("dp", "rep"), None),
        P(("dp", "rep")),
        P(None, ("dp", "rep")),
        P(None, ("dp", "rep")),
        P(("dp", "rep")),
        P(None, ("dp", "rep")),
        P(None, ("dp", "rep")),
        P(("dp", "rep")),
        P(None, ("dp", "rep")),
        P(None, ("dp", "rep")),
        P(("dp", "rep")),
    )
    out_specs = (
        P(),
        P(("dp", "rep"), None),
        P(None, ("dp", "rep")),
        P(None, ("dp", "rep")),
        P(("dp", "rep")),
        P(None, ("dp", "rep")),
        P(None, ("dp", "rep")),
        P(("dp", "rep")),
        P(None, ("dp", "rep")),
        P(None, ("dp", "rep")),
        P(("dp", "rep")),
        P(None, ("dp", "rep")),
        P(None, ("dp", "rep")),
        P(("dp", "rep")),
    )
    return jax.shard_map(shards, mesh=mesh, in_specs=in_specs, out_specs=out_specs, check_vma=False)
```
